32 devices in a mesh: dp: 8 (over z, y), pair: 4 (over x, core).
Axes of the slice: x: 2, y: 2, z: 4, core: 2. Of those that a mesh axis runs over, the one named last changes fastest.
Arguments:
- token_owner: int32 [64, 512, 1], P(('dp', 'pair')), may hold values from 0 to 7; in each aligned block of 1024 rows (0 to 1023, 1024 to 2047, ..., all dimensions but the last counted through in order) at most 256 rows name the same one
- token_row: int32 [64, 512], P(('dp', 'pair')), may hold values from 0 to 4015
- lengths: int32 [64], P(('dp', 'pair')), may hold values from 1 to 512, 20480 in all
- positives: int32 [64], replicated, may hold values from 0 to 63
- negatives: int32 [64, 7], replicated, may hold values from 0 to 63
- neg_counts: int32 [64], replicated, may hold values from 1 to 7
- embed_table: float32 [32128, 768], P('dp'), may hold values from -6 to 6
- embed_first: float32 [32128, 768], P('dp'), may hold values from -2.861023e-06 to 2.861023e-06
- embed_second: float32 [32128, 768], P('dp'), may hold values from 1.968368e-14 to 7.873472e-14
- qkv_weight: float32 [768, 2304], P(('dp', 'pair')), may hold values from -0.21875 to 0.21875
- qkv_first: float32 [768, 2304], P(('dp', 'pair')), may hold values from -5.722046e-06 to 5.722046e-06
- qkv_second: float32 [768, 2304], P(('dp', 'pair')), may hold values from 7.873472e-14 to 3.1493888e-13
- out_weight: float32 [768, 768], P(('dp', 'pair')), may hold values from -1.75 to 1.75
- out_first: float32 [768, 768], P(('dp', 'pair')), may hold values from -5.722046e-06 to 5.722046e-06
- out_second: float32 [768, 768], P(('dp', 'pair')), may hold values from 7.873472e-14 to 3.1493888e-13
- in_weight: float32 [768, 3072], P(('dp', 'pair')), may hold values from -0.21875 to 0.21875
- in_first: float32 [768, 3072], P(('dp', 'pair')), may hold values from -5.722046e-06 to 5.722046e-06
- in_second: float32 [768, 3072], P(('dp', 'pair')), may hold values from 7.873472e-14 to 3.1493888e-13
- down_weight: float32 [3072, 768], P(('dp', 'pair')), may hold values from -0.109375 to 0.109375
- down_first: float32 [3072, 768], P(('dp', 'pair')), may hold values from -5.722046e-06 to 5.722046e-06
- down_second: float32 [3072, 768], P(('dp', 'pair')), may hold values from 7.873472e-14 to 3.1493888e-13
- norm_gains: float32 [3, 768], replicated, may hold values from 0.5 to 1.5
- gains_first: float32 [3, 768], replicated, may hold values from -2.2888184e-05 to 2.2888184e-05
- gains_second: float32 [3, 768], replicated, may hold values from 1.2597555e-12 to 5.039022e-12
- position_bias: float32 [32, 12], replicated, may hold values from -3 to 3
- bias_first: float32 [32, 12], replicated, may hold values from -2.2888184e-05 to 2.2888184e-05
- bias_second: float32 [32, 12], replicated, may hold values from 1.2597555e-12 to 5.039022e-12
Outputs:
- loss_value: float32 [], replicated
- clip_norm: float32 [], replicated
- embed_new: float32 [32128, 768], P('dp')
- embed_first_new: float32 [32128, 768], P('dp')
- embed_second_new: float32 [32128, 768], P('dp')
- qkv_new: float32 [768, 2304], P(('dp', 'pair'))
- qkv_first_new: float32 [768, 2304], P(('dp', 'pair'))
- qkv_second_new: float32 [768, 2304], P(('dp', 'pair'))
- out_new: float32 [768, 768], P(('dp', 'pair'))
- out_first_new: float32 [768, 768], P(('dp', 'pair'))
- out_second_new: float32 [768, 768], P(('dp', 'pair'))
- in_new: float32 [768, 3072], P(('dp', 'pair'))
- in_first_new: float32 [768, 3072], P(('dp', 'pair'))
- in_second_new: float32 [768, 3072], P(('dp', 'pair'))
- down_new: float32 [3072, 768], P(('dp', 'pair'))
- down_first_new: float32 [3072, 768], P(('dp', 'pair'))
- down_second_new: float32 [3072, 768], P(('dp', 'pair'))
- gains_new: float32 [3, 768], replicated
- gains_first_new: float32 [3, 768], replicated
- gains_second_new: float32 [3, 768], replicated
- bias_new: float32 [32, 12], replicated
- bias_first_new: float32 [32, 12], replicated
- bias_second_new: float32 [32, 12], replicated
The draws below stay inside these ranges and needn't reach their ends.
Inputs may be any that keep to these rules, and one draw needn't show every extreme that they name: `token_owner`: within each aligned block of 1024 tokens, no owner is named by more than 256 tokens, a bound that some block reaches. The lengths add up to 20480, and the longest is exactly 512.
All inputs are finite; a program needn't handle non-finite values. No bound on the sum of `lengths` on one device may be relied on, other than what follows from the above.
Results may differ from the reference program's by a relative error of at most 0.012.
The reference program's roundings to bfloat16 on the way count: a program that leaves them out, or rounds other values in their place, can miss the bound.
Values may be sent and summed in bfloat16 or wider, within the bound.
A program may use at most 256 MiB of HBM per device.

```python
import math
import jax
import jax.numpy as jnp
import numpy as np
from jax import lax

D = 768
H = 12
HD = 64
FF = 3072
VOCAB = 32128
NB = 32
REACH = 128
L = 512
NEG = 7
STEP = 5
TOK_DEV = 1024
DOCS = 64
ROWS_DEV = 4016
CAP = 256
N_DP = 8


def place_ends(result, stream_key, smallest, high):
    shape = result.shape
    place = [jax.random.randint(jax.random.fold_in(stream_key, axis), (), 0, shape[axis]) for axis in range(len(shape))]
    result = result.at[tuple(place)].set(smallest)
    longest = shape.index(max(shape))
    place[longest] = (place[longest] + 1) % shape[longest]
    return result.at[tuple(place)].set(high)


def block_levels(rng, extent, split, low, top_value):
    def one(position, blocks):
        heights = jax.random.uniform(jax.random.fold_in(jax.random.fold_in(rng, 6), position), (blocks,), jnp.float32, low / len(split), top_value / len(split))
        return jnp.repeat(jnp.exp(heights), extent[position] // blocks).reshape((-1,) + (1,) * (len(extent) - position - 1))

    factor_of = one(*split[0])
    for cut in split[1:]:
        factor_of = factor_of * one(*cut)
    return factor_of


def profile(number_of, total, reach, skew):
    loads = [(1 << 20) // math.isqrt(rank ** skew) + 1 for rank in range(2, number_of + 1)]
    surplus, counts = total - reach - (number_of - 1), [1] * (number_of - 1)
    while surplus > 0:
        free = [i for i in range(number_of - 1) if counts[i] < reach]
        mass, budget = sum([loads[i] for i in free]), surplus
        for i in free:
            addition = min(reach - counts[i], max(1, budget * loads[i] // mass), surplus)
            counts[i] = counts[i] + addition
            surplus = surplus - addition
    return np.array([reach] + counts)


def ragged(own_key, amount, total, bound, lean):
    if amount == 2:
        one = jax.random.randint(own_key, (), max(1, total - bound), min(bound, total - 1) + 1)
        return jnp.stack([one, total - one])
    sizes = jnp.asarray(profile(amount, total, bound, lean), jnp.int32)
    couples = (amount - 1) // 2
    donor, receiver = sizes[1:1 + 2 * couples:2], sizes[2:2 + 2 * couples:2]
    slack = jnp.minimum(donor - 1, bound - receiver)
    passed = jax.random.randint(jax.random.fold_in(own_key, 1), (couples,), 0, 1 << 20) % (slack + 1)
    sizes = sizes.at[1:1 + 2 * couples:2].set(donor - passed).at[2:2 + 2 * couples:2].set(receiver + passed)
    return sizes[jax.random.permutation(jax.random.fold_in(own_key, 2), amount)]


def assign_block(key, own, number, rows, count, top, limit, skew):
    ranking = jax.random.permutation(key, count)
    packed, usual = portions_of(count, rows * top, limit, skew, True), portions_of(count, rows * top, limit, skew, False)
    places = jnp.arange(count)

    def named(sizes, offset_by):
        used = int((sizes > 0).sum())
        fixed = max(1, used // 4)
        passed = fixed + (places - fixed + offset_by * (used - fixed)) % max(1, count - fixed)
        return jnp.zeros((count,), jnp.int32).at[ranking[jnp.where(places < fixed, places, passed)]].set(jnp.asarray(sizes, jnp.int32))

    sizes = jnp.where(number % 4 == 0, named(packed, number // 4), named(usual, number - number // 4 - 1))
    mixed = jax.random.permutation(jax.random.fold_in(own, 3), count)
    donor, receiver = mixed[0:count // 2 * 2:2], mixed[1:count // 2 * 2:2]
    room = jnp.minimum(sizes[donor] - 1, limit - sizes[receiver]) // 2
    room = jnp.where((donor == ranking[0]) | (receiver == ranking[0]) | (sizes[receiver] == 0), 0, jnp.maximum(room, 0))
    passed = jax.random.randint(jax.random.fold_in(own, 4), (count // 2,), 0, 1 << 20) % (room + 1)
    sizes = sizes.at[donor].add(-passed).at[receiver].add(passed)
    members = jnp.searchsorted(jnp.cumsum(sizes), jnp.arange(rows * top), side="right").astype(jnp.int32)
    grid = members.reshape(top, rows).T
    grid = grid[jax.random.permutation(jax.random.fold_in(own, 1), rows)]
    offset_by = jax.random.randint(jax.random.fold_in(own, 2), (rows, 1), 0, top)
    return jnp.take_along_axis(grid, (jnp.arange(top)[None, :] + offset_by) % top, axis=1)


def portions_of(number_of, total, limit, lean, full):
    loads = [(1 << 20) // math.isqrt(grade ** lean) + 1 for grade in range(1, number_of + 1)]
    largest = limit if full else min(limit, max(-(-total // number_of), total * loads[0] // sum(loads)))
    least = 1 if total - largest >= number_of - 1 else 0
    holding, rest = [largest] + [least] * (number_of - 1), total - largest - least * (number_of - 1)
    while rest > 0:
        movable = [i for i in range(1, number_of) if holding[i] < largest] or [i for i in range(1, number_of) if holding[i] < limit]
        pool, left = sum([loads[i] for i in movable]), rest
        for i in movable:
            extra = min(limit - holding[i], max(1, left * loads[i] // pool), rest)
            holding[i] = holding[i] + extra
            rest = rest - extra
    return np.array(holding)


def centred(own_key, dims, deviation, bound, pieces=(), dtype=jnp.bfloat16):
    drawn = deviation * jax.random.normal(own_key, dims, jnp.float32)
    if pieces:
        drawn = drawn * block_levels(own_key, dims, pieces, -0.22, 0.18)
    return jnp.clip(drawn, -bound, bound).astype(dtype)


def setup_inputs(seed: int = 0) -> dict:
    streams_of = jax.random.split(jax.random.key(seed), 28)
    token_owner_keys = jax.random.split(jax.random.fold_in(streams_of[0], 1), DOCS * L // TOK_DEV)
    token_owner_turns = jax.random.permutation(jax.random.fold_in(streams_of[0], 3), DOCS * L // TOK_DEV)
    token_owner = jax.vmap(lambda own, number: assign_block(jax.random.fold_in(streams_of[0], 2), own, number, TOK_DEV, N_DP, 1, CAP, 2))(token_owner_keys, token_owner_turns).reshape((DOCS, L, 1))
    token_row = place_ends(jax.random.randint(streams_of[1], (DOCS, L), 0, ROWS_DEV), jax.random.fold_in(streams_of[1], 1), 0, ROWS_DEV - 1).astype(jnp.int32)
    lengths = ragged(streams_of[2], DOCS, DOCS * L * 5 // 8, L, 2).astype(jnp.int32)
    positives = place_ends(jax.random.randint(streams_of[3], (DOCS,), 0, DOCS), jax.random.fold_in(streams_of[3], 1), 0, DOCS - 1).astype(jnp.int32)
    negatives = place_ends(jax.random.randint(streams_of[4], (DOCS, NEG), 0, DOCS), jax.random.fold_in(streams_of[4], 1), 0, DOCS - 1).astype(jnp.int32)
    neg_counts = place_ends(jax.random.randint(streams_of[5], (DOCS,), 1, NEG + 1), jax.random.fold_in(streams_of[5], 1), 1, NEG).astype(jnp.int32)
    embed_table = centred(streams_of[6], (VOCAB, D), 1.0, 6.0, ((0, 8),), jnp.float32)
    embed_first = centred(streams_of[7], (VOCAB, D), (0.055 * (VOCAB * D + 4 * D * D + 2 * D * FF) ** -0.5 / 20), 2.86102294921875e-06, ((0, 8),), jnp.float32)
    embed_second = jnp.clip(jnp.exp(math.log(7.873472110831586e-14) - 1.3862944 * jax.random.uniform(streams_of[8], (VOCAB, D), jnp.float32) ** block_levels(streams_of[8], (VOCAB, D), ((0, 8),), -0.2, 0.2)), 1.9683680277078966e-14, 7.873472110831586e-14)
    qkv_weight = centred(streams_of[9], (D, 3 * D), D ** -0.5, 0.21875, ((0, 32),), jnp.float32)
    qkv_first = centred(streams_of[10], (D, 3 * D), (0.11 * (VOCAB * D + 4 * D * D + 2 * D * FF) ** -0.5 / 20), 5.7220458984375e-06, ((0, 32),), jnp.float32)
    qkv_second = jnp.clip(jnp.exp(math.log(3.1493888443326346e-13) - 1.3862944 * jax.random.uniform(streams_of[11], (D, 3 * D), jnp.float32) ** block_levels(streams_of[11], (D, 3 * D), ((0, 32),), -0.2, 0.2)), 7.873472110831586e-14, 3.1493888443326346e-13)
    out_weight = centred(streams_of[12], (D, D), (max(1, D // 64)) ** -0.5, 1.75, ((0, 32),), jnp.float32)
    out_first = centred(streams_of[13], (D, D), (0.11 * (VOCAB * D + 4 * D * D + 2 * D * FF) ** -0.5 / 20), 5.7220458984375e-06, ((0, 32),), jnp.float32)
    out_second = jnp.clip(jnp.exp(math.log(3.1493888443326346e-13) - 1.3862944 * jax.random.uniform(streams_of[14], (D, D), jnp.float32) ** block_levels(streams_of[14], (D, D), ((0, 32),), -0.2, 0.2)), 7.873472110831586e-14, 3.1493888443326346e-13)
    in_weight = centred(streams_of[15], (D, FF), D ** -0.5, 0.21875, ((0, 32),), jnp.float32)
    in_first = centred(streams_of[16], (D, FF), (0.11 * (VOCAB * D + 4 * D * D + 2 * D * FF) ** -0.5 / 20), 5.7220458984375e-06, ((0, 32),), jnp.float32)
    in_second = jnp.clip(jnp.exp(math.log(3.1493888443326346e-13) - 1.3862944 * jax.random.uniform(streams_of[17], (D, FF), jnp.float32) ** block_levels(streams_of[17], (D, FF), ((0, 32),), -0.2, 0.2)), 7.873472110831586e-14, 3.1493888443326346e-13)
    down_weight = centred(streams_of[18], (FF, D), FF ** -0.5, 0.109375, ((0, 32),), jnp.float32)
    down_first = centred(streams_of[19], (FF, D), (0.11 * (VOCAB * D + 4 * D * D + 2 * D * FF) ** -0.5 / 20), 5.7220458984375e-06, ((0, 32),), jnp.float32)
    down_second = jnp.clip(jnp.exp(math.log(3.1493888443326346e-13) - 1.3862944 * jax.random.uniform(streams_of[20], (FF, D), jnp.float32) ** block_levels(streams_of[20], (FF, D), ((0, 32),), -0.2, 0.2)), 7.873472110831586e-14, 3.1493888443326346e-13)
    norm_gains = jnp.clip(1.0 + 0.1 * jax.random.normal(streams_of[21], (3, D), jnp.float32), 0.5, 1.5)
    gains_first = centred(streams_of[22], (3, D), (0.44 * (VOCAB * D + 4 * D * D + 2 * D * FF) ** -0.5 / 20), 2.288818359375e-05, (), jnp.float32)
    gains_second = jnp.clip(jnp.exp(jax.random.uniform(streams_of[23], (3, D), jnp.float32, math.log(1.2597555377330538e-12), math.log(5.039022150932215e-12))), 1.2597555377330538e-12, 5.039022150932215e-12)
    position_bias = centred(streams_of[24], (NB, H), 0.5, 3.0, (), jnp.float32)
    bias_first = centred(streams_of[25], (NB, H), (0.44 * (VOCAB * D + 4 * D * D + 2 * D * FF) ** -0.5 / 20), 2.288818359375e-05, (), jnp.float32)
    bias_second = jnp.clip(jnp.exp(jax.random.uniform(streams_of[26], (NB, H), jnp.float32, math.log(1.2597555377330538e-12), math.log(5.039022150932215e-12))), 1.2597555377330538e-12, 5.039022150932215e-12)
    return dict(token_owner=token_owner, token_row=token_row, lengths=lengths, positives=positives, negatives=negatives, neg_counts=neg_counts, embed_table=embed_table, embed_first=embed_first, embed_second=embed_second, qkv_weight=qkv_weight, qkv_first=qkv_first, qkv_second=qkv_second, out_weight=out_weight, out_first=out_first, out_second=out_second, in_weight=in_weight, in_first=in_first, in_second=in_second, down_weight=down_weight, down_first=down_first, down_second=down_second, norm_gains=norm_gains, gains_first=gains_first, gains_second=gains_second, position_bias=position_bias, bias_first=bias_first, bias_second=bias_second)


rms_eps = 1e-06
clip_limit = 0.05
margin = 1.0
sim_scale = 20.0
beta_one = 0.9
beta_two = 0.999
adam_eps = 1e-08
HIGHEST = lax.Precision.HIGHEST

@jax.custom_vjp
def low(v):
    return lax.optimization_barrier(v.astype(jnp.bfloat16)).astype(jnp.float32)

@jax.custom_vjp
def low_back(v):
    return v

def low_keep(v):
    return (low(v), None)

def low_pass(kept, grad):
    return (grad,)

def back_keep(v):
    return (v, None)

def back_low(kept, grad):
    return (low(grad),)
low.defvjp(low_keep, low_pass)
low_back.defvjp(back_keep, back_low)

def bucket_of(offsets, bucket_count, reach_limit):
    half_count = bucket_count // 2
    exact_count = half_count // 2
    sign_base = jnp.where(offsets > 0, half_count, 0).astype(jnp.int32)
    distance = jnp.abs(offsets).astype(jnp.int32)
    far_bucket = jnp.full(offsets.shape, exact_count, jnp.int32)
    for level_index in range(1, half_count - exact_count):
        threshold = int(math.ceil(exact_count * (reach_limit / exact_count) ** (level_index / (half_count - exact_count)) - 1e-09))
        far_bucket = far_bucket + (distance >= threshold).astype(jnp.int32)
    return sign_base + jnp.where(distance < exact_count, distance, far_bucket)

def rms_norm(values, gain):
    return values * lax.rsqrt(lax.optimization_barrier(jnp.mean(values * values, axis=-1, keepdims=True)) + rms_eps) * gain

def matmul(left, right):
    return jnp.dot(left, right, precision=HIGHEST)

def margin_loss(pooled, positives, negatives, neg_counts):
    unit = pooled * lax.rsqrt(lax.optimization_barrier(jnp.sum(pooled * pooled, axis=-1, keepdims=True)) + 1e-06)
    similar = sim_scale * jnp.dot(unit, unit.T, precision=HIGHEST)
    chosen = jnp.take_along_axis(similar, positives[:, None], axis=1)
    against = jnp.take_along_axis(similar, negatives, axis=1)
    live_slots = jnp.arange(negatives.shape[1])[None, :] < neg_counts[:, None]
    terms = jnp.where(live_slots, jax.nn.softplus(margin - chosen + against), 0.0)
    return jnp.mean(lax.optimization_barrier(jnp.sum(terms, axis=1)) / neg_counts.astype(jnp.float32))

def doc_forward(embedded_rows, doc_length, matrices, gain_rows, bias_full):
    qkv_mat, out_mat, in_mat, down_mat = matrices
    live_keys = jnp.arange(L) < doc_length
    normed = low(rms_norm(embedded_rows, gain_rows[0]))
    qkv_rows = low_back(low(matmul(normed, qkv_mat)))
    query_heads = qkv_rows[:, :D].reshape(L, H, HD)
    key_heads = qkv_rows[:, D:2 * D].reshape(L, H, HD)
    value_heads = qkv_rows[:, 2 * D:].reshape(L, H, HD)
    scores = low_back(jnp.einsum('qhd,khd->hqk', query_heads, key_heads, precision=HIGHEST) * 0.125 + bias_full)
    scores = jnp.where(live_keys[None, None, :], scores, -1000000000.0)
    probabilities = low(jax.nn.softmax(scores, axis=-1))
    attended = jnp.einsum('hqk,khd->qhd', probabilities, value_heads, precision=HIGHEST).reshape(L, D)
    attended = low_back(low(attended))
    residual = embedded_rows + low_back(matmul(attended, out_mat))
    normed_two = low(rms_norm(residual, gain_rows[1]))
    hidden = low(jax.nn.relu(low_back(matmul(normed_two, in_mat))))
    output_rows = residual + low_back(matmul(hidden, down_mat))
    normed_three = rms_norm(output_rows, gain_rows[2])
    return lax.optimization_barrier(jnp.sum(jnp.where(live_keys[:, None], normed_three, 0.0), axis=0)) / doc_length.astype(jnp.float32)

def adam_step(weight, first, second, grad, rate, shrink):
    first_new = beta_one * first + (1.0 - beta_one) * grad
    second_new = beta_two * second + (1.0 - beta_two) * grad * grad
    first_hat = first_new / (1.0 - beta_one ** STEP)
    second_hat = second_new / (1.0 - beta_two ** STEP)
    weight_new = weight - rate * (first_hat / (jnp.sqrt(second_hat) + adam_eps) + shrink * weight)
    return (weight_new, first_new, second_new)

def reference(token_owner, token_row, lengths, positives, negatives, neg_counts, embed_table, embed_first, embed_second, qkv_weight, qkv_first, qkv_second, out_weight, out_first, out_second, in_weight, in_first, in_second, down_weight, down_first, down_second, norm_gains, gains_first, gains_second, position_bias, bias_first, bias_second):
    token_ids = (token_owner[:, :, 0] * ROWS_DEV + token_row).astype(jnp.int32)
    positions = jnp.arange(L)
    buckets = bucket_of(positions[None, :] - positions[:, None], NB, REACH)

    def forward(parameters):
        table_w, qkv_w, out_w, in_w, down_w, gain_w, bias_w = parameters
        matrices = (low(qkv_w), low(out_w), low(in_w), low(down_w))
        embedded = low(table_w[token_ids])
        bias_full = jnp.transpose(bias_w[buckets], (2, 0, 1))

        def group_pool(group):
            group_rows, group_lengths = group
            return jax.vmap(lambda one_rows, one_length: doc_forward(one_rows, one_length, matrices, gain_w, bias_full))(group_rows, group_lengths)
        pooled = lax.map(jax.checkpoint(group_pool), (embedded.reshape(DOCS // 8, 8, L, D), lengths.reshape(DOCS // 8, 8)))
        return margin_loss(pooled.reshape(DOCS, D), positives, negatives, neg_counts)
    parameters = (embed_table, qkv_weight, out_weight, in_weight, down_weight, norm_gains, position_bias)
    loss_value, pullback = jax.vjp(forward, parameters)
    gradients = pullback(jnp.ones((), jnp.float32))[0]
    squares_total = jnp.sum(jnp.stack([jnp.sum(grad_piece * grad_piece) for grad_piece in gradients]))
    clip_norm = jnp.sqrt(squares_total)
    factor = jnp.minimum(1.0, clip_limit / clip_norm)
    clipped = [grad_piece * factor for grad_piece in gradients]
    table_out = adam_step(embed_table, embed_first, embed_second, clipped[0], 1.0, 0.01)
    qkv_out = adam_step(qkv_weight, qkv_first, qkv_second, clipped[1], 0.05, 0.01)
    out_out = adam_step(out_weight, out_first, out_second, clipped[2], 0.05, 0.01)
    in_out = adam_step(in_weight, in_first, in_second, clipped[3], 0.05, 0.01)
    down_out = adam_step(down_weight, down_first, down_second, clipped[4], 0.05, 0.01)
    gains_out = adam_step(norm_gains, gains_first, gains_second, clipped[5], 1.0, 0.0)
    bias_out = adam_step(position_bias, bias_first, bias_second, clipped[6], 0.3, 0.0)
    return (loss_value, clip_norm, table_out[0], table_out[1], table_out[2], qkv_out[0], qkv_out[1], qkv_out[2], out_out[0], out_out[1], out_out[2], in_out[0], in_out[1], in_out[2], down_out[0], down_out[1], down_out[2], gains_out[0], gains_out[1], gains_out[2], bias_out[0], bias_out[1], bias_out[2])
```

```python
import math

import jax
import jax.numpy as jnp
from jax import lax
from jax.sharding import PartitionSpec as P

REACH = 128
STEP = 5


rms_eps = 1e-06
clip_limit = 0.05
margin = 1.0
sim_scale = 20.0
beta_one = 0.9
beta_two = 0.999
adam_eps = 1e-08
HIGHEST = lax.Precision.HIGHEST
CONTRACT_ROWS = (((0,), (0,)), ((), ()))
CONTRACT_COLS = (((1,), (1,)), ((), ()))


def bucket_of(offsets, bucket_count, reach_limit):
    half_count = bucket_count // 2
    exact_count = half_count // 2
    sign_base = jnp.where(offsets > 0, half_count, 0).astype(jnp.int32)
    distance = jnp.abs(offsets)
    far_bucket = jnp.full(offsets.shape, exact_count, jnp.int32)
    for level_index in range(1, half_count - exact_count):
        threshold = int(
            math.ceil(
                exact_count
                * (reach_limit / exact_count) ** (level_index / (half_count - exact_count))
                - 1e-09
            )
        )
        far_bucket = far_bucket + (distance >= threshold).astype(jnp.int32)
    return sign_base + jnp.where(distance < exact_count, distance, far_bucket)


def rms_forward(values, gain):
    inverse = lax.rsqrt(jnp.mean(values * values, axis=-1, keepdims=True) + rms_eps)
    return (values * inverse * gain, inverse)


def rms_backward(values, inverse, gain, upstream):
    scaled = upstream * gain
    normed = values * inverse
    grad_values = inverse * (scaled - normed * jnp.mean(scaled * normed, axis=-1, keepdims=True))
    return (grad_values, jnp.sum(upstream * normed, axis=0))


def margin_loss(pooled, positives, negatives, neg_counts):
    unit = pooled * lax.rsqrt(jnp.sum(pooled * pooled, axis=-1, keepdims=True) + 1e-06)
    similar = sim_scale * jnp.dot(unit, unit.T, precision=HIGHEST)
    chosen = jnp.take_along_axis(similar, positives[:, None], axis=1)
    against = jnp.take_along_axis(similar, negatives, axis=1)
    live_slots = jnp.arange(negatives.shape[1])[None, :] < neg_counts[:, None]
    terms = jnp.where(live_slots, jax.nn.softplus(margin - chosen + against), 0.0)
    return jnp.mean(jnp.sum(terms, axis=1) / neg_counts.astype(jnp.float32))


def doc_scores(query_heads, key_heads, bias_full, live_keys):
    scores = (
        jnp.einsum("qhd,khd->hqk", query_heads, key_heads, preferred_element_type=jnp.float32)
        * 0.125
        + bias_full
    )
    return jnp.where(live_keys[None, None, :], scores, -1000000000.0)


def attend_forward(query_heads, key_heads, value_heads, bias_full, live_keys):
    scores = doc_scores(query_heads, key_heads, bias_full, live_keys)
    highest = jnp.max(scores, axis=-1, keepdims=True)
    weights = jnp.exp(scores - highest)
    totals = jnp.sum(weights, axis=-1, keepdims=True)
    probabilities = (weights / totals).astype(jnp.bfloat16)
    attended = jnp.einsum(
        "hqk,khd->qhd", probabilities, value_heads, preferred_element_type=jnp.float32
    )
    return (attended, highest + jnp.log(totals))


def attend_backward(
    query_heads, key_heads, value_heads, bias_full, live_keys, logsum, grad_attended
):
    probabilities = jnp.exp(doc_scores(query_heads, key_heads, bias_full, live_keys) - logsum)
    grad_value = jnp.einsum(
        "hqk,qhd->khd",
        probabilities.astype(jnp.bfloat16),
        grad_attended,
        preferred_element_type=jnp.float32,
    )
    grad_prob = jnp.einsum(
        "qhd,khd->hqk", grad_attended, value_heads, preferred_element_type=jnp.float32
    )
    grad_score = probabilities * (
        grad_prob - jnp.sum(probabilities * grad_prob, axis=-1, keepdims=True)
    )
    grad_low = grad_score.astype(jnp.bfloat16)
    grad_query = (
        jnp.einsum("hqk,khd->qhd", grad_low, key_heads, preferred_element_type=jnp.float32) * 0.125
    )
    grad_key = (
        jnp.einsum("hqk,qhd->khd", grad_low, query_heads, preferred_element_type=jnp.float32)
        * 0.125
    )
    return (grad_query, grad_key, grad_value, grad_low)


def adam_step(weight, first, second, grad, rate, shrink):
    first_new = beta_one * first + (1.0 - beta_one) * grad
    second_new = beta_two * second + (1.0 - beta_two) * grad * grad
    first_hat = first_new / (1.0 - beta_one**STEP)
    second_hat = second_new / (1.0 - beta_two**STEP)
    weight_new = weight - rate * (first_hat / (jnp.sqrt(second_hat) + adam_eps) + shrink * weight)
    return (weight_new, first_new, second_new)


def local(
    token_owner,
    token_row,
    lengths,
    positives,
    negatives,
    neg_counts,
    embed_table,
    embed_first,
    embed_second,
    qkv_weight,
    qkv_first,
    qkv_second,
    out_weight,
    out_first,
    out_second,
    in_weight,
    in_first,
    in_second,
    down_weight,
    down_first,
    down_second,
    norm_gains,
    gains_first,
    gains_second,
    position_bias,
    bias_first,
    bias_second,
):
    doc_count = lengths.shape[0]
    seq_len = token_row.shape[1]
    model_width = embed_table.shape[1]
    head_count = position_bias.shape[1]
    bucket_count = position_bias.shape[0]
    tok_total = doc_count * seq_len
    owners = lax.axis_size("dp")
    capacity = max(2, 2 * tok_total // owners)
    low_mats = (
        qkv_weight.astype(jnp.bfloat16),
        out_weight.astype(jnp.bfloat16),
        in_weight.astype(jnp.bfloat16),
        down_weight.astype(jnp.bfloat16),
    )
    qkv_full, out_full, in_full, down_full = (
        lax.all_gather(low_mats[0], ("dp", "pair"), axis=0, tiled=True),
        lax.all_gather(low_mats[1], ("dp", "pair"), axis=0, tiled=True),
        lax.all_gather(low_mats[2], ("dp", "pair"), axis=0, tiled=True),
        lax.all_gather(low_mats[3], ("dp", "pair"), axis=0, tiled=True),
    )
    tok_owner = token_owner.reshape(-1)
    tok_row = token_row.reshape(-1)
    owner_hits = (tok_owner[:, None] == jnp.arange(owners, dtype=jnp.int32)[None, :]).astype(
        jnp.int32
    )
    slot_rank = jnp.sum((jnp.cumsum(owner_hits, axis=0) - 1) * owner_hits, axis=1)
    requests = jnp.zeros((owners, capacity), jnp.int32).at[tok_owner, slot_rank].set(tok_row)
    asked_rows = lax.all_to_all(requests, "dp", split_axis=0, concat_axis=0, tiled=True)
    looked = jnp.take(embed_table, asked_rows.reshape(-1), axis=0).astype(jnp.bfloat16)
    answer = lax.all_to_all(
        looked.reshape(asked_rows.shape + (model_width,)),
        "dp",
        split_axis=0,
        concat_axis=0,
        tiled=True,
    )
    replies, asked_rows = (answer, asked_rows)
    embedded = replies[tok_owner, slot_rank].astype(jnp.float32)
    positions = jnp.arange(seq_len)
    live = positions[None, :] < lengths[:, None]
    pair_buckets = bucket_of(
        (positions[None, :] - positions[:, None]).reshape(-1), bucket_count, REACH
    )
    pair_hits = (jnp.arange(bucket_count)[:, None] == pair_buckets[None, :]).astype(jnp.float32)
    bias_full = jnp.dot(position_bias.T, pair_hits, precision=HIGHEST).reshape(
        head_count, seq_len, seq_len
    )
    bucket_map = pair_hits.astype(jnp.bfloat16)

    def split_doc(source, doc_index):
        doc_rows = source[doc_index * seq_len : (doc_index + 1) * seq_len]
        return tuple(
            (
                doc_rows[:, member * model_width : (member + 1) * model_width].reshape(
                    seq_len, head_count, -1
                )
                for member in range(3)
            )
        )

    normed_one, inverse_one = rms_forward(embedded, norm_gains[0])
    normed_one = normed_one.astype(jnp.bfloat16)
    qkv_rows = jnp.dot(normed_one, qkv_full, preferred_element_type=jnp.float32).astype(
        jnp.bfloat16
    )
    attended_parts = []
    logsum_parts = []
    for doc_index in range(doc_count):
        query_heads, key_heads, value_heads = split_doc(qkv_rows, doc_index)
        doc_out, logsum = attend_forward(
            query_heads, key_heads, value_heads, bias_full, live[doc_index]
        )
        attended_parts.append(doc_out.reshape(seq_len, model_width))
        logsum_parts.append(logsum)
    attended = jnp.concatenate(attended_parts, axis=0).astype(jnp.bfloat16)
    residual = embedded + jnp.dot(attended, out_full, preferred_element_type=jnp.float32)
    normed_two, inverse_two = rms_forward(residual, norm_gains[1])
    normed_two = normed_two.astype(jnp.bfloat16)
    hidden = jax.nn.relu(jnp.dot(normed_two, in_full, preferred_element_type=jnp.float32)).astype(
        jnp.bfloat16
    )
    output_rows = residual + jnp.dot(hidden, down_full, preferred_element_type=jnp.float32)
    normed_three, inverse_three = rms_forward(output_rows, norm_gains[2])
    live_rows = live.reshape(-1, 1)
    length_float = lengths.astype(jnp.float32)
    pooled_local = (
        jnp.sum(
            jnp.where(live_rows, normed_three, 0.0).reshape(doc_count, seq_len, model_width), axis=1
        )
        / length_float[:, None]
    )
    pooled_all = lax.all_gather(pooled_local, ("dp", "pair"), axis=0, tiled=True)
    loss_value, loss_pullback = jax.vjp(
        lambda pooled_in: margin_loss(pooled_in, positives, negatives, neg_counts), pooled_all
    )
    grad_pooled_all = loss_pullback(jnp.ones((), jnp.float32))[0]
    grad_pooled = lax.dynamic_slice_in_dim(
        grad_pooled_all, lax.axis_index(("dp", "pair")) * doc_count, doc_count, 0
    )
    grad_three = jnp.where(
        live_rows, jnp.repeat(grad_pooled / length_float[:, None], seq_len, axis=0), 0.0
    )
    qkv_back, out_back, in_back, down_back = (qkv_full, out_full, in_full, down_full)
    grad_output, gain_three = rms_backward(output_rows, inverse_three, norm_gains[2], grad_three)
    grad_branch = grad_output.astype(jnp.bfloat16)
    grad_down = lax.dot_general(
        hidden, grad_branch, CONTRACT_ROWS, preferred_element_type=jnp.float32
    )
    grad_hidden = lax.dot_general(
        grad_branch, down_back, CONTRACT_COLS, preferred_element_type=jnp.float32
    )
    grad_pre = jnp.where(hidden > 0, grad_hidden, 0.0).astype(jnp.bfloat16)
    grad_in = lax.dot_general(
        normed_two, grad_pre, CONTRACT_ROWS, preferred_element_type=jnp.float32
    )
    grad_normed_two = lax.dot_general(
        grad_pre, in_back, CONTRACT_COLS, preferred_element_type=jnp.float32
    )
    grad_res_part, gain_two = rms_backward(residual, inverse_two, norm_gains[1], grad_normed_two)
    grad_residual = grad_output + grad_res_part
    grad_attn_branch = grad_residual.astype(jnp.bfloat16)
    grad_out = lax.dot_general(
        attended, grad_attn_branch, CONTRACT_ROWS, preferred_element_type=jnp.float32
    )
    grad_attended = lax.dot_general(
        grad_attn_branch, out_back, CONTRACT_COLS, preferred_element_type=jnp.float32
    ).astype(jnp.bfloat16)
    grad_qkv_parts = []
    bias_grad_heads = jnp.zeros((head_count, bucket_count), jnp.float32)
    for doc_index in range(doc_count):
        query_heads, key_heads, value_heads = split_doc(qkv_rows, doc_index)
        grad_doc = grad_attended[doc_index * seq_len : (doc_index + 1) * seq_len].reshape(
            seq_len, head_count, -1
        )
        grad_query, grad_key, grad_value, grad_low = attend_backward(
            query_heads,
            key_heads,
            value_heads,
            bias_full,
            live[doc_index],
            logsum_parts[doc_index],
            grad_doc,
        )
        grad_qkv_parts.append(
            jnp.concatenate(
                [
                    grad_query.reshape(seq_len, model_width),
                    grad_key.reshape(seq_len, model_width),
                    grad_value.reshape(seq_len, model_width),
                ],
                axis=1,
            )
        )
        bias_grad_heads = bias_grad_heads + lax.dot_general(
            grad_low.reshape(head_count, -1),
            bucket_map,
            CONTRACT_COLS,
            preferred_element_type=jnp.float32,
        )
    bias_grad_local = bias_grad_heads.T
    grad_qkv_rows = jnp.concatenate(grad_qkv_parts, axis=0).astype(jnp.bfloat16)
    grad_qkv = lax.dot_general(
        normed_one, grad_qkv_rows, CONTRACT_ROWS, preferred_element_type=jnp.float32
    )
    grad_normed_one = lax.dot_general(
        grad_qkv_rows, qkv_back, CONTRACT_COLS, preferred_element_type=jnp.float32
    )
    grad_emb_part, gain_one = rms_backward(embedded, inverse_one, norm_gains[0], grad_normed_one)
    grad_embedded = grad_residual + grad_emb_part
    sendback = (
        jnp.zeros((owners, capacity, model_width), jnp.bfloat16)
        .at[tok_owner, slot_rank]
        .set(grad_embedded.astype(jnp.bfloat16))
    )
    arrived = lax.all_to_all(sendback, "dp", split_axis=0, concat_axis=0, tiled=True)
    table_grad = jax.ops.segment_sum(
        arrived.reshape(-1, model_width).astype(jnp.float32),
        asked_rows.reshape(-1),
        num_segments=embed_table.shape[0],
    )
    table_grad = lax.psum(table_grad.astype(jnp.bfloat16), "pair").astype(jnp.float32)
    weight_grads = (
        lax.psum_scatter(grad_qkv.astype(jnp.bfloat16), ("dp", "pair"), scatter_dimension=0, tiled=True).astype(jnp.float32),
        lax.psum_scatter(grad_out.astype(jnp.bfloat16), ("dp", "pair"), scatter_dimension=0, tiled=True).astype(jnp.float32),
        lax.psum_scatter(grad_in.astype(jnp.bfloat16), ("dp", "pair"), scatter_dimension=0, tiled=True).astype(jnp.float32),
        lax.psum_scatter(grad_down.astype(jnp.bfloat16), ("dp", "pair"), scatter_dimension=0, tiled=True).astype(jnp.float32),
    )
    pair_first = (lax.axis_index("pair") == 0).astype(jnp.float32)
    square_part = jnp.sum(
        jnp.stack([jnp.sum(grad_piece * grad_piece) for grad_piece in weight_grads])
    ) + pair_first * jnp.sum(table_grad * table_grad)
    gain_grad, bias_grad, square_sum = lax.psum(
        (jnp.stack([gain_one, gain_two, gain_three]), bias_grad_local, square_part), ("dp", "pair")
    )
    clip_norm = jnp.sqrt(
        square_sum + jnp.sum(gain_grad * gain_grad) + jnp.sum(bias_grad * bias_grad)
    )
    factor = jnp.minimum(1.0, clip_limit / clip_norm)
    table_out = adam_step(embed_table, embed_first, embed_second, table_grad * factor, 1.0, 0.01)
    qkv_out = adam_step(qkv_weight, qkv_first, qkv_second, weight_grads[0] * factor, 0.05, 0.01)
    out_out = adam_step(out_weight, out_first, out_second, weight_grads[1] * factor, 0.05, 0.01)
    in_out = adam_step(in_weight, in_first, in_second, weight_grads[2] * factor, 0.05, 0.01)
    down_out = adam_step(down_weight, down_first, down_second, weight_grads[3] * factor, 0.05, 0.01)
    gains_out = adam_step(norm_gains, gains_first, gains_second, gain_grad * factor, 1.0, 0.0)
    bias_out = adam_step(position_bias, bias_first, bias_second, bias_grad * factor, 0.3, 0.0)
    return (
        loss_value,
        clip_norm,
        table_out[0],
        table_out[1],
        table_out[2],
        qkv_out[0],
        qkv_out[1],
        qkv_out[2],
        out_out[0],
        out_out[1],
        out_out[2],
        in_out[0],
        in_out[1],
        in_out[2],
        down_out[0],
        down_out[1],
        down_out[2],
        gains_out[0],
        gains_out[1],
        gains_out[2],
        bias_out[0],
        bias_out[1],
        bias_out[2],
    )


def solution(mesh):
    return jax.shard_map(
        local,
        mesh=mesh,
        in_specs=(
            P(("dp", "pair"), None, None),
            P(("dp", "pair"), None),
            P(("dp", "pair")),
            P(),
            P(),
            P(),
            P("dp", None),
            P("dp", None),
            P("dp", None),
            P(("dp", "pair"), None),
            P(("dp", "pair"), None),
            P(("dp", "pair"), None),
            P(("dp", "pair"), None),
            P(("dp", "pair"), None),
            P(("dp", "pair"), None),
            P(("dp", "pair"), None),
            P(("dp", "pair"), None),
            P(("dp", "pair"), None),
            P(("dp", "pair"), None),
            P(("dp", "pair"), None),
            P(("dp", "pair"), None),
            P(),
            P(),
            P(),
            P(),
            P(),
            P(),
        ),
        out_specs=(
            P(),
            P(),
            P("dp", None),
            P("dp", None),
            P("dp", None),
            P(("dp", "pair"), None),
            P(("dp", "pair"), None),
            P(("dp", "pair"), None),
            P(("dp", "pair"), None),
            P(("dp", "pair"), None),
            P(("dp", "pair"), None),
            P(("dp", "pair"), None),
            P(("dp", "pair"), None),
            P(("dp", "pair"), None),
            P(("dp", "pair"), None),
            P(("dp", "pair"), None),
            P(("dp", "pair"), None),
            P(),
            P(),
            P(),
            P(),
            P(),
            P(),
        ),
        check_vma=False,
    )
```

```python
import functools
import math

import jax
import jax.numpy as jnp
from jax import lax
from jax.experimental import pallas as pl
from jax.experimental.pallas import tpu as pltpu
from jax.sharding import PartitionSpec as P

REACH = 128
STEP = 5


rms_eps = 1e-06
clip_limit = 0.05
margin = 1.0
sim_scale = 20.0
beta_one = 0.9
beta_two = 0.999
adam_eps = 1e-08
HIGHEST = lax.Precision.HIGHEST
CONTRACT_ROWS = (((0,), (0,)), ((), ()))
CONTRACT_COLS = (((1,), (1,)), ((), ()))


def bucket_of(offsets, bucket_count, reach_limit):
    half_count = bucket_count // 2
    exact_count = half_count // 2
    sign_base = jnp.where(offsets > 0, half_count, 0).astype(jnp.int32)
    distance = jnp.abs(offsets)
    far_bucket = jnp.full(offsets.shape, exact_count, jnp.int32)
    for level_index in range(1, half_count - exact_count):
        threshold = int(
            math.ceil(
                exact_count
                * (reach_limit / exact_count) ** (level_index / (half_count - exact_count))
                - 1e-09
            )
        )
        far_bucket = far_bucket + (distance >= threshold).astype(jnp.int32)
    return sign_base + jnp.where(distance < exact_count, distance, far_bucket)


def rms_forward(values, gain):
    inverse = lax.rsqrt(jnp.mean(values * values, axis=-1, keepdims=True) + rms_eps)
    return (values * inverse * gain, inverse)


def rms_backward(values, inverse, gain, upstream):
    scaled = upstream * gain
    normed = values * inverse
    grad_values = inverse * (scaled - normed * jnp.mean(scaled * normed, axis=-1, keepdims=True))
    return (grad_values, jnp.sum(upstream * normed, axis=0))


def margin_loss(pooled, positives, negatives, neg_counts):
    unit = pooled * lax.rsqrt(jnp.sum(pooled * pooled, axis=-1, keepdims=True) + 1e-06)
    similar = sim_scale * jnp.dot(unit, unit.T, precision=HIGHEST)
    chosen = jnp.take_along_axis(similar, positives[:, None], axis=1)
    against = jnp.take_along_axis(similar, negatives, axis=1)
    live_slots = jnp.arange(negatives.shape[1])[None, :] < neg_counts[:, None]
    terms = jnp.where(live_slots, jax.nn.softplus(margin - chosen + against), 0.0)
    return jnp.mean(jnp.sum(terms, axis=1) / neg_counts.astype(jnp.float32))


def doc_scores(query_heads, key_heads, bias_full, live_keys):
    scores = (
        jnp.einsum("qhd,khd->hqk", query_heads, key_heads, preferred_element_type=jnp.float32)
        * 0.125
        + bias_full
    )
    return jnp.where(live_keys[None, None, :], scores, -1000000000.0)


def attend_forward(query_heads, key_heads, value_heads, bias_full, live_keys):
    scores = doc_scores(query_heads, key_heads, bias_full, live_keys)
    highest = jnp.max(scores, axis=-1, keepdims=True)
    weights = jnp.exp(scores - highest)
    totals = jnp.sum(weights, axis=-1, keepdims=True)
    probabilities = (weights / totals).astype(jnp.bfloat16)
    attended = jnp.einsum(
        "hqk,khd->qhd", probabilities, value_heads, preferred_element_type=jnp.float32
    )
    return (attended, highest + jnp.log(totals))


def attend_backward(
    query_heads, key_heads, value_heads, bias_full, live_keys, logsum, grad_attended
):
    probabilities = jnp.exp(doc_scores(query_heads, key_heads, bias_full, live_keys) - logsum)
    grad_value = jnp.einsum(
        "hqk,qhd->khd",
        probabilities.astype(jnp.bfloat16),
        grad_attended,
        preferred_element_type=jnp.float32,
    )
    grad_prob = jnp.einsum(
        "qhd,khd->hqk", grad_attended, value_heads, preferred_element_type=jnp.float32
    )
    grad_score = probabilities * (
        grad_prob - jnp.sum(probabilities * grad_prob, axis=-1, keepdims=True)
    )
    grad_low = grad_score.astype(jnp.bfloat16)
    grad_query = (
        jnp.einsum("hqk,khd->qhd", grad_low, key_heads, preferred_element_type=jnp.float32) * 0.125
    )
    grad_key = (
        jnp.einsum("hqk,qhd->khd", grad_low, query_heads, preferred_element_type=jnp.float32)
        * 0.125
    )
    return (grad_query, grad_key, grad_value, grad_low)


def adam_step(weight, first, second, grad, rate, shrink):
    first_new = beta_one * first + (1.0 - beta_one) * grad
    second_new = beta_two * second + (1.0 - beta_two) * grad * grad
    first_hat = first_new / (1.0 - beta_one**STEP)
    second_hat = second_new / (1.0 - beta_two**STEP)
    weight_new = weight - rate * (first_hat / (jnp.sqrt(second_hat) + adam_eps) + shrink * weight)
    return (weight_new, first_new, second_new)


MESH = pl.DeviceIdType.MESH
VMEM_LIMIT = 64 * 1024 * 1024 - 65536
ANY = pl.BlockSpec(memory_space=pl.ANY)
VM = pl.BlockSpec(memory_space=pltpu.VMEM)


def place(index, n_pair):
    return {"dp": index // n_pair, "pair": lax.rem(index, n_pair)}


def remote(src, dst, send, recv, target):
    return pltpu.make_async_remote_copy(
        src, dst, send, recv, device_id=target, device_id_type=MESH
    )


def greet(targets):
    sem = pltpu.get_barrier_semaphore()
    for target in targets:
        pl.semaphore_signal(sem, inc=1, device_id=target, device_id_type=MESH)
    pl.semaphore_wait(sem, len(targets))


def my_index(n_pair):
    return lax.axis_index("dp") * n_pair + lax.axis_index("pair")


def bit_order(n_dp, n_pair, color):
    dp_bits, pair_bits = (n_dp - 1).bit_length(), (n_pair - 1).bit_length()
    high = list(reversed(range(pair_bits + 1, pair_bits + dp_bits))) + [pair_bits]
    side = list(reversed(range(1, pair_bits)))
    return high + side if color == 0 else side + high


def offset(order, position):
    return sum(((position >> step) & 1) << bit for step, bit in enumerate(order))


def scatter_kernel(n_dp, n_pair, pieces, n_in, *refs):
    k = len(pieces)
    ins, outs = refs[:n_in], refs[n_in : 2 * n_in]
    accs = refs[2 * n_in : 2 * n_in + k]
    gots = refs[2 * n_in + k : 2 * n_in + 2 * k]
    lsem, csend, crecv, send, recv = refs[2 * n_in + 2 * k :]
    me = my_index(n_pair)
    n = n_dp * n_pair
    steps = (n - 1).bit_length() - 1
    half = 1 << steps
    orders = [bit_order(n_dp, n_pair, color) for _, _, _, color in pieces]
    greet([place(me ^ (1 << bit), n_pair) for bit in range(steps + 1)])

    def source(a, block):
        which, low, high, _ = pieces[a]
        return ins[which].at[block, :, pl.ds(low, high - low)]

    def core_send(a, upper):
        lo = half // 2 if upper else 0
        for p in range(lo, lo + half // 2):
            block = me ^ (offset(orders[a], p) + 1)
            remote(source(a, block), gots[a].at[p], csend.at[a, upper], crecv.at[a, upper], place(me ^ 1, n_pair)).start()

    def load(a):
        for p in range(half):
            pltpu.make_async_copy(source(a, me ^ offset(orders[a], p)), accs[a].at[p], lsem.at[a]).start()

    def core_copy(a, upper):
        lo = half // 2 if upper else 0
        part = pl.ds(lo, half // 2)
        return remote(gots[a].at[part], gots[a].at[part], csend.at[a, upper], crecv.at[a, upper], place(me ^ 1, n_pair))

    def add(a, lo, count, base):
        def body(j, carry):
            accs[a][lo + j] = (
                accs[a][lo + j].astype(jnp.float32) + gots[a][base + lo + j].astype(jnp.float32)
            ).astype(jnp.bfloat16)
            return carry
        lax.fori_loop(0, count, body, 0)

    def base_of(s):
        return half + half - (2 << s)

    def hop(a, s):
        return remote(
            accs[a].at[pl.ds(1 << s, 1 << s)], gots[a].at[pl.ds(base_of(s), 1 << s)],
            send.at[a, s], recv.at[a, s], place(me ^ (1 << orders[a][s]), n_pair),
        )

    for upper in (1, 0):
        for a in range(k):
            core_send(a, upper)
            if upper:
                load(a)
    for a in range(k):
        pltpu.make_async_copy(accs[a], accs[a], lsem.at[a]).wait()
        core_copy(a, 1).wait_recv()
        add(a, half // 2, half // 2, 0)
        hop(a, steps - 1).start()
    for a in range(k):
        core_copy(a, 0).wait_recv()
        add(a, 0, half // 2, 0)
    for s in reversed(range(steps)):
        for a in range(k):
            hop(a, s).wait_recv()
            if s:
                mid = 1 << (s - 1)
                add(a, mid, mid, base_of(s))
                hop(a, s - 1).start()
                add(a, 0, mid, base_of(s))
            else:
                which, low, high, _ = pieces[a]
                outs[which][:, low:high] = accs[a][0].astype(jnp.float32) + gots[a][
                    base_of(0)
                ].astype(jnp.float32)
    for a in range(k):
        core_copy(a, 1).wait_send()
        core_copy(a, 0).wait_send()
        for s in range(steps):
            hop(a, s).wait_send()


def scatter_all(grads, pieces, n_dp, n_pair, cid):
    n, k = n_dp * n_pair, len(pieces)
    steps = (n - 1).bit_length() - 1
    half = n // 2
    shape = lambda p, lead: (lead, grads[p[0]].shape[1], p[2] - p[1])
    return pl.pallas_call(
        functools.partial(scatter_kernel, n_dp, n_pair, pieces, len(grads)),
        out_shape=[jax.ShapeDtypeStruct(g.shape[1:], jnp.float32) for g in grads],
        in_specs=[ANY] * len(grads),
        out_specs=[VM] * len(grads),
        scratch_shapes=[pltpu.VMEM(shape(p, half), jnp.bfloat16) for p in pieces]
        + [pltpu.VMEM(shape(p, 2 * half - 1), jnp.bfloat16) for p in pieces]
        + [
            pltpu.SemaphoreType.DMA((k,)),
            pltpu.SemaphoreType.DMA((k, 2)),
            pltpu.SemaphoreType.DMA((k, 2)),
            pltpu.SemaphoreType.DMA((k, steps)),
            pltpu.SemaphoreType.DMA((k, steps)),
        ],
        compiler_params=pltpu.CompilerParams(
            collective_id=cid, has_side_effects=True, vmem_limit_bytes=VMEM_LIMIT
        ),
        name="weight_grads_sum",
    )(*grads)


def spread(n, n_pair, block, everyone, send, recv, own_sem):
    me = my_index(n_pair)
    sem = pltpu.get_barrier_semaphore()

    def hello(k, carry):
        pl.semaphore_signal(sem, inc=1, device_id=place(me ^ k, n_pair), device_id_type=MESH)
        return carry

    lax.fori_loop(1, n, hello, 0)
    own = pltpu.make_async_copy(block, everyone.at[me], own_sem)
    own.start()
    pl.semaphore_wait(sem, n - 1)

    def go(k, carry):
        remote(block, everyone.at[me], send.at[k], recv.at[k], place(me ^ k, n_pair)).start()
        return carry

    lax.fori_loop(1, n, go, 0)
    own.wait()

    def done(k, carry):
        remote(block, everyone.at[me ^ k], send.at[k], recv.at[k], place(me ^ k, n_pair)).wait()
        return carry

    lax.fori_loop(1, n, done, 0)


def total_kernel(n, n_pair, x_ref, o_ref, everyone, send, recv, own_sem):
    spread(n, n_pair, x_ref, everyone, send, recv, own_sem)
    def add(j, total):
        return total + everyone[j]
    o_ref[...] = lax.fori_loop(1, n, add, everyone[0])


def small_total(x, n_dp, n_pair, cid):
    n = n_dp * n_pair
    return pl.pallas_call(
        functools.partial(total_kernel, n, n_pair),
        out_shape=jax.ShapeDtypeStruct(x.shape, x.dtype),
        in_specs=[VM], out_specs=VM,
        scratch_shapes=[pltpu.VMEM((n,) + x.shape, x.dtype), pltpu.SemaphoreType.DMA((n,)), pltpu.SemaphoreType.DMA((n,)), pltpu.SemaphoreType.DMA],
        compiler_params=pltpu.CompilerParams(collective_id=cid, has_side_effects=True),
        name="small_total",
    )(x)


def loss_kernel(n, n_pair, docs, x_ref, pos_ref, neg_ref, count_ref, loss_ref, grad_ref, everyone, grads, send, recv, own_sem):
    spread(n, n_pair, x_ref, everyone, send, recv, own_sem)
    total = n * docs
    width = x_ref.shape[1]
    pooled = everyone[...].reshape(total, width)
    inverse = lax.rsqrt(jnp.sum(pooled * pooled, axis=1, keepdims=True) + 1e-06)
    unit = pooled * inverse
    similar = 20.0 * lax.dot_general(unit, unit, (((1,), (1,)), ((), ())), precision=HIGHEST, preferred_element_type=jnp.float32)
    columns = lax.broadcasted_iota(jnp.int32, (total, total), 1)
    is_pos = columns == pos_ref[...]
    chosen = jnp.sum(jnp.where(is_pos, similar, 0.0), axis=1, keepdims=True)
    counts = count_ref[...]
    weight = 1.0 / (counts.astype(jnp.float32) * total)
    loss_rows = jnp.zeros((total, 1), jnp.float32)
    grad_similar = jnp.zeros((total, total), jnp.float32)
    pulled = jnp.zeros((total, 1), jnp.float32)
    for slot in range(neg_ref.shape[1]):
        is_neg = columns == neg_ref[:, slot : slot + 1]
        against = jnp.sum(jnp.where(is_neg, similar, 0.0), axis=1, keepdims=True)
        value = 1.0 - chosen + against
        used = slot < counts
        soft = jnp.maximum(value, 0.0) + jnp.log1p(jnp.exp(-jnp.abs(value)))
        loss_rows = loss_rows + jnp.where(used, soft, 0.0)
        slope = jnp.where(used, weight / (1.0 + jnp.exp(-value)), 0.0)
        grad_similar = grad_similar + jnp.where(is_neg, slope, 0.0)
        pulled = pulled + slope
    grad_similar = grad_similar - jnp.where(is_pos, pulled, 0.0)
    loss_ref[...] = jnp.sum(loss_rows * weight, axis=0, keepdims=True)
    dims = (((1,), (0,)), ((), ()))
    grad_unit = lax.dot_general(grad_similar, unit, dims, precision=HIGHEST, preferred_element_type=jnp.float32)
    grad_unit = grad_unit + lax.dot_general(grad_similar, unit, (((0,), (0,)), ((), ())), precision=HIGHEST, preferred_element_type=jnp.float32)
    grad_unit = 20.0 * grad_unit
    inner = jnp.sum(grad_unit * unit, axis=1, keepdims=True)
    grads[...] = (inverse * (grad_unit - unit * inner)).reshape(n, docs, width)
    grad_ref[...] = grads[my_index(n_pair)]


def pooled_loss(pooled, positives, negatives, counts, n_dp, n_pair, cid):
    n = n_dp * n_pair
    docs, width = pooled.shape
    return pl.pallas_call(
        functools.partial(loss_kernel, n, n_pair, docs),
        out_shape=[jax.ShapeDtypeStruct((1, 1), jnp.float32), jax.ShapeDtypeStruct(pooled.shape, jnp.float32)],
        in_specs=[VM] * 4, out_specs=[VM] * 2,
        scratch_shapes=[pltpu.VMEM((n,) + pooled.shape, jnp.float32), pltpu.VMEM((n,) + pooled.shape, jnp.float32),
            pltpu.SemaphoreType.DMA((n,)), pltpu.SemaphoreType.DMA((n,)), pltpu.SemaphoreType.DMA],
        compiler_params=pltpu.CompilerParams(collective_id=cid, has_side_effects=True),
        name="pooled_loss",
    )(pooled, positives[:, None], negatives, counts[:, None])


def table_kernel(n_pair, rows, chunk, arr_ref, ask_ref, out_ref, sq_ref, hot, stage, part, got_c, out_x, got_x, fin, fin_other,
                 csend, crecv, xsend, xrecv, fsend, frecv, wsem):
    me_dp, me_pair = lax.axis_index("dp"), lax.axis_index("pair")
    core = lax.rem(me_pair, 2)
    partner = {"dp": me_dp, "pair": me_pair ^ 1}
    across = {"dp": me_dp, "pair": me_pair ^ 2}
    count = rows // 2 // chunk
    greet([partner, across])
    slots = ask_ref.shape[1]

    def summed(base):
        ids = lax.broadcasted_iota(jnp.int32, (chunk, slots), 0) + base
        hot[...] = jnp.where(ids == ask_ref[...], 1.0, 0.0).astype(jnp.bfloat16)
        return jnp.dot(hot[...], arr_ref[...], preferred_element_type=jnp.float32)

    def c_copy(i):
        return remote(stage.at[i], got_c.at[i], csend.at[i], crecv.at[i], partner)

    def x_copy(i):
        return remote(out_x.at[i], got_x.at[i], xsend.at[i], xrecv.at[i], across)

    def f_copy(i):
        return remote(fin.at[i], fin_other.at[i], fsend.at[i], frecv.at[i], partner)

    for i in range(count):
        stage[i] = summed((1 - core) * (rows // 2) + i * chunk).astype(jnp.bfloat16)
        c_copy(i).start()
    for i in range(count):
        part[...] = summed(core * (rows // 2) + i * chunk)
        c_copy(i).wait_recv()
        out_x[i] = (part[...] + got_c[i].astype(jnp.float32)).astype(jnp.bfloat16)
        x_copy(i).start()
    square = jnp.zeros((1, 1), jnp.float32)
    for i in range(count):
        x_copy(i).wait_recv()
        value = (out_x[i].astype(jnp.float32) + got_x[i].astype(jnp.float32)).astype(jnp.bfloat16)
        fin[i] = value
        f_copy(i).start()
        pltpu.make_async_copy(fin.at[i], out_ref.at[pl.ds(core * (rows // 2) + i * chunk, chunk)], wsem.at[0]).start()
        wide = value.astype(jnp.float32)
        square = square + jnp.sum(jnp.sum(wide * wide, axis=0, keepdims=True), axis=1, keepdims=True)
    sq_ref[...] = jnp.where(me_pair < 2, square, 0.0)
    for i in range(count):
        f_copy(i).wait_recv()
        pltpu.make_async_copy(fin_other.at[i], out_ref.at[pl.ds((1 - core) * (rows // 2) + i * chunk, chunk)], wsem.at[1]).start()
    for i in range(count):
        c_copy(i).wait_send()
        x_copy(i).wait_send()
        f_copy(i).wait_send()
    pltpu.make_async_copy(fin, fin, wsem.at[0]).wait()
    pltpu.make_async_copy(fin_other, fin_other, wsem.at[1]).wait()


def table_total(arrived, asked, rows, n_pair, cid):
    chunk, width = 512, arrived.shape[1]
    count = rows // 2 // chunk
    box = pltpu.VMEM((count, chunk, width), jnp.bfloat16)
    sem = pltpu.SemaphoreType.DMA((count,))
    return pl.pallas_call(
        functools.partial(table_kernel, n_pair, rows, chunk),
        out_shape=[jax.ShapeDtypeStruct((rows, width), jnp.bfloat16), jax.ShapeDtypeStruct((1, 1), jnp.float32)],
        in_specs=[VM, VM], out_specs=[ANY, VM],
        scratch_shapes=[pltpu.VMEM((chunk, asked.shape[1]), jnp.bfloat16), box, pltpu.VMEM((chunk, width), jnp.float32), box, box, box, box, box,
            sem, sem, sem, sem, sem, sem, pltpu.SemaphoreType.DMA((2,))],
        compiler_params=pltpu.CompilerParams(collective_id=cid, has_side_effects=True, vmem_limit_bytes=VMEM_LIMIT),
        name="table_total",
    )(arrived, asked)


def gather_kernel(n_dp, n_pair, pieces, n_in, *refs):
    k = len(pieces)
    ins, outs = refs[:n_in], refs[n_in : 2 * n_in]
    bufs = refs[2 * n_in : 2 * n_in + k]
    send, recv, csend, crecv, wsem, isem = refs[2 * n_in + k :]
    me = my_index(n_pair)
    steps = (n_dp * n_pair - 1).bit_length() - 1
    half = 1 << steps
    orders = [bit_order(n_dp, n_pair, color) for _, _, _, color in pieces]

    def load(a):
        which, low, high, _ = pieces[a]
        return pltpu.make_async_copy(
            ins[which].at[:, pl.ds(low, high - low)], bufs[a].at[0], isem.at[a]
        )

    for a in range(k):
        load(a).start()
    greet([place(me ^ (1 << bit), n_pair) for bit in range(steps + 1)])

    def write_out(a, lo, count, core):
        which, low, high, _ = pieces[a]
        for p in range(lo, lo + count):
            block = me ^ (offset(orders[a], p) + core)
            pltpu.make_async_copy(
                bufs[a].at[p + core * half],
                outs[which].at[block, :, pl.ds(low, high - low)],
                wsem.at[a],
            ).start()

    def forward(a, s):
        lo, count = (0, 1) if s == 0 else (1 << (s - 1), 1 << (s - 1))
        return remote(
            bufs[a].at[pl.ds(lo, count)],
            bufs[a].at[pl.ds(half + lo, count)],
            csend.at[a, s],
            crecv.at[a, s],
            place(me ^ 1, n_pair),
        )

    def hop(a, s):
        return remote(
            bufs[a].at[pl.ds(0, 1 << s)],
            bufs[a].at[pl.ds(1 << s, 1 << s)],
            send.at[a, s],
            recv.at[a, s],
            place(me ^ (1 << orders[a][s]), n_pair),
        )

    for a in range(k):
        load(a).wait()
        hop(a, 0).start()
    for a in range(k):
        forward(a, 0).start()
        write_out(a, 0, 1, 0)
    for s in range(steps):
        for a in range(k):
            hop(a, s).wait_recv()
            if s + 1 < steps:
                hop(a, s + 1).start()
            forward(a, s + 1).start()
            write_out(a, 1 << s, 1 << s, 0)
        for a in range(k):
            forward(a, s).wait_recv()
            lo, count = (0, 1) if s == 0 else (1 << (s - 1), 1 << (s - 1))
            write_out(a, lo, count, 1)
    for a in range(k):
        forward(a, steps).wait_recv()
        write_out(a, half // 2, half // 2, 1)
    for a in range(k):
        for s in range(steps):
            hop(a, s).wait_send()
        for s in range(steps + 1):
            forward(a, s).wait_send()
        pltpu.make_async_copy(bufs[a], bufs[a], wsem.at[a]).wait()


def gather_all(shards, pieces, n_dp, n_pair, cid):
    n, k = n_dp * n_pair, len(pieces)
    steps = (n - 1).bit_length() - 1
    return pl.pallas_call(
        functools.partial(gather_kernel, n_dp, n_pair, pieces, len(shards)),
        out_shape=[jax.ShapeDtypeStruct((n,) + s.shape, s.dtype) for s in shards],
        in_specs=[ANY] * len(shards),
        out_specs=[ANY] * len(shards),
        scratch_shapes=[
            pltpu.VMEM((n, shards[p[0]].shape[0], p[2] - p[1]), jnp.bfloat16) for p in pieces
        ]
        + [
            pltpu.SemaphoreType.DMA((k, steps)),
            pltpu.SemaphoreType.DMA((k, steps)),
            pltpu.SemaphoreType.DMA((k, steps + 1)),
            pltpu.SemaphoreType.DMA((k, steps + 1)),
            pltpu.SemaphoreType.DMA((k,)),
            pltpu.SemaphoreType.DMA((k,)),
        ],
        compiler_params=pltpu.CompilerParams(
            collective_id=cid, has_side_effects=True, vmem_limit_bytes=VMEM_LIMIT
        ),
        name="weights_gather",
    )(*shards)

def exchange_kernel(n_dp, x_ref, o_ref, send, recv, lsem):
    me = lax.axis_index("dp"); pr = lax.axis_index("pair")
    sem = pltpu.get_barrier_semaphore()
    def greet(k, _):
        pl.semaphore_signal(sem, inc=1, device_id={"dp": lax.rem(me + k, n_dp), "pair": pr}, device_id_type=MESH)
        return 0
    lax.fori_loop(1, n_dp, greet, 0)
    pl.semaphore_wait(sem, n_dp - 1)
    own = pltpu.make_async_copy(x_ref.at[me], o_ref.at[me], lsem); own.start()
    def cp(k):
        dst = lax.rem(me + k, n_dp)
        return pltpu.make_async_remote_copy(x_ref.at[dst], o_ref.at[me], send.at[k], recv.at[k],
            device_id={"dp": dst, "pair": pr}, device_id_type=MESH)
    def go(k, _):
        cp(k).start(); return 0
    lax.fori_loop(1, n_dp, go, 0)
    def done(k, _):
        src = lax.rem(me + n_dp - k, n_dp)
        c = pltpu.make_async_remote_copy(x_ref.at[me], o_ref.at[src], send.at[k], recv.at[k],
            device_id={"dp": src, "pair": pr}, device_id_type=MESH)
        c.wait(); return 0
    own.wait()
    lax.fori_loop(1, n_dp, done, 0)

def exchange(x, n_dp, cid):
    return pl.pallas_call(
        functools.partial(exchange_kernel, n_dp),
        out_shape=jax.ShapeDtypeStruct(x.shape, x.dtype),
        in_specs=[pl.BlockSpec(memory_space=pltpu.VMEM)], out_specs=pl.BlockSpec(memory_space=pltpu.VMEM),
        scratch_shapes=[pltpu.SemaphoreType.DMA((n_dp,)), pltpu.SemaphoreType.DMA((n_dp,)), pltpu.SemaphoreType.DMA],
        compiler_params=pltpu.CompilerParams(collective_id=cid, has_side_effects=True, vmem_limit_bytes=VMEM_LIMIT),
        name="rows_exchange",
    )(x)

def weight_pieces(widths):
    qkv_cols, out_cols, in_cols, down_cols = widths
    cut = down_cols * 2 // 3 // 128 * 128
    return [
        (2, 0, in_cols, 0),
        (0, 0, qkv_cols, 1),
        (1, 0, out_cols, 0),
        (3, 0, cut, 0),
        (3, cut, down_cols, 1),
    ]

def local_plain(
    token_owner,
    token_row,
    lengths,
    positives,
    negatives,
    neg_counts,
    embed_table,
    embed_first,
    embed_second,
    qkv_weight,
    qkv_first,
    qkv_second,
    out_weight,
    out_first,
    out_second,
    in_weight,
    in_first,
    in_second,
    down_weight,
    down_first,
    down_second,
    norm_gains,
    gains_first,
    gains_second,
    position_bias,
    bias_first,
    bias_second,
):
    doc_count = lengths.shape[0]
    seq_len = token_row.shape[1]
    model_width = embed_table.shape[1]
    head_count = position_bias.shape[1]
    bucket_count = position_bias.shape[0]
    tok_total = doc_count * seq_len
    owners = lax.axis_size("dp")
    capacity = max(2, 2 * tok_total // owners)
    low_mats = (
        qkv_weight.astype(jnp.bfloat16),
        out_weight.astype(jnp.bfloat16),
        in_weight.astype(jnp.bfloat16),
        down_weight.astype(jnp.bfloat16),
    )
    qkv_full, out_full, in_full, down_full = (
        lax.all_gather(low_mats[0], ("dp", "pair"), axis=0, tiled=True),
        lax.all_gather(low_mats[1], ("dp", "pair"), axis=0, tiled=True),
        lax.all_gather(low_mats[2], ("dp", "pair"), axis=0, tiled=True),
        lax.all_gather(low_mats[3], ("dp", "pair"), axis=0, tiled=True),
    )
    tok_owner = token_owner.reshape(-1)
    tok_row = token_row.reshape(-1)
    owner_hits = (tok_owner[:, None] == jnp.arange(owners, dtype=jnp.int32)[None, :]).astype(
        jnp.int32
    )
    slot_rank = jnp.sum((jnp.cumsum(owner_hits, axis=0) - 1) * owner_hits, axis=1)
    requests = jnp.zeros((owners, capacity), jnp.int32).at[tok_owner, slot_rank].set(tok_row)
    asked_rows = lax.all_to_all(requests, "dp", split_axis=0, concat_axis=0, tiled=True)
    looked = jnp.take(embed_table, asked_rows.reshape(-1), axis=0).astype(jnp.bfloat16)
    answer = lax.all_to_all(
        looked.reshape(asked_rows.shape + (model_width,)),
        "dp",
        split_axis=0,
        concat_axis=0,
        tiled=True,
    )
    replies, asked_rows = (answer, asked_rows)
    embedded = replies[tok_owner, slot_rank].astype(jnp.float32)
    positions = jnp.arange(seq_len)
    live = positions[None, :] < lengths[:, None]
    pair_buckets = bucket_of(
        (positions[None, :] - positions[:, None]).reshape(-1), bucket_count, REACH
    )
    pair_hits = (jnp.arange(bucket_count)[:, None] == pair_buckets[None, :]).astype(jnp.float32)
    bias_full = jnp.dot(position_bias.T, pair_hits, precision=HIGHEST).reshape(
        head_count, seq_len, seq_len
    )
    bucket_map = pair_hits.astype(jnp.bfloat16)

    def split_doc(source, doc_index):
        doc_rows = source[doc_index * seq_len : (doc_index + 1) * seq_len]
        return tuple(
            (
                doc_rows[:, member * model_width : (member + 1) * model_width].reshape(
                    seq_len, head_count, -1
                )
                for member in range(3)
            )
        )

    normed_one, inverse_one = rms_forward(embedded, norm_gains[0])
    normed_one = normed_one.astype(jnp.bfloat16)
    qkv_rows = jnp.dot(normed_one, qkv_full, preferred_element_type=jnp.float32).astype(
        jnp.bfloat16
    )
    attended_parts = []
    logsum_parts = []
    for doc_index in range(doc_count):
        query_heads, key_heads, value_heads = split_doc(qkv_rows, doc_index)
        doc_out, logsum = attend_forward(
            query_heads, key_heads, value_heads, bias_full, live[doc_index]
        )
        attended_parts.append(doc_out.reshape(seq_len, model_width))
        logsum_parts.append(logsum)
    attended = jnp.concatenate(attended_parts, axis=0).astype(jnp.bfloat16)
    residual = embedded + jnp.dot(attended, out_full, preferred_element_type=jnp.float32)
    normed_two, inverse_two = rms_forward(residual, norm_gains[1])
    normed_two = normed_two.astype(jnp.bfloat16)
    hidden = jax.nn.relu(jnp.dot(normed_two, in_full, preferred_element_type=jnp.float32)).astype(
        jnp.bfloat16
    )
    output_rows = residual + jnp.dot(hidden, down_full, preferred_element_type=jnp.float32)
    normed_three, inverse_three = rms_forward(output_rows, norm_gains[2])
    live_rows = live.reshape(-1, 1)
    length_float = lengths.astype(jnp.float32)
    pooled_local = (
        jnp.sum(
            jnp.where(live_rows, normed_three, 0.0).reshape(doc_count, seq_len, model_width), axis=1
        )
        / length_float[:, None]
    )
    pooled_all = lax.all_gather(pooled_local, ("dp", "pair"), axis=0, tiled=True)
    loss_value, loss_pullback = jax.vjp(
        lambda pooled_in: margin_loss(pooled_in, positives, negatives, neg_counts), pooled_all
    )
    grad_pooled_all = loss_pullback(jnp.ones((), jnp.float32))[0]
    grad_pooled = lax.dynamic_slice_in_dim(
        grad_pooled_all, lax.axis_index(("dp", "pair")) * doc_count, doc_count, 0
    )
    grad_three = jnp.where(
        live_rows, jnp.repeat(grad_pooled / length_float[:, None], seq_len, axis=0), 0.0
    )
    qkv_back, out_back, in_back, down_back = (qkv_full, out_full, in_full, down_full)
    grad_output, gain_three = rms_backward(output_rows, inverse_three, norm_gains[2], grad_three)
    grad_branch = grad_output.astype(jnp.bfloat16)
    grad_down = lax.dot_general(
        hidden, grad_branch, CONTRACT_ROWS, preferred_element_type=jnp.float32
    )
    grad_hidden = lax.dot_general(
        grad_branch, down_back, CONTRACT_COLS, preferred_element_type=jnp.float32
    )
    grad_pre = jnp.where(hidden > 0, grad_hidden, 0.0).astype(jnp.bfloat16)
    grad_in = lax.dot_general(
        normed_two, grad_pre, CONTRACT_ROWS, preferred_element_type=jnp.float32
    )
    grad_normed_two = lax.dot_general(
        grad_pre, in_back, CONTRACT_COLS, preferred_element_type=jnp.float32
    )
    grad_res_part, gain_two = rms_backward(residual, inverse_two, norm_gains[1], grad_normed_two)
    grad_residual = grad_output + grad_res_part
    grad_attn_branch = grad_residual.astype(jnp.bfloat16)
    grad_out = lax.dot_general(
        attended, grad_attn_branch, CONTRACT_ROWS, preferred_element_type=jnp.float32
    )
    grad_attended = lax.dot_general(
        grad_attn_branch, out_back, CONTRACT_COLS, preferred_element_type=jnp.float32
    ).astype(jnp.bfloat16)
    grad_qkv_parts = []
    bias_grad_heads = jnp.zeros((head_count, bucket_count), jnp.float32)
    for doc_index in range(doc_count):
        query_heads, key_heads, value_heads = split_doc(qkv_rows, doc_index)
        grad_doc = grad_attended[doc_index * seq_len : (doc_index + 1) * seq_len].reshape(
            seq_len, head_count, -1
        )
        grad_query, grad_key, grad_value, grad_low = attend_backward(
            query_heads,
            key_heads,
            value_heads,
            bias_full,
            live[doc_index],
            logsum_parts[doc_index],
            grad_doc,
        )
        grad_qkv_parts.append(
            jnp.concatenate(
                [
                    grad_query.reshape(seq_len, model_width),
                    grad_key.reshape(seq_len, model_width),
                    grad_value.reshape(seq_len, model_width),
                ],
                axis=1,
            )
        )
        bias_grad_heads = bias_grad_heads + lax.dot_general(
            grad_low.reshape(head_count, -1),
            bucket_map,
            CONTRACT_COLS,
            preferred_element_type=jnp.float32,
        )
    bias_grad_local = bias_grad_heads.T
    grad_qkv_rows = jnp.concatenate(grad_qkv_parts, axis=0).astype(jnp.bfloat16)
    grad_qkv = lax.dot_general(
        normed_one, grad_qkv_rows, CONTRACT_ROWS, preferred_element_type=jnp.float32
    )
    grad_normed_one = lax.dot_general(
        grad_qkv_rows, qkv_back, CONTRACT_COLS, preferred_element_type=jnp.float32
    )
    grad_emb_part, gain_one = rms_backward(embedded, inverse_one, norm_gains[0], grad_normed_one)
    grad_embedded = grad_residual + grad_emb_part
    sendback = (
        jnp.zeros((owners, capacity, model_width), jnp.float32)
        .at[tok_owner, slot_rank]
        .set(grad_embedded)
    )
    arrived = lax.all_to_all(sendback, "dp", split_axis=0, concat_axis=0, tiled=True)
    table_grad = jax.ops.segment_sum(
        arrived.reshape(-1, model_width), asked_rows.reshape(-1), num_segments=embed_table.shape[0]
    )
    table_grad = lax.psum(table_grad, "pair")
    weight_grads = (
        lax.psum_scatter(grad_qkv, ("dp", "pair"), scatter_dimension=0, tiled=True),
        lax.psum_scatter(grad_out, ("dp", "pair"), scatter_dimension=0, tiled=True),
        lax.psum_scatter(grad_in, ("dp", "pair"), scatter_dimension=0, tiled=True),
        lax.psum_scatter(grad_down, ("dp", "pair"), scatter_dimension=0, tiled=True),
    )
    pair_first = (lax.axis_index("pair") == 0).astype(jnp.float32)
    square_part = jnp.sum(
        jnp.stack([jnp.sum(grad_piece * grad_piece) for grad_piece in weight_grads])
    ) + pair_first * jnp.sum(table_grad * table_grad)
    gain_grad, bias_grad, square_sum = lax.psum(
        (jnp.stack([gain_one, gain_two, gain_three]), bias_grad_local, square_part), ("dp", "pair")
    )
    clip_norm = jnp.sqrt(
        square_sum + jnp.sum(gain_grad * gain_grad) + jnp.sum(bias_grad * bias_grad)
    )
    factor = jnp.minimum(1.0, clip_limit / clip_norm)
    table_out = adam_step(embed_table, embed_first, embed_second, table_grad * factor, 1.0, 0.01)
    qkv_out = adam_step(qkv_weight, qkv_first, qkv_second, weight_grads[0] * factor, 0.05, 0.01)
    out_out = adam_step(out_weight, out_first, out_second, weight_grads[1] * factor, 0.05, 0.01)
    in_out = adam_step(in_weight, in_first, in_second, weight_grads[2] * factor, 0.05, 0.01)
    down_out = adam_step(down_weight, down_first, down_second, weight_grads[3] * factor, 0.05, 0.01)
    gains_out = adam_step(norm_gains, gains_first, gains_second, gain_grad * factor, 1.0, 0.0)
    bias_out = adam_step(position_bias, bias_first, bias_second, bias_grad * factor, 0.3, 0.0)
    return (
        loss_value,
        clip_norm,
        table_out[0],
        table_out[1],
        table_out[2],
        qkv_out[0],
        qkv_out[1],
        qkv_out[2],
        out_out[0],
        out_out[1],
        out_out[2],
        in_out[0],
        in_out[1],
        in_out[2],
        down_out[0],
        down_out[1],
        down_out[2],
        gains_out[0],
        gains_out[1],
        gains_out[2],
        bias_out[0],
        bias_out[1],
        bias_out[2],
    )


def local_fast(
    token_owner,
    token_row,
    lengths,
    positives,
    negatives,
    neg_counts,
    embed_table,
    embed_first,
    embed_second,
    qkv_weight,
    qkv_first,
    qkv_second,
    out_weight,
    out_first,
    out_second,
    in_weight,
    in_first,
    in_second,
    down_weight,
    down_first,
    down_second,
    norm_gains,
    gains_first,
    gains_second,
    position_bias,
    bias_first,
    bias_second,
):
    doc_count = lengths.shape[0]
    seq_len = token_row.shape[1]
    model_width = embed_table.shape[1]
    head_count = position_bias.shape[1]
    bucket_count = position_bias.shape[0]
    tok_total = doc_count * seq_len
    owners = lax.axis_size("dp")
    capacity = max(2, 2 * tok_total // owners)
    low_mats = (
        qkv_weight.astype(jnp.bfloat16),
        out_weight.astype(jnp.bfloat16),
        in_weight.astype(jnp.bfloat16),
        down_weight.astype(jnp.bfloat16),
    )
    holders = lax.axis_size("pair")
    pieces = weight_pieces([low.shape[1] for low in low_mats])
    qkv_full, out_full, in_full, down_full = (
        full.reshape(-1, full.shape[2])
        for full in gather_all(low_mats, pieces, owners, holders, 1)
    )
    tok_owner = token_owner.reshape(-1)
    tok_row = token_row.reshape(-1)
    owner_hits = (tok_owner[:, None] == jnp.arange(owners, dtype=jnp.int32)[None, :]).astype(
        jnp.int32
    )
    slot_rank = jnp.sum((jnp.cumsum(owner_hits, axis=0) - 1) * owner_hits, axis=1)
    requests = jnp.zeros((owners, capacity), jnp.int32).at[tok_owner, slot_rank].set(tok_row)
    asked_rows = lax.all_to_all(requests, "dp", split_axis=0, concat_axis=0, tiled=True)
    looked = jnp.take(embed_table, asked_rows.reshape(-1), axis=0).astype(jnp.bfloat16)
    answer = exchange(looked.reshape(asked_rows.shape + (model_width,)), owners, 2)
    replies, asked_rows = (answer, asked_rows)
    embedded = replies[tok_owner, slot_rank].astype(jnp.float32)
    positions = jnp.arange(seq_len)
    live = positions[None, :] < lengths[:, None]
    pair_buckets = bucket_of(
        (positions[None, :] - positions[:, None]).reshape(-1), bucket_count, REACH
    )
    pair_hits = (jnp.arange(bucket_count)[:, None] == pair_buckets[None, :]).astype(jnp.float32)
    bias_full = jnp.dot(position_bias.T, pair_hits, precision=HIGHEST).reshape(
        head_count, seq_len, seq_len
    )
    bucket_map = pair_hits.astype(jnp.bfloat16)

    def split_doc(source, doc_index):
        doc_rows = source[doc_index * seq_len : (doc_index + 1) * seq_len]
        return tuple(
            (
                doc_rows[:, member * model_width : (member + 1) * model_width].reshape(
                    seq_len, head_count, -1
                )
                for member in range(3)
            )
        )

    normed_one, inverse_one = rms_forward(embedded, norm_gains[0])
    normed_one = normed_one.astype(jnp.bfloat16)
    qkv_rows = jnp.dot(normed_one, qkv_full, preferred_element_type=jnp.float32).astype(
        jnp.bfloat16
    )
    attended_parts = []
    logsum_parts = []
    for doc_index in range(doc_count):
        query_heads, key_heads, value_heads = split_doc(qkv_rows, doc_index)
        doc_out, logsum = attend_forward(
            query_heads, key_heads, value_heads, bias_full, live[doc_index]
        )
        attended_parts.append(doc_out.reshape(seq_len, model_width))
        logsum_parts.append(logsum)
    attended = jnp.concatenate(attended_parts, axis=0).astype(jnp.bfloat16)
    residual = embedded + jnp.dot(attended, out_full, preferred_element_type=jnp.float32)
    normed_two, inverse_two = rms_forward(residual, norm_gains[1])
    normed_two = normed_two.astype(jnp.bfloat16)
    hidden = jax.nn.relu(jnp.dot(normed_two, in_full, preferred_element_type=jnp.float32)).astype(
        jnp.bfloat16
    )
    output_rows = residual + jnp.dot(hidden, down_full, preferred_element_type=jnp.float32)
    normed_three, inverse_three = rms_forward(output_rows, norm_gains[2])
    live_rows = live.reshape(-1, 1)
    length_float = lengths.astype(jnp.float32)
    pooled_local = (
        jnp.sum(
            jnp.where(live_rows, normed_three, 0.0).reshape(doc_count, seq_len, model_width), axis=1
        )
        / length_float[:, None]
    )
    loss_cell, grad_pooled = pooled_loss(
        pooled_local, positives, negatives, neg_counts, owners, holders, 3
    )
    loss_value = loss_cell[0, 0]
    grad_three = jnp.where(
        live_rows, jnp.repeat(grad_pooled / length_float[:, None], seq_len, axis=0), 0.0
    )
    qkv_back, out_back, in_back, down_back = (qkv_full, out_full, in_full, down_full)
    grad_output, gain_three = rms_backward(output_rows, inverse_three, norm_gains[2], grad_three)
    grad_branch = grad_output.astype(jnp.bfloat16)
    grad_down = lax.dot_general(
        hidden, grad_branch, CONTRACT_ROWS, preferred_element_type=jnp.float32
    )
    grad_hidden = lax.dot_general(
        grad_branch, down_back, CONTRACT_COLS, preferred_element_type=jnp.float32
    )
    grad_pre = jnp.where(hidden > 0, grad_hidden, 0.0).astype(jnp.bfloat16)
    grad_in = lax.dot_general(
        normed_two, grad_pre, CONTRACT_ROWS, preferred_element_type=jnp.float32
    )
    grad_normed_two = lax.dot_general(
        grad_pre, in_back, CONTRACT_COLS, preferred_element_type=jnp.float32
    )
    grad_res_part, gain_two = rms_backward(residual, inverse_two, norm_gains[1], grad_normed_two)
    grad_residual = grad_output + grad_res_part
    grad_attn_branch = grad_residual.astype(jnp.bfloat16)
    grad_out = lax.dot_general(
        attended, grad_attn_branch, CONTRACT_ROWS, preferred_element_type=jnp.float32
    )
    grad_attended = lax.dot_general(
        grad_attn_branch, out_back, CONTRACT_COLS, preferred_element_type=jnp.float32
    ).astype(jnp.bfloat16)
    grad_qkv_parts = []
    bias_grad_heads = jnp.zeros((head_count, bucket_count), jnp.float32)
    for doc_index in range(doc_count):
        query_heads, key_heads, value_heads = split_doc(qkv_rows, doc_index)
        grad_doc = grad_attended[doc_index * seq_len : (doc_index + 1) * seq_len].reshape(
            seq_len, head_count, -1
        )
        grad_query, grad_key, grad_value, grad_low = attend_backward(
            query_heads,
            key_heads,
            value_heads,
            bias_full,
            live[doc_index],
            logsum_parts[doc_index],
            grad_doc,
        )
        grad_qkv_parts.append(
            jnp.concatenate(
                [
                    grad_query.reshape(seq_len, model_width),
                    grad_key.reshape(seq_len, model_width),
                    grad_value.reshape(seq_len, model_width),
                ],
                axis=1,
            )
        )
        bias_grad_heads = bias_grad_heads + lax.dot_general(
            grad_low.reshape(head_count, -1),
            bucket_map,
            CONTRACT_COLS,
            preferred_element_type=jnp.float32,
        )
    bias_grad_local = bias_grad_heads.T
    grad_qkv_rows = jnp.concatenate(grad_qkv_parts, axis=0).astype(jnp.bfloat16)
    grad_qkv = lax.dot_general(
        normed_one, grad_qkv_rows, CONTRACT_ROWS, preferred_element_type=jnp.float32
    )
    grad_normed_one = lax.dot_general(
        grad_qkv_rows, qkv_back, CONTRACT_COLS, preferred_element_type=jnp.float32
    )
    grad_emb_part, gain_one = rms_backward(embedded, inverse_one, norm_gains[0], grad_normed_one)
    grad_embedded = grad_residual + grad_emb_part
    sendback = (
        jnp.zeros((owners, capacity, model_width), jnp.bfloat16)
        .at[tok_owner, slot_rank]
        .set(grad_embedded.astype(jnp.bfloat16))
    )
    arrived = exchange(sendback, owners, 4)
    table_rows = embed_table.shape[0]
    table_grad, table_square = table_total(
        arrived.reshape(-1, model_width),
        asked_rows.reshape(1, -1),
        -(-table_rows // 1024) * 1024,
        holders,
        5,
    )
    table_grad = table_grad[:table_rows].astype(jnp.float32)
    parts = owners * holders
    weight_grads = scatter_all(
        [
            grad.astype(jnp.bfloat16).reshape(parts, -1, grad.shape[1])
            for grad in (grad_qkv, grad_out, grad_in, grad_down)
        ],
        pieces,
        owners,
        holders,
        6,
    )
    square_part = table_square[0, 0] + jnp.sum(
        jnp.stack([jnp.sum(grad_piece * grad_piece) for grad_piece in weight_grads])
    )
    small = jnp.concatenate(
        [
            jnp.stack([gain_one, gain_two, gain_three]).reshape(-1),
            bias_grad_local.reshape(-1),
            square_part.reshape(1),
        ]
    )
    small_size = small.shape[0]
    small_rows = -(-small_size // 1024) * 8
    small = jnp.pad(small, (0, small_rows * 128 - small_size)).reshape(small_rows, 128)
    small = small_total(small, owners, holders, 7).reshape(-1)
    gain_grad = small[: 3 * model_width].reshape(3, model_width)
    bias_grad = small[3 * model_width : small_size - 1].reshape(bucket_count, head_count)
    square_sum = small[small_size - 1]
    clip_norm = jnp.sqrt(
        square_sum + jnp.sum(gain_grad * gain_grad) + jnp.sum(bias_grad * bias_grad)
    )
    factor = jnp.minimum(1.0, clip_limit / clip_norm)
    table_out = adam_step(embed_table, embed_first, embed_second, table_grad * factor, 1.0, 0.01)
    qkv_out = adam_step(qkv_weight, qkv_first, qkv_second, weight_grads[0] * factor, 0.05, 0.01)
    out_out = adam_step(out_weight, out_first, out_second, weight_grads[1] * factor, 0.05, 0.01)
    in_out = adam_step(in_weight, in_first, in_second, weight_grads[2] * factor, 0.05, 0.01)
    down_out = adam_step(down_weight, down_first, down_second, weight_grads[3] * factor, 0.05, 0.01)
    gains_out = adam_step(norm_gains, gains_first, gains_second, gain_grad * factor, 1.0, 0.0)
    bias_out = adam_step(position_bias, bias_first, bias_second, bias_grad * factor, 0.3, 0.0)
    return (
        loss_value,
        clip_norm,
        table_out[0],
        table_out[1],
        table_out[2],
        qkv_out[0],
        qkv_out[1],
        qkv_out[2],
        out_out[0],
        out_out[1],
        out_out[2],
        in_out[0],
        in_out[1],
        in_out[2],
        down_out[0],
        down_out[1],
        down_out[2],
        gains_out[0],
        gains_out[1],
        gains_out[2],
        bias_out[0],
        bias_out[1],
        bias_out[2],
    )


def local(*arrays):
    n_dp, n_pair = lax.axis_size("dp"), lax.axis_size("pair")
    lengths, qkv_weight, down_weight = arrays[2], arrays[9], arrays[18]
    fits = (
        n_pair == 4
        and n_dp & (n_dp - 1) == 0
        and qkv_weight.shape[0] % 8 == 0
        and down_weight.shape[0] % 8 == 0
        and lengths.shape[0] == 2
        and 2 * arrays[1].size // n_dp % 128 == 0
    )
    return (local_fast if fits else local_plain)(*arrays)


def solution(mesh):
    return jax.shard_map(
        local,
        mesh=mesh,
        in_specs=(
            P(("dp", "pair"), None, None),
            P(("dp", "pair"), None),
            P(("dp", "pair")),
            P(),
            P(),
            P(),
            P("dp", None),
            P("dp", None),
            P("dp", None),
            P(("dp", "pair"), None),
            P(("dp", "pair"), None),
            P(("dp", "pair"), None),
            P(("dp", "pair"), None),
            P(("dp", "pair"), None),
            P(("dp", "pair"), None),
            P(("dp", "pair"), None),
            P(("dp", "pair"), None),
            P(("dp", "pair"), None),
            P(("dp", "pair"), None),
            P(("dp", "pair"), None),
            P(("dp", "pair"), None),
            P(),
            P(),
            P(),
            P(),
            P(),
            P(),
        ),
        out_specs=(
            P(),
            P(),
            P("dp", None),
            P("dp", None),
            P("dp", None),
            P(("dp", "pair"), None),
            P(("dp", "pair"), None),
            P(("dp", "pair"), None),
            P(("dp", "pair"), None),
            P(("dp", "pair"), None),
            P(("dp", "pair"), None),
            P(("dp", "pair"), None),
            P(("dp", "pair"), None),
            P(("dp", "pair"), None),
            P(("dp", "pair"), None),
            P(("dp", "pair"), None),
            P(("dp", "pair"), None),
            P(),
            P(),
            P(),
            P(),
            P(),
            P(),
        ),
        check_vma=False,
    )
```

```python
import functools
import math

import jax
import jax.numpy as jnp
from jax import lax
from jax.experimental import pallas as pl
from jax.experimental.pallas import tpu as pltpu
from jax.sharding import PartitionSpec as P

REACH = 128
STEP = 5


rms_eps = 1e-06
clip_limit = 0.05
margin = 1.0
sim_scale = 20.0
beta_one = 0.9
beta_two = 0.999
adam_eps = 1e-08
HIGHEST = lax.Precision.HIGHEST
CONTRACT_ROWS = (((0,), (0,)), ((), ()))
CONTRACT_COLS = (((1,), (1,)), ((), ()))


def bucket_of(offsets, bucket_count, reach_limit):
    half_count = bucket_count // 2
    exact_count = half_count // 2
    sign_base = jnp.where(offsets > 0, half_count, 0).astype(jnp.int32)
    distance = jnp.abs(offsets)
    far_bucket = jnp.full(offsets.shape, exact_count, jnp.int32)
    for level_index in range(1, half_count - exact_count):
        threshold = int(
            math.ceil(
                exact_count
                * (reach_limit / exact_count) ** (level_index / (half_count - exact_count))
                - 1e-09
            )
        )
        far_bucket = far_bucket + (distance >= threshold).astype(jnp.int32)
    return sign_base + jnp.where(distance < exact_count, distance, far_bucket)


def rms_forward(values, gain):
    inverse = lax.rsqrt(jnp.mean(values * values, axis=-1, keepdims=True) + rms_eps)
    return (values * inverse * gain, inverse)


def rms_backward(values, inverse, gain, upstream):
    scaled = upstream * gain
    normed = values * inverse
    grad_values = inverse * (scaled - normed * jnp.mean(scaled * normed, axis=-1, keepdims=True))
    return (grad_values, jnp.sum(upstream * normed, axis=0))


def margin_loss(pooled, positives, negatives, neg_counts):
    unit = pooled * lax.rsqrt(jnp.sum(pooled * pooled, axis=-1, keepdims=True) + 1e-06)
    similar = sim_scale * jnp.dot(unit, unit.T, precision=HIGHEST)
    chosen = jnp.take_along_axis(similar, positives[:, None], axis=1)
    against = jnp.take_along_axis(similar, negatives, axis=1)
    live_slots = jnp.arange(negatives.shape[1])[None, :] < neg_counts[:, None]
    terms = jnp.where(live_slots, jax.nn.softplus(margin - chosen + against), 0.0)
    return jnp.mean(jnp.sum(terms, axis=1) / neg_counts.astype(jnp.float32))


def doc_scores(query_heads, key_heads, bias_full, live_keys):
    scores = (
        jnp.einsum("qhd,khd->hqk", query_heads, key_heads, preferred_element_type=jnp.float32)
        * 0.125
        + bias_full
    )
    return jnp.where(live_keys[None, None, :], scores, -1000000000.0)


def attend_forward(query_heads, key_heads, value_heads, bias_full, live_keys):
    scores = doc_scores(query_heads, key_heads, bias_full, live_keys)
    highest = jnp.max(scores, axis=-1, keepdims=True)
    weights = jnp.exp(scores - highest)
    totals = jnp.sum(weights, axis=-1, keepdims=True)
    probabilities = (weights / totals).astype(jnp.bfloat16)
    attended = jnp.einsum(
        "hqk,khd->qhd", probabilities, value_heads, preferred_element_type=jnp.float32
    )
    return (attended, highest + jnp.log(totals))


def attend_backward(
    query_heads, key_heads, value_heads, bias_full, live_keys, logsum, grad_attended
):
    probabilities = jnp.exp(doc_scores(query_heads, key_heads, bias_full, live_keys) - logsum)
    grad_value = jnp.einsum(
        "hqk,qhd->khd",
        probabilities.astype(jnp.bfloat16),
        grad_attended,
        preferred_element_type=jnp.float32,
    )
    grad_prob = jnp.einsum(
        "qhd,khd->hqk", grad_attended, value_heads, preferred_element_type=jnp.float32
    )
    grad_score = probabilities * (
        grad_prob - jnp.sum(probabilities * grad_prob, axis=-1, keepdims=True)
    )
    grad_low = grad_score.astype(jnp.bfloat16)
    grad_query = (
        jnp.einsum("hqk,khd->qhd", grad_low, key_heads, preferred_element_type=jnp.float32) * 0.125
    )
    grad_key = (
        jnp.einsum("hqk,qhd->khd", grad_low, query_heads, preferred_element_type=jnp.float32)
        * 0.125
    )
    return (grad_query, grad_key, grad_value, grad_low)


def adam_step(weight, first, second, grad, rate, shrink):
    first_new = beta_one * first + (1.0 - beta_one) * grad
    second_new = beta_two * second + (1.0 - beta_two) * grad * grad
    first_hat = first_new / (1.0 - beta_one**STEP)
    second_hat = second_new / (1.0 - beta_two**STEP)
    weight_new = weight - rate * (first_hat / (jnp.sqrt(second_hat) + adam_eps) + shrink * weight)
    return (weight_new, first_new, second_new)


MESH = pl.DeviceIdType.MESH
VMEM_LIMIT = 64 * 1024 * 1024 - 65536
ANY = pl.BlockSpec(memory_space=pl.ANY)
VM = pl.BlockSpec(memory_space=pltpu.VMEM)


def place(index, n_pair):
    return {"dp": index // n_pair, "pair": lax.rem(index, n_pair)}


def remote(src, dst, send, recv, target):
    return pltpu.make_async_remote_copy(
        src, dst, send, recv, device_id=target, device_id_type=MESH
    )


def greet(targets):
    sem = pltpu.get_barrier_semaphore()
    for target in targets:
        pl.semaphore_signal(sem, inc=1, device_id=target, device_id_type=MESH)
    pl.semaphore_wait(sem, len(targets))


def my_index(n_pair):
    return lax.axis_index("dp") * n_pair + lax.axis_index("pair")


def bit_order(n_dp, n_pair, color):
    dp_bits, pair_bits = (n_dp - 1).bit_length(), (n_pair - 1).bit_length()
    high = list(reversed(range(pair_bits + 1, pair_bits + dp_bits))) + [pair_bits]
    side = list(reversed(range(1, pair_bits)))
    return high + side if color == 0 else side + high


def offset(order, position):
    return sum(((position >> step) & 1) << bit for step, bit in enumerate(order))


def scatter_kernel(n_dp, n_pair, pieces, n_in, *refs):
    k = len(pieces)
    ins, outs = refs[:n_in], refs[n_in : 2 * n_in]
    accs = refs[2 * n_in : 2 * n_in + k]
    gots = refs[2 * n_in + k : 2 * n_in + 2 * k]
    lsem, csend, crecv, send, recv = refs[2 * n_in + 2 * k :]
    me = my_index(n_pair)
    n = n_dp * n_pair
    steps = (n - 1).bit_length() - 1
    half = 1 << steps
    orders = [bit_order(n_dp, n_pair, color) for _, _, _, color in pieces]
    greet([place(me ^ (1 << bit), n_pair) for bit in range(steps + 1)])

    def source(a, block):
        which, low, high, _ = pieces[a]
        return ins[which].at[block, :, pl.ds(low, high - low)]

    def core_send(a, upper):
        lo = half // 2 if upper else 0
        for p in range(lo, lo + half // 2):
            block = me ^ (offset(orders[a], p) + 1)
            remote(source(a, block), gots[a].at[p], csend.at[a, upper], crecv.at[a, upper], place(me ^ 1, n_pair)).start()

    def load(a):
        for p in range(half):
            pltpu.make_async_copy(source(a, me ^ offset(orders[a], p)), accs[a].at[p], lsem.at[a]).start()

    def core_copy(a, upper):
        lo = half // 2 if upper else 0
        part = pl.ds(lo, half // 2)
        return remote(gots[a].at[part], gots[a].at[part], csend.at[a, upper], crecv.at[a, upper], place(me ^ 1, n_pair))

    def add(a, lo, count, base):
        def body(j, carry):
            accs[a][lo + j] = (
                accs[a][lo + j].astype(jnp.float32) + gots[a][base + lo + j].astype(jnp.float32)
            ).astype(jnp.bfloat16)
            return carry
        lax.fori_loop(0, count, body, 0)

    def base_of(s):
        return half + half - (2 << s)

    def hop(a, s):
        return remote(
            accs[a].at[pl.ds(1 << s, 1 << s)], gots[a].at[pl.ds(base_of(s), 1 << s)],
            send.at[a, s], recv.at[a, s], place(me ^ (1 << orders[a][s]), n_pair),
        )

    for upper in (1, 0):
        for a in range(k):
            core_send(a, upper)
            if upper:
                load(a)
    for a in range(k):
        pltpu.make_async_copy(accs[a], accs[a], lsem.at[a]).wait()
        core_copy(a, 1).wait_recv()
        add(a, half // 2, half // 2, 0)
        hop(a, steps - 1).start()
    for a in range(k):
        core_copy(a, 0).wait_recv()
        add(a, 0, half // 2, 0)
    for s in reversed(range(steps)):
        for a in range(k):
            hop(a, s).wait_recv()
            if s:
                mid = 1 << (s - 1)
                add(a, mid, mid, base_of(s))
                hop(a, s - 1).start()
                add(a, 0, mid, base_of(s))
            else:
                which, low, high, _ = pieces[a]
                outs[which][:, low:high] = accs[a][0].astype(jnp.float32) + gots[a][
                    base_of(0)
                ].astype(jnp.float32)
    for a in range(k):
        core_copy(a, 1).wait_send()
        core_copy(a, 0).wait_send()
        for s in range(steps):
            hop(a, s).wait_send()


def scatter_all(grads, pieces, n_dp, n_pair, cid):
    n, k = n_dp * n_pair, len(pieces)
    steps = (n - 1).bit_length() - 1
    half = n // 2
    shape = lambda p, lead: (lead, grads[p[0]].shape[1], p[2] - p[1])
    return pl.pallas_call(
        functools.partial(scatter_kernel, n_dp, n_pair, pieces, len(grads)),
        out_shape=[jax.ShapeDtypeStruct(g.shape[1:], jnp.float32) for g in grads],
        in_specs=[ANY] * len(grads),
        out_specs=[VM] * len(grads),
        scratch_shapes=[pltpu.VMEM(shape(p, half), jnp.bfloat16) for p in pieces]
        + [pltpu.VMEM(shape(p, 2 * half - 1), jnp.bfloat16) for p in pieces]
        + [
            pltpu.SemaphoreType.DMA((k,)),
            pltpu.SemaphoreType.DMA((k, 2)),
            pltpu.SemaphoreType.DMA((k, 2)),
            pltpu.SemaphoreType.DMA((k, steps)),
            pltpu.SemaphoreType.DMA((k, steps)),
        ],
        compiler_params=pltpu.CompilerParams(
            collective_id=cid, has_side_effects=True, vmem_limit_bytes=VMEM_LIMIT
        ),
        name="weight_grads_sum",
    )(*grads)


def spread(n, n_pair, block, everyone, send, recv, own_sem):
    me = my_index(n_pair)
    sem = pltpu.get_barrier_semaphore()

    def hello(k, carry):
        pl.semaphore_signal(sem, inc=1, device_id=place(me ^ k, n_pair), device_id_type=MESH)
        return carry

    lax.fori_loop(1, n, hello, 0)
    own = pltpu.make_async_copy(block, everyone.at[me], own_sem)
    own.start()
    pl.semaphore_wait(sem, n - 1)

    def go(k, carry):
        remote(block, everyone.at[me], send.at[k], recv.at[k], place(me ^ k, n_pair)).start()
        return carry

    lax.fori_loop(1, n, go, 0)
    own.wait()

    def done(k, carry):
        remote(block, everyone.at[me ^ k], send.at[k], recv.at[k], place(me ^ k, n_pair)).wait()
        return carry

    lax.fori_loop(1, n, done, 0)


def total_kernel(n, n_pair, x_ref, o_ref, everyone, send, recv, own_sem):
    spread(n, n_pair, x_ref, everyone, send, recv, own_sem)
    def add(j, total):
        return total + everyone[j]
    o_ref[...] = lax.fori_loop(1, n, add, everyone[0])


def small_total(x, n_dp, n_pair, cid):
    n = n_dp * n_pair
    return pl.pallas_call(
        functools.partial(total_kernel, n, n_pair),
        out_shape=jax.ShapeDtypeStruct(x.shape, x.dtype),
        in_specs=[VM], out_specs=VM,
        scratch_shapes=[pltpu.VMEM((n,) + x.shape, x.dtype), pltpu.SemaphoreType.DMA((n,)), pltpu.SemaphoreType.DMA((n,)), pltpu.SemaphoreType.DMA],
        compiler_params=pltpu.CompilerParams(collective_id=cid, has_side_effects=True),
        name="small_total",
    )(x)


def loss_kernel(n, n_pair, docs, x_ref, pos_ref, neg_ref, count_ref, loss_ref, grad_ref, everyone, grads, send, recv, own_sem):
    spread(n, n_pair, x_ref, everyone, send, recv, own_sem)
    total = n * docs
    width = x_ref.shape[1]
    pooled = everyone[...].reshape(total, width)
    inverse = lax.rsqrt(jnp.sum(pooled * pooled, axis=1, keepdims=True) + 1e-06)
    unit = pooled * inverse
    similar = 20.0 * lax.dot_general(unit, unit, (((1,), (1,)), ((), ())), precision=HIGHEST, preferred_element_type=jnp.float32)
    columns = lax.broadcasted_iota(jnp.int32, (total, total), 1)
    is_pos = columns == pos_ref[...]
    chosen = jnp.sum(jnp.where(is_pos, similar, 0.0), axis=1, keepdims=True)
    counts = count_ref[...]
    weight = 1.0 / (counts.astype(jnp.float32) * total)
    loss_rows = jnp.zeros((total, 1), jnp.float32)
    grad_similar = jnp.zeros((total, total), jnp.float32)
    pulled = jnp.zeros((total, 1), jnp.float32)
    for slot in range(neg_ref.shape[1]):
        is_neg = columns == neg_ref[:, slot : slot + 1]
        against = jnp.sum(jnp.where(is_neg, similar, 0.0), axis=1, keepdims=True)
        value = 1.0 - chosen + against
        used = slot < counts
        soft = jnp.maximum(value, 0.0) + jnp.log1p(jnp.exp(-jnp.abs(value)))
        loss_rows = loss_rows + jnp.where(used, soft, 0.0)
        slope = jnp.where(used, weight / (1.0 + jnp.exp(-value)), 0.0)
        grad_similar = grad_similar + jnp.where(is_neg, slope, 0.0)
        pulled = pulled + slope
    grad_similar = grad_similar - jnp.where(is_pos, pulled, 0.0)
    loss_ref[...] = jnp.sum(loss_rows * weight, axis=0, keepdims=True)
    dims = (((1,), (0,)), ((), ()))
    grad_unit = lax.dot_general(grad_similar, unit, dims, precision=HIGHEST, preferred_element_type=jnp.float32)
    grad_unit = grad_unit + lax.dot_general(grad_similar, unit, (((0,), (0,)), ((), ())), precision=HIGHEST, preferred_element_type=jnp.float32)
    grad_unit = 20.0 * grad_unit
    inner = jnp.sum(grad_unit * unit, axis=1, keepdims=True)
    grads[...] = (inverse * (grad_unit - unit * inner)).reshape(n, docs, width)
    grad_ref[...] = grads[my_index(n_pair)]


def pooled_loss(pooled, positives, negatives, counts, n_dp, n_pair, cid):
    n = n_dp * n_pair
    docs, width = pooled.shape
    return pl.pallas_call(
        functools.partial(loss_kernel, n, n_pair, docs),
        out_shape=[jax.ShapeDtypeStruct((1, 1), jnp.float32), jax.ShapeDtypeStruct(pooled.shape, jnp.float32)],
        in_specs=[VM] * 4, out_specs=[VM] * 2,
        scratch_shapes=[pltpu.VMEM((n,) + pooled.shape, jnp.float32), pltpu.VMEM((n,) + pooled.shape, jnp.float32),
            pltpu.SemaphoreType.DMA((n,)), pltpu.SemaphoreType.DMA((n,)), pltpu.SemaphoreType.DMA],
        compiler_params=pltpu.CompilerParams(collective_id=cid, has_side_effects=True),
        name="pooled_loss",
    )(pooled, positives[:, None], negatives, counts[:, None])


def table_kernel(n_pair, rows, chunk, arr_ref, ask_ref, out_ref, sq_ref, hot, stage, part, got_c, out_x, got_x, fin, fin_other,
                 csend, crecv, xsend, xrecv, fsend, frecv, wsem):
    me_dp, me_pair = lax.axis_index("dp"), lax.axis_index("pair")
    core = lax.rem(me_pair, 2)
    partner = {"dp": me_dp, "pair": me_pair ^ 1}
    across = {"dp": me_dp, "pair": me_pair ^ 2}
    count = rows // 2 // chunk
    greet([partner, across])
    slots = ask_ref.shape[1]

    def summed(base):
        ids = lax.broadcasted_iota(jnp.int32, (chunk, slots), 0) + base
        hot[...] = jnp.where(ids == ask_ref[...], 1.0, 0.0).astype(jnp.bfloat16)
        return jnp.dot(hot[...], arr_ref[...], preferred_element_type=jnp.float32)

    def c_copy(i):
        return remote(stage.at[i], got_c.at[i], csend.at[i], crecv.at[i], partner)

    def x_copy(i):
        return remote(out_x.at[i], got_x.at[i], xsend.at[i], xrecv.at[i], across)

    def f_copy(i):
        return remote(fin.at[i], fin_other.at[i], fsend.at[i], frecv.at[i], partner)

    for i in range(count):
        stage[i] = summed((1 - core) * (rows // 2) + i * chunk).astype(jnp.bfloat16)
        c_copy(i).start()
    for i in range(count):
        part[...] = summed(core * (rows // 2) + i * chunk)
        c_copy(i).wait_recv()
        out_x[i] = (part[...] + got_c[i].astype(jnp.float32)).astype(jnp.bfloat16)
        x_copy(i).start()
    square = jnp.zeros((1, 1), jnp.float32)
    for i in range(count):
        x_copy(i).wait_recv()
        value = (out_x[i].astype(jnp.float32) + got_x[i].astype(jnp.float32)).astype(jnp.bfloat16)
        fin[i] = value
        f_copy(i).start()
        pltpu.make_async_copy(fin.at[i], out_ref.at[pl.ds(core * (rows // 2) + i * chunk, chunk)], wsem.at[0]).start()
        wide = value.astype(jnp.float32)
        square = square + jnp.sum(jnp.sum(wide * wide, axis=0, keepdims=True), axis=1, keepdims=True)
    sq_ref[...] = jnp.where(me_pair < 2, square, 0.0)
    for i in range(count):
        f_copy(i).wait_recv()
        pltpu.make_async_copy(fin_other.at[i], out_ref.at[pl.ds((1 - core) * (rows // 2) + i * chunk, chunk)], wsem.at[1]).start()
    for i in range(count):
        c_copy(i).wait_send()
        x_copy(i).wait_send()
        f_copy(i).wait_send()
    pltpu.make_async_copy(fin, fin, wsem.at[0]).wait()
    pltpu.make_async_copy(fin_other, fin_other, wsem.at[1]).wait()


def table_total(arrived, asked, rows, n_pair, cid):
    chunk, width = 512, arrived.shape[1]
    count = rows // 2 // chunk
    box = pltpu.VMEM((count, chunk, width), jnp.bfloat16)
    sem = pltpu.SemaphoreType.DMA((count,))
    return pl.pallas_call(
        functools.partial(table_kernel, n_pair, rows, chunk),
        out_shape=[jax.ShapeDtypeStruct((rows, width), jnp.bfloat16), jax.ShapeDtypeStruct((1, 1), jnp.float32)],
        in_specs=[VM, VM], out_specs=[ANY, VM],
        scratch_shapes=[pltpu.VMEM((chunk, asked.shape[1]), jnp.bfloat16), box, pltpu.VMEM((chunk, width), jnp.float32), box, box, box, box, box,
            sem, sem, sem, sem, sem, sem, pltpu.SemaphoreType.DMA((2,))],
        compiler_params=pltpu.CompilerParams(collective_id=cid, has_side_effects=True, vmem_limit_bytes=VMEM_LIMIT),
        name="table_total",
    )(arrived, asked)


def gather_kernel(n_dp, n_pair, pieces, n_in, *refs):
    k = len(pieces)
    ins, outs = refs[:n_in], refs[n_in : 2 * n_in]
    bufs = refs[2 * n_in : 2 * n_in + k]
    send, recv, csend, crecv, wsem, isem = refs[2 * n_in + k :]
    me = my_index(n_pair)
    steps = (n_dp * n_pair - 1).bit_length() - 1
    half = 1 << steps
    orders = [bit_order(n_dp, n_pair, color) for _, _, _, color in pieces]

    def load(a):
        which, low, high, _ = pieces[a]
        return pltpu.make_async_copy(
            ins[which].at[:, pl.ds(low, high - low)], bufs[a].at[0], isem.at[a]
        )

    for a in range(k):
        load(a).start()
    greet([place(me ^ (1 << bit), n_pair) for bit in range(steps + 1)])

    def write_out(a, lo, count, core):
        which, low, high, _ = pieces[a]
        for p in range(lo, lo + count):
            block = me ^ (offset(orders[a], p) + core)
            pltpu.make_async_copy(
                bufs[a].at[p + core * half],
                outs[which].at[block, :, pl.ds(low, high - low)],
                wsem.at[a],
            ).start()

    def forward(a, s):
        lo, count = (0, 1) if s == 0 else (1 << (s - 1), 1 << (s - 1))
        return remote(
            bufs[a].at[pl.ds(lo, count)],
            bufs[a].at[pl.ds(half + lo, count)],
            csend.at[a, s],
            crecv.at[a, s],
            place(me ^ 1, n_pair),
        )

    def hop(a, s):
        return remote(
            bufs[a].at[pl.ds(0, 1 << s)],
            bufs[a].at[pl.ds(1 << s, 1 << s)],
            send.at[a, s],
            recv.at[a, s],
            place(me ^ (1 << orders[a][s]), n_pair),
        )

    for a in range(k):
        load(a).wait()
        hop(a, 0).start()
    for a in range(k):
        forward(a, 0).start()
        write_out(a, 0, 1, 0)
    for s in range(steps):
        for a in range(k):
            hop(a, s).wait_recv()
            if s + 1 < steps:
                hop(a, s + 1).start()
            forward(a, s + 1).start()
            write_out(a, 1 << s, 1 << s, 0)
        for a in range(k):
            forward(a, s).wait_recv()
            lo, count = (0, 1) if s == 0 else (1 << (s - 1), 1 << (s - 1))
            write_out(a, lo, count, 1)
    for a in range(k):
        forward(a, steps).wait_recv()
        write_out(a, half // 2, half // 2, 1)
    for a in range(k):
        for s in range(steps):
            hop(a, s).wait_send()
        for s in range(steps + 1):
            forward(a, s).wait_send()
        pltpu.make_async_copy(bufs[a], bufs[a], wsem.at[a]).wait()


def gather_all(shards, pieces, n_dp, n_pair, cid):
    n, k = n_dp * n_pair, len(pieces)
    steps = (n - 1).bit_length() - 1
    return pl.pallas_call(
        functools.partial(gather_kernel, n_dp, n_pair, pieces, len(shards)),
        out_shape=[jax.ShapeDtypeStruct((n,) + s.shape, s.dtype) for s in shards],
        in_specs=[ANY] * len(shards),
        out_specs=[ANY] * len(shards),
        scratch_shapes=[
            pltpu.VMEM((n, shards[p[0]].shape[0], p[2] - p[1]), jnp.bfloat16) for p in pieces
        ]
        + [
            pltpu.SemaphoreType.DMA((k, steps)),
            pltpu.SemaphoreType.DMA((k, steps)),
            pltpu.SemaphoreType.DMA((k, steps + 1)),
            pltpu.SemaphoreType.DMA((k, steps + 1)),
            pltpu.SemaphoreType.DMA((k,)),
            pltpu.SemaphoreType.DMA((k,)),
        ],
        compiler_params=pltpu.CompilerParams(
            collective_id=cid, has_side_effects=True, vmem_limit_bytes=VMEM_LIMIT
        ),
        name="weights_gather",
    )(*shards)

def exchange_kernel(n_dp, x_ref, o_ref, send, recv, lsem):
    me = lax.axis_index("dp"); pr = lax.axis_index("pair")
    sem = pltpu.get_barrier_semaphore()
    def greet(k, _):
        pl.semaphore_signal(sem, inc=1, device_id={"dp": lax.rem(me + k, n_dp), "pair": pr}, device_id_type=MESH)
        return 0
    lax.fori_loop(1, n_dp, greet, 0)
    pl.semaphore_wait(sem, n_dp - 1)
    own = pltpu.make_async_copy(x_ref.at[me], o_ref.at[me], lsem); own.start()
    def cp(k):
        dst = lax.rem(me + k, n_dp)
        return pltpu.make_async_remote_copy(x_ref.at[dst], o_ref.at[me], send.at[k], recv.at[k],
            device_id={"dp": dst, "pair": pr}, device_id_type=MESH)
    def go(k, _):
        cp(k).start(); return 0
    lax.fori_loop(1, n_dp, go, 0)
    def done(k, _):
        src = lax.rem(me + n_dp - k, n_dp)
        c = pltpu.make_async_remote_copy(x_ref.at[me], o_ref.at[src], send.at[k], recv.at[k],
            device_id={"dp": src, "pair": pr}, device_id_type=MESH)
        c.wait(); return 0
    own.wait()
    lax.fori_loop(1, n_dp, done, 0)

def exchange(x, n_dp, cid):
    return pl.pallas_call(
        functools.partial(exchange_kernel, n_dp),
        out_shape=jax.ShapeDtypeStruct(x.shape, x.dtype),
        in_specs=[pl.BlockSpec(memory_space=pltpu.VMEM)], out_specs=pl.BlockSpec(memory_space=pltpu.VMEM),
        scratch_shapes=[pltpu.SemaphoreType.DMA((n_dp,)), pltpu.SemaphoreType.DMA((n_dp,)), pltpu.SemaphoreType.DMA],
        compiler_params=pltpu.CompilerParams(collective_id=cid, has_side_effects=True, vmem_limit_bytes=VMEM_LIMIT),
        name="rows_exchange",
    )(x)


NT = (((1,), (1,)), ((), ()))
TN = (((0,), (0,)), ((), ()))

def band(w_ref, h, table, seq):
    tiles = seq // 128
    for d in range(1 - tiles, tiles):
        low = seq + 128 * d - 128
        x = jnp.broadcast_to(w_ref[0, h : h + 1, low : low + 256], (128, 256))
        tile = pltpu.roll(x, 0, 1, stride=1, stride_axis=0)[:, 128:]
        for a in range(tiles):
            if 0 <= a + d < tiles:
                table[h, a * 128 : a * 128 + 128, (a + d) * 128 : (a + d) * 128 + 128] = tile

def forward_kernel(len_ref, q_ref, k_ref, v_ref, w_ref, o_ref, table):
    seq = q_ref.shape[0]
    doc = pl.program_id(1)
    @pl.when(doc == 0)
    def _():
        for h in range(2):
            band(w_ref, h, table, seq)
    length = len_ref[doc]
    lane = lax.broadcasted_iota(jnp.int32, (seq, 128), 1)
    column = lax.broadcasted_iota(jnp.int32, (1, seq), 1)
    q = q_ref[...] * jnp.bfloat16(0.125)
    k = k_ref[...]
    v = v_ref[...]
    got = []
    for h in range(2):
        mine = (lane < 64) == (h == 0)
        s = lax.dot_general(jnp.where(mine, q, 0), k, NT, preferred_element_type=jnp.float32)
        s = jnp.where(column < length, s + table[h], -1000000000.0)
        e = jnp.exp(s - jnp.max(s, axis=1, keepdims=True))
        p = (e * (1.0 / jnp.sum(e, axis=1, keepdims=True))).astype(jnp.bfloat16)
        got.append(jnp.dot(p, v, preferred_element_type=jnp.float32))
    o_ref[...] = jnp.where(lane < 64, got[0], got[1]).astype(o_ref.dtype)

def attention(lengths, qkv, w, seq):
    tokens = qkv.shape[0]
    pairs = w.shape[0]
    docs = tokens // seq
    spec = lambda base: pl.BlockSpec((seq, 128), lambda h, d, *_: (d, base + h))
    return pl.pallas_call(
        forward_kernel,
        grid_spec=pltpu.PrefetchScalarGridSpec(
            num_scalar_prefetch=1, grid=(pairs, docs),
            in_specs=[spec(0), spec(pairs), spec(2 * pairs), pl.BlockSpec((1, 2, 2 * seq), lambda h, d, *_: (h, 0, 0))],
            out_specs=spec(0),
            scratch_shapes=[pltpu.VMEM((2, seq, seq), jnp.float32)]),
        out_shape=jax.ShapeDtypeStruct((tokens, pairs * 128), jnp.bfloat16),
        compiler_params=pltpu.CompilerParams(dimension_semantics=("arbitrary", "arbitrary"), vmem_limit_bytes=50 * 1024 * 1024),
        name="attention",
    )(lengths, qkv, qkv, qkv, w)

def backward_kernel(len_ref, q_ref, k_ref, v_ref, g_ref, w_ref, o_ref, z_ref, table, total):
    seq = q_ref.shape[0]
    tiles = seq // 128
    doc = pl.program_id(1)
    @pl.when(doc == 0)
    def _():
        for h in range(2):
            band(w_ref, h, table, seq)
        total[...] = jnp.zeros_like(total)
    length = len_ref[doc]
    lane = lax.broadcasted_iota(jnp.int32, (seq, 128), 1)
    row = lax.broadcasted_iota(jnp.int32, (seq, 1), 0)
    q = q_ref[...] * jnp.bfloat16(0.125)
    k = k_ref[...]
    v = v_ref[...]
    g = g_ref[...]
    parts = []
    for h in range(2):
        mine = (lane < 64) == (h == 0)
        s = lax.dot_general(k, jnp.where(mine, q, 0), NT, preferred_element_type=jnp.float32)
        s = jnp.where(row < length, s + table[h], -1000000000.0)
        e = jnp.exp(s - jnp.max(s, axis=0, keepdims=True))
        p = e * (1.0 / jnp.sum(e, axis=0, keepdims=True))
        dv = jnp.dot(p.astype(jnp.bfloat16), g, preferred_element_type=jnp.float32)
        dp = lax.dot_general(v, jnp.where(mine, g, 0), NT, preferred_element_type=jnp.float32)
        ds = (p * (dp - jnp.sum(p * dp, axis=0, keepdims=True))).astype(jnp.bfloat16)
        total[h] += ds.astype(jnp.float32)
        dk = jnp.dot(ds, q, preferred_element_type=jnp.float32)
        dq = lax.dot_general(ds, k, TN, preferred_element_type=jnp.float32) * 0.125
        parts.append((dq, dk, dv))
    for i in range(3):
        o_ref[i] = jnp.where(lane < 64, parts[0][i], parts[1][i]).astype(o_ref.dtype)
    @pl.when(doc == pl.num_programs(1) - 1)
    def _():
        r = lax.broadcasted_iota(jnp.int32, (128, 128), 0)
        c = lax.broadcasted_iota(jnp.int32, (128, 128), 1)
        flip = jnp.where(r + c == 127, 1.0, 0.0)
        z_ref[...] = jnp.zeros_like(z_ref)
        for h in range(2):
            def block(d):
                return sum(total[h, a * 128 : a * 128 + 128, (a - d) * 128 : (a - d) * 128 + 128] for a in range(tiles) if 0 <= a - d < tiles)
            for d in (-1, 0, 1):
                x = jnp.dot(flip, block(d), precision=HIGHEST, preferred_element_type=jnp.float32)
                x = jnp.concatenate([x, jnp.zeros_like(x)], axis=1)
                x = pltpu.roll(x, 0, 1, stride=1, stride_axis=0)
                z_ref[0, h, d + 1 : d + 2, :] = jnp.sum(x, axis=0, keepdims=True)
            z_ref[0, h, 3:4, 0:128] = jnp.sum(sum(block(-d) for d in range(2, tiles)), axis=0, keepdims=True)
            z_ref[0, h, 4:5, 0:128] = jnp.sum(sum(block(d) for d in range(2, tiles)), axis=0, keepdims=True)

def attention_back(lengths, qkv, g, w, seq):
    tokens = qkv.shape[0]
    pairs = w.shape[0]
    docs = tokens // seq
    spec = lambda base: pl.BlockSpec((seq, 128), lambda h, d, *_: (d, base + h))
    return pl.pallas_call(
        backward_kernel,
        grid_spec=pltpu.PrefetchScalarGridSpec(
            num_scalar_prefetch=1, grid=(pairs, docs),
            in_specs=[spec(0), spec(pairs), spec(2 * pairs), spec(0), pl.BlockSpec((1, 2, 2 * seq), lambda h, d, *_: (h, 0, 0))],
            out_specs=[pl.BlockSpec((3, seq, 128), lambda h, d, *_: (0, d, h)), pl.BlockSpec((1, 2, 8, 256), lambda h, d, *_: (h, 0, 0, 0))],
            scratch_shapes=[pltpu.VMEM((2, seq, seq), jnp.float32), pltpu.VMEM((2, seq, seq), jnp.float32)]),
        out_shape=[jax.ShapeDtypeStruct((3, tokens, pairs * 128), jnp.bfloat16), jax.ShapeDtypeStruct((pairs, 2, 8, 256), jnp.float32)],
        compiler_params=pltpu.CompilerParams(dimension_semantics=("arbitrary", "arbitrary"), vmem_limit_bytes=50 * 1024 * 1024),
        name="attention_back",
    )(lengths, qkv, qkv, qkv, g, w)

def bias_rows(position_bias, seq, sign):
    nb, heads = position_bias.shape
    buckets = bucket_of(sign * (jnp.arange(2 * seq) - seq), nb, REACH)
    hits = (jnp.arange(nb)[:, None] == buckets[None, :]).astype(jnp.float32)
    return jnp.dot(position_bias.T, hits, precision=HIGHEST).reshape(heads // 2, 2, 2 * seq)

def bias_gradient(z, seq, nb):
    heads = z.shape[0] * 2
    j = jnp.arange(256)
    offs = [jnp.where(j < 255, 128 * d + 127 - j, 0) for d in (-1, 0, 1)] + [jnp.full((256,), 1 - seq), jnp.full((256,), seq - 1)]
    offs = jnp.concatenate(offs + [jnp.zeros((768,), jnp.int32)])
    hits = (bucket_of(offs, nb, REACH)[:, None] == jnp.arange(nb)[None, :]).astype(jnp.float32)
    return jnp.dot(z.reshape(heads, 2048), hits, precision=HIGHEST).T

def weight_pieces(widths):
    down = len(widths) - 1
    cut = widths[down] * 2 // 3 // 128 * 128
    pieces = [(down - 1, 0, widths[down - 1], 0)]
    pieces += [(which, 0, widths[which], 1) for which in range(down - 2)]
    pieces += [(down - 2, 0, widths[down - 2], 0)]
    return pieces + [(down, 0, cut, 0), (down, cut, widths[down], 1)]


def local_plain(
    token_owner,
    token_row,
    lengths,
    positives,
    negatives,
    neg_counts,
    embed_table,
    embed_first,
    embed_second,
    qkv_weight,
    qkv_first,
    qkv_second,
    out_weight,
    out_first,
    out_second,
    in_weight,
    in_first,
    in_second,
    down_weight,
    down_first,
    down_second,
    norm_gains,
    gains_first,
    gains_second,
    position_bias,
    bias_first,
    bias_second,
):
    doc_count = lengths.shape[0]
    seq_len = token_row.shape[1]
    model_width = embed_table.shape[1]
    head_count = position_bias.shape[1]
    bucket_count = position_bias.shape[0]
    tok_total = doc_count * seq_len
    owners = lax.axis_size("dp")
    capacity = max(2, 2 * tok_total // owners)
    low_mats = (
        qkv_weight.astype(jnp.bfloat16),
        out_weight.astype(jnp.bfloat16),
        in_weight.astype(jnp.bfloat16),
        down_weight.astype(jnp.bfloat16),
    )
    qkv_full, out_full, in_full, down_full = (
        lax.all_gather(low_mats[0], ("dp", "pair"), axis=0, tiled=True),
        lax.all_gather(low_mats[1], ("dp", "pair"), axis=0, tiled=True),
        lax.all_gather(low_mats[2], ("dp", "pair"), axis=0, tiled=True),
        lax.all_gather(low_mats[3], ("dp", "pair"), axis=0, tiled=True),
    )
    tok_owner = token_owner.reshape(-1)
    tok_row = token_row.reshape(-1)
    owner_hits = (tok_owner[:, None] == jnp.arange(owners, dtype=jnp.int32)[None, :]).astype(
        jnp.int32
    )
    slot_rank = jnp.sum((jnp.cumsum(owner_hits, axis=0) - 1) * owner_hits, axis=1)
    requests = jnp.zeros((owners, capacity), jnp.int32).at[tok_owner, slot_rank].set(tok_row)
    asked_rows = lax.all_to_all(requests, "dp", split_axis=0, concat_axis=0, tiled=True)
    looked = jnp.take(embed_table, asked_rows.reshape(-1), axis=0).astype(jnp.bfloat16)
    answer = lax.all_to_all(
        looked.reshape(asked_rows.shape + (model_width,)),
        "dp",
        split_axis=0,
        concat_axis=0,
        tiled=True,
    )
    replies, asked_rows = (answer, asked_rows)
    embedded = replies[tok_owner, slot_rank].astype(jnp.float32)
    positions = jnp.arange(seq_len)
    live = positions[None, :] < lengths[:, None]
    pair_buckets = bucket_of(
        (positions[None, :] - positions[:, None]).reshape(-1), bucket_count, REACH
    )
    pair_hits = (jnp.arange(bucket_count)[:, None] == pair_buckets[None, :]).astype(jnp.float32)
    bias_full = jnp.dot(position_bias.T, pair_hits, precision=HIGHEST).reshape(
        head_count, seq_len, seq_len
    )
    bucket_map = pair_hits.astype(jnp.bfloat16)

    def split_doc(source, doc_index):
        doc_rows = source[doc_index * seq_len : (doc_index + 1) * seq_len]
        return tuple(
            (
                doc_rows[:, member * model_width : (member + 1) * model_width].reshape(
                    seq_len, head_count, -1
                )
                for member in range(3)
            )
        )

    normed_one, inverse_one = rms_forward(embedded, norm_gains[0])
    normed_one = normed_one.astype(jnp.bfloat16)
    qkv_rows = jnp.dot(normed_one, qkv_full, preferred_element_type=jnp.float32).astype(
        jnp.bfloat16
    )
    attended_parts = []
    logsum_parts = []
    for doc_index in range(doc_count):
        query_heads, key_heads, value_heads = split_doc(qkv_rows, doc_index)
        doc_out, logsum = attend_forward(
            query_heads, key_heads, value_heads, bias_full, live[doc_index]
        )
        attended_parts.append(doc_out.reshape(seq_len, model_width))
        logsum_parts.append(logsum)
    attended = jnp.concatenate(attended_parts, axis=0).astype(jnp.bfloat16)
    residual = embedded + jnp.dot(attended, out_full, preferred_element_type=jnp.float32)
    normed_two, inverse_two = rms_forward(residual, norm_gains[1])
    normed_two = normed_two.astype(jnp.bfloat16)
    hidden = jax.nn.relu(jnp.dot(normed_two, in_full, preferred_element_type=jnp.float32)).astype(
        jnp.bfloat16
    )
    output_rows = residual + jnp.dot(hidden, down_full, preferred_element_type=jnp.float32)
    normed_three, inverse_three = rms_forward(output_rows, norm_gains[2])
    live_rows = live.reshape(-1, 1)
    length_float = lengths.astype(jnp.float32)
    pooled_local = (
        jnp.sum(
            jnp.where(live_rows, normed_three, 0.0).reshape(doc_count, seq_len, model_width), axis=1
        )
        / length_float[:, None]
    )
    pooled_all = lax.all_gather(pooled_local, ("dp", "pair"), axis=0, tiled=True)
    loss_value, loss_pullback = jax.vjp(
        lambda pooled_in: margin_loss(pooled_in, positives, negatives, neg_counts), pooled_all
    )
    grad_pooled_all = loss_pullback(jnp.ones((), jnp.float32))[0]
    grad_pooled = lax.dynamic_slice_in_dim(
        grad_pooled_all, lax.axis_index(("dp", "pair")) * doc_count, doc_count, 0
    )
    grad_three = jnp.where(
        live_rows, jnp.repeat(grad_pooled / length_float[:, None], seq_len, axis=0), 0.0
    )
    qkv_back, out_back, in_back, down_back = (qkv_full, out_full, in_full, down_full)
    grad_output, gain_three = rms_backward(output_rows, inverse_three, norm_gains[2], grad_three)
    grad_branch = grad_output.astype(jnp.bfloat16)
    grad_down = lax.dot_general(
        hidden, grad_branch, CONTRACT_ROWS, preferred_element_type=jnp.float32
    )
    grad_hidden = lax.dot_general(
        grad_branch, down_back, CONTRACT_COLS, preferred_element_type=jnp.float32
    )
    grad_pre = jnp.where(hidden > 0, grad_hidden, 0.0).astype(jnp.bfloat16)
    grad_in = lax.dot_general(
        normed_two, grad_pre, CONTRACT_ROWS, preferred_element_type=jnp.float32
    )
    grad_normed_two = lax.dot_general(
        grad_pre, in_back, CONTRACT_COLS, preferred_element_type=jnp.float32
    )
    grad_res_part, gain_two = rms_backward(residual, inverse_two, norm_gains[1], grad_normed_two)
    grad_residual = grad_output + grad_res_part
    grad_attn_branch = grad_residual.astype(jnp.bfloat16)
    grad_out = lax.dot_general(
        attended, grad_attn_branch, CONTRACT_ROWS, preferred_element_type=jnp.float32
    )
    grad_attended = lax.dot_general(
        grad_attn_branch, out_back, CONTRACT_COLS, preferred_element_type=jnp.float32
    ).astype(jnp.bfloat16)
    grad_qkv_parts = []
    bias_grad_heads = jnp.zeros((head_count, bucket_count), jnp.float32)
    for doc_index in range(doc_count):
        query_heads, key_heads, value_heads = split_doc(qkv_rows, doc_index)
        grad_doc = grad_attended[doc_index * seq_len : (doc_index + 1) * seq_len].reshape(
            seq_len, head_count, -1
        )
        grad_query, grad_key, grad_value, grad_low = attend_backward(
            query_heads,
            key_heads,
            value_heads,
            bias_full,
            live[doc_index],
            logsum_parts[doc_index],
            grad_doc,
        )
        grad_qkv_parts.append(
            jnp.concatenate(
                [
                    grad_query.reshape(seq_len, model_width),
                    grad_key.reshape(seq_len, model_width),
                    grad_value.reshape(seq_len, model_width),
                ],
                axis=1,
            )
        )
        bias_grad_heads = bias_grad_heads + lax.dot_general(
            grad_low.reshape(head_count, -1),
            bucket_map,
            CONTRACT_COLS,
            preferred_element_type=jnp.float32,
        )
    bias_grad_local = bias_grad_heads.T
    grad_qkv_rows = jnp.concatenate(grad_qkv_parts, axis=0).astype(jnp.bfloat16)
    grad_qkv = lax.dot_general(
        normed_one, grad_qkv_rows, CONTRACT_ROWS, preferred_element_type=jnp.float32
    )
    grad_normed_one = lax.dot_general(
        grad_qkv_rows, qkv_back, CONTRACT_COLS, preferred_element_type=jnp.float32
    )
    grad_emb_part, gain_one = rms_backward(embedded, inverse_one, norm_gains[0], grad_normed_one)
    grad_embedded = grad_residual + grad_emb_part
    sendback = (
        jnp.zeros((owners, capacity, model_width), jnp.float32)
        .at[tok_owner, slot_rank]
        .set(grad_embedded)
    )
    arrived = lax.all_to_all(sendback, "dp", split_axis=0, concat_axis=0, tiled=True)
    table_grad = jax.ops.segment_sum(
        arrived.reshape(-1, model_width), asked_rows.reshape(-1), num_segments=embed_table.shape[0]
    )
    table_grad = lax.psum(table_grad, "pair")
    weight_grads = (
        lax.psum_scatter(grad_qkv, ("dp", "pair"), scatter_dimension=0, tiled=True),
        lax.psum_scatter(grad_out, ("dp", "pair"), scatter_dimension=0, tiled=True),
        lax.psum_scatter(grad_in, ("dp", "pair"), scatter_dimension=0, tiled=True),
        lax.psum_scatter(grad_down, ("dp", "pair"), scatter_dimension=0, tiled=True),
    )
    pair_first = (lax.axis_index("pair") == 0).astype(jnp.float32)
    square_part = jnp.sum(
        jnp.stack([jnp.sum(grad_piece * grad_piece) for grad_piece in weight_grads])
    ) + pair_first * jnp.sum(table_grad * table_grad)
    gain_grad, bias_grad, square_sum = lax.psum(
        (jnp.stack([gain_one, gain_two, gain_three]), bias_grad_local, square_part), ("dp", "pair")
    )
    clip_norm = jnp.sqrt(
        square_sum + jnp.sum(gain_grad * gain_grad) + jnp.sum(bias_grad * bias_grad)
    )
    factor = jnp.minimum(1.0, clip_limit / clip_norm)
    table_out = adam_step(embed_table, embed_first, embed_second, table_grad * factor, 1.0, 0.01)
    qkv_out = adam_step(qkv_weight, qkv_first, qkv_second, weight_grads[0] * factor, 0.05, 0.01)
    out_out = adam_step(out_weight, out_first, out_second, weight_grads[1] * factor, 0.05, 0.01)
    in_out = adam_step(in_weight, in_first, in_second, weight_grads[2] * factor, 0.05, 0.01)
    down_out = adam_step(down_weight, down_first, down_second, weight_grads[3] * factor, 0.05, 0.01)
    gains_out = adam_step(norm_gains, gains_first, gains_second, gain_grad * factor, 1.0, 0.0)
    bias_out = adam_step(position_bias, bias_first, bias_second, bias_grad * factor, 0.3, 0.0)
    return (
        loss_value,
        clip_norm,
        table_out[0],
        table_out[1],
        table_out[2],
        qkv_out[0],
        qkv_out[1],
        qkv_out[2],
        out_out[0],
        out_out[1],
        out_out[2],
        in_out[0],
        in_out[1],
        in_out[2],
        down_out[0],
        down_out[1],
        down_out[2],
        gains_out[0],
        gains_out[1],
        gains_out[2],
        bias_out[0],
        bias_out[1],
        bias_out[2],
    )


def local_fast(
    token_owner,
    token_row,
    lengths,
    positives,
    negatives,
    neg_counts,
    embed_table,
    embed_first,
    embed_second,
    qkv_weight,
    qkv_first,
    qkv_second,
    out_weight,
    out_first,
    out_second,
    in_weight,
    in_first,
    in_second,
    down_weight,
    down_first,
    down_second,
    norm_gains,
    gains_first,
    gains_second,
    position_bias,
    bias_first,
    bias_second,
):
    doc_count = lengths.shape[0]
    seq_len = token_row.shape[1]
    model_width = embed_table.shape[1]
    head_count = position_bias.shape[1]
    bucket_count = position_bias.shape[0]
    tok_total = doc_count * seq_len
    owners = lax.axis_size("dp")
    capacity = max(2, 2 * tok_total // owners)
    low_mats = (
        qkv_weight.astype(jnp.bfloat16),
        out_weight.astype(jnp.bfloat16),
        in_weight.astype(jnp.bfloat16),
        down_weight.astype(jnp.bfloat16),
    )
    holders = lax.axis_size("pair")
    pieces = weight_pieces([low.shape[1] for low in low_mats])
    qkv_full, out_full, in_full, down_full = (
        full.reshape(-1, full.shape[2])
        for full in gather_all(low_mats, pieces, owners, holders, 1)
    )
    tok_owner = token_owner.reshape(-1)
    tok_row = token_row.reshape(-1)
    owner_hits = (tok_owner[:, None] == jnp.arange(owners, dtype=jnp.int32)[None, :]).astype(
        jnp.int32
    )
    slot_rank = jnp.sum((jnp.cumsum(owner_hits, axis=0) - 1) * owner_hits, axis=1)
    requests = jnp.zeros((owners, capacity), jnp.int32).at[tok_owner, slot_rank].set(tok_row)
    asked_rows = lax.all_to_all(requests, "dp", split_axis=0, concat_axis=0, tiled=True)
    looked = jnp.take(embed_table, asked_rows.reshape(-1), axis=0).astype(jnp.bfloat16)
    answer = exchange(looked.reshape(asked_rows.shape + (model_width,)), owners, 2)
    replies, asked_rows = (answer, asked_rows)
    embedded = replies[tok_owner, slot_rank].astype(jnp.float32)
    positions = jnp.arange(seq_len)
    live = positions[None, :] < lengths[:, None]
    normed_one, inverse_one = rms_forward(embedded, norm_gains[0])
    normed_one = normed_one.astype(jnp.bfloat16)
    qkv_rows = jnp.dot(normed_one, qkv_full, preferred_element_type=jnp.float32).astype(
        jnp.bfloat16
    )
    attended = attention(lengths, qkv_rows, bias_rows(position_bias, seq_len, 1), seq_len)
    residual = embedded + jnp.dot(attended, out_full, preferred_element_type=jnp.float32)
    normed_two, inverse_two = rms_forward(residual, norm_gains[1])
    normed_two = normed_two.astype(jnp.bfloat16)
    hidden = jax.nn.relu(jnp.dot(normed_two, in_full, preferred_element_type=jnp.float32)).astype(
        jnp.bfloat16
    )
    output_rows = residual + jnp.dot(hidden, down_full, preferred_element_type=jnp.float32)
    normed_three, inverse_three = rms_forward(output_rows, norm_gains[2])
    live_rows = live.reshape(-1, 1)
    length_float = lengths.astype(jnp.float32)
    pooled_local = (
        jnp.sum(
            jnp.where(live_rows, normed_three, 0.0).reshape(doc_count, seq_len, model_width), axis=1
        )
        / length_float[:, None]
    )
    loss_cell, grad_pooled = pooled_loss(
        pooled_local, positives, negatives, neg_counts, owners, holders, 3
    )
    loss_value = loss_cell[0, 0]
    grad_three = jnp.where(
        live_rows, jnp.repeat(grad_pooled / length_float[:, None], seq_len, axis=0), 0.0
    )
    qkv_back, out_back, in_back, down_back = (qkv_full, out_full, in_full, down_full)
    grad_output, gain_three = rms_backward(output_rows, inverse_three, norm_gains[2], grad_three)
    grad_branch = grad_output.astype(jnp.bfloat16)
    grad_down = lax.dot_general(
        hidden, grad_branch, CONTRACT_ROWS, preferred_element_type=jnp.float32
    )
    grad_hidden = lax.dot_general(
        grad_branch, down_back, CONTRACT_COLS, preferred_element_type=jnp.float32
    )
    grad_pre = jnp.where(hidden > 0, grad_hidden, 0.0).astype(jnp.bfloat16)
    grad_in = lax.dot_general(
        normed_two, grad_pre, CONTRACT_ROWS, preferred_element_type=jnp.float32
    )
    grad_normed_two = lax.dot_general(
        grad_pre, in_back, CONTRACT_COLS, preferred_element_type=jnp.float32
    )
    grad_res_part, gain_two = rms_backward(residual, inverse_two, norm_gains[1], grad_normed_two)
    grad_residual = grad_output + grad_res_part
    grad_attn_branch = grad_residual.astype(jnp.bfloat16)
    grad_out = lax.dot_general(
        attended, grad_attn_branch, CONTRACT_ROWS, preferred_element_type=jnp.float32
    )
    grad_attended = lax.dot_general(
        grad_attn_branch, out_back, CONTRACT_COLS, preferred_element_type=jnp.float32
    ).astype(jnp.bfloat16)
    grad_parts, diagonals = attention_back(
        lengths, qkv_rows, grad_attended, bias_rows(position_bias, seq_len, -1), seq_len
    )
    bias_grad_local = bias_gradient(diagonals, seq_len, bucket_count)
    grad_qkv = [
        lax.dot_general(normed_one, part, CONTRACT_ROWS, preferred_element_type=jnp.float32)
        for part in grad_parts
    ]
    grad_normed_one = sum(
        lax.dot_general(
            part,
            qkv_back[:, index * model_width : (index + 1) * model_width],
            CONTRACT_COLS,
            preferred_element_type=jnp.float32,
        )
        for index, part in enumerate(grad_parts)
    )
    grad_emb_part, gain_one = rms_backward(embedded, inverse_one, norm_gains[0], grad_normed_one)
    grad_embedded = grad_residual + grad_emb_part
    sendback = (
        jnp.zeros((owners, capacity, model_width), jnp.bfloat16)
        .at[tok_owner, slot_rank]
        .set(grad_embedded.astype(jnp.bfloat16))
    )
    arrived = exchange(sendback, owners, 4)
    table_rows = embed_table.shape[0]
    table_grad, table_square = table_total(
        arrived.reshape(-1, model_width),
        asked_rows.reshape(1, -1),
        -(-table_rows // 1024) * 1024,
        holders,
        5,
    )
    table_grad = table_grad[:table_rows].astype(jnp.float32)
    parts = owners * holders
    weight_grads = scatter_all(
        [
            grad.astype(jnp.bfloat16).reshape(parts, -1, grad.shape[1])
            for grad in (*grad_qkv, grad_out, grad_in, grad_down)
        ],
        weight_pieces([model_width] * 4 + [grad_in.shape[1], model_width]),
        owners,
        holders,
        6,
    )
    weight_grads = (jnp.concatenate(weight_grads[:3], axis=1), *weight_grads[3:])
    square_part = table_square[0, 0] + jnp.sum(
        jnp.stack([jnp.sum(grad_piece * grad_piece) for grad_piece in weight_grads])
    )
    small = jnp.concatenate(
        [
            jnp.stack([gain_one, gain_two, gain_three]).reshape(-1),
            bias_grad_local.reshape(-1),
            square_part.reshape(1),
        ]
    )
    small_size = small.shape[0]
    small_rows = -(-small_size // 1024) * 8
    small = jnp.pad(small, (0, small_rows * 128 - small_size)).reshape(small_rows, 128)
    small = small_total(small, owners, holders, 7).reshape(-1)
    gain_grad = small[: 3 * model_width].reshape(3, model_width)
    bias_grad = small[3 * model_width : small_size - 1].reshape(bucket_count, head_count)
    square_sum = small[small_size - 1]
    clip_norm = jnp.sqrt(
        square_sum + jnp.sum(gain_grad * gain_grad) + jnp.sum(bias_grad * bias_grad)
    )
    factor = jnp.minimum(1.0, clip_limit / clip_norm)
    table_out = adam_step(embed_table, embed_first, embed_second, table_grad * factor, 1.0, 0.01)
    qkv_out = adam_step(qkv_weight, qkv_first, qkv_second, weight_grads[0] * factor, 0.05, 0.01)
    out_out = adam_step(out_weight, out_first, out_second, weight_grads[1] * factor, 0.05, 0.01)
    in_out = adam_step(in_weight, in_first, in_second, weight_grads[2] * factor, 0.05, 0.01)
    down_out = adam_step(down_weight, down_first, down_second, weight_grads[3] * factor, 0.05, 0.01)
    gains_out = adam_step(norm_gains, gains_first, gains_second, gain_grad * factor, 1.0, 0.0)
    bias_out = adam_step(position_bias, bias_first, bias_second, bias_grad * factor, 0.3, 0.0)
    return (
        loss_value,
        clip_norm,
        table_out[0],
        table_out[1],
        table_out[2],
        qkv_out[0],
        qkv_out[1],
        qkv_out[2],
        out_out[0],
        out_out[1],
        out_out[2],
        in_out[0],
        in_out[1],
        in_out[2],
        down_out[0],
        down_out[1],
        down_out[2],
        gains_out[0],
        gains_out[1],
        gains_out[2],
        bias_out[0],
        bias_out[1],
        bias_out[2],
    )


def local(*arrays):
    n_dp, n_pair = lax.axis_size("dp"), lax.axis_size("pair")
    lengths, qkv_weight, down_weight = arrays[2], arrays[9], arrays[18]
    fits = (
        n_pair == 4
        and n_dp & (n_dp - 1) == 0
        and qkv_weight.shape[0] % 8 == 0
        and down_weight.shape[0] % 8 == 0
        and lengths.shape[0] == 2
        and 2 * arrays[1].size // n_dp % 128 == 0
    )
    return (local_fast if fits else local_plain)(*arrays)


def solution(mesh):
    return jax.shard_map(
        local,
        mesh=mesh,
        in_specs=(
            P(("dp", "pair"), None, None),
            P(("dp", "pair"), None),
            P(("dp", "pair")),
            P(),
            P(),
            P(),
            P("dp", None),
            P("dp", None),
            P("dp", None),
            P(("dp", "pair"), None),
            P(("dp", "pair"), None),
            P(("dp", "pair"), None),
            P(("dp", "pair"), None),
            P(("dp", "pair"), None),
            P(("dp", "pair"), None),
            P(("dp", "pair"), None),
            P(("dp", "pair"), None),
            P(("dp", "pair"), None),
            P(("dp", "pair"), None),
            P(("dp", "pair"), None),
            P(("dp", "pair"), None),
            P(),
            P(),
            P(),
            P(),
            P(),
            P(),
        ),
        out_specs=(
            P(),
            P(),
            P("dp", None),
            P("dp", None),
            P("dp", None),
            P(("dp", "pair"), None),
            P(("dp", "pair"), None),
            P(("dp", "pair"), None),
            P(("dp", "pair"), None),
            P(("dp", "pair"), None),
            P(("dp", "pair"), None),
            P(("dp", "pair"), None),
            P(("dp", "pair"), None),
            P(("dp", "pair"), None),
            P(("dp", "pair"), None),
            P(("dp", "pair"), None),
            P(("dp", "pair"), None),
            P(),
            P(),
            P(),
            P(),
            P(),
            P(),
        ),
        check_vma=False,
    )
```

```python
import functools
import math

import jax
import jax.numpy as jnp
from jax import lax
from jax.experimental import pallas as pl
from jax.experimental.pallas import tpu as pltpu
from jax.sharding import PartitionSpec as P

REACH = 128
STEP = 5


rms_eps = 1e-06
clip_limit = 0.05
margin = 1.0
sim_scale = 20.0
beta_one = 0.9
beta_two = 0.999
adam_eps = 1e-08
HIGHEST = lax.Precision.HIGHEST
CONTRACT_ROWS = (((0,), (0,)), ((), ()))
CONTRACT_COLS = (((1,), (1,)), ((), ()))


def bucket_of(offsets, bucket_count, reach_limit):
    half_count = bucket_count // 2
    exact_count = half_count // 2
    sign_base = jnp.where(offsets > 0, half_count, 0).astype(jnp.int32)
    distance = jnp.abs(offsets)
    far_bucket = jnp.full(offsets.shape, exact_count, jnp.int32)
    for level_index in range(1, half_count - exact_count):
        threshold = int(
            math.ceil(
                exact_count
                * (reach_limit / exact_count) ** (level_index / (half_count - exact_count))
                - 1e-09
            )
        )
        far_bucket = far_bucket + (distance >= threshold).astype(jnp.int32)
    return sign_base + jnp.where(distance < exact_count, distance, far_bucket)


def rms_forward(values, gain):
    inverse = lax.rsqrt(jnp.mean(values * values, axis=-1, keepdims=True) + rms_eps)
    return (values * inverse * gain, inverse)


def rms_backward(values, inverse, gain, upstream):
    scaled = upstream * gain
    normed = values * inverse
    grad_values = inverse * (scaled - normed * jnp.mean(scaled * normed, axis=-1, keepdims=True))
    return (grad_values, jnp.sum(upstream * normed, axis=0))


def margin_loss(pooled, positives, negatives, neg_counts):
    unit = pooled * lax.rsqrt(jnp.sum(pooled * pooled, axis=-1, keepdims=True) + 1e-06)
    similar = sim_scale * jnp.dot(unit, unit.T, precision=HIGHEST)
    chosen = jnp.take_along_axis(similar, positives[:, None], axis=1)
    against = jnp.take_along_axis(similar, negatives, axis=1)
    live_slots = jnp.arange(negatives.shape[1])[None, :] < neg_counts[:, None]
    terms = jnp.where(live_slots, jax.nn.softplus(margin - chosen + against), 0.0)
    return jnp.mean(jnp.sum(terms, axis=1) / neg_counts.astype(jnp.float32))


def doc_scores(query_heads, key_heads, bias_full, live_keys):
    scores = (
        jnp.einsum("qhd,khd->hqk", query_heads, key_heads, preferred_element_type=jnp.float32)
        * 0.125
        + bias_full
    )
    return jnp.where(live_keys[None, None, :], scores, -1000000000.0)


def attend_forward(query_heads, key_heads, value_heads, bias_full, live_keys):
    scores = doc_scores(query_heads, key_heads, bias_full, live_keys)
    highest = jnp.max(scores, axis=-1, keepdims=True)
    weights = jnp.exp(scores - highest)
    totals = jnp.sum(weights, axis=-1, keepdims=True)
    probabilities = (weights / totals).astype(jnp.bfloat16)
    attended = jnp.einsum(
        "hqk,khd->qhd", probabilities, value_heads, preferred_element_type=jnp.float32
    )
    return (attended, highest + jnp.log(totals))


def attend_backward(
    query_heads, key_heads, value_heads, bias_full, live_keys, logsum, grad_attended
):
    probabilities = jnp.exp(doc_scores(query_heads, key_heads, bias_full, live_keys) - logsum)
    grad_value = jnp.einsum(
        "hqk,qhd->khd",
        probabilities.astype(jnp.bfloat16),
        grad_attended,
        preferred_element_type=jnp.float32,
    )
    grad_prob = jnp.einsum(
        "qhd,khd->hqk", grad_attended, value_heads, preferred_element_type=jnp.float32
    )
    grad_score = probabilities * (
        grad_prob - jnp.sum(probabilities * grad_prob, axis=-1, keepdims=True)
    )
    grad_low = grad_score.astype(jnp.bfloat16)
    grad_query = (
        jnp.einsum("hqk,khd->qhd", grad_low, key_heads, preferred_element_type=jnp.float32) * 0.125
    )
    grad_key = (
        jnp.einsum("hqk,qhd->khd", grad_low, query_heads, preferred_element_type=jnp.float32)
        * 0.125
    )
    return (grad_query, grad_key, grad_value, grad_low)


def adam_step(weight, first, second, grad, rate, shrink):
    first_new = beta_one * first + (1.0 - beta_one) * grad
    second_new = beta_two * second + (1.0 - beta_two) * grad * grad
    first_hat = first_new / (1.0 - beta_one**STEP)
    second_hat = second_new / (1.0 - beta_two**STEP)
    weight_new = weight - rate * (first_hat / (jnp.sqrt(second_hat) + adam_eps) + shrink * weight)
    return (weight_new, first_new, second_new)


MESH = pl.DeviceIdType.MESH
VMEM_LIMIT = 64 * 1024 * 1024 - 65536
ANY = pl.BlockSpec(memory_space=pl.ANY)
VM = pl.BlockSpec(memory_space=pltpu.VMEM)


def place(index, n_pair):
    return {"dp": index // n_pair, "pair": lax.rem(index, n_pair)}


def remote(src, dst, send, recv, target):
    return pltpu.make_async_remote_copy(
        src, dst, send, recv, device_id=target, device_id_type=MESH
    )


def greet(targets):
    sem = pltpu.get_barrier_semaphore()
    for target in targets:
        pl.semaphore_signal(sem, inc=1, device_id=target, device_id_type=MESH)
    pl.semaphore_wait(sem, len(targets))


def my_index(n_pair):
    return lax.axis_index("dp") * n_pair + lax.axis_index("pair")


def bit_order(n_dp, n_pair, color):
    dp_bits, pair_bits = (n_dp - 1).bit_length(), (n_pair - 1).bit_length()
    high = list(reversed(range(pair_bits + 1, pair_bits + dp_bits))) + [pair_bits]
    side = list(reversed(range(1, pair_bits)))
    return high + side if color == 0 else side + high


def offset(order, position):
    return sum(((position >> step) & 1) << bit for step, bit in enumerate(order))


def scatter_kernel(n_dp, n_pair, pieces, n_in, *refs):
    k = len(pieces)
    ins, outs = refs[:n_in], refs[n_in : 2 * n_in]
    accs = refs[2 * n_in : 2 * n_in + k]
    gots = refs[2 * n_in + k : 2 * n_in + 2 * k]
    lsem, csend, crecv, send, recv = refs[2 * n_in + 2 * k :]
    me = my_index(n_pair)
    n = n_dp * n_pair
    steps = (n - 1).bit_length() - 1
    half = 1 << steps
    orders = [bit_order(n_dp, n_pair, color) for _, _, _, color in pieces]
    greet([place(me ^ (1 << bit), n_pair) for bit in range(steps + 1)])

    def source(a, block):
        which, low, high, _ = pieces[a]
        return ins[which].at[block, :, pl.ds(low, high - low)]

    def core_send(a, upper):
        lo = half // 2 if upper else 0
        for p in range(lo, lo + half // 2):
            block = me ^ (offset(orders[a], p) + 1)
            remote(source(a, block), gots[a].at[p], csend.at[a, upper], crecv.at[a, upper], place(me ^ 1, n_pair)).start()

    def load(a):
        for p in range(half):
            pltpu.make_async_copy(source(a, me ^ offset(orders[a], p)), accs[a].at[p], lsem.at[a]).start()

    def core_copy(a, upper):
        lo = half // 2 if upper else 0
        part = pl.ds(lo, half // 2)
        return remote(gots[a].at[part], gots[a].at[part], csend.at[a, upper], crecv.at[a, upper], place(me ^ 1, n_pair))

    def add(a, lo, count, base):
        def body(j, carry):
            accs[a][lo + j] = (
                accs[a][lo + j].astype(jnp.float32) + gots[a][base + lo + j].astype(jnp.float32)
            ).astype(jnp.bfloat16)
            return carry
        lax.fori_loop(0, count, body, 0)

    def base_of(s):
        return half + half - (2 << s)

    def hop(a, s):
        return remote(
            accs[a].at[pl.ds(1 << s, 1 << s)], gots[a].at[pl.ds(base_of(s), 1 << s)],
            send.at[a, s], recv.at[a, s], place(me ^ (1 << orders[a][s]), n_pair),
        )

    for upper in (1, 0):
        for a in range(k):
            core_send(a, upper)
            if upper:
                load(a)
    for a in range(k):
        pltpu.make_async_copy(accs[a], accs[a], lsem.at[a]).wait()
        core_copy(a, 1).wait_recv()
        add(a, half // 2, half // 2, 0)
        hop(a, steps - 1).start()
    for a in range(k):
        core_copy(a, 0).wait_recv()
        add(a, 0, half // 2, 0)
    for s in reversed(range(steps)):
        for a in range(k):
            hop(a, s).wait_recv()
            if s:
                mid = 1 << (s - 1)
                add(a, mid, mid, base_of(s))
                hop(a, s - 1).start()
                add(a, 0, mid, base_of(s))
            else:
                which, low, high, _ = pieces[a]
                outs[which][:, low:high] = accs[a][0].astype(jnp.float32) + gots[a][
                    base_of(0)
                ].astype(jnp.float32)
    for a in range(k):
        core_copy(a, 1).wait_send()
        core_copy(a, 0).wait_send()
        for s in range(steps):
            hop(a, s).wait_send()


def scatter_all(grads, pieces, n_dp, n_pair, cid):
    n, k = n_dp * n_pair, len(pieces)
    steps = (n - 1).bit_length() - 1
    half = n // 2
    shape = lambda p, lead: (lead, grads[p[0]].shape[1], p[2] - p[1])
    return pl.pallas_call(
        functools.partial(scatter_kernel, n_dp, n_pair, pieces, len(grads)),
        out_shape=[jax.ShapeDtypeStruct(g.shape[1:], jnp.float32) for g in grads],
        in_specs=[ANY] * len(grads),
        out_specs=[VM] * len(grads),
        scratch_shapes=[pltpu.VMEM(shape(p, half), jnp.bfloat16) for p in pieces]
        + [pltpu.VMEM(shape(p, 2 * half - 1), jnp.bfloat16) for p in pieces]
        + [
            pltpu.SemaphoreType.DMA((k,)),
            pltpu.SemaphoreType.DMA((k, 2)),
            pltpu.SemaphoreType.DMA((k, 2)),
            pltpu.SemaphoreType.DMA((k, steps)),
            pltpu.SemaphoreType.DMA((k, steps)),
        ],
        compiler_params=pltpu.CompilerParams(
            collective_id=cid, has_side_effects=True, vmem_limit_bytes=VMEM_LIMIT
        ),
        name="weight_grads_sum",
    )(*grads)


def spread(n, n_pair, block, everyone, send, recv, own_sem):
    me = my_index(n_pair)
    sem = pltpu.get_barrier_semaphore()

    def hello(k, carry):
        pl.semaphore_signal(sem, inc=1, device_id=place(me ^ k, n_pair), device_id_type=MESH)
        return carry

    lax.fori_loop(1, n, hello, 0)
    own = pltpu.make_async_copy(block, everyone.at[me], own_sem)
    own.start()
    pl.semaphore_wait(sem, n - 1)

    def go(k, carry):
        remote(block, everyone.at[me], send.at[k], recv.at[k], place(me ^ k, n_pair)).start()
        return carry

    lax.fori_loop(1, n, go, 0)
    own.wait()

    def done(k, carry):
        remote(block, everyone.at[me ^ k], send.at[k], recv.at[k], place(me ^ k, n_pair)).wait()
        return carry

    lax.fori_loop(1, n, done, 0)


def total_kernel(n, n_pair, x_ref, o_ref, everyone, send, recv, own_sem):
    spread(n, n_pair, x_ref, everyone, send, recv, own_sem)
    def add(j, total):
        return total + everyone[j]
    o_ref[...] = lax.fori_loop(1, n, add, everyone[0])


def small_total(x, n_dp, n_pair, cid):
    n = n_dp * n_pair
    return pl.pallas_call(
        functools.partial(total_kernel, n, n_pair),
        out_shape=jax.ShapeDtypeStruct(x.shape, x.dtype),
        in_specs=[VM], out_specs=VM,
        scratch_shapes=[pltpu.VMEM((n,) + x.shape, x.dtype), pltpu.SemaphoreType.DMA((n,)), pltpu.SemaphoreType.DMA((n,)), pltpu.SemaphoreType.DMA],
        compiler_params=pltpu.CompilerParams(collective_id=cid, has_side_effects=True),
        name="small_total",
    )(x)


def loss_kernel(n, n_pair, docs, x_ref, pos_ref, neg_ref, count_ref, loss_ref, grad_ref, everyone, grads, send, recv, own_sem):
    spread(n, n_pair, x_ref, everyone, send, recv, own_sem)
    total = n * docs
    width = x_ref.shape[1]
    pooled = everyone[...].reshape(total, width)
    inverse = lax.rsqrt(jnp.sum(pooled * pooled, axis=1, keepdims=True) + 1e-06)
    unit = pooled * inverse
    similar = 20.0 * lax.dot_general(unit, unit, (((1,), (1,)), ((), ())), precision=HIGHEST, preferred_element_type=jnp.float32)
    columns = lax.broadcasted_iota(jnp.int32, (total, total), 1)
    is_pos = columns == pos_ref[...]
    chosen = jnp.sum(jnp.where(is_pos, similar, 0.0), axis=1, keepdims=True)
    counts = count_ref[...]
    weight = 1.0 / (counts.astype(jnp.float32) * total)
    loss_rows = jnp.zeros((total, 1), jnp.float32)
    grad_similar = jnp.zeros((total, total), jnp.float32)
    pulled = jnp.zeros((total, 1), jnp.float32)
    for slot in range(neg_ref.shape[1]):
        is_neg = columns == neg_ref[:, slot : slot + 1]
        against = jnp.sum(jnp.where(is_neg, similar, 0.0), axis=1, keepdims=True)
        value = 1.0 - chosen + against
        used = slot < counts
        soft = jnp.maximum(value, 0.0) + jnp.log1p(jnp.exp(-jnp.abs(value)))
        loss_rows = loss_rows + jnp.where(used, soft, 0.0)
        slope = jnp.where(used, weight / (1.0 + jnp.exp(-value)), 0.0)
        grad_similar = grad_similar + jnp.where(is_neg, slope, 0.0)
        pulled = pulled + slope
    grad_similar = grad_similar - jnp.where(is_pos, pulled, 0.0)
    loss_ref[...] = jnp.sum(loss_rows * weight, axis=0, keepdims=True)
    dims = (((1,), (0,)), ((), ()))
    grad_unit = lax.dot_general(grad_similar, unit, dims, precision=HIGHEST, preferred_element_type=jnp.float32)
    grad_unit = grad_unit + lax.dot_general(grad_similar, unit, (((0,), (0,)), ((), ())), precision=HIGHEST, preferred_element_type=jnp.float32)
    grad_unit = 20.0 * grad_unit
    inner = jnp.sum(grad_unit * unit, axis=1, keepdims=True)
    grads[...] = (inverse * (grad_unit - unit * inner)).reshape(n, docs, width)
    grad_ref[...] = grads[my_index(n_pair)]


def pooled_loss(pooled, positives, negatives, counts, n_dp, n_pair, cid):
    n = n_dp * n_pair
    docs, width = pooled.shape
    return pl.pallas_call(
        functools.partial(loss_kernel, n, n_pair, docs),
        out_shape=[jax.ShapeDtypeStruct((1, 1), jnp.float32), jax.ShapeDtypeStruct(pooled.shape, jnp.float32)],
        in_specs=[VM] * 4, out_specs=[VM] * 2,
        scratch_shapes=[pltpu.VMEM((n,) + pooled.shape, jnp.float32), pltpu.VMEM((n,) + pooled.shape, jnp.float32),
            pltpu.SemaphoreType.DMA((n,)), pltpu.SemaphoreType.DMA((n,)), pltpu.SemaphoreType.DMA],
        compiler_params=pltpu.CompilerParams(collective_id=cid, has_side_effects=True),
        name="pooled_loss",
    )(pooled, positives[:, None], negatives, counts[:, None])


def table_kernel(n_pair, rows, chunk, arr_ref, ask_ref, out_ref, sq_ref, hot, stage, part, got_c, out_x, got_x, fin, fin_other,
                 csend, crecv, xsend, xrecv, fsend, frecv, wsem):
    me_dp, me_pair = lax.axis_index("dp"), lax.axis_index("pair")
    core = lax.rem(me_pair, 2)
    partner = {"dp": me_dp, "pair": me_pair ^ 1}
    across = {"dp": me_dp, "pair": me_pair ^ 2}
    count = rows // 2 // chunk
    greet([partner, across])
    slots = ask_ref.shape[1]

    def summed(base):
        ids = lax.broadcasted_iota(jnp.int32, (chunk, slots), 0) + base
        hot[...] = jnp.where(ids == ask_ref[...], 1.0, 0.0).astype(jnp.bfloat16)
        return jnp.dot(hot[...], arr_ref[...], preferred_element_type=jnp.float32)

    def c_copy(i):
        return remote(stage.at[i], got_c.at[i], csend.at[i], crecv.at[i], partner)

    def x_copy(i):
        return remote(out_x.at[i], got_x.at[i], xsend.at[i], xrecv.at[i], across)

    def f_copy(i):
        return remote(fin.at[i], fin_other.at[i], fsend.at[i], frecv.at[i], partner)

    for i in range(count):
        stage[i] = summed((1 - core) * (rows // 2) + i * chunk).astype(jnp.bfloat16)
        c_copy(i).start()
    for i in range(count):
        part[...] = summed(core * (rows // 2) + i * chunk)
        c_copy(i).wait_recv()
        out_x[i] = (part[...] + got_c[i].astype(jnp.float32)).astype(jnp.bfloat16)
        x_copy(i).start()
    square = jnp.zeros((1, 1), jnp.float32)
    for i in range(count):
        x_copy(i).wait_recv()
        value = (out_x[i].astype(jnp.float32) + got_x[i].astype(jnp.float32)).astype(jnp.bfloat16)
        fin[i] = value
        f_copy(i).start()
        pltpu.make_async_copy(fin.at[i], out_ref.at[pl.ds(core * (rows // 2) + i * chunk, chunk)], wsem.at[0]).start()
        wide = value.astype(jnp.float32)
        square = square + jnp.sum(jnp.sum(wide * wide, axis=0, keepdims=True), axis=1, keepdims=True)
    sq_ref[...] = jnp.where(me_pair < 2, square, 0.0)
    for i in range(count):
        f_copy(i).wait_recv()
        pltpu.make_async_copy(fin_other.at[i], out_ref.at[pl.ds((1 - core) * (rows // 2) + i * chunk, chunk)], wsem.at[1]).start()
    for i in range(count):
        c_copy(i).wait_send()
        x_copy(i).wait_send()
        f_copy(i).wait_send()
    pltpu.make_async_copy(fin, fin, wsem.at[0]).wait()
    pltpu.make_async_copy(fin_other, fin_other, wsem.at[1]).wait()


def table_total(arrived, asked, rows, n_pair, cid):
    chunk, width = 512, arrived.shape[1]
    count = rows // 2 // chunk
    box = pltpu.VMEM((count, chunk, width), jnp.bfloat16)
    sem = pltpu.SemaphoreType.DMA((count,))
    return pl.pallas_call(
        functools.partial(table_kernel, n_pair, rows, chunk),
        out_shape=[jax.ShapeDtypeStruct((rows, width), jnp.bfloat16), jax.ShapeDtypeStruct((1, 1), jnp.float32)],
        in_specs=[VM, VM], out_specs=[ANY, VM],
        scratch_shapes=[pltpu.VMEM((chunk, asked.shape[1]), jnp.bfloat16), box, pltpu.VMEM((chunk, width), jnp.float32), box, box, box, box, box,
            sem, sem, sem, sem, sem, sem, pltpu.SemaphoreType.DMA((2,))],
        compiler_params=pltpu.CompilerParams(collective_id=cid, has_side_effects=True, vmem_limit_bytes=VMEM_LIMIT),
        name="table_total",
    )(arrived, asked)


def exchange_kernel(n_dp, x_ref, o_ref, send, recv, lsem):
    me = lax.axis_index("dp"); pr = lax.axis_index("pair")
    sem = pltpu.get_barrier_semaphore()
    def greet(k, _):
        pl.semaphore_signal(sem, inc=1, device_id={"dp": lax.rem(me + k, n_dp), "pair": pr}, device_id_type=MESH)
        return 0
    lax.fori_loop(1, n_dp, greet, 0)
    pl.semaphore_wait(sem, n_dp - 1)
    own = pltpu.make_async_copy(x_ref.at[me], o_ref.at[me], lsem); own.start()
    def cp(k):
        dst = lax.rem(me + k, n_dp)
        return pltpu.make_async_remote_copy(x_ref.at[dst], o_ref.at[me], send.at[k], recv.at[k],
            device_id={"dp": dst, "pair": pr}, device_id_type=MESH)
    def go(k, _):
        cp(k).start(); return 0
    lax.fori_loop(1, n_dp, go, 0)
    def done(k, _):
        src = lax.rem(me + n_dp - k, n_dp)
        c = pltpu.make_async_remote_copy(x_ref.at[me], o_ref.at[src], send.at[k], recv.at[k],
            device_id={"dp": src, "pair": pr}, device_id_type=MESH)
        c.wait(); return 0
    own.wait()
    lax.fori_loop(1, n_dp, done, 0)

def exchange(x, n_dp, cid):
    return pl.pallas_call(
        functools.partial(exchange_kernel, n_dp),
        out_shape=jax.ShapeDtypeStruct(x.shape, x.dtype),
        in_specs=[pl.BlockSpec(memory_space=pltpu.VMEM)], out_specs=pl.BlockSpec(memory_space=pltpu.VMEM),
        scratch_shapes=[pltpu.SemaphoreType.DMA((n_dp,)), pltpu.SemaphoreType.DMA((n_dp,)), pltpu.SemaphoreType.DMA],
        compiler_params=pltpu.CompilerParams(collective_id=cid, has_side_effects=True, vmem_limit_bytes=VMEM_LIMIT),
        name="rows_exchange",
    )(x)


NT = (((1,), (1,)), ((), ()))
TN = (((0,), (0,)), ((), ()))

def band(w_ref, h, table, seq):
    tiles = seq // 128
    for d in range(1 - tiles, tiles):
        low = seq + 128 * d - 128
        x = jnp.broadcast_to(w_ref[0, h : h + 1, low : low + 256], (128, 256))
        tile = pltpu.roll(x, 0, 1, stride=1, stride_axis=0)[:, 128:]
        for a in range(tiles):
            if 0 <= a + d < tiles:
                table[h, a * 128 : a * 128 + 128, (a + d) * 128 : (a + d) * 128 + 128] = tile

def forward_kernel(len_ref, q_ref, k_ref, v_ref, w_ref, o_ref, table):
    seq = q_ref.shape[0]
    doc = pl.program_id(1)
    @pl.when(doc == 0)
    def _():
        for h in range(2):
            band(w_ref, h, table, seq)
    length = len_ref[doc]
    lane = lax.broadcasted_iota(jnp.int32, (seq, 128), 1)
    column = lax.broadcasted_iota(jnp.int32, (1, seq), 1)
    q = q_ref[...] * jnp.bfloat16(0.125)
    k = k_ref[...]
    v = v_ref[...]
    got = []
    for h in range(2):
        mine = (lane < 64) == (h == 0)
        s = lax.dot_general(jnp.where(mine, q, 0), k, NT, preferred_element_type=jnp.float32)
        s = jnp.where(column < length, s + table[h], -1000000000.0)
        e = jnp.exp(s - jnp.max(s, axis=1, keepdims=True))
        p = (e * (1.0 / jnp.sum(e, axis=1, keepdims=True))).astype(jnp.bfloat16)
        got.append(jnp.dot(p, v, preferred_element_type=jnp.float32))
    o_ref[...] = jnp.where(lane < 64, got[0], got[1]).astype(o_ref.dtype)

def attention(lengths, qkv, w, seq):
    tokens = qkv.shape[0]
    pairs = w.shape[0]
    docs = tokens // seq
    spec = lambda base: pl.BlockSpec((seq, 128), lambda h, d, *_: (d, base + h))
    return pl.pallas_call(
        forward_kernel,
        grid_spec=pltpu.PrefetchScalarGridSpec(
            num_scalar_prefetch=1, grid=(pairs, docs),
            in_specs=[spec(0), spec(pairs), spec(2 * pairs), pl.BlockSpec((1, 2, 2 * seq), lambda h, d, *_: (h, 0, 0))],
            out_specs=spec(0),
            scratch_shapes=[pltpu.VMEM((2, seq, seq), jnp.float32)]),
        out_shape=jax.ShapeDtypeStruct((tokens, pairs * 128), jnp.bfloat16),
        compiler_params=pltpu.CompilerParams(dimension_semantics=("arbitrary", "arbitrary"), vmem_limit_bytes=50 * 1024 * 1024),
        name="attention",
    )(lengths, qkv, qkv, qkv, w)

def backward_kernel(len_ref, q_ref, k_ref, v_ref, g_ref, w_ref, o_ref, z_ref, table, total):
    seq = q_ref.shape[0]
    tiles = seq // 128
    doc = pl.program_id(1)
    @pl.when(doc == 0)
    def _():
        for h in range(2):
            band(w_ref, h, table, seq)
        total[...] = jnp.zeros_like(total)
    length = len_ref[doc]
    lane = lax.broadcasted_iota(jnp.int32, (seq, 128), 1)
    row = lax.broadcasted_iota(jnp.int32, (seq, 1), 0)
    q = q_ref[...] * jnp.bfloat16(0.125)
    k = k_ref[...]
    v = v_ref[...]
    g = g_ref[...]
    parts = []
    for h in range(2):
        mine = (lane < 64) == (h == 0)
        s = lax.dot_general(k, jnp.where(mine, q, 0), NT, preferred_element_type=jnp.float32)
        s = jnp.where(row < length, s + table[h], -1000000000.0)
        e = jnp.exp(s - jnp.max(s, axis=0, keepdims=True))
        p = e * (1.0 / jnp.sum(e, axis=0, keepdims=True))
        dv = jnp.dot(p.astype(jnp.bfloat16), g, preferred_element_type=jnp.float32)
        dp = lax.dot_general(v, jnp.where(mine, g, 0), NT, preferred_element_type=jnp.float32)
        ds = (p * (dp - jnp.sum(p * dp, axis=0, keepdims=True))).astype(jnp.bfloat16)
        total[h] += ds.astype(jnp.float32)
        dk = jnp.dot(ds, q, preferred_element_type=jnp.float32)
        dq = lax.dot_general(ds, k, TN, preferred_element_type=jnp.float32) * 0.125
        parts.append((dq, dk, dv))
    for i in range(3):
        o_ref[i] = jnp.where(lane < 64, parts[0][i], parts[1][i]).astype(o_ref.dtype)
    @pl.when(doc == pl.num_programs(1) - 1)
    def _():
        r = lax.broadcasted_iota(jnp.int32, (128, 128), 0)
        c = lax.broadcasted_iota(jnp.int32, (128, 128), 1)
        flip = jnp.where(r + c == 127, 1.0, 0.0)
        z_ref[...] = jnp.zeros_like(z_ref)
        for h in range(2):
            def block(d):
                return sum(total[h, a * 128 : a * 128 + 128, (a - d) * 128 : (a - d) * 128 + 128] for a in range(tiles) if 0 <= a - d < tiles)
            for d in (-1, 0, 1):
                x = jnp.dot(flip, block(d), precision=HIGHEST, preferred_element_type=jnp.float32)
                x = jnp.concatenate([x, jnp.zeros_like(x)], axis=1)
                x = pltpu.roll(x, 0, 1, stride=1, stride_axis=0)
                z_ref[0, h, d + 1 : d + 2, :] = jnp.sum(x, axis=0, keepdims=True)
            z_ref[0, h, 3:4, 0:128] = jnp.sum(sum(block(-d) for d in range(2, tiles)), axis=0, keepdims=True)
            z_ref[0, h, 4:5, 0:128] = jnp.sum(sum(block(d) for d in range(2, tiles)), axis=0, keepdims=True)

def attention_back(lengths, qkv, g, w, seq):
    tokens = qkv.shape[0]
    pairs = w.shape[0]
    docs = tokens // seq
    spec = lambda base: pl.BlockSpec((seq, 128), lambda h, d, *_: (d, base + h))
    return pl.pallas_call(
        backward_kernel,
        grid_spec=pltpu.PrefetchScalarGridSpec(
            num_scalar_prefetch=1, grid=(pairs, docs),
            in_specs=[spec(0), spec(pairs), spec(2 * pairs), spec(0), pl.BlockSpec((1, 2, 2 * seq), lambda h, d, *_: (h, 0, 0))],
            out_specs=[pl.BlockSpec((3, seq, 128), lambda h, d, *_: (0, d, h)), pl.BlockSpec((1, 2, 8, 256), lambda h, d, *_: (h, 0, 0, 0))],
            scratch_shapes=[pltpu.VMEM((2, seq, seq), jnp.float32), pltpu.VMEM((2, seq, seq), jnp.float32)]),
        out_shape=[jax.ShapeDtypeStruct((3, tokens, pairs * 128), jnp.bfloat16), jax.ShapeDtypeStruct((pairs, 2, 8, 256), jnp.float32)],
        compiler_params=pltpu.CompilerParams(dimension_semantics=("arbitrary", "arbitrary"), vmem_limit_bytes=50 * 1024 * 1024),
        name="attention_back",
    )(lengths, qkv, qkv, qkv, g, w)

def bias_rows(position_bias, seq, sign):
    nb, heads = position_bias.shape
    buckets = bucket_of(sign * (jnp.arange(2 * seq) - seq), nb, REACH)
    hits = (jnp.arange(nb)[:, None] == buckets[None, :]).astype(jnp.float32)
    return jnp.dot(position_bias.T, hits, precision=HIGHEST).reshape(heads // 2, 2, 2 * seq)

def bias_gradient(z, seq, nb):
    heads = z.shape[0] * 2
    j = jnp.arange(256)
    offs = [jnp.where(j < 255, 128 * d + 127 - j, 0) for d in (-1, 0, 1)] + [jnp.full((256,), 1 - seq), jnp.full((256,), seq - 1)]
    offs = jnp.concatenate(offs + [jnp.zeros((768,), jnp.int32)])
    hits = (bucket_of(offs, nb, REACH)[:, None] == jnp.arange(nb)[None, :]).astype(jnp.float32)
    return jnp.dot(z.reshape(heads, 2048), hits, precision=HIGHEST).T

def weight_pieces(widths):
    down = len(widths) - 1
    cut = widths[down] * 2 // 3 // 128 * 128
    pieces = [(down - 1, 0, widths[down - 1], 0)]
    pieces += [(which, 0, widths[which], 1) for which in range(down - 2)]
    pieces += [(down - 2, 0, widths[down - 2], 0)]
    return pieces + [(down, 0, cut, 0), (down, cut, widths[down], 1)]


NN = (((1,), (0,)), ((), ()))


def triangle(size):
    rows = lax.broadcasted_iota(jnp.int32, (size, size), 0)
    columns = lax.broadcasted_iota(jnp.int32, (size, size), 1)
    return jnp.where(rows < columns, 1.0, 0.0).astype(jnp.bfloat16)


def digits(numbers):
    high = numbers // 64
    row = lax.broadcasted_iota(jnp.int32, (8, numbers.shape[1]), 0)
    both = jnp.where(row == 0, high, jnp.where(row == 1, numbers - 64 * high, 0))
    return both.astype(jnp.float32).astype(jnp.bfloat16)


def upright(pairs):
    row = lax.broadcasted_iota(jnp.int32, (8, 128), 0)
    value = jnp.where(row == 0, 64.0, jnp.where(row == 1, 1.0, 0.0)).astype(jnp.bfloat16)
    return lax.dot_general(pairs, value, TN, preferred_element_type=jnp.float32)


def hits_by_lane(numbers, width, base):
    lane = lax.broadcasted_iota(jnp.int32, (1, 128), 1).astype(jnp.float32) + base
    tiles = [
        jnp.where(numbers == lane + 128.0 * tile, 1.0, 0.0).astype(jnp.bfloat16)
        for tile in range(width // 128)
    ]
    return jnp.concatenate(tiles, axis=1)


def front_kernel(n_dp, n_pair, pieces, n_in, *refs):
    k = len(pieces)
    owner_ref, row_ref, table_ref = refs[:3]
    shards = refs[3 : 3 + n_in]
    emb_ref, key_ref, asked_ref = refs[3 + n_in : 6 + n_in]
    outs = refs[6 + n_in : 6 + 2 * n_in]
    rest = refs[6 + 2 * n_in :]
    bufs, rest = rest[:k], rest[k:]
    (wide, table, ask_out, ask_in, rows_out, rows_in, total, hop_send, hop_recv, core_send,
     core_recv, out_sem, table_sem, ask_send, ask_recv, row_send, row_recv) = rest
    dp, pair = lax.axis_index("dp"), lax.axis_index("pair")
    me = dp * n_pair + pair
    steps = (n_dp * n_pair - 1).bit_length() - 1
    half = 1 << steps
    orders = [bit_order(n_dp, n_pair, color) for _, _, _, color in pieces]
    tokens = owner_ref.shape[1]
    cap = ask_out.shape[2]
    table_rows = table_ref.shape[0]
    load = pltpu.make_async_copy(table_ref, wide, table_sem)
    load.start()
    peers = [{"dp": dp ^ j, "pair": pair} for j in range(1, n_dp)]
    sem = pltpu.get_barrier_semaphore()
    mates = [{"dp": dp, "pair": pair ^ j} for j in (1, 2)]
    for target in peers + mates:
        pl.semaphore_signal(sem, inc=1, device_id=target, device_id_type=MESH)
    for a, (which, low, high, _) in enumerate(pieces):
        bufs[a][0] = shards[which][:, low:high].astype(jnp.bfloat16)

    owner = owner_ref[...]
    by_owner = lax.broadcasted_iota(jnp.int32, (n_dp, tokens), 0) == owner
    ranks = jnp.dot(
        jnp.where(by_owner, 1.0, 0.0).astype(jnp.bfloat16),
        triangle(tokens),
        preferred_element_type=jnp.float32,
    )
    rank = jnp.sum(jnp.where(by_owner, ranks, 0.0), axis=0, keepdims=True)
    key = owner * cap + rank.astype(jnp.int32)
    key_ref[...] = key
    wanted = digits(row_ref[...])
    for j in range(n_dp):
        slot = lax.broadcasted_iota(jnp.int32, (cap, tokens), 0) + (dp ^ j) * cap
        chosen = jnp.where(slot == key, 1.0, 0.0).astype(jnp.bfloat16)
        ask_out[j] = lax.dot_general(wanted, chosen, NT, preferred_element_type=jnp.float32)
    pl.semaphore_wait(sem, n_dp + 1)

    def ask(j):
        return remote(ask_out.at[j], ask_in.at[j], ask_send.at[j], ask_recv.at[j], peers[j - 1])

    def reply(j):
        return remote(rows_out.at[j], rows_in.at[j], row_send.at[j], row_recv.at[j], peers[j - 1])

    def forward(a, s):
        lo, count = (0, 1) if s == 0 else (1 << (s - 1), 1 << (s - 1))
        return remote(
            bufs[a].at[pl.ds(lo, count)],
            bufs[a].at[pl.ds(half + lo, count)],
            core_send.at[a, s],
            core_recv.at[a, s],
            place(me ^ 1, n_pair),
        )

    def hop(a, s):
        return remote(
            bufs[a].at[pl.ds(0, 1 << s)],
            bufs[a].at[pl.ds(1 << s, 1 << s)],
            hop_send.at[a, s],
            hop_recv.at[a, s],
            place(me ^ (1 << orders[a][s]), n_pair),
        )

    def write_out(a, lo, count, core):
        which, low, high, _ = pieces[a]
        for p in range(lo, lo + count):
            block = me ^ (offset(orders[a], p) + core)
            pltpu.make_async_copy(
                bufs[a].at[p + core * half],
                outs[which].at[block, :, pl.ds(low, high - low)],
                out_sem.at[a],
            ).start()

    def weights_step(s):
        for a in range(k):
            hop(a, s).wait_recv()
            if s + 1 < steps:
                hop(a, s + 1).start()
            forward(a, s + 1).start()
            write_out(a, 1 << s, 1 << s, 0)
        for a in range(k):
            forward(a, s).wait_recv()
            lo, count = (0, 1) if s == 0 else (1 << (s - 1), 1 << (s - 1))
            write_out(a, lo, count, 1)

    far = sorted(range(1, n_dp), reverse=True)
    for j in far:
        ask(j).start()
    for a in range(k):
        hop(a, 0).start()
    for a in range(k):
        forward(a, 0).start()
        write_out(a, 0, 1, 0)
    load.wait()

    def narrow(i, carry):
        part = pl.ds(pl.multiple_of(i * 16, 16), 16)
        table[part] = wide[part].astype(jnp.bfloat16)
        return carry

    lax.fori_loop(0, table_rows // 16, narrow, 0)
    if table.shape[0] > table_rows:
        table[table_rows:] = jnp.zeros((table.shape[0] - table_rows, table.shape[1]), jnp.bfloat16)

    def answer(j, target):
        asked = ask_out if j == 0 else ask_in
        hit = hits_by_lane(upright(asked[j].astype(jnp.bfloat16)), table.shape[0], 0.0)
        target[j] = jnp.dot(hit, table[...], preferred_element_type=jnp.float32).astype(jnp.bfloat16)
        asked_ref[j] = (64.0 * asked[j, 0:1] + asked[j, 1:2]).astype(jnp.int32)

    for turn, j in enumerate(far):
        ask(j).wait_recv()
        answer(j, rows_out)
        reply(j).start()
        if turn == 1:
            weights_step(0)
        if turn == 4:
            weights_step(1)
    answer(0, rows_in)
    upright_key = upright(digits(key))

    def seat(j, first):
        place_hit = hits_by_lane(upright_key, cap, ((dp ^ j) * cap).astype(jnp.float32))
        got = jnp.dot(place_hit, rows_in[j], preferred_element_type=jnp.float32)
        total[...] = got if first else total[...] + got

    seat(0, True)
    near = list(reversed(far))
    for turn, j in enumerate(near):
        reply(j).wait_recv()
        seat(j, False)
        if turn == len(near) // 3:
            for s in range(2, steps - 1):
                weights_step(s)
    emb_ref[...] = total[...].astype(jnp.bfloat16)
    weights_step(steps - 1)
    for a in range(k):
        forward(a, steps).wait_recv()
        write_out(a, half // 2, half // 2, 1)
    for j in far:
        ask(j).wait_send()
        reply(j).wait_send()
    for a in range(k):
        for s in range(steps):
            hop(a, s).wait_send()
        for s in range(steps + 1):
            forward(a, s).wait_send()
        pltpu.make_async_copy(bufs[a], bufs[a], out_sem.at[a]).wait()


def front(owner, row, table, shards, pieces, cap, n_dp, n_pair, cid):
    n, k = n_dp * n_pair, len(pieces)
    steps = (n - 1).bit_length() - 1
    tokens = owner.shape[1]
    table_rows, width = table.shape
    padded = -(-table_rows // 256) * 256
    sem = pltpu.SemaphoreType.DMA
    return pl.pallas_call(
        functools.partial(front_kernel, n_dp, n_pair, pieces, len(shards)),
        out_shape=[
            jax.ShapeDtypeStruct((tokens, width), jnp.bfloat16),
            jax.ShapeDtypeStruct((1, tokens), jnp.int32),
            jax.ShapeDtypeStruct((n_dp, 1, cap), jnp.int32),
        ]
        + [jax.ShapeDtypeStruct((n,) + s.shape, jnp.bfloat16) for s in shards],
        in_specs=[VM, VM, ANY] + [VM] * len(shards),
        out_specs=[VM] * 3 + [ANY] * len(shards),
        scratch_shapes=[
            pltpu.VMEM((n, shards[p[0]].shape[0], p[2] - p[1]), jnp.bfloat16) for p in pieces
        ]
        + [
            pltpu.VMEM((table_rows, width), jnp.float32),
            pltpu.VMEM((padded, width), jnp.bfloat16),
            pltpu.VMEM((n_dp, 8, cap), jnp.float32),
            pltpu.VMEM((n_dp, 8, cap), jnp.float32),
            pltpu.VMEM((n_dp, cap, width), jnp.bfloat16),
            pltpu.VMEM((n_dp, cap, width), jnp.bfloat16),
            pltpu.VMEM((tokens, width), jnp.float32),
            sem((k, steps)),
            sem((k, steps)),
            sem((k, steps + 1)),
            sem((k, steps + 1)),
            sem((k,)),
            sem,
            sem((n_dp,)),
            sem((n_dp,)),
            sem((n_dp,)),
            sem((n_dp,)),
        ],
        compiler_params=pltpu.CompilerParams(
            collective_id=cid, has_side_effects=True, vmem_limit_bytes=VMEM_LIMIT
        ),
        name="rows_and_weights",
    )(owner, row, table, *shards)


def local_plain(
    token_owner,
    token_row,
    lengths,
    positives,
    negatives,
    neg_counts,
    embed_table,
    embed_first,
    embed_second,
    qkv_weight,
    qkv_first,
    qkv_second,
    out_weight,
    out_first,
    out_second,
    in_weight,
    in_first,
    in_second,
    down_weight,
    down_first,
    down_second,
    norm_gains,
    gains_first,
    gains_second,
    position_bias,
    bias_first,
    bias_second,
):
    doc_count = lengths.shape[0]
    seq_len = token_row.shape[1]
    model_width = embed_table.shape[1]
    head_count = position_bias.shape[1]
    bucket_count = position_bias.shape[0]
    tok_total = doc_count * seq_len
    owners = lax.axis_size("dp")
    capacity = max(2, 2 * tok_total // owners)
    low_mats = (
        qkv_weight.astype(jnp.bfloat16),
        out_weight.astype(jnp.bfloat16),
        in_weight.astype(jnp.bfloat16),
        down_weight.astype(jnp.bfloat16),
    )
    qkv_full, out_full, in_full, down_full = (
        lax.all_gather(low_mats[0], ("dp", "pair"), axis=0, tiled=True),
        lax.all_gather(low_mats[1], ("dp", "pair"), axis=0, tiled=True),
        lax.all_gather(low_mats[2], ("dp", "pair"), axis=0, tiled=True),
        lax.all_gather(low_mats[3], ("dp", "pair"), axis=0, tiled=True),
    )
    tok_owner = token_owner.reshape(-1)
    tok_row = token_row.reshape(-1)
    owner_hits = (tok_owner[:, None] == jnp.arange(owners, dtype=jnp.int32)[None, :]).astype(
        jnp.int32
    )
    slot_rank = jnp.sum((jnp.cumsum(owner_hits, axis=0) - 1) * owner_hits, axis=1)
    requests = jnp.zeros((owners, capacity), jnp.int32).at[tok_owner, slot_rank].set(tok_row)
    asked_rows = lax.all_to_all(requests, "dp", split_axis=0, concat_axis=0, tiled=True)
    looked = jnp.take(embed_table, asked_rows.reshape(-1), axis=0).astype(jnp.bfloat16)
    answer = lax.all_to_all(
        looked.reshape(asked_rows.shape + (model_width,)),
        "dp",
        split_axis=0,
        concat_axis=0,
        tiled=True,
    )
    replies, asked_rows = (answer, asked_rows)
    embedded = replies[tok_owner, slot_rank].astype(jnp.float32)
    positions = jnp.arange(seq_len)
    live = positions[None, :] < lengths[:, None]
    pair_buckets = bucket_of(
        (positions[None, :] - positions[:, None]).reshape(-1), bucket_count, REACH
    )
    pair_hits = (jnp.arange(bucket_count)[:, None] == pair_buckets[None, :]).astype(jnp.float32)
    bias_full = jnp.dot(position_bias.T, pair_hits, precision=HIGHEST).reshape(
        head_count, seq_len, seq_len
    )
    bucket_map = pair_hits.astype(jnp.bfloat16)

    def split_doc(source, doc_index):
        doc_rows = source[doc_index * seq_len : (doc_index + 1) * seq_len]
        return tuple(
            (
                doc_rows[:, member * model_width : (member + 1) * model_width].reshape(
                    seq_len, head_count, -1
                )
                for member in range(3)
            )
        )

    normed_one, inverse_one = rms_forward(embedded, norm_gains[0])
    normed_one = normed_one.astype(jnp.bfloat16)
    qkv_rows = jnp.dot(normed_one, qkv_full, preferred_element_type=jnp.float32).astype(
        jnp.bfloat16
    )
    attended_parts = []
    logsum_parts = []
    for doc_index in range(doc_count):
        query_heads, key_heads, value_heads = split_doc(qkv_rows, doc_index)
        doc_out, logsum = attend_forward(
            query_heads, key_heads, value_heads, bias_full, live[doc_index]
        )
        attended_parts.append(doc_out.reshape(seq_len, model_width))
        logsum_parts.append(logsum)
    attended = jnp.concatenate(attended_parts, axis=0).astype(jnp.bfloat16)
    residual = embedded + jnp.dot(attended, out_full, preferred_element_type=jnp.float32)
    normed_two, inverse_two = rms_forward(residual, norm_gains[1])
    normed_two = normed_two.astype(jnp.bfloat16)
    hidden = jax.nn.relu(jnp.dot(normed_two, in_full, preferred_element_type=jnp.float32)).astype(
        jnp.bfloat16
    )
    output_rows = residual + jnp.dot(hidden, down_full, preferred_element_type=jnp.float32)
    normed_three, inverse_three = rms_forward(output_rows, norm_gains[2])
    live_rows = live.reshape(-1, 1)
    length_float = lengths.astype(jnp.float32)
    pooled_local = (
        jnp.sum(
            jnp.where(live_rows, normed_three, 0.0).reshape(doc_count, seq_len, model_width), axis=1
        )
        / length_float[:, None]
    )
    pooled_all = lax.all_gather(pooled_local, ("dp", "pair"), axis=0, tiled=True)
    loss_value, loss_pullback = jax.vjp(
        lambda pooled_in: margin_loss(pooled_in, positives, negatives, neg_counts), pooled_all
    )
    grad_pooled_all = loss_pullback(jnp.ones((), jnp.float32))[0]
    grad_pooled = lax.dynamic_slice_in_dim(
        grad_pooled_all, lax.axis_index(("dp", "pair")) * doc_count, doc_count, 0
    )
    grad_three = jnp.where(
        live_rows, jnp.repeat(grad_pooled / length_float[:, None], seq_len, axis=0), 0.0
    )
    qkv_back, out_back, in_back, down_back = (qkv_full, out_full, in_full, down_full)
    grad_output, gain_three = rms_backward(output_rows, inverse_three, norm_gains[2], grad_three)
    grad_branch = grad_output.astype(jnp.bfloat16)
    grad_down = lax.dot_general(
        hidden, grad_branch, CONTRACT_ROWS, preferred_element_type=jnp.float32
    )
    grad_hidden = lax.dot_general(
        grad_branch, down_back, CONTRACT_COLS, preferred_element_type=jnp.float32
    )
    grad_pre = jnp.where(hidden > 0, grad_hidden, 0.0).astype(jnp.bfloat16)
    grad_in = lax.dot_general(
        normed_two, grad_pre, CONTRACT_ROWS, preferred_element_type=jnp.float32
    )
    grad_normed_two = lax.dot_general(
        grad_pre, in_back, CONTRACT_COLS, preferred_element_type=jnp.float32
    )
    grad_res_part, gain_two = rms_backward(residual, inverse_two, norm_gains[1], grad_normed_two)
    grad_residual = grad_output + grad_res_part
    grad_attn_branch = grad_residual.astype(jnp.bfloat16)
    grad_out = lax.dot_general(
        attended, grad_attn_branch, CONTRACT_ROWS, preferred_element_type=jnp.float32
    )
    grad_attended = lax.dot_general(
        grad_attn_branch, out_back, CONTRACT_COLS, preferred_element_type=jnp.float32
    ).astype(jnp.bfloat16)
    grad_qkv_parts = []
    bias_grad_heads = jnp.zeros((head_count, bucket_count), jnp.float32)
    for doc_index in range(doc_count):
        query_heads, key_heads, value_heads = split_doc(qkv_rows, doc_index)
        grad_doc = grad_attended[doc_index * seq_len : (doc_index + 1) * seq_len].reshape(
            seq_len, head_count, -1
        )
        grad_query, grad_key, grad_value, grad_low = attend_backward(
            query_heads,
            key_heads,
            value_heads,
            bias_full,
            live[doc_index],
            logsum_parts[doc_index],
            grad_doc,
        )
        grad_qkv_parts.append(
            jnp.concatenate(
                [
                    grad_query.reshape(seq_len, model_width),
                    grad_key.reshape(seq_len, model_width),
                    grad_value.reshape(seq_len, model_width),
                ],
                axis=1,
            )
        )
        bias_grad_heads = bias_grad_heads + lax.dot_general(
            grad_low.reshape(head_count, -1),
            bucket_map,
            CONTRACT_COLS,
            preferred_element_type=jnp.float32,
        )
    bias_grad_local = bias_grad_heads.T
    grad_qkv_rows = jnp.concatenate(grad_qkv_parts, axis=0).astype(jnp.bfloat16)
    grad_qkv = lax.dot_general(
        normed_one, grad_qkv_rows, CONTRACT_ROWS, preferred_element_type=jnp.float32
    )
    grad_normed_one = lax.dot_general(
        grad_qkv_rows, qkv_back, CONTRACT_COLS, preferred_element_type=jnp.float32
    )
    grad_emb_part, gain_one = rms_backward(embedded, inverse_one, norm_gains[0], grad_normed_one)
    grad_embedded = grad_residual + grad_emb_part
    sendback = (
        jnp.zeros((owners, capacity, model_width), jnp.float32)
        .at[tok_owner, slot_rank]
        .set(grad_embedded)
    )
    arrived = lax.all_to_all(sendback, "dp", split_axis=0, concat_axis=0, tiled=True)
    table_grad = jax.ops.segment_sum(
        arrived.reshape(-1, model_width), asked_rows.reshape(-1), num_segments=embed_table.shape[0]
    )
    table_grad = lax.psum(table_grad, "pair")
    weight_grads = (
        lax.psum_scatter(grad_qkv, ("dp", "pair"), scatter_dimension=0, tiled=True),
        lax.psum_scatter(grad_out, ("dp", "pair"), scatter_dimension=0, tiled=True),
        lax.psum_scatter(grad_in, ("dp", "pair"), scatter_dimension=0, tiled=True),
        lax.psum_scatter(grad_down, ("dp", "pair"), scatter_dimension=0, tiled=True),
    )
    pair_first = (lax.axis_index("pair") == 0).astype(jnp.float32)
    square_part = jnp.sum(
        jnp.stack([jnp.sum(grad_piece * grad_piece) for grad_piece in weight_grads])
    ) + pair_first * jnp.sum(table_grad * table_grad)
    gain_grad, bias_grad, square_sum = lax.psum(
        (jnp.stack([gain_one, gain_two, gain_three]), bias_grad_local, square_part), ("dp", "pair")
    )
    clip_norm = jnp.sqrt(
        square_sum + jnp.sum(gain_grad * gain_grad) + jnp.sum(bias_grad * bias_grad)
    )
    factor = jnp.minimum(1.0, clip_limit / clip_norm)
    table_out = adam_step(embed_table, embed_first, embed_second, table_grad * factor, 1.0, 0.01)
    qkv_out = adam_step(qkv_weight, qkv_first, qkv_second, weight_grads[0] * factor, 0.05, 0.01)
    out_out = adam_step(out_weight, out_first, out_second, weight_grads[1] * factor, 0.05, 0.01)
    in_out = adam_step(in_weight, in_first, in_second, weight_grads[2] * factor, 0.05, 0.01)
    down_out = adam_step(down_weight, down_first, down_second, weight_grads[3] * factor, 0.05, 0.01)
    gains_out = adam_step(norm_gains, gains_first, gains_second, gain_grad * factor, 1.0, 0.0)
    bias_out = adam_step(position_bias, bias_first, bias_second, bias_grad * factor, 0.3, 0.0)
    return (
        loss_value,
        clip_norm,
        table_out[0],
        table_out[1],
        table_out[2],
        qkv_out[0],
        qkv_out[1],
        qkv_out[2],
        out_out[0],
        out_out[1],
        out_out[2],
        in_out[0],
        in_out[1],
        in_out[2],
        down_out[0],
        down_out[1],
        down_out[2],
        gains_out[0],
        gains_out[1],
        gains_out[2],
        bias_out[0],
        bias_out[1],
        bias_out[2],
    )


def local_fast(
    token_owner,
    token_row,
    lengths,
    positives,
    negatives,
    neg_counts,
    embed_table,
    embed_first,
    embed_second,
    qkv_weight,
    qkv_first,
    qkv_second,
    out_weight,
    out_first,
    out_second,
    in_weight,
    in_first,
    in_second,
    down_weight,
    down_first,
    down_second,
    norm_gains,
    gains_first,
    gains_second,
    position_bias,
    bias_first,
    bias_second,
):
    doc_count = lengths.shape[0]
    seq_len = token_row.shape[1]
    model_width = embed_table.shape[1]
    head_count = position_bias.shape[1]
    bucket_count = position_bias.shape[0]
    tok_total = doc_count * seq_len
    owners = lax.axis_size("dp")
    capacity = max(2, 2 * tok_total // owners)
    holders = lax.axis_size("pair")
    shards = (qkv_weight, out_weight, in_weight, down_weight)
    embedded_low, slot_keys, asked_rows, *full = front(
        token_owner.reshape(1, -1),
        token_row.reshape(1, -1),
        embed_table,
        shards,
        weight_pieces([shard.shape[1] for shard in shards]),
        capacity,
        owners,
        holders,
        1,
    )
    qkv_full, out_full, in_full, down_full = (
        matrix.reshape(-1, matrix.shape[2]) for matrix in full
    )
    embedded = embedded_low.astype(jnp.float32)
    positions = jnp.arange(seq_len)
    live = positions[None, :] < lengths[:, None]
    normed_one, inverse_one = rms_forward(embedded, norm_gains[0])
    normed_one = normed_one.astype(jnp.bfloat16)
    qkv_rows = jnp.dot(normed_one, qkv_full, preferred_element_type=jnp.float32).astype(
        jnp.bfloat16
    )
    attended = attention(lengths, qkv_rows, bias_rows(position_bias, seq_len, 1), seq_len)
    residual = embedded + jnp.dot(attended, out_full, preferred_element_type=jnp.float32)
    normed_two, inverse_two = rms_forward(residual, norm_gains[1])
    normed_two = normed_two.astype(jnp.bfloat16)
    hidden = jax.nn.relu(jnp.dot(normed_two, in_full, preferred_element_type=jnp.float32)).astype(
        jnp.bfloat16
    )
    output_rows = residual + jnp.dot(hidden, down_full, preferred_element_type=jnp.float32)
    normed_three, inverse_three = rms_forward(output_rows, norm_gains[2])
    live_rows = live.reshape(-1, 1)
    length_float = lengths.astype(jnp.float32)
    pooled_local = (
        jnp.sum(
            jnp.where(live_rows, normed_three, 0.0).reshape(doc_count, seq_len, model_width), axis=1
        )
        / length_float[:, None]
    )
    loss_cell, grad_pooled = pooled_loss(
        pooled_local, positives, negatives, neg_counts, owners, holders, 3
    )
    loss_value = loss_cell[0, 0]
    grad_three = jnp.where(
        live_rows, jnp.repeat(grad_pooled / length_float[:, None], seq_len, axis=0), 0.0
    )
    qkv_back, out_back, in_back, down_back = (qkv_full, out_full, in_full, down_full)
    grad_output, gain_three = rms_backward(output_rows, inverse_three, norm_gains[2], grad_three)
    grad_branch = grad_output.astype(jnp.bfloat16)
    grad_down = lax.dot_general(
        hidden, grad_branch, CONTRACT_ROWS, preferred_element_type=jnp.float32
    )
    grad_hidden = lax.dot_general(
        grad_branch, down_back, CONTRACT_COLS, preferred_element_type=jnp.float32
    )
    grad_pre = jnp.where(hidden > 0, grad_hidden, 0.0).astype(jnp.bfloat16)
    grad_in = lax.dot_general(
        normed_two, grad_pre, CONTRACT_ROWS, preferred_element_type=jnp.float32
    )
    grad_normed_two = lax.dot_general(
        grad_pre, in_back, CONTRACT_COLS, preferred_element_type=jnp.float32
    )
    grad_res_part, gain_two = rms_backward(residual, inverse_two, norm_gains[1], grad_normed_two)
    grad_residual = grad_output + grad_res_part
    grad_attn_branch = grad_residual.astype(jnp.bfloat16)
    grad_out = lax.dot_general(
        attended, grad_attn_branch, CONTRACT_ROWS, preferred_element_type=jnp.float32
    )
    grad_attended = lax.dot_general(
        grad_attn_branch, out_back, CONTRACT_COLS, preferred_element_type=jnp.float32
    ).astype(jnp.bfloat16)
    grad_parts, diagonals = attention_back(
        lengths, qkv_rows, grad_attended, bias_rows(position_bias, seq_len, -1), seq_len
    )
    bias_grad_local = bias_gradient(diagonals, seq_len, bucket_count)
    grad_qkv = [
        lax.dot_general(normed_one, part, CONTRACT_ROWS, preferred_element_type=jnp.float32)
        for part in grad_parts
    ]
    grad_normed_one = sum(
        lax.dot_general(
            part,
            qkv_back[:, index * model_width : (index + 1) * model_width],
            CONTRACT_COLS,
            preferred_element_type=jnp.float32,
        )
        for index, part in enumerate(grad_parts)
    )
    grad_emb_part, gain_one = rms_backward(embedded, inverse_one, norm_gains[0], grad_normed_one)
    grad_embedded = grad_residual + grad_emb_part
    sendback = (
        jnp.zeros((owners * capacity, model_width), jnp.bfloat16)
        .at[slot_keys[0]]
        .set(grad_embedded.astype(jnp.bfloat16))
    ).reshape(owners, capacity, model_width)
    arrived = exchange(sendback, owners, 4)
    arrived = arrived[lax.axis_index("dp") ^ jnp.arange(owners)]
    table_rows = embed_table.shape[0]
    table_grad, table_square = table_total(
        arrived.reshape(-1, model_width),
        asked_rows.reshape(1, -1),
        -(-table_rows // 1024) * 1024,
        holders,
        5,
    )
    table_grad = table_grad[:table_rows].astype(jnp.float32)
    parts = owners * holders
    weight_grads = scatter_all(
        [
            grad.astype(jnp.bfloat16).reshape(parts, -1, grad.shape[1])
            for grad in (*grad_qkv, grad_out, grad_in, grad_down)
        ],
        weight_pieces([model_width] * 4 + [grad_in.shape[1], model_width]),
        owners,
        holders,
        6,
    )
    weight_grads = (jnp.concatenate(weight_grads[:3], axis=1), *weight_grads[3:])
    square_part = table_square[0, 0] + jnp.sum(
        jnp.stack([jnp.sum(grad_piece * grad_piece) for grad_piece in weight_grads])
    )
    small = jnp.concatenate(
        [
            jnp.stack([gain_one, gain_two, gain_three]).reshape(-1),
            bias_grad_local.reshape(-1),
            square_part.reshape(1),
        ]
    )
    small_size = small.shape[0]
    small_rows = -(-small_size // 1024) * 8
    small = jnp.pad(small, (0, small_rows * 128 - small_size)).reshape(small_rows, 128)
    small = small_total(small, owners, holders, 7).reshape(-1)
    gain_grad = small[: 3 * model_width].reshape(3, model_width)
    bias_grad = small[3 * model_width : small_size - 1].reshape(bucket_count, head_count)
    square_sum = small[small_size - 1]
    clip_norm = jnp.sqrt(
        square_sum + jnp.sum(gain_grad * gain_grad) + jnp.sum(bias_grad * bias_grad)
    )
    factor = jnp.minimum(1.0, clip_limit / clip_norm)
    table_out = adam_step(embed_table, embed_first, embed_second, table_grad * factor, 1.0, 0.01)
    qkv_out = adam_step(qkv_weight, qkv_first, qkv_second, weight_grads[0] * factor, 0.05, 0.01)
    out_out = adam_step(out_weight, out_first, out_second, weight_grads[1] * factor, 0.05, 0.01)
    in_out = adam_step(in_weight, in_first, in_second, weight_grads[2] * factor, 0.05, 0.01)
    down_out = adam_step(down_weight, down_first, down_second, weight_grads[3] * factor, 0.05, 0.01)
    gains_out = adam_step(norm_gains, gains_first, gains_second, gain_grad * factor, 1.0, 0.0)
    bias_out = adam_step(position_bias, bias_first, bias_second, bias_grad * factor, 0.3, 0.0)
    return (
        loss_value,
        clip_norm,
        table_out[0],
        table_out[1],
        table_out[2],
        qkv_out[0],
        qkv_out[1],
        qkv_out[2],
        out_out[0],
        out_out[1],
        out_out[2],
        in_out[0],
        in_out[1],
        in_out[2],
        down_out[0],
        down_out[1],
        down_out[2],
        gains_out[0],
        gains_out[1],
        gains_out[2],
        bias_out[0],
        bias_out[1],
        bias_out[2],
    )


def local(*arrays):
    n_dp, n_pair = lax.axis_size("dp"), lax.axis_size("pair")
    lengths, qkv_weight, down_weight = arrays[2], arrays[9], arrays[18]
    fits = (
        n_pair == 4
        and n_dp & (n_dp - 1) == 0
        and qkv_weight.shape[0] % 8 == 0
        and down_weight.shape[0] % 8 == 0
        and lengths.shape[0] == 2
        and 2 * arrays[1].size // n_dp % 128 == 0
    )
    return (local_fast if fits else local_plain)(*arrays)


def solution(mesh):
    return jax.shard_map(
        local,
        mesh=mesh,
        in_specs=(
            P(("dp", "pair"), None, None),
            P(("dp", "pair"), None),
            P(("dp", "pair")),
            P(),
            P(),
            P(),
            P("dp", None),
            P("dp", None),
            P("dp", None),
            P(("dp", "pair"), None),
            P(("dp", "pair"), None),
            P(("dp", "pair"), None),
            P(("dp", "pair"), None),
            P(("dp", "pair"), None),
            P(("dp", "pair"), None),
            P(("dp", "pair"), None),
            P(("dp", "pair"), None),
            P(("dp", "pair"), None),
            P(("dp", "pair"), None),
            P(("dp", "pair"), None),
            P(("dp", "pair"), None),
            P(),
            P(),
            P(),
            P(),
            P(),
            P(),
        ),
        out_specs=(
            P(),
            P(),
            P("dp", None),
            P("dp", None),
            P("dp", None),
            P(("dp", "pair"), None),
            P(("dp", "pair"), None),
            P(("dp", "pair"), None),
            P(("dp", "pair"), None),
            P(("dp", "pair"), None),
            P(("dp", "pair"), None),
            P(("dp", "pair"), None),
            P(("dp", "pair"), None),
            P(("dp", "pair"), None),
            P(("dp", "pair"), None),
            P(("dp", "pair"), None),
            P(("dp", "pair"), None),
            P(),
            P(),
            P(),
            P(),
            P(),
            P(),
        ),
        check_vma=False,
    )
```

```python
import functools
import math

import jax
import jax.numpy as jnp
from jax import lax
from jax.experimental import pallas as pl
from jax.experimental.pallas import tpu as pltpu
from jax.sharding import PartitionSpec as P

REACH = 128
STEP = 5


rms_eps = 1e-06
clip_limit = 0.05
margin = 1.0
sim_scale = 20.0
beta_one = 0.9
beta_two = 0.999
adam_eps = 1e-08
HIGHEST = lax.Precision.HIGHEST
CONTRACT_ROWS = (((0,), (0,)), ((), ()))
CONTRACT_COLS = (((1,), (1,)), ((), ()))


def bucket_of(offsets, bucket_count, reach_limit):
    half_count = bucket_count // 2
    exact_count = half_count // 2
    sign_base = jnp.where(offsets > 0, half_count, 0).astype(jnp.int32)
    distance = jnp.abs(offsets)
    far_bucket = jnp.full(offsets.shape, exact_count, jnp.int32)
    for level_index in range(1, half_count - exact_count):
        threshold = int(
            math.ceil(
                exact_count
                * (reach_limit / exact_count) ** (level_index / (half_count - exact_count))
                - 1e-09
            )
        )
        far_bucket = far_bucket + (distance >= threshold).astype(jnp.int32)
    return sign_base + jnp.where(distance < exact_count, distance, far_bucket)


def rms_forward(values, gain):
    inverse = lax.rsqrt(jnp.mean(values * values, axis=-1, keepdims=True) + rms_eps)
    return (values * inverse * gain, inverse)


def rms_backward(values, inverse, gain, upstream):
    scaled = upstream * gain
    normed = values * inverse
    grad_values = inverse * (scaled - normed * jnp.mean(scaled * normed, axis=-1, keepdims=True))
    return (grad_values, jnp.sum(upstream * normed, axis=0))


def margin_loss(pooled, positives, negatives, neg_counts):
    unit = pooled * lax.rsqrt(jnp.sum(pooled * pooled, axis=-1, keepdims=True) + 1e-06)
    similar = sim_scale * jnp.dot(unit, unit.T, precision=HIGHEST)
    chosen = jnp.take_along_axis(similar, positives[:, None], axis=1)
    against = jnp.take_along_axis(similar, negatives, axis=1)
    live_slots = jnp.arange(negatives.shape[1])[None, :] < neg_counts[:, None]
    terms = jnp.where(live_slots, jax.nn.softplus(margin - chosen + against), 0.0)
    return jnp.mean(jnp.sum(terms, axis=1) / neg_counts.astype(jnp.float32))


def doc_scores(query_heads, key_heads, bias_full, live_keys):
    scores = (
        jnp.einsum("qhd,khd->hqk", query_heads, key_heads, preferred_element_type=jnp.float32)
        * 0.125
        + bias_full
    )
    return jnp.where(live_keys[None, None, :], scores, -1000000000.0)


def attend_forward(query_heads, key_heads, value_heads, bias_full, live_keys):
    scores = doc_scores(query_heads, key_heads, bias_full, live_keys)
    highest = jnp.max(scores, axis=-1, keepdims=True)
    weights = jnp.exp(scores - highest)
    totals = jnp.sum(weights, axis=-1, keepdims=True)
    probabilities = (weights / totals).astype(jnp.bfloat16)
    attended = jnp.einsum(
        "hqk,khd->qhd", probabilities, value_heads, preferred_element_type=jnp.float32
    )
    return (attended, highest + jnp.log(totals))


def attend_backward(
    query_heads, key_heads, value_heads, bias_full, live_keys, logsum, grad_attended
):
    probabilities = jnp.exp(doc_scores(query_heads, key_heads, bias_full, live_keys) - logsum)
    grad_value = jnp.einsum(
        "hqk,qhd->khd",
        probabilities.astype(jnp.bfloat16),
        grad_attended,
        preferred_element_type=jnp.float32,
    )
    grad_prob = jnp.einsum(
        "qhd,khd->hqk", grad_attended, value_heads, preferred_element_type=jnp.float32
    )
    grad_score = probabilities * (
        grad_prob - jnp.sum(probabilities * grad_prob, axis=-1, keepdims=True)
    )
    grad_low = grad_score.astype(jnp.bfloat16)
    grad_query = (
        jnp.einsum("hqk,khd->qhd", grad_low, key_heads, preferred_element_type=jnp.float32) * 0.125
    )
    grad_key = (
        jnp.einsum("hqk,qhd->khd", grad_low, query_heads, preferred_element_type=jnp.float32)
        * 0.125
    )
    return (grad_query, grad_key, grad_value, grad_low)


def adam_step(weight, first, second, grad, rate, shrink):
    first_new = beta_one * first + (1.0 - beta_one) * grad
    second_new = beta_two * second + (1.0 - beta_two) * grad * grad
    first_hat = first_new / (1.0 - beta_one**STEP)
    second_hat = second_new / (1.0 - beta_two**STEP)
    weight_new = weight - rate * (first_hat / (jnp.sqrt(second_hat) + adam_eps) + shrink * weight)
    return (weight_new, first_new, second_new)


MESH = pl.DeviceIdType.MESH
VMEM_LIMIT = 64 * 1024 * 1024 - 65536
ANY = pl.BlockSpec(memory_space=pl.ANY)
VM = pl.BlockSpec(memory_space=pltpu.VMEM)


def place(index, n_pair):
    return {"dp": index // n_pair, "pair": lax.rem(index, n_pair)}


def remote(src, dst, send, recv, target):
    return pltpu.make_async_remote_copy(
        src, dst, send, recv, device_id=target, device_id_type=MESH
    )


def greet(targets):
    sem = pltpu.get_barrier_semaphore()
    for target in targets:
        pl.semaphore_signal(sem, inc=1, device_id=target, device_id_type=MESH)
    pl.semaphore_wait(sem, len(targets))


def my_index(n_pair):
    return lax.axis_index("dp") * n_pair + lax.axis_index("pair")


def bit_order(n_dp, n_pair, color):
    dp_bits, pair_bits = (n_dp - 1).bit_length(), (n_pair - 1).bit_length()
    high = list(reversed(range(pair_bits + 1, pair_bits + dp_bits))) + [pair_bits]
    side = list(reversed(range(1, pair_bits)))
    return high + side if color == 0 else side + high


def offset(order, position):
    return sum(((position >> step) & 1) << bit for step, bit in enumerate(order))


def spread(n, n_pair, block, everyone, send, recv, own_sem):
    me = my_index(n_pair)
    sem = pltpu.get_barrier_semaphore()

    def hello(k, carry):
        pl.semaphore_signal(sem, inc=1, device_id=place(me ^ k, n_pair), device_id_type=MESH)
        return carry

    lax.fori_loop(1, n, hello, 0)
    own = pltpu.make_async_copy(block, everyone.at[me], own_sem)
    own.start()
    pl.semaphore_wait(sem, n - 1)

    def go(k, carry):
        remote(block, everyone.at[me], send.at[k], recv.at[k], place(me ^ k, n_pair)).start()
        return carry

    lax.fori_loop(1, n, go, 0)
    own.wait()

    def done(k, carry):
        remote(block, everyone.at[me ^ k], send.at[k], recv.at[k], place(me ^ k, n_pair)).wait()
        return carry

    lax.fori_loop(1, n, done, 0)


def total_kernel(n, n_pair, x_ref, o_ref, everyone, send, recv, own_sem):
    spread(n, n_pair, x_ref, everyone, send, recv, own_sem)
    def add(j, total):
        return total + everyone[j]
    o_ref[...] = lax.fori_loop(1, n, add, everyone[0])


def small_total(x, n_dp, n_pair, cid):
    n = n_dp * n_pair
    return pl.pallas_call(
        functools.partial(total_kernel, n, n_pair),
        out_shape=jax.ShapeDtypeStruct(x.shape, x.dtype),
        in_specs=[VM], out_specs=VM,
        scratch_shapes=[pltpu.VMEM((n,) + x.shape, x.dtype), pltpu.SemaphoreType.DMA((n,)), pltpu.SemaphoreType.DMA((n,)), pltpu.SemaphoreType.DMA],
        compiler_params=pltpu.CompilerParams(collective_id=cid, has_side_effects=True),
        name="small_total",
    )(x)


def loss_kernel(n, n_pair, docs, x_ref, pos_ref, neg_ref, count_ref, loss_ref, grad_ref, everyone, grads, send, recv, own_sem):
    spread(n, n_pair, x_ref, everyone, send, recv, own_sem)
    total = n * docs
    width = x_ref.shape[1]
    pooled = everyone[...].reshape(total, width)
    inverse = lax.rsqrt(jnp.sum(pooled * pooled, axis=1, keepdims=True) + 1e-06)
    unit = pooled * inverse
    similar = 20.0 * lax.dot_general(unit, unit, (((1,), (1,)), ((), ())), precision=HIGHEST, preferred_element_type=jnp.float32)
    columns = lax.broadcasted_iota(jnp.int32, (total, total), 1)
    is_pos = columns == pos_ref[...]
    chosen = jnp.sum(jnp.where(is_pos, similar, 0.0), axis=1, keepdims=True)
    counts = count_ref[...]
    weight = 1.0 / (counts.astype(jnp.float32) * total)
    loss_rows = jnp.zeros((total, 1), jnp.float32)
    grad_similar = jnp.zeros((total, total), jnp.float32)
    pulled = jnp.zeros((total, 1), jnp.float32)
    for slot in range(neg_ref.shape[1]):
        is_neg = columns == neg_ref[:, slot : slot + 1]
        against = jnp.sum(jnp.where(is_neg, similar, 0.0), axis=1, keepdims=True)
        value = 1.0 - chosen + against
        used = slot < counts
        soft = jnp.maximum(value, 0.0) + jnp.log1p(jnp.exp(-jnp.abs(value)))
        loss_rows = loss_rows + jnp.where(used, soft, 0.0)
        slope = jnp.where(used, weight / (1.0 + jnp.exp(-value)), 0.0)
        grad_similar = grad_similar + jnp.where(is_neg, slope, 0.0)
        pulled = pulled + slope
    grad_similar = grad_similar - jnp.where(is_pos, pulled, 0.0)
    loss_ref[...] = jnp.sum(loss_rows * weight, axis=0, keepdims=True)
    dims = (((1,), (0,)), ((), ()))
    grad_unit = lax.dot_general(grad_similar, unit, dims, precision=HIGHEST, preferred_element_type=jnp.float32)
    grad_unit = grad_unit + lax.dot_general(grad_similar, unit, (((0,), (0,)), ((), ())), precision=HIGHEST, preferred_element_type=jnp.float32)
    grad_unit = 20.0 * grad_unit
    inner = jnp.sum(grad_unit * unit, axis=1, keepdims=True)
    grads[...] = (inverse * (grad_unit - unit * inner)).reshape(n, docs, width)
    grad_ref[...] = grads[my_index(n_pair)]


def pooled_loss(pooled, positives, negatives, counts, n_dp, n_pair, cid):
    n = n_dp * n_pair
    docs, width = pooled.shape
    return pl.pallas_call(
        functools.partial(loss_kernel, n, n_pair, docs),
        out_shape=[jax.ShapeDtypeStruct((1, 1), jnp.float32), jax.ShapeDtypeStruct(pooled.shape, jnp.float32)],
        in_specs=[VM] * 4, out_specs=[VM] * 2,
        scratch_shapes=[pltpu.VMEM((n,) + pooled.shape, jnp.float32), pltpu.VMEM((n,) + pooled.shape, jnp.float32),
            pltpu.SemaphoreType.DMA((n,)), pltpu.SemaphoreType.DMA((n,)), pltpu.SemaphoreType.DMA],
        compiler_params=pltpu.CompilerParams(collective_id=cid, has_side_effects=True),
        name="pooled_loss",
    )(pooled, positives[:, None], negatives, counts[:, None])


NT = (((1,), (1,)), ((), ()))
TN = (((0,), (0,)), ((), ()))

def band(w_ref, h, table, seq):
    tiles = seq // 128
    for d in range(1 - tiles, tiles):
        low = seq + 128 * d - 128
        x = jnp.broadcast_to(w_ref[0, h : h + 1, low : low + 256], (128, 256))
        tile = pltpu.roll(x, 0, 1, stride=1, stride_axis=0)[:, 128:]
        for a in range(tiles):
            if 0 <= a + d < tiles:
                table[h, a * 128 : a * 128 + 128, (a + d) * 128 : (a + d) * 128 + 128] = tile

def forward_kernel(len_ref, q_ref, k_ref, v_ref, w_ref, o_ref, table):
    seq = q_ref.shape[0]
    doc = pl.program_id(1)
    @pl.when(doc == 0)
    def _():
        for h in range(2):
            band(w_ref, h, table, seq)
    length = len_ref[doc]
    lane = lax.broadcasted_iota(jnp.int32, (seq, 128), 1)
    column = lax.broadcasted_iota(jnp.int32, (1, seq), 1)
    q = q_ref[...] * jnp.bfloat16(0.125)
    k = k_ref[...]
    v = v_ref[...]
    got = []
    for h in range(2):
        mine = (lane < 64) == (h == 0)
        s = lax.dot_general(jnp.where(mine, q, 0), k, NT, preferred_element_type=jnp.float32)
        s = jnp.where(column < length, s + table[h], -1000000000.0)
        e = jnp.exp(s - jnp.max(s, axis=1, keepdims=True))
        p = (e * (1.0 / jnp.sum(e, axis=1, keepdims=True))).astype(jnp.bfloat16)
        got.append(jnp.dot(p, v, preferred_element_type=jnp.float32))
    o_ref[...] = jnp.where(lane < 64, got[0], got[1]).astype(o_ref.dtype)

def attention(lengths, qkv, w, seq):
    tokens = qkv.shape[0]
    pairs = w.shape[0]
    docs = tokens // seq
    spec = lambda base: pl.BlockSpec((seq, 128), lambda h, d, *_: (d, base + h))
    return pl.pallas_call(
        forward_kernel,
        grid_spec=pltpu.PrefetchScalarGridSpec(
            num_scalar_prefetch=1, grid=(pairs, docs),
            in_specs=[spec(0), spec(pairs), spec(2 * pairs), pl.BlockSpec((1, 2, 2 * seq), lambda h, d, *_: (h, 0, 0))],
            out_specs=spec(0),
            scratch_shapes=[pltpu.VMEM((2, seq, seq), jnp.float32)]),
        out_shape=jax.ShapeDtypeStruct((tokens, pairs * 128), jnp.bfloat16),
        compiler_params=pltpu.CompilerParams(dimension_semantics=("arbitrary", "arbitrary"), vmem_limit_bytes=50 * 1024 * 1024),
        name="attention",
    )(lengths, qkv, qkv, qkv, w)

def backward_kernel(len_ref, q_ref, k_ref, v_ref, g_ref, w_ref, o_ref, z_ref, table, total, box, sem):
    seq = q_ref.shape[0]
    tiles = seq // 128
    doc = pl.program_id(1)
    @pl.when(doc == 0)
    def _():
        for h in range(2):
            band(w_ref, h, table, seq)
        total[...] = jnp.zeros_like(total)
    length = len_ref[doc]
    lane = lax.broadcasted_iota(jnp.int32, (seq, 128), 1)
    row = lax.broadcasted_iota(jnp.int32, (seq, 1), 0)
    q = q_ref[...] * jnp.bfloat16(0.125)
    k = k_ref[...]
    v = v_ref[...]
    g = g_ref[...]
    parts = []
    for h in range(2):
        mine = (lane < 64) == (h == 0)
        s = lax.dot_general(k, jnp.where(mine, q, 0), NT, preferred_element_type=jnp.float32)
        s = jnp.where(row < length, s + table[h], -1000000000.0)
        e = jnp.exp(s - jnp.max(s, axis=0, keepdims=True))
        p = e * (1.0 / jnp.sum(e, axis=0, keepdims=True))
        dv = jnp.dot(p.astype(jnp.bfloat16), g, preferred_element_type=jnp.float32)
        dp = lax.dot_general(v, jnp.where(mine, g, 0), NT, preferred_element_type=jnp.float32)
        ds = (p * (dp - jnp.sum(p * dp, axis=0, keepdims=True))).astype(jnp.bfloat16)
        total[h] += ds.astype(jnp.float32)
        dk = jnp.dot(ds, q, preferred_element_type=jnp.float32)
        dq = lax.dot_general(ds, k, TN, preferred_element_type=jnp.float32) * 0.125
        parts.append((dq, dk, dv))
    pair, pairs, docs = pl.program_id(0), pl.num_programs(0), pl.num_programs(1)
    step = pair * docs + doc
    slot = lax.rem(step, 2)

    def out(i):
        rows = pl.ds(pl.multiple_of(doc * seq, seq), seq)
        columns = pl.ds(pl.multiple_of((i * pairs + pair) * 128, 128), 128)
        return pltpu.make_async_copy(box.at[slot, i], o_ref.at[rows, columns], sem.at[slot, i])

    for i in range(3):
        @pl.when(step >= 2)
        def _():
            out(i).wait()
        box[slot, i] = jnp.where(lane < 64, parts[0][i], parts[1][i]).astype(o_ref.dtype)
        out(i).start()

    @pl.when(step == pairs * docs - 1)
    def _():
        for i in range(3):
            out(i).wait()
            pltpu.make_async_copy(box.at[1 - slot, i], box.at[1 - slot, i], sem.at[1 - slot, i]).wait()
    @pl.when(doc == pl.num_programs(1) - 1)
    def _():
        r = lax.broadcasted_iota(jnp.int32, (128, 128), 0)
        c = lax.broadcasted_iota(jnp.int32, (128, 128), 1)
        flip = jnp.where(r + c == 127, 1.0, 0.0)
        z_ref[...] = jnp.zeros_like(z_ref)
        for h in range(2):
            def block(d):
                return sum(total[h, a * 128 : a * 128 + 128, (a - d) * 128 : (a - d) * 128 + 128] for a in range(tiles) if 0 <= a - d < tiles)
            for d in (-1, 0, 1):
                x = jnp.dot(flip, block(d), precision=HIGHEST, preferred_element_type=jnp.float32)
                x = jnp.concatenate([x, jnp.zeros_like(x)], axis=1)
                x = pltpu.roll(x, 0, 1, stride=1, stride_axis=0)
                z_ref[0, h, d + 1 : d + 2, :] = jnp.sum(x, axis=0, keepdims=True)
            z_ref[0, h, 3:4, 0:128] = jnp.sum(sum(block(-d) for d in range(2, tiles)), axis=0, keepdims=True)
            z_ref[0, h, 4:5, 0:128] = jnp.sum(sum(block(d) for d in range(2, tiles)), axis=0, keepdims=True)

def attention_back(lengths, qkv, g, w, seq):
    tokens = qkv.shape[0]
    pairs = w.shape[0]
    docs = tokens // seq
    spec = lambda base: pl.BlockSpec((seq, 128), lambda h, d, *_: (d, base + h))
    return pl.pallas_call(
        backward_kernel,
        grid_spec=pltpu.PrefetchScalarGridSpec(
            num_scalar_prefetch=1, grid=(pairs, docs),
            in_specs=[spec(0), spec(pairs), spec(2 * pairs), spec(0), pl.BlockSpec((1, 2, 2 * seq), lambda h, d, *_: (h, 0, 0))],
            out_specs=[pl.BlockSpec(memory_space=pl.ANY), pl.BlockSpec((1, 2, 8, 256), lambda h, d, *_: (h, 0, 0, 0))],
            scratch_shapes=[pltpu.VMEM((2, seq, seq), jnp.float32), pltpu.VMEM((2, seq, seq), jnp.float32), pltpu.VMEM((2, 3, seq, 128), jnp.bfloat16), pltpu.SemaphoreType.DMA((2, 3))]),
        out_shape=[jax.ShapeDtypeStruct((tokens, 3 * pairs * 128), jnp.bfloat16), jax.ShapeDtypeStruct((pairs, 2, 8, 256), jnp.float32)],
        compiler_params=pltpu.CompilerParams(dimension_semantics=("arbitrary", "arbitrary"), vmem_limit_bytes=50 * 1024 * 1024),
        name="attention_back",
    )(lengths, qkv, qkv, qkv, g, w)

def bias_rows(position_bias, seq, sign):
    nb, heads = position_bias.shape
    buckets = bucket_of(sign * (jnp.arange(2 * seq) - seq), nb, REACH)
    hits = (jnp.arange(nb)[:, None] == buckets[None, :]).astype(jnp.float32)
    return jnp.dot(position_bias.T, hits, precision=HIGHEST).reshape(heads // 2, 2, 2 * seq)

def bias_gradient(z, seq, nb):
    heads = z.shape[0] * 2
    j = jnp.arange(256)
    offs = [jnp.where(j < 255, 128 * d + 127 - j, 0) for d in (-1, 0, 1)] + [jnp.full((256,), 1 - seq), jnp.full((256,), seq - 1)]
    offs = jnp.concatenate(offs + [jnp.zeros((768,), jnp.int32)])
    hits = (bucket_of(offs, nb, REACH)[:, None] == jnp.arange(nb)[None, :]).astype(jnp.float32)
    return jnp.dot(z.reshape(heads, 2048), hits, precision=HIGHEST).T

def weight_pieces(widths):
    cut = widths[3] * 2 // 3 // 128 * 128
    return [
        (0, 0, widths[0], 1),
        (2, 0, widths[2], 0),
        (1, 0, widths[1], 0),
        (3, 0, cut, 0),
        (3, cut, widths[3], 1),
    ]


def gradient_pieces(widths):
    cut = widths[3] // 3 // 128 * 128
    return [
        (2, 0, widths[2], 0),
        (0, 0, widths[0], 1),
        (3, 0, cut, 0),
        (3, cut, widths[3], 1),
        (1, 0, widths[1], 1),
    ]


NN = (((1,), (0,)), ((), ()))


def stage(r):
    return (0, 1) if r == 0 else (1 << (r - 1), 1 << (r - 1))


class Gather:
    def __init__(self, n_dp, n_pair, pieces, outs, bufs, sems):
        self.n_pair, self.pieces, self.outs, self.bufs = n_pair, pieces, outs, bufs
        self.hop_sem, self.side_sem, self.core_sem, self.out_sem = sems
        self.me = my_index(n_pair)
        self.hops = (n_dp * n_pair - 1).bit_length() - 2
        self.orders = [bit_order(n_dp, n_pair, piece[3]) for piece in pieces]
        self.count = len(pieces)

    def send(self, a, lo, count, to, sem, which, bit):
        return remote(
            self.bufs[a].at[pl.ds(lo, count)],
            self.bufs[a].at[pl.ds(to, count)],
            sem.at[0, a, which],
            sem.at[1, a, which],
            place(self.me ^ (1 << bit), self.n_pair),
        )

    def hop(self, a, r):
        return self.send(a, 0, 1 << r, 1 << r, self.hop_sem, r, self.orders[a][r])

    def side(self, a, r):
        lo, count = stage(r)
        return self.send(a, lo, count, (1 << self.hops) + lo, self.side_sem, r, self.orders[a][self.hops])

    def core(self, a, r, sided):
        lo, count = stage(r)
        lo = lo + (sided << self.hops)
        return self.send(
            a, lo, count, (2 << self.hops) + lo, self.core_sem, 2 * r + sided, 0
        )

    def write_out(self, a, lo, count):
        which, low, high, _ = self.pieces[a]
        for p in range(lo, lo + count):
            block = self.me ^ offset(self.orders[a] + [0], p)
            pltpu.make_async_copy(
                self.bufs[a].at[p], self.outs[which].at[block, :, pl.ds(low, high - low)], self.out_sem.at[a]
            ).start()

    def held(self, r):
        lo, count = stage(r)
        for a in range(self.count):
            if r:
                self.hop(a, r - 1).wait_recv()
            if r < self.hops:
                self.hop(a, r).start()
            self.side(a, r).start()
            self.core(a, r, 0).start()
        for a in range(self.count):
            self.write_out(a, lo, count)

    def sided(self, r):
        lo, count = stage(r)
        for a in range(self.count):
            self.side(a, r).wait_recv()
            self.core(a, r, 1).start()
            self.write_out(a, (1 << self.hops) + lo, count)

    def cored(self, r):
        lo, count = stage(r)
        for sided in (0, 1):
            for a in range(self.count):
                self.core(a, r, sided).wait_recv()
                self.write_out(a, (2 << self.hops) + (sided << self.hops) + lo, count)

    def finish(self):
        for a in range(self.count):
            for r in range(self.hops):
                self.hop(a, r).wait_send()
            for r in range(self.hops + 1):
                self.side(a, r).wait_send()
                self.core(a, r, 0).wait_send()
                self.core(a, r, 1).wait_send()
            pltpu.make_async_copy(self.bufs[a], self.bufs[a], self.out_sem.at[a]).wait()


def triangle(size):
    rows = lax.broadcasted_iota(jnp.int32, (size, size), 0)
    columns = lax.broadcasted_iota(jnp.int32, (size, size), 1)
    return jnp.where(rows < columns, 1.0, 0.0).astype(jnp.bfloat16)


def digits(numbers):
    high = numbers // 64
    row = lax.broadcasted_iota(jnp.int32, (8, numbers.shape[1]), 0)
    both = jnp.where(row == 0, high, jnp.where(row == 1, numbers - 64 * high, 0))
    return both.astype(jnp.float32).astype(jnp.bfloat16)


def upright(pairs):
    row = lax.broadcasted_iota(jnp.int32, (8, 128), 0)
    value = jnp.where(row == 0, 64.0, jnp.where(row == 1, 1.0, 0.0)).astype(jnp.bfloat16)
    return lax.dot_general(pairs, value, TN, preferred_element_type=jnp.float32)


def hits_by_lane(numbers, width, base):
    lane = lax.broadcasted_iota(jnp.int32, (1, 128), 1).astype(jnp.float32) + base
    tiles = [
        jnp.where(numbers == lane + 128.0 * tile, 1.0, 0.0).astype(jnp.bfloat16)
        for tile in range(width // 128)
    ]
    return jnp.concatenate(tiles, axis=1)


def front_kernel(n_dp, n_pair, pieces, n_in, *refs):
    k = len(pieces)
    owner_ref, row_ref, table_ref = refs[:3]
    shards = refs[3 : 3 + n_in]
    emb_ref, key_ref, asked_ref = refs[3 + n_in : 6 + n_in]
    outs = refs[6 + n_in : 6 + 2 * n_in]
    rest = refs[6 + 2 * n_in :]
    bufs, rest = rest[:k], rest[k:]
    wide, table, ask_out, ask_in, rows_out, rows_in, total = rest[:7]
    table_sem, ask_sem, row_sem, *sems = rest[7:]
    dp, pair = lax.axis_index("dp"), lax.axis_index("pair")
    weights = Gather(n_dp, n_pair, pieces, outs, bufs, sems)
    tokens = owner_ref.shape[1]
    cap = ask_out.shape[2]
    table_rows = table_ref.shape[0]
    load = pltpu.make_async_copy(table_ref, wide, table_sem)
    load.start()
    peers = [{"dp": dp ^ j, "pair": pair} for j in range(1, n_dp)]
    sem = pltpu.get_barrier_semaphore()
    mates = [{"dp": dp, "pair": pair ^ j} for j in (1, 2)]
    for target in peers + mates:
        pl.semaphore_signal(sem, inc=1, device_id=target, device_id_type=MESH)
    for a, (which, low, high, _) in enumerate(pieces):
        bufs[a][0] = shards[which][:, low:high].astype(jnp.bfloat16)
    pl.semaphore_wait(sem, n_dp + 1)
    weights.held(0)

    owner = owner_ref[...]
    by_owner = lax.broadcasted_iota(jnp.int32, (n_dp, tokens), 0) == owner
    ranks = jnp.dot(
        jnp.where(by_owner, 1.0, 0.0).astype(jnp.bfloat16),
        triangle(tokens),
        preferred_element_type=jnp.float32,
    )
    rank = jnp.sum(jnp.where(by_owner, ranks, 0.0), axis=0, keepdims=True)
    key = owner * cap + rank.astype(jnp.int32)
    key_ref[...] = key
    wanted = digits(row_ref[...])

    def ask(j):
        return remote(ask_out.at[j], ask_in.at[j], ask_sem.at[0, j], ask_sem.at[1, j], peers[j - 1])

    def reply(j):
        return remote(
            rows_out.at[j], rows_in.at[j], row_sem.at[0, j], row_sem.at[1, j], peers[j - 1]
        )

    far = sorted(range(1, n_dp), reverse=True)
    for j in far + [0]:
        slot = lax.broadcasted_iota(jnp.int32, (cap, tokens), 0) + (dp ^ j) * cap
        chosen = jnp.where(slot == key, 1.0, 0.0).astype(jnp.bfloat16)
        ask_out[j] = lax.dot_general(wanted, chosen, NT, preferred_element_type=jnp.float32)
        if j:
            ask(j).start()
    weights.held(1)
    load.wait()

    def narrow(i, carry):
        part = pl.ds(pl.multiple_of(i * 16, 16), 16)
        table[part] = wide[part].astype(jnp.bfloat16)
        return carry

    lax.fori_loop(0, table_rows // 16, narrow, 0)
    if table.shape[0] > table_rows:
        table[table_rows:] = jnp.zeros((table.shape[0] - table_rows, table.shape[1]), jnp.bfloat16)

    def answer(j, target):
        asked = ask_out if j == 0 else ask_in
        hit = hits_by_lane(upright(asked[j].astype(jnp.bfloat16)), table.shape[0], 0.0)
        target[j] = jnp.dot(hit, table[...], preferred_element_type=jnp.float32).astype(jnp.bfloat16)
        asked_ref[j] = (64.0 * asked[j, 0:1] + asked[j, 1:2]).astype(jnp.int32)

    for turn, j in enumerate(far):
        ask(j).wait_recv()
        answer(j, rows_out)
        reply(j).start()
        if turn == n_dp // 4:
            weights.held(2)
            weights.sided(0)
    answer(0, rows_in)
    weights.sided(1)
    upright_key = upright(digits(key))

    def seat(j, first):
        place_hit = hits_by_lane(upright_key, cap, ((dp ^ j) * cap).astype(jnp.float32))
        got = jnp.dot(place_hit, rows_in[j], preferred_element_type=jnp.float32)
        total[...] = got if first else total[...] + got

    seat(0, True)
    weights.cored(0)
    for r in range(3, weights.hops + 1):
        weights.held(r)
        weights.sided(r - 1)
        weights.cored(r - 2)
    for j in far:
        reply(j).wait_recv()
        seat(j, False)
    emb_ref[...] = total[...].astype(jnp.bfloat16)
    weights.sided(weights.hops)
    for r in (weights.hops - 1, weights.hops):
        weights.cored(r)
    for j in far:
        ask(j).wait_send()
        reply(j).wait_send()
    weights.finish()


def front(owner, row, table, shards, pieces, cap, n_dp, n_pair, cid):
    n, k = n_dp * n_pair, len(pieces)
    hops = (n - 1).bit_length() - 2
    tokens = owner.shape[1]
    table_rows, width = table.shape
    padded = -(-table_rows // 256) * 256
    sem = pltpu.SemaphoreType.DMA
    return pl.pallas_call(
        functools.partial(front_kernel, n_dp, n_pair, pieces, len(shards)),
        out_shape=[
            jax.ShapeDtypeStruct((tokens, width), jnp.bfloat16),
            jax.ShapeDtypeStruct((1, tokens), jnp.int32),
            jax.ShapeDtypeStruct((n_dp, 1, cap), jnp.int32),
        ]
        + [jax.ShapeDtypeStruct((n,) + s.shape, jnp.bfloat16) for s in shards],
        in_specs=[VM, VM, ANY] + [VM] * len(shards),
        out_specs=[VM] * 3 + [ANY] * len(shards),
        scratch_shapes=[
            pltpu.VMEM((n, shards[p[0]].shape[0], p[2] - p[1]), jnp.bfloat16) for p in pieces
        ]
        + [
            pltpu.VMEM((table_rows, width), jnp.float32),
            pltpu.VMEM((padded, width), jnp.bfloat16),
            pltpu.VMEM((n_dp, 8, cap), jnp.float32),
            pltpu.VMEM((n_dp, 8, cap), jnp.float32),
            pltpu.VMEM((n_dp, cap, width), jnp.bfloat16),
            pltpu.VMEM((n_dp, cap, width), jnp.bfloat16),
            pltpu.VMEM((tokens, width), jnp.float32),
            sem,
            sem((2, n_dp)),
            sem((2, n_dp)),
            sem((2, k, hops)),
            sem((2, k, hops + 1)),
            sem((2, k, 2 * hops + 2)),
            sem((k,)),
        ],
        compiler_params=pltpu.CompilerParams(
            collective_id=cid, has_side_effects=True, vmem_limit_bytes=VMEM_LIMIT
        ),
        name="rows_and_weights",
    )(owner, row, table, *shards)


class Scatter:
    def __init__(self, n_dp, n_pair, pieces, ins, outs, boxes, sems):
        self.n_pair, self.pieces, self.ins, self.outs = n_pair, pieces, ins, outs
        k = len(pieces)
        self.acc, self.from_core = boxes[:k], boxes[k : 2 * k]
        self.from_side, self.from_hop = boxes[2 * k : 3 * k], boxes[3 * k :]
        self.load_sem, self.core_sem, self.side_sem, self.hop_sem = sems
        self.me = my_index(n_pair)
        self.hops = (n_dp * n_pair - 1).bit_length() - 2
        self.orders = [bit_order(n_dp, n_pair, piece[3]) for piece in pieces]
        self.count = k

    def source(self, a, block):
        which, low, high, _ = self.pieces[a]
        return self.ins[which].at[block, :, pl.ds(low, high - low)]

    def near(self, bit):
        return place(self.me ^ (1 << bit), self.n_pair)

    def load(self):
        for a in range(self.count):
            for p in range(2 << self.hops):
                pltpu.make_async_copy(
                    self.source(a, self.me ^ offset(self.orders[a], p)),
                    self.acc[a].at[p],
                    self.load_sem.at[a],
                ).start()

    def loaded(self):
        for a in range(self.count):
            pltpu.make_async_copy(self.acc[a], self.acc[a], self.load_sem.at[a]).wait()

    def core(self, a, r, sided, part=None):
        lo, count = stage(r)
        lo = lo + (sided << self.hops)
        to = self.from_core[a].at[pl.ds(lo, count)]
        source = to
        if part is not None:
            to = self.from_core[a].at[lo + part]
            source = self.source(a, self.me ^ (offset(self.orders[a], lo + part) + 1))
        slot = 2 * r + sided
        return remote(
            source, to, self.core_sem.at[0, a, slot], self.core_sem.at[1, a, slot], self.near(0)
        )

    def core_out(self, r):
        for sided in (1, 0):
            for a in range(self.count):
                for part in range(stage(r)[1]):
                    self.core(a, r, sided, part).start()

    def add(self, a, lo, count, box, at):
        acc = self.acc[a]

        def body(j, carry):
            acc[lo + j] = (
                acc[lo + j].astype(jnp.float32) + box[at + j].astype(jnp.float32)
            ).astype(jnp.bfloat16)
            return carry

        lax.fori_loop(0, count, body, 0)

    def side(self, a, r):
        lo, count = stage(r)
        return remote(
            self.acc[a].at[pl.ds((1 << self.hops) + lo, count)],
            self.from_side[a].at[pl.ds(lo, count)],
            self.side_sem.at[0, a, r],
            self.side_sem.at[1, a, r],
            self.near(self.orders[a][self.hops]),
        )

    def hop(self, a, r):
        return remote(
            self.acc[a].at[pl.ds(1 << r, 1 << r)],
            self.from_hop[a].at[pl.ds(self.hop_base(r), 1 << r)],
            self.hop_sem.at[0, a, r],
            self.hop_sem.at[1, a, r],
            self.near(self.orders[a][r]),
        )

    def hop_base(self, r):
        return (1 << self.hops) - (2 << r)

    def core_in(self, r):
        lo, count = stage(r)
        for sided in (1, 0):
            for a in range(self.count):
                self.core(a, r, sided).wait_recv()
                at = lo + (sided << self.hops)
                self.add(a, at, count, self.from_core[a], at)
                if sided:
                    self.side(a, r).start()

    def side_in(self, r):
        lo, count = stage(r)
        for a in range(self.count):
            self.side(a, r).wait_recv()
            self.add(a, lo, count, self.from_side[a], lo)
            if r == self.hops:
                self.hop(a, r - 1).start()

    def hop_in(self, r):
        for a in range(self.count):
            self.hop(a, r).wait_recv()
            base = self.hop_base(r)
            if r:
                mid = 1 << (r - 1)
                self.add(a, mid, mid, self.from_hop[a], base + mid)
                self.hop(a, r - 1).start()
                self.add(a, 0, mid, self.from_hop[a], base)
            else:
                which, low, high, _ = self.pieces[a]
                self.outs[which][:, low:high] = self.acc[a][0].astype(jnp.float32) + self.from_hop[
                    a
                ][base].astype(jnp.float32)

    def finish(self):
        for a in range(self.count):
            for r in range(self.hops):
                self.hop(a, r).wait_send()
            for r in range(self.hops + 1):
                self.side(a, r).wait_send()
                self.core(a, r, 0).wait_send()
                self.core(a, r, 1).wait_send()


def back_kernel(n_dp, n_pair, pieces, n_in, chunk, *refs):
    k = len(pieces)
    grad_ref, key_ref, ask_ref = refs[:3]
    ins = refs[3 : 3 + n_in]
    out_ref, square_ref = refs[3 + n_in : 5 + n_in]
    outs = refs[5 + n_in : 5 + 2 * n_in]
    rest = refs[5 + 2 * n_in :]
    boxes, rest = rest[: 4 * k], rest[4 * k :]
    hits, rows_out, rows_in, hot, part, stage_out, got_core, out_side, got_side, other = rest[:10]
    row_sem, core_sem, side_sem, last_sem, out_sem, *sems = rest[10:]
    dp, pair = lax.axis_index("dp"), lax.axis_index("pair")
    core = lax.rem(pair, 2)
    weights = Scatter(n_dp, n_pair, pieces, ins, outs, boxes, sems)
    groups, _, cap, width = rows_out.shape
    slots = ask_ref.shape[1]
    count = stage_out.shape[1]
    half = count * chunk
    tokens = key_ref.shape[1]
    peers = [{"dp": dp ^ j, "pair": pair} for j in range(1, n_dp)]
    partner, across = {"dp": dp, "pair": pair ^ 1}, {"dp": dp, "pair": pair ^ 2}
    weights.load()
    greet(peers + [partner, across])
    weights.core_out(weights.hops)

    def row(g, j):
        return remote(
            rows_out.at[g, j],
            rows_in.at[g, pl.ds(j * cap, cap)],
            row_sem.at[0, g, j],
            row_sem.at[1, g, j],
            peers[j - 1],
        )

    far = sorted(range(1, n_dp), reverse=True)

    def rows_send(g):
        columns = pl.ds(g * width, width)
        for j in far + [0]:
            if g == 0:
                slot = lax.broadcasted_iota(jnp.int32, (cap, tokens), 0) + (dp ^ j) * cap
                hits[j] = jnp.where(slot == key_ref[...], 1.0, 0.0).astype(jnp.bfloat16)
            got = jnp.dot(hits[j], grad_ref[:, columns], preferred_element_type=jnp.float32)
            if j:
                rows_out[g, j] = got.astype(jnp.bfloat16)
                row(g, j).start()
            else:
                rows_in[g, 0:cap] = got.astype(jnp.bfloat16)

    def summed(g, base):
        ids = lax.broadcasted_iota(jnp.int32, (chunk, slots), 0) + base
        hot[...] = jnp.where(ids == ask_ref[...], 1.0, 0.0).astype(jnp.bfloat16)
        return jnp.dot(hot[...], rows_in[g], preferred_element_type=jnp.float32)

    def to_core(g, i):
        return remote(
            stage_out.at[g, i], got_core.at[g, i], core_sem.at[0, g, i], core_sem.at[1, g, i], partner
        )

    def to_side(g, i):
        return remote(
            out_side.at[g, i], got_side.at[g, i], side_sem.at[0, g, i], side_sem.at[1, g, i], across
        )

    def to_other(g, i):
        return remote(
            out_side.at[g, i], other.at[g, i], last_sem.at[0, g, i], last_sem.at[1, g, i], partner
        )

    def write_out(box, g, i, which):
        rows = pl.ds(which * half + i * chunk, chunk)
        return pltpu.make_async_copy(
            box.at[g, i], out_ref.at[rows, pl.ds(g * width, width)], out_sem.at[g, i]
        )

    def local_sums(g):
        for j in far:
            row(g, j).wait_recv()
        for i in range(count):
            stage_out[g, i] = summed(g, (1 - core) * half + i * chunk).astype(jnp.bfloat16)
            to_core(g, i).start()
        for i in range(count):
            part[...] = summed(g, core * half + i * chunk)
            to_core(g, i).wait_recv()
            out_side[g, i] = (part[...] + got_core[g, i].astype(jnp.float32)).astype(jnp.bfloat16)
            to_side(g, i).start()

    def finish_sums(g, square):
        for i in range(count):
            to_side(g, i).wait()
            wide = out_side[g, i].astype(jnp.float32) + got_side[g, i].astype(jnp.float32)
            value = wide.astype(jnp.bfloat16)
            out_side[g, i] = value
            to_other(g, i).start()
            write_out(out_side, g, i, core).start()
            wide = value.astype(jnp.float32)
            square = square + jnp.sum(wide * wide, axis=0, keepdims=True)
        return square

    def hand_over(g):
        for i in range(count):
            to_other(g, i).wait_recv()
            write_out(out_side, g, i, core).wait()
            write_out(other, g, i, 1 - core).start()

    rows_send(0)
    for r in reversed(range(weights.hops)):
        weights.core_out(r)
    for g in range(1, groups):
        rows_send(g)
    weights.loaded()
    for r in reversed(range(weights.hops + 1)):
        weights.core_in(r)
    square = jnp.zeros((1, width), jnp.float32)
    turn = weights.hops
    for g in range(groups):
        local_sums(g)
        if g == 0:
            for r in reversed(range(weights.hops + 1)):
                weights.side_in(r)
        else:
            square = finish_sums(g - 1, square)
            if turn > 1:
                turn = turn - 1
                weights.hop_in(turn)
    square = finish_sums(groups - 1, square)
    while turn > 0:
        turn = turn - 1
        weights.hop_in(turn)
    square = jnp.sum(square, axis=1, keepdims=True)
    square_ref[...] = jnp.where(pair < 2, square, 0.0)
    for g in range(groups):
        hand_over(g)
    for g in range(groups):
        for j in far:
            row(g, j).wait_send()
        for i in range(count):
            to_core(g, i).wait_send()
            to_other(g, i).wait_send()
            write_out(other, g, i, 1 - core).wait()
    weights.finish()


def back(grad, key, asked, grads, pieces, table_rows, groups, cid):
    n_dp, n_pair = lax.axis_size("dp"), lax.axis_size("pair")
    n, k = n_dp * n_pair, len(pieces)
    hops = (n - 1).bit_length() - 2
    chunk = 512
    rows = -(-table_rows // (2 * chunk)) * 2 * chunk
    count = rows // 2 // chunk
    tokens, full = grad.shape
    width = full // groups
    slots = asked.shape[1]
    cap = slots // n_dp
    sem = pltpu.SemaphoreType.DMA
    box = pltpu.VMEM((groups, count, chunk, width), jnp.bfloat16)

    def blocks(lead):
        return [
            pltpu.VMEM((lead, grads[p[0]].shape[1], p[2] - p[1]), jnp.bfloat16) for p in pieces
        ]

    return pl.pallas_call(
        functools.partial(back_kernel, n_dp, n_pair, pieces, len(grads), chunk),
        out_shape=[
            jax.ShapeDtypeStruct((rows, full), jnp.bfloat16),
            jax.ShapeDtypeStruct((1, 1), jnp.float32),
        ]
        + [jax.ShapeDtypeStruct(g.shape[1:], jnp.float32) for g in grads],
        in_specs=[VM] * 3 + [ANY] * len(grads),
        out_specs=[ANY, VM] + [VM] * len(grads),
        scratch_shapes=blocks(n // 2)
        + blocks(n // 2)
        + blocks(n // 4)
        + blocks(n // 4 - 1)
        + [
            pltpu.VMEM((n_dp, cap, tokens), jnp.bfloat16),
            pltpu.VMEM((groups, n_dp, cap, width), jnp.bfloat16),
            pltpu.VMEM((groups, slots, width), jnp.bfloat16),
            pltpu.VMEM((chunk, slots), jnp.bfloat16),
            pltpu.VMEM((chunk, width), jnp.float32),
            box,
            box,
            box,
            box,
            box,
            sem((2, groups, n_dp)),
            sem((2, groups, count)),
            sem((2, groups, count)),
            sem((2, groups, count)),
            sem((groups, count)),
            sem((k,)),
            sem((2, k, 2 * hops + 2)),
            sem((2, k, hops + 1)),
            sem((2, k, hops)),
        ],
        compiler_params=pltpu.CompilerParams(
            collective_id=cid, has_side_effects=True, vmem_limit_bytes=VMEM_LIMIT
        ),
        name="table_and_weights",
    )(grad, key, asked, *grads)


def local_plain(
    token_owner,
    token_row,
    lengths,
    positives,
    negatives,
    neg_counts,
    embed_table,
    embed_first,
    embed_second,
    qkv_weight,
    qkv_first,
    qkv_second,
    out_weight,
    out_first,
    out_second,
    in_weight,
    in_first,
    in_second,
    down_weight,
    down_first,
    down_second,
    norm_gains,
    gains_first,
    gains_second,
    position_bias,
    bias_first,
    bias_second,
):
    doc_count = lengths.shape[0]
    seq_len = token_row.shape[1]
    model_width = embed_table.shape[1]
    head_count = position_bias.shape[1]
    bucket_count = position_bias.shape[0]
    tok_total = doc_count * seq_len
    owners = lax.axis_size("dp")
    capacity = max(2, 2 * tok_total // owners)
    low_mats = (
        qkv_weight.astype(jnp.bfloat16),
        out_weight.astype(jnp.bfloat16),
        in_weight.astype(jnp.bfloat16),
        down_weight.astype(jnp.bfloat16),
    )
    qkv_full, out_full, in_full, down_full = (
        lax.all_gather(low_mats[0], ("dp", "pair"), axis=0, tiled=True),
        lax.all_gather(low_mats[1], ("dp", "pair"), axis=0, tiled=True),
        lax.all_gather(low_mats[2], ("dp", "pair"), axis=0, tiled=True),
        lax.all_gather(low_mats[3], ("dp", "pair"), axis=0, tiled=True),
    )
    tok_owner = token_owner.reshape(-1)
    tok_row = token_row.reshape(-1)
    owner_hits = (tok_owner[:, None] == jnp.arange(owners, dtype=jnp.int32)[None, :]).astype(
        jnp.int32
    )
    slot_rank = jnp.sum((jnp.cumsum(owner_hits, axis=0) - 1) * owner_hits, axis=1)
    requests = jnp.zeros((owners, capacity), jnp.int32).at[tok_owner, slot_rank].set(tok_row)
    asked_rows = lax.all_to_all(requests, "dp", split_axis=0, concat_axis=0, tiled=True)
    looked = jnp.take(embed_table, asked_rows.reshape(-1), axis=0).astype(jnp.bfloat16)
    answer = lax.all_to_all(
        looked.reshape(asked_rows.shape + (model_width,)),
        "dp",
        split_axis=0,
        concat_axis=0,
        tiled=True,
    )
    replies, asked_rows = (answer, asked_rows)
    embedded = replies[tok_owner, slot_rank].astype(jnp.float32)
    positions = jnp.arange(seq_len)
    live = positions[None, :] < lengths[:, None]
    pair_buckets = bucket_of(
        (positions[None, :] - positions[:, None]).reshape(-1), bucket_count, REACH
    )
    pair_hits = (jnp.arange(bucket_count)[:, None] == pair_buckets[None, :]).astype(jnp.float32)
    bias_full = jnp.dot(position_bias.T, pair_hits, precision=HIGHEST).reshape(
        head_count, seq_len, seq_len
    )
    bucket_map = pair_hits.astype(jnp.bfloat16)

    def split_doc(source, doc_index):
        doc_rows = source[doc_index * seq_len : (doc_index + 1) * seq_len]
        return tuple(
            (
                doc_rows[:, member * model_width : (member + 1) * model_width].reshape(
                    seq_len, head_count, -1
                )
                for member in range(3)
            )
        )

    normed_one, inverse_one = rms_forward(embedded, norm_gains[0])
    normed_one = normed_one.astype(jnp.bfloat16)
    qkv_rows = jnp.dot(normed_one, qkv_full, preferred_element_type=jnp.float32).astype(
        jnp.bfloat16
    )
    attended_parts = []
    logsum_parts = []
    for doc_index in range(doc_count):
        query_heads, key_heads, value_heads = split_doc(qkv_rows, doc_index)
        doc_out, logsum = attend_forward(
            query_heads, key_heads, value_heads, bias_full, live[doc_index]
        )
        attended_parts.append(doc_out.reshape(seq_len, model_width))
        logsum_parts.append(logsum)
    attended = jnp.concatenate(attended_parts, axis=0).astype(jnp.bfloat16)
    residual = embedded + jnp.dot(attended, out_full, preferred_element_type=jnp.float32)
    normed_two, inverse_two = rms_forward(residual, norm_gains[1])
    normed_two = normed_two.astype(jnp.bfloat16)
    hidden = jax.nn.relu(jnp.dot(normed_two, in_full, preferred_element_type=jnp.float32)).astype(
        jnp.bfloat16
    )
    output_rows = residual + jnp.dot(hidden, down_full, preferred_element_type=jnp.float32)
    normed_three, inverse_three = rms_forward(output_rows, norm_gains[2])
    live_rows = live.reshape(-1, 1)
    length_float = lengths.astype(jnp.float32)
    pooled_local = (
        jnp.sum(
            jnp.where(live_rows, normed_three, 0.0).reshape(doc_count, seq_len, model_width), axis=1
        )
        / length_float[:, None]
    )
    pooled_all = lax.all_gather(pooled_local, ("dp", "pair"), axis=0, tiled=True)
    loss_value, loss_pullback = jax.vjp(
        lambda pooled_in: margin_loss(pooled_in, positives, negatives, neg_counts), pooled_all
    )
    grad_pooled_all = loss_pullback(jnp.ones((), jnp.float32))[0]
    grad_pooled = lax.dynamic_slice_in_dim(
        grad_pooled_all, lax.axis_index(("dp", "pair")) * doc_count, doc_count, 0
    )
    grad_three = jnp.where(
        live_rows, jnp.repeat(grad_pooled / length_float[:, None], seq_len, axis=0), 0.0
    )
    qkv_back, out_back, in_back, down_back = (qkv_full, out_full, in_full, down_full)
    grad_output, gain_three = rms_backward(output_rows, inverse_three, norm_gains[2], grad_three)
    grad_branch = grad_output.astype(jnp.bfloat16)
    grad_down = lax.dot_general(
        hidden, grad_branch, CONTRACT_ROWS, preferred_element_type=jnp.float32
    )
    grad_hidden = lax.dot_general(
        grad_branch, down_back, CONTRACT_COLS, preferred_element_type=jnp.float32
    )
    grad_pre = jnp.where(hidden > 0, grad_hidden, 0.0).astype(jnp.bfloat16)
    grad_in = lax.dot_general(
        normed_two, grad_pre, CONTRACT_ROWS, preferred_element_type=jnp.float32
    )
    grad_normed_two = lax.dot_general(
        grad_pre, in_back, CONTRACT_COLS, preferred_element_type=jnp.float32
    )
    grad_res_part, gain_two = rms_backward(residual, inverse_two, norm_gains[1], grad_normed_two)
    grad_residual = grad_output + grad_res_part
    grad_attn_branch = grad_residual.astype(jnp.bfloat16)
    grad_out = lax.dot_general(
        attended, grad_attn_branch, CONTRACT_ROWS, preferred_element_type=jnp.float32
    )
    grad_attended = lax.dot_general(
        grad_attn_branch, out_back, CONTRACT_COLS, preferred_element_type=jnp.float32
    ).astype(jnp.bfloat16)
    grad_qkv_parts = []
    bias_grad_heads = jnp.zeros((head_count, bucket_count), jnp.float32)
    for doc_index in range(doc_count):
        query_heads, key_heads, value_heads = split_doc(qkv_rows, doc_index)
        grad_doc = grad_attended[doc_index * seq_len : (doc_index + 1) * seq_len].reshape(
            seq_len, head_count, -1
        )
        grad_query, grad_key, grad_value, grad_low = attend_backward(
            query_heads,
            key_heads,
            value_heads,
            bias_full,
            live[doc_index],
            logsum_parts[doc_index],
            grad_doc,
        )
        grad_qkv_parts.append(
            jnp.concatenate(
                [
                    grad_query.reshape(seq_len, model_width),
                    grad_key.reshape(seq_len, model_width),
                    grad_value.reshape(seq_len, model_width),
                ],
                axis=1,
            )
        )
        bias_grad_heads = bias_grad_heads + lax.dot_general(
            grad_low.reshape(head_count, -1),
            bucket_map,
            CONTRACT_COLS,
            preferred_element_type=jnp.float32,
        )
    bias_grad_local = bias_grad_heads.T
    grad_qkv_rows = jnp.concatenate(grad_qkv_parts, axis=0).astype(jnp.bfloat16)
    grad_qkv = lax.dot_general(
        normed_one, grad_qkv_rows, CONTRACT_ROWS, preferred_element_type=jnp.float32
    )
    grad_normed_one = lax.dot_general(
        grad_qkv_rows, qkv_back, CONTRACT_COLS, preferred_element_type=jnp.float32
    )
    grad_emb_part, gain_one = rms_backward(embedded, inverse_one, norm_gains[0], grad_normed_one)
    grad_embedded = grad_residual + grad_emb_part
    sendback = (
        jnp.zeros((owners, capacity, model_width), jnp.float32)
        .at[tok_owner, slot_rank]
        .set(grad_embedded)
    )
    arrived = lax.all_to_all(sendback, "dp", split_axis=0, concat_axis=0, tiled=True)
    table_grad = jax.ops.segment_sum(
        arrived.reshape(-1, model_width), asked_rows.reshape(-1), num_segments=embed_table.shape[0]
    )
    table_grad = lax.psum(table_grad, "pair")
    weight_grads = (
        lax.psum_scatter(grad_qkv, ("dp", "pair"), scatter_dimension=0, tiled=True),
        lax.psum_scatter(grad_out, ("dp", "pair"), scatter_dimension=0, tiled=True),
        lax.psum_scatter(grad_in, ("dp", "pair"), scatter_dimension=0, tiled=True),
        lax.psum_scatter(grad_down, ("dp", "pair"), scatter_dimension=0, tiled=True),
    )
    pair_first = (lax.axis_index("pair") == 0).astype(jnp.float32)
    square_part = jnp.sum(
        jnp.stack([jnp.sum(grad_piece * grad_piece) for grad_piece in weight_grads])
    ) + pair_first * jnp.sum(table_grad * table_grad)
    gain_grad, bias_grad, square_sum = lax.psum(
        (jnp.stack([gain_one, gain_two, gain_three]), bias_grad_local, square_part), ("dp", "pair")
    )
    clip_norm = jnp.sqrt(
        square_sum + jnp.sum(gain_grad * gain_grad) + jnp.sum(bias_grad * bias_grad)
    )
    factor = jnp.minimum(1.0, clip_limit / clip_norm)
    table_out = adam_step(embed_table, embed_first, embed_second, table_grad * factor, 1.0, 0.01)
    qkv_out = adam_step(qkv_weight, qkv_first, qkv_second, weight_grads[0] * factor, 0.05, 0.01)
    out_out = adam_step(out_weight, out_first, out_second, weight_grads[1] * factor, 0.05, 0.01)
    in_out = adam_step(in_weight, in_first, in_second, weight_grads[2] * factor, 0.05, 0.01)
    down_out = adam_step(down_weight, down_first, down_second, weight_grads[3] * factor, 0.05, 0.01)
    gains_out = adam_step(norm_gains, gains_first, gains_second, gain_grad * factor, 1.0, 0.0)
    bias_out = adam_step(position_bias, bias_first, bias_second, bias_grad * factor, 0.3, 0.0)
    return (
        loss_value,
        clip_norm,
        table_out[0],
        table_out[1],
        table_out[2],
        qkv_out[0],
        qkv_out[1],
        qkv_out[2],
        out_out[0],
        out_out[1],
        out_out[2],
        in_out[0],
        in_out[1],
        in_out[2],
        down_out[0],
        down_out[1],
        down_out[2],
        gains_out[0],
        gains_out[1],
        gains_out[2],
        bias_out[0],
        bias_out[1],
        bias_out[2],
    )


def local_fast(
    token_owner,
    token_row,
    lengths,
    positives,
    negatives,
    neg_counts,
    embed_table,
    embed_first,
    embed_second,
    qkv_weight,
    qkv_first,
    qkv_second,
    out_weight,
    out_first,
    out_second,
    in_weight,
    in_first,
    in_second,
    down_weight,
    down_first,
    down_second,
    norm_gains,
    gains_first,
    gains_second,
    position_bias,
    bias_first,
    bias_second,
):
    doc_count = lengths.shape[0]
    seq_len = token_row.shape[1]
    model_width = embed_table.shape[1]
    head_count = position_bias.shape[1]
    bucket_count = position_bias.shape[0]
    tok_total = doc_count * seq_len
    owners = lax.axis_size("dp")
    capacity = max(2, 2 * tok_total // owners)
    holders = lax.axis_size("pair")
    shards = (qkv_weight, out_weight, in_weight, down_weight)
    embedded_low, slot_keys, asked_rows, *full = front(
        token_owner.reshape(1, -1),
        token_row.reshape(1, -1),
        embed_table,
        shards,
        weight_pieces([shard.shape[1] for shard in shards]),
        capacity,
        owners,
        holders,
        1,
    )
    qkv_full, out_full, in_full, down_full = (
        matrix.reshape(-1, matrix.shape[2]) for matrix in full
    )
    embedded = embedded_low.astype(jnp.float32)
    positions = jnp.arange(seq_len)
    live = positions[None, :] < lengths[:, None]
    normed_one, inverse_one = rms_forward(embedded, norm_gains[0])
    normed_one = normed_one.astype(jnp.bfloat16)
    qkv_rows = jnp.dot(normed_one, qkv_full, preferred_element_type=jnp.float32).astype(
        jnp.bfloat16
    )
    attended = attention(lengths, qkv_rows, bias_rows(position_bias, seq_len, 1), seq_len)
    residual = embedded + jnp.dot(attended, out_full, preferred_element_type=jnp.float32)
    normed_two, inverse_two = rms_forward(residual, norm_gains[1])
    normed_two = normed_two.astype(jnp.bfloat16)
    hidden = jax.nn.relu(jnp.dot(normed_two, in_full, preferred_element_type=jnp.float32)).astype(
        jnp.bfloat16
    )
    output_rows = residual + jnp.dot(hidden, down_full, preferred_element_type=jnp.float32)
    normed_three, inverse_three = rms_forward(output_rows, norm_gains[2])
    live_rows = live.reshape(-1, 1)
    length_float = lengths.astype(jnp.float32)
    pooled_local = (
        jnp.sum(
            jnp.where(live_rows, normed_three, 0.0).reshape(doc_count, seq_len, model_width), axis=1
        )
        / length_float[:, None]
    )
    loss_cell, grad_pooled = pooled_loss(
        pooled_local, positives, negatives, neg_counts, owners, holders, 3
    )
    loss_value = loss_cell[0, 0]
    grad_three = jnp.where(
        live_rows, jnp.repeat(grad_pooled / length_float[:, None], seq_len, axis=0), 0.0
    )
    qkv_back, out_back, in_back, down_back = (qkv_full, out_full, in_full, down_full)
    grad_output, gain_three = rms_backward(output_rows, inverse_three, norm_gains[2], grad_three)
    grad_branch = grad_output.astype(jnp.bfloat16)
    grad_down = lax.dot_general(
        hidden, grad_branch, CONTRACT_ROWS, preferred_element_type=jnp.float32
    )
    grad_hidden = lax.dot_general(
        grad_branch, down_back, CONTRACT_COLS, preferred_element_type=jnp.float32
    )
    grad_pre = jnp.where(hidden > 0, grad_hidden, 0.0).astype(jnp.bfloat16)
    grad_in = lax.dot_general(
        normed_two, grad_pre, CONTRACT_ROWS, preferred_element_type=jnp.float32
    )
    grad_normed_two = lax.dot_general(
        grad_pre, in_back, CONTRACT_COLS, preferred_element_type=jnp.float32
    )
    grad_res_part, gain_two = rms_backward(residual, inverse_two, norm_gains[1], grad_normed_two)
    grad_residual = grad_output + grad_res_part
    grad_attn_branch = grad_residual.astype(jnp.bfloat16)
    grad_out = lax.dot_general(
        attended, grad_attn_branch, CONTRACT_ROWS, preferred_element_type=jnp.float32
    )
    grad_attended = lax.dot_general(
        grad_attn_branch, out_back, CONTRACT_COLS, preferred_element_type=jnp.float32
    ).astype(jnp.bfloat16)
    grad_qkv_rows, diagonals = attention_back(
        lengths, qkv_rows, grad_attended, bias_rows(position_bias, seq_len, -1), seq_len
    )
    bias_grad_local = bias_gradient(diagonals, seq_len, bucket_count)
    grad_qkv = lax.dot_general(
        normed_one, grad_qkv_rows, CONTRACT_ROWS, preferred_element_type=jnp.float32
    )
    grad_normed_one = lax.dot_general(
        grad_qkv_rows, qkv_back, CONTRACT_COLS, preferred_element_type=jnp.float32
    )
    grad_emb_part, gain_one = rms_backward(embedded, inverse_one, norm_gains[0], grad_normed_one)
    grad_embedded = grad_residual + grad_emb_part
    table_rows = embed_table.shape[0]
    parts = owners * holders
    table_grad, table_square, *weight_grads = back(
        grad_embedded.astype(jnp.bfloat16),
        slot_keys,
        asked_rows.reshape(1, -1),
        [
            grad.astype(jnp.bfloat16).reshape(parts, -1, grad.shape[1])
            for grad in (grad_qkv, grad_out, grad_in, grad_down)
        ],
        gradient_pieces([grad.shape[1] for grad in (grad_qkv, grad_out, grad_in, grad_down)]),
        table_rows,
        3 if model_width % 384 == 0 else 1,
        2,
    )
    table_grad = table_grad[:table_rows].astype(jnp.float32)
    square_part = table_square[0, 0] + jnp.sum(
        jnp.stack([jnp.sum(grad_piece * grad_piece) for grad_piece in weight_grads])
    )
    small = jnp.concatenate(
        [
            jnp.stack([gain_one, gain_two, gain_three]).reshape(-1),
            bias_grad_local.reshape(-1),
            square_part.reshape(1),
        ]
    )
    small_size = small.shape[0]
    small_rows = -(-small_size // 1024) * 8
    small = jnp.pad(small, (0, small_rows * 128 - small_size)).reshape(small_rows, 128)
    small = small_total(small, owners, holders, 7).reshape(-1)
    gain_grad = small[: 3 * model_width].reshape(3, model_width)
    bias_grad = small[3 * model_width : small_size - 1].reshape(bucket_count, head_count)
    square_sum = small[small_size - 1]
    clip_norm = jnp.sqrt(
        square_sum + jnp.sum(gain_grad * gain_grad) + jnp.sum(bias_grad * bias_grad)
    )
    factor = jnp.minimum(1.0, clip_limit / clip_norm)
    table_out = adam_step(embed_table, embed_first, embed_second, table_grad * factor, 1.0, 0.01)
    qkv_out = adam_step(qkv_weight, qkv_first, qkv_second, weight_grads[0] * factor, 0.05, 0.01)
    out_out = adam_step(out_weight, out_first, out_second, weight_grads[1] * factor, 0.05, 0.01)
    in_out = adam_step(in_weight, in_first, in_second, weight_grads[2] * factor, 0.05, 0.01)
    down_out = adam_step(down_weight, down_first, down_second, weight_grads[3] * factor, 0.05, 0.01)
    gains_out = adam_step(norm_gains, gains_first, gains_second, gain_grad * factor, 1.0, 0.0)
    bias_out = adam_step(position_bias, bias_first, bias_second, bias_grad * factor, 0.3, 0.0)
    return (
        loss_value,
        clip_norm,
        table_out[0],
        table_out[1],
        table_out[2],
        qkv_out[0],
        qkv_out[1],
        qkv_out[2],
        out_out[0],
        out_out[1],
        out_out[2],
        in_out[0],
        in_out[1],
        in_out[2],
        down_out[0],
        down_out[1],
        down_out[2],
        gains_out[0],
        gains_out[1],
        gains_out[2],
        bias_out[0],
        bias_out[1],
        bias_out[2],
    )


def local(*arrays):
    n_dp, n_pair = lax.axis_size("dp"), lax.axis_size("pair")
    lengths, qkv_weight, down_weight = arrays[2], arrays[9], arrays[18]
    fits = (
        n_pair == 4
        and n_dp & (n_dp - 1) == 0
        and qkv_weight.shape[0] % 8 == 0
        and down_weight.shape[0] % 8 == 0
        and lengths.shape[0] == 2
        and 2 * arrays[1].size // n_dp % 128 == 0
    )
    return (local_fast if fits else local_plain)(*arrays)


def solution(mesh):
    return jax.shard_map(
        local,
        mesh=mesh,
        in_specs=(
            P(("dp", "pair"), None, None),
            P(("dp", "pair"), None),
            P(("dp", "pair")),
            P(),
            P(),
            P(),
            P("dp", None),
            P("dp", None),
            P("dp", None),
            P(("dp", "pair"), None),
            P(("dp", "pair"), None),
            P(("dp", "pair"), None),
            P(("dp", "pair"), None),
            P(("dp", "pair"), None),
            P(("dp", "pair"), None),
            P(("dp", "pair"), None),
            P(("dp", "pair"), None),
            P(("dp", "pair"), None),
            P(("dp", "pair"), None),
            P(("dp", "pair"), None),
            P(("dp", "pair"), None),
            P(),
            P(),
            P(),
            P(),
            P(),
            P(),
        ),
        out_specs=(
            P(),
            P(),
            P("dp", None),
            P("dp", None),
            P("dp", None),
            P(("dp", "pair"), None),
            P(("dp", "pair"), None),
            P(("dp", "pair"), None),
            P(("dp", "pair"), None),
            P(("dp", "pair"), None),
            P(("dp", "pair"), None),
            P(("dp", "pair"), None),
            P(("dp", "pair"), None),
            P(("dp", "pair"), None),
            P(("dp", "pair"), None),
            P(("dp", "pair"), None),
            P(("dp", "pair"), None),
            P(),
            P(),
            P(),
            P(),
            P(),
            P(),
        ),
        check_vma=False,
    )
```

```python
import functools
import math

import jax
import jax.numpy as jnp
import numpy as np
from jax import lax
from jax.experimental import pallas as pl
from jax.experimental.pallas import tpu as pltpu
from jax.sharding import PartitionSpec as P

REACH = 128
STEP = 5


rms_eps = 1e-06
clip_limit = 0.05
margin = 1.0
sim_scale = 20.0
beta_one = 0.9
beta_two = 0.999
adam_eps = 1e-08
HIGHEST = lax.Precision.HIGHEST
CONTRACT_ROWS = (((0,), (0,)), ((), ()))
CONTRACT_COLS = (((1,), (1,)), ((), ()))


def bucket_of(offsets, bucket_count, reach_limit):
    half_count = bucket_count // 2
    exact_count = half_count // 2
    sign_base = jnp.where(offsets > 0, half_count, 0).astype(jnp.int32)
    distance = jnp.abs(offsets)
    far_bucket = jnp.full(offsets.shape, exact_count, jnp.int32)
    for level_index in range(1, half_count - exact_count):
        threshold = int(
            math.ceil(
                exact_count
                * (reach_limit / exact_count) ** (level_index / (half_count - exact_count))
                - 1e-09
            )
        )
        far_bucket = far_bucket + (distance >= threshold).astype(jnp.int32)
    return sign_base + jnp.where(distance < exact_count, distance, far_bucket)


def rms_forward(values, gain):
    inverse = lax.rsqrt(jnp.mean(values * values, axis=-1, keepdims=True) + rms_eps)
    return (values * inverse * gain, inverse)


def rms_backward(values, inverse, gain, upstream):
    scaled = upstream * gain
    normed = values * inverse
    grad_values = inverse * (scaled - normed * jnp.mean(scaled * normed, axis=-1, keepdims=True))
    return (grad_values, jnp.sum(upstream * normed, axis=0))


def margin_loss(pooled, positives, negatives, neg_counts):
    unit = pooled * lax.rsqrt(jnp.sum(pooled * pooled, axis=-1, keepdims=True) + 1e-06)
    similar = sim_scale * jnp.dot(unit, unit.T, precision=HIGHEST)
    chosen = jnp.take_along_axis(similar, positives[:, None], axis=1)
    against = jnp.take_along_axis(similar, negatives, axis=1)
    live_slots = jnp.arange(negatives.shape[1])[None, :] < neg_counts[:, None]
    terms = jnp.where(live_slots, jax.nn.softplus(margin - chosen + against), 0.0)
    return jnp.mean(jnp.sum(terms, axis=1) / neg_counts.astype(jnp.float32))


def doc_scores(query_heads, key_heads, bias_full, live_keys):
    scores = (
        jnp.einsum("qhd,khd->hqk", query_heads, key_heads, preferred_element_type=jnp.float32)
        * 0.125
        + bias_full
    )
    return jnp.where(live_keys[None, None, :], scores, -1000000000.0)


def attend_forward(query_heads, key_heads, value_heads, bias_full, live_keys):
    scores = doc_scores(query_heads, key_heads, bias_full, live_keys)
    highest = jnp.max(scores, axis=-1, keepdims=True)
    weights = jnp.exp(scores - highest)
    totals = jnp.sum(weights, axis=-1, keepdims=True)
    probabilities = (weights / totals).astype(jnp.bfloat16)
    attended = jnp.einsum(
        "hqk,khd->qhd", probabilities, value_heads, preferred_element_type=jnp.float32
    )
    return (attended, highest + jnp.log(totals))


def attend_backward(
    query_heads, key_heads, value_heads, bias_full, live_keys, logsum, grad_attended
):
    probabilities = jnp.exp(doc_scores(query_heads, key_heads, bias_full, live_keys) - logsum)
    grad_value = jnp.einsum(
        "hqk,qhd->khd",
        probabilities.astype(jnp.bfloat16),
        grad_attended,
        preferred_element_type=jnp.float32,
    )
    grad_prob = jnp.einsum(
        "qhd,khd->hqk", grad_attended, value_heads, preferred_element_type=jnp.float32
    )
    grad_score = probabilities * (
        grad_prob - jnp.sum(probabilities * grad_prob, axis=-1, keepdims=True)
    )
    grad_low = grad_score.astype(jnp.bfloat16)
    grad_query = (
        jnp.einsum("hqk,khd->qhd", grad_low, key_heads, preferred_element_type=jnp.float32) * 0.125
    )
    grad_key = (
        jnp.einsum("hqk,qhd->khd", grad_low, query_heads, preferred_element_type=jnp.float32)
        * 0.125
    )
    return (grad_query, grad_key, grad_value, grad_low)


def adam_step(weight, first, second, grad, rate, shrink):
    first_new = beta_one * first + (1.0 - beta_one) * grad
    second_new = beta_two * second + (1.0 - beta_two) * grad * grad
    first_hat = first_new / (1.0 - beta_one**STEP)
    second_hat = second_new / (1.0 - beta_two**STEP)
    weight_new = weight - rate * (first_hat / (jnp.sqrt(second_hat) + adam_eps) + shrink * weight)
    return (weight_new, first_new, second_new)


MESH = pl.DeviceIdType.MESH
VMEM_LIMIT = 64 * 1024 * 1024 - 65536
ANY = pl.BlockSpec(memory_space=pl.ANY)
VM = pl.BlockSpec(memory_space=pltpu.VMEM)


def place(index, n_pair):
    return {"dp": index // n_pair, "pair": lax.rem(index, n_pair)}


def remote(src, dst, send, recv, target):
    return pltpu.make_async_remote_copy(
        src, dst, send, recv, device_id=target, device_id_type=MESH
    )


def greet(targets):
    sem = pltpu.get_barrier_semaphore()
    for target in targets:
        pl.semaphore_signal(sem, inc=1, device_id=target, device_id_type=MESH)
    pl.semaphore_wait(sem, len(targets))


def my_index(n_pair):
    return lax.axis_index("dp") * n_pair + lax.axis_index("pair")


def bit_order(n_dp, n_pair, color):
    dp_bits, pair_bits = (n_dp - 1).bit_length(), (n_pair - 1).bit_length()
    high = list(reversed(range(pair_bits + 1, pair_bits + dp_bits))) + [pair_bits]
    side = list(reversed(range(1, pair_bits)))
    return high + side if color == 0 else side + high


def offset(order, position):
    return sum(((position >> step) & 1) << bit for step, bit in enumerate(order))


class Rounds:
    def __init__(self, n_dp, n_pair, dp_sem, pair_sem, own_sem):
        self.n_dp, self.n_pair = n_dp, n_pair
        self.dp_sem, self.pair_sem, self.own_sem = dp_sem, pair_sem, own_sem
        self.dp, self.pair = lax.axis_index("dp"), lax.axis_index("pair")
        sem = pltpu.get_barrier_semaphore()
        targets = [{"dp": self.dp ^ j, "pair": self.pair} for j in range(1, n_dp)]
        targets += [{"dp": self.dp, "pair": self.pair ^ j} for j in range(1, n_pair)]
        for target in targets:
            pl.semaphore_signal(sem, inc=1, device_id=target, device_id_type=MESH)
        self.entered = lambda: pl.semaphore_wait(sem, len(targets))

    def over_dp(self, block, by_dp):
        def copy(j, slot):
            target = {"dp": self.dp ^ j, "pair": self.pair}
            return remote(block, by_dp.at[slot], self.dp_sem.at[0, j], self.dp_sem.at[1, j], target)

        self.exchange(block, by_dp, self.dp, self.n_dp, copy)

    def over_pair(self, block, by_pair):
        def copy(j, slot):
            target = {"dp": self.dp, "pair": self.pair ^ j}
            return remote(
                block, by_pair.at[slot], self.pair_sem.at[0, j], self.pair_sem.at[1, j], target
            )

        self.exchange(block, by_pair, self.pair, self.n_pair, copy)

    def exchange(self, block, places, me, size, copy):
        own = pltpu.make_async_copy(block, places.at[me], self.own_sem)
        own.start()
        for j in reversed(range(1, size)):
            copy(j, me).start()
        own.wait()
        for j in range(1, size):
            copy(j, me ^ j).wait_recv()
        for j in range(1, size):
            copy(j, me).wait_send()


def round_sems(n_dp, n_pair):
    sem = pltpu.SemaphoreType.DMA
    return [sem((2, n_dp)), sem((2, n_pair)), sem]


def loss_kernel(
    n_dp, n_pair, x_ref, pos_ref, neg_ref, count_ref, loss_ref, grad_ref, by_dp, by_pair, unit, *sems
):
    rounds = Rounds(n_dp, n_pair, *sems)
    rounds.entered()
    rounds.over_dp(x_ref, by_dp)
    rounds.over_pair(by_dp, by_pair)
    docs, width = x_ref.shape
    total = n_dp * n_pair * docs
    for d in range(n_dp):
        for p in range(n_pair):
            base = (d * n_pair + p) * docs
            unit[base : base + docs] = by_pair[p, d]
    pooled = unit[...]
    inverse = lax.rsqrt(jnp.sum(pooled * pooled, axis=1, keepdims=True) + 1e-06)
    units = pooled * inverse
    similar = 20.0 * lax.dot_general(
        units, units, NT, precision=HIGHEST, preferred_element_type=jnp.float32
    )
    partner = lax.broadcasted_iota(jnp.int32, (total, total), 0)
    is_pos = partner == pos_ref[...]
    chosen = jnp.sum(jnp.where(is_pos, similar, 0.0), axis=0, keepdims=True)
    counts = count_ref[...]
    weight = 1.0 / (counts.astype(jnp.float32) * total)
    losses = jnp.zeros((1, total), jnp.float32)
    slopes = jnp.zeros((1, total), jnp.float32)
    grad_similar = jnp.zeros((total, total), jnp.float32)
    for slot in range(neg_ref.shape[0]):
        is_neg = partner == neg_ref[slot : slot + 1, :]
        against = jnp.sum(jnp.where(is_neg, similar, 0.0), axis=0, keepdims=True)
        value = margin - chosen + against
        used = slot < counts
        soft = jnp.maximum(value, 0.0) + jnp.log1p(jnp.exp(-jnp.abs(value)))
        losses = losses + jnp.where(used, soft, 0.0)
        slope = jnp.where(used, weight / (1.0 + jnp.exp(-value)), 0.0)
        grad_similar = grad_similar + jnp.where(is_neg, slope, 0.0)
        slopes = slopes + slope
    grad_similar = grad_similar - jnp.where(is_pos, slopes, 0.0)
    loss_ref[...] = jnp.sum(losses * weight, axis=1, keepdims=True)
    grad_units = sim_scale * (
        jnp.dot(grad_similar, units, precision=HIGHEST, preferred_element_type=jnp.float32)
        + lax.dot_general(
            grad_similar, units, TN, precision=HIGHEST, preferred_element_type=jnp.float32
        )
    )
    inner = jnp.sum(grad_units * units, axis=1, keepdims=True)
    unit[...] = inverse * (grad_units - units * inner)
    for d in range(n_dp):
        for p in range(n_pair):
            base = (d * n_pair + p) * docs

            @pl.when((rounds.dp == d) & (rounds.pair == p))
            def _():
                grad_ref[...] = unit[base : base + docs]


def pooled_loss(pooled, positives, negatives, counts, cid):
    n_dp, n_pair = lax.axis_size("dp"), lax.axis_size("pair")
    docs, width = pooled.shape
    return pl.pallas_call(
        functools.partial(loss_kernel, n_dp, n_pair),
        out_shape=[
            jax.ShapeDtypeStruct((1, 1), jnp.float32),
            jax.ShapeDtypeStruct(pooled.shape, jnp.float32),
        ],
        in_specs=[VM] * 4,
        out_specs=[VM] * 2,
        scratch_shapes=[
            pltpu.VMEM((n_dp, docs, width), jnp.float32),
            pltpu.VMEM((n_pair, n_dp, docs, width), jnp.float32),
            pltpu.VMEM((n_dp * n_pair * docs, width), jnp.float32),
        ]
        + round_sems(n_dp, n_pair),
        compiler_params=pltpu.CompilerParams(collective_id=cid, has_side_effects=True),
        name="pooled_loss",
    )(pooled, positives.reshape(1, -1), negatives.T, counts.reshape(1, -1))


NT = (((1,), (1,)), ((), ()))
TN = (((0,), (0,)), ((), ()))

def band(w_ref, row, h, table, seq):
    tiles = seq // 128
    for d in range(1 - tiles, tiles):
        low = seq + 128 * d - 128
        x = jnp.broadcast_to(w_ref[pl.ds(row, 1), low : low + 256], (128, 256))
        tile = pltpu.roll(x, 0, 1, stride=1, stride_axis=0)[:, 128:]
        for a in range(tiles):
            if 0 <= a + d < tiles:
                table[h, a * 128 : a * 128 + 128, (a + d) * 128 : (a + d) * 128 + 128] = tile

def forward_kernel(len_ref, q_ref, k_ref, v_ref, w_ref, o_ref, table):
    seq = q_ref.shape[0]
    doc = pl.program_id(1)
    @pl.when(doc == 0)
    def _():
        for h in range(2):
            band(w_ref, 2 * pl.program_id(0) + h, h, table, seq)
    length = len_ref[doc]
    lane = lax.broadcasted_iota(jnp.int32, (seq, 128), 1)
    column = lax.broadcasted_iota(jnp.int32, (1, seq), 1)
    q = q_ref[...] * jnp.bfloat16(0.125)
    k = k_ref[...]
    v = v_ref[...]
    got = []
    for h in range(2):
        mine = (lane < 64) == (h == 0)
        s = lax.dot_general(jnp.where(mine, q, 0), k, NT, preferred_element_type=jnp.float32)
        s = jnp.where(column < length, s + table[h], -1000000000.0)
        e = jnp.exp(s - jnp.max(s, axis=1, keepdims=True))
        p = (e * (1.0 / jnp.sum(e, axis=1, keepdims=True))).astype(jnp.bfloat16)
        got.append(jnp.dot(p, v, preferred_element_type=jnp.float32))
    o_ref[...] = jnp.where(lane < 64, got[0], got[1]).astype(o_ref.dtype)

def attention(lengths, qkv, w, seq):
    tokens = qkv.shape[0]
    pairs = w.shape[0] // 2
    docs = tokens // seq
    spec = lambda base: pl.BlockSpec((seq, 128), lambda h, d, *_: (d, base + h))
    return pl.pallas_call(
        forward_kernel,
        grid_spec=pltpu.PrefetchScalarGridSpec(
            num_scalar_prefetch=1, grid=(pairs, docs),
            in_specs=[spec(0), spec(pairs), spec(2 * pairs), pl.BlockSpec(w.shape, lambda h, d, *_: (0, 0))],
            out_specs=spec(0),
            scratch_shapes=[pltpu.VMEM((2, seq, seq), jnp.float32)]),
        out_shape=jax.ShapeDtypeStruct((tokens, pairs * 128), jnp.bfloat16),
        compiler_params=pltpu.CompilerParams(dimension_semantics=("arbitrary", "arbitrary"), vmem_limit_bytes=50 * 1024 * 1024),
        name="attention",
    )(lengths, qkv, qkv, qkv, w)

def backward_kernel(len_ref, q_ref, k_ref, v_ref, g_ref, w_ref, o_ref, z_ref, table, total, box, sem):
    seq = q_ref.shape[0]
    tiles = seq // 128
    doc = pl.program_id(1)
    @pl.when(doc == 0)
    def _():
        for h in range(2):
            band(w_ref, 2 * pl.program_id(0) + h, h, table, seq)
        total[...] = jnp.zeros_like(total)
    length = len_ref[doc]
    lane = lax.broadcasted_iota(jnp.int32, (seq, 128), 1)
    row = lax.broadcasted_iota(jnp.int32, (seq, 1), 0)
    q = q_ref[...] * jnp.bfloat16(0.125)
    k = k_ref[...]
    v = v_ref[...]
    g = g_ref[...]
    parts = []
    for h in range(2):
        mine = (lane < 64) == (h == 0)
        s = lax.dot_general(k, jnp.where(mine, q, 0), NT, preferred_element_type=jnp.float32)
        s = jnp.where(row < length, s + table[h], -1000000000.0)
        e = jnp.exp(s - jnp.max(s, axis=0, keepdims=True))
        p = e * (1.0 / jnp.sum(e, axis=0, keepdims=True))
        dv = jnp.dot(p.astype(jnp.bfloat16), g, preferred_element_type=jnp.float32)
        dp = lax.dot_general(v, jnp.where(mine, g, 0), NT, preferred_element_type=jnp.float32)
        ds = (p * (dp - jnp.sum(p * dp, axis=0, keepdims=True))).astype(jnp.bfloat16)
        total[h] += ds.astype(jnp.float32)
        dk = jnp.dot(ds, q, preferred_element_type=jnp.float32)
        dq = lax.dot_general(ds, k, TN, preferred_element_type=jnp.float32) * 0.125
        parts.append((dq, dk, dv))
    pair, pairs, docs = pl.program_id(0), pl.num_programs(0), pl.num_programs(1)
    step = pair * docs + doc
    slot = lax.rem(step, 2)

    def out(i):
        rows = pl.ds(pl.multiple_of(doc * seq, seq), seq)
        columns = pl.ds(pl.multiple_of((i * pairs + pair) * 128, 128), 128)
        return pltpu.make_async_copy(box.at[slot, i], o_ref.at[rows, columns], sem.at[slot, i])

    for i in range(3):
        @pl.when(step >= 2)
        def _():
            out(i).wait()
        box[slot, i] = jnp.where(lane < 64, parts[0][i], parts[1][i]).astype(o_ref.dtype)
        out(i).start()

    @pl.when(step == pairs * docs - 1)
    def _():
        for i in range(3):
            out(i).wait()
            pltpu.make_async_copy(box.at[1 - slot, i], box.at[1 - slot, i], sem.at[1 - slot, i]).wait()
    @pl.when(doc == pl.num_programs(1) - 1)
    def _():
        r = lax.broadcasted_iota(jnp.int32, (128, 128), 0)
        c = lax.broadcasted_iota(jnp.int32, (128, 128), 1)
        flip = jnp.where(r + c == 127, 1.0, 0.0)
        z_ref[...] = jnp.zeros_like(z_ref)
        for h in range(2):
            def block(d):
                return sum(total[h, a * 128 : a * 128 + 128, (a - d) * 128 : (a - d) * 128 + 128] for a in range(tiles) if 0 <= a - d < tiles)
            for d in (-1, 0, 1):
                x = jnp.dot(flip, block(d), precision=HIGHEST, preferred_element_type=jnp.float32)
                x = jnp.concatenate([x, jnp.zeros_like(x)], axis=1)
                x = pltpu.roll(x, 0, 1, stride=1, stride_axis=0)
                z_ref[0, h, d + 1 : d + 2, :] = jnp.sum(x, axis=0, keepdims=True)
            z_ref[0, h, 3:4, 0:128] = jnp.sum(sum(block(-d) for d in range(2, tiles)), axis=0, keepdims=True)
            z_ref[0, h, 4:5, 0:128] = jnp.sum(sum(block(d) for d in range(2, tiles)), axis=0, keepdims=True)

def attention_back(lengths, qkv, g, w, seq):
    tokens = qkv.shape[0]
    pairs = w.shape[0] // 2
    docs = tokens // seq
    spec = lambda base: pl.BlockSpec((seq, 128), lambda h, d, *_: (d, base + h))
    return pl.pallas_call(
        backward_kernel,
        grid_spec=pltpu.PrefetchScalarGridSpec(
            num_scalar_prefetch=1, grid=(pairs, docs),
            in_specs=[spec(0), spec(pairs), spec(2 * pairs), spec(0), pl.BlockSpec(w.shape, lambda h, d, *_: (0, 0))],
            out_specs=[pl.BlockSpec(memory_space=pl.ANY), pl.BlockSpec((1, 2, 8, 256), lambda h, d, *_: (h, 0, 0, 0))],
            scratch_shapes=[pltpu.VMEM((2, seq, seq), jnp.float32), pltpu.VMEM((2, seq, seq), jnp.float32), pltpu.VMEM((2, 3, seq, 128), jnp.bfloat16), pltpu.SemaphoreType.DMA((2, 3))]),
        out_shape=[jax.ShapeDtypeStruct((tokens, 3 * pairs * 128), jnp.bfloat16), jax.ShapeDtypeStruct((pairs, 2, 8, 256), jnp.float32)],
        compiler_params=pltpu.CompilerParams(dimension_semantics=("arbitrary", "arbitrary"), vmem_limit_bytes=50 * 1024 * 1024),
        name="attention_back",
    )(lengths, qkv, qkv, qkv, g, w)

def bucket_hits(offsets, buckets):
    half = buckets // 2
    exact = half // 2
    distance = np.abs(offsets)
    far = np.full(offsets.shape, exact)
    for level in range(1, half - exact):
        limit = math.ceil(exact * (REACH / exact) ** (level / (half - exact)) - 1e-09)
        far = far + (distance >= limit)
    bucket = np.where(offsets > 0, half, 0) + np.where(distance < exact, distance, far)
    return (bucket[:, None] == np.arange(buckets)[None, :]).astype(np.float32)


def bias_rows(bias, seq, sign):
    hits = bucket_hits(sign * (np.arange(2 * seq) - seq), bias.shape[1])
    return jnp.dot(bias, hits.T, precision=HIGHEST)


def bias_gradient(sums, seq, buckets):
    heads, width = sums.shape[0] * 2, sums.shape[2] * sums.shape[3]
    j = np.arange(256)
    offsets = [np.where(j < 255, 128 * d + 127 - j, 0) for d in (-1, 0, 1)]
    offsets += [np.full((256,), 1 - seq), np.full((256,), seq - 1)]
    hits = bucket_hits(np.concatenate(offsets), buckets)
    hits = np.concatenate([hits, np.zeros((width - hits.shape[0], buckets), np.float32)])
    return jnp.dot(sums.reshape(heads, width), hits, precision=HIGHEST)


def weight_pieces(widths):
    cut = widths[3] * 2 // 3 // 128 * 128
    return [
        (0, 0, widths[0], 1),
        (2, 0, widths[2], 0),
        (1, 0, widths[1], 0),
        (3, 0, cut, 0),
        (3, cut, widths[3], 1),
    ]


def gradient_pieces(widths):
    cut = widths[3] // 3 // 128 * 128
    return [
        (2, 0, widths[2], 0),
        (0, 0, widths[0], 1),
        (3, 0, cut, 0),
        (3, cut, widths[3], 1),
        (1, 0, widths[1], 1),
    ]


NN = (((1,), (0,)), ((), ()))


def stage(r):
    return (0, 1) if r == 0 else (1 << (r - 1), 1 << (r - 1))


class Gather:
    def __init__(self, n_dp, n_pair, pieces, outs, bufs, sems):
        self.n_pair, self.pieces, self.outs, self.bufs = n_pair, pieces, outs, bufs
        self.hop_sem, self.side_sem, self.core_sem, self.out_sem = sems
        self.me = my_index(n_pair)
        self.hops = (n_dp * n_pair - 1).bit_length() - 2
        self.orders = [bit_order(n_dp, n_pair, piece[3]) for piece in pieces]
        self.count = len(pieces)

    def send(self, a, lo, count, to, sem, which, bit):
        return remote(
            self.bufs[a].at[pl.ds(lo, count)],
            self.bufs[a].at[pl.ds(to, count)],
            sem.at[0, a, which],
            sem.at[1, a, which],
            place(self.me ^ (1 << bit), self.n_pair),
        )

    def hop(self, a, r):
        return self.send(a, 0, 1 << r, 1 << r, self.hop_sem, r, self.orders[a][r])

    def side(self, a, r):
        lo, count = stage(r)
        return self.send(a, lo, count, (1 << self.hops) + lo, self.side_sem, r, self.orders[a][self.hops])

    def core(self, a, r, sided):
        lo, count = stage(r)
        lo = lo + (sided << self.hops)
        return self.send(
            a, lo, count, (2 << self.hops) + lo, self.core_sem, 2 * r + sided, 0
        )

    def write_out(self, a, lo, count):
        which, low, high, _ = self.pieces[a]
        for p in range(lo, lo + count):
            block = self.me ^ offset(self.orders[a] + [0], p)
            pltpu.make_async_copy(
                self.bufs[a].at[p], self.outs[which].at[block, :, pl.ds(low, high - low)], self.out_sem.at[a]
            ).start()

    def held(self, r):
        lo, count = stage(r)
        for a in range(self.count):
            if r:
                self.hop(a, r - 1).wait_recv()
            if r < self.hops:
                self.hop(a, r).start()
            self.side(a, r).start()
            self.core(a, r, 0).start()
        for a in range(self.count):
            self.write_out(a, lo, count)

    def sided(self, r):
        lo, count = stage(r)
        for a in range(self.count):
            self.side(a, r).wait_recv()
            self.core(a, r, 1).start()
            self.write_out(a, (1 << self.hops) + lo, count)

    def cored(self, r):
        lo, count = stage(r)
        for sided in (0, 1):
            for a in range(self.count):
                self.core(a, r, sided).wait_recv()
                self.write_out(a, (2 << self.hops) + (sided << self.hops) + lo, count)

    def finish(self):
        for a in range(self.count):
            for r in range(self.hops):
                self.hop(a, r).wait_send()
            for r in range(self.hops + 1):
                self.side(a, r).wait_send()
                self.core(a, r, 0).wait_send()
                self.core(a, r, 1).wait_send()
            pltpu.make_async_copy(self.bufs[a], self.bufs[a], self.out_sem.at[a]).wait()


def triangle(size):
    rows = lax.broadcasted_iota(jnp.int32, (size, size), 0)
    columns = lax.broadcasted_iota(jnp.int32, (size, size), 1)
    return jnp.where(rows < columns, 1.0, 0.0).astype(jnp.bfloat16)


def digits(numbers):
    high = numbers // 64
    row = lax.broadcasted_iota(jnp.int32, (8, numbers.shape[1]), 0)
    both = jnp.where(row == 0, high, jnp.where(row == 1, numbers - 64 * high, 0))
    return both.astype(jnp.float32).astype(jnp.bfloat16)


def upright(pairs):
    row = lax.broadcasted_iota(jnp.int32, (8, 128), 0)
    value = jnp.where(row == 0, 64.0, jnp.where(row == 1, 1.0, 0.0)).astype(jnp.bfloat16)
    return lax.dot_general(pairs, value, TN, preferred_element_type=jnp.float32)


def hits_by_lane(numbers, width, base):
    lane = lax.broadcasted_iota(jnp.int32, (1, 128), 1).astype(jnp.float32) + base
    tiles = [
        jnp.where(numbers == lane + 128.0 * tile, 1.0, 0.0).astype(jnp.bfloat16)
        for tile in range(width // 128)
    ]
    return jnp.concatenate(tiles, axis=1)


def front_kernel(n_dp, n_pair, pieces, n_in, *refs):
    k = len(pieces)
    owner_ref, row_ref, table_ref = refs[:3]
    shards = refs[3 : 3 + n_in]
    emb_ref, key_ref, asked_ref = refs[3 + n_in : 6 + n_in]
    outs = refs[6 + n_in : 6 + 2 * n_in]
    rest = refs[6 + 2 * n_in :]
    bufs, rest = rest[:k], rest[k:]
    wide, table, ask_out, ask_in, rows_out, rows_in, total = rest[:7]
    table_sem, ask_sem, row_sem, *sems = rest[7:]
    dp, pair = lax.axis_index("dp"), lax.axis_index("pair")
    weights = Gather(n_dp, n_pair, pieces, outs, bufs, sems)
    tokens = owner_ref.shape[1]
    cap = ask_out.shape[2]
    table_rows = table_ref.shape[0]
    load = pltpu.make_async_copy(table_ref, wide, table_sem)
    load.start()
    peers = [{"dp": dp ^ j, "pair": pair} for j in range(1, n_dp)]
    sem = pltpu.get_barrier_semaphore()
    mates = [{"dp": dp, "pair": pair ^ j} for j in (1, 2)]
    for target in peers + mates:
        pl.semaphore_signal(sem, inc=1, device_id=target, device_id_type=MESH)
    for a, (which, low, high, _) in enumerate(pieces):
        bufs[a][0] = shards[which][:, low:high].astype(jnp.bfloat16)
    pl.semaphore_wait(sem, n_dp + 1)
    weights.held(0)

    owner = owner_ref[...]
    by_owner = lax.broadcasted_iota(jnp.int32, (n_dp, tokens), 0) == owner
    ranks = jnp.dot(
        jnp.where(by_owner, 1.0, 0.0).astype(jnp.bfloat16),
        triangle(tokens),
        preferred_element_type=jnp.float32,
    )
    rank = jnp.sum(jnp.where(by_owner, ranks, 0.0), axis=0, keepdims=True)
    key = owner * cap + rank.astype(jnp.int32)
    key_ref[...] = key
    wanted = digits(row_ref[...])

    def ask(j):
        return remote(ask_out.at[j], ask_in.at[j], ask_sem.at[0, j], ask_sem.at[1, j], peers[j - 1])

    def reply(j):
        return remote(
            rows_out.at[j], rows_in.at[j], row_sem.at[0, j], row_sem.at[1, j], peers[j - 1]
        )

    far = sorted(range(1, n_dp), reverse=True)
    for j in far + [0]:
        slot = lax.broadcasted_iota(jnp.int32, (cap, tokens), 0) + (dp ^ j) * cap
        chosen = jnp.where(slot == key, 1.0, 0.0).astype(jnp.bfloat16)
        ask_out[j] = lax.dot_general(wanted, chosen, NT, preferred_element_type=jnp.float32)
        if j:
            ask(j).start()
    weights.held(1)
    load.wait()

    def narrow(i, carry):
        part = pl.ds(pl.multiple_of(i * 16, 16), 16)
        table[part] = wide[part].astype(jnp.bfloat16)
        return carry

    lax.fori_loop(0, table_rows // 16, narrow, 0)
    if table.shape[0] > table_rows:
        table[table_rows:] = jnp.zeros((table.shape[0] - table_rows, table.shape[1]), jnp.bfloat16)

    def answer(j, target):
        asked = ask_out if j == 0 else ask_in
        hit = hits_by_lane(upright(asked[j].astype(jnp.bfloat16)), table.shape[0], 0.0)
        target[j] = jnp.dot(hit, table[...], preferred_element_type=jnp.float32).astype(jnp.bfloat16)
        asked_ref[j] = (64.0 * asked[j, 0:1] + asked[j, 1:2]).astype(jnp.int32)

    for turn, j in enumerate(far):
        ask(j).wait_recv()
        answer(j, rows_out)
        reply(j).start()
        if turn == n_dp // 4:
            weights.held(2)
            weights.sided(0)
    answer(0, rows_in)
    weights.sided(1)
    upright_key = upright(digits(key))

    def seat(j, first):
        place_hit = hits_by_lane(upright_key, cap, ((dp ^ j) * cap).astype(jnp.float32))
        got = jnp.dot(place_hit, rows_in[j], preferred_element_type=jnp.float32)
        total[...] = got if first else total[...] + got

    seat(0, True)
    weights.cored(0)
    for r in range(3, weights.hops + 1):
        weights.held(r)
        weights.sided(r - 1)
        weights.cored(r - 2)
    for j in far:
        reply(j).wait_recv()
        seat(j, False)
    emb_ref[...] = total[...].astype(jnp.bfloat16)
    weights.sided(weights.hops)
    for r in (weights.hops - 1, weights.hops):
        weights.cored(r)
    for j in far:
        ask(j).wait_send()
        reply(j).wait_send()
    weights.finish()


def front(owner, row, table, shards, pieces, cap, n_dp, n_pair, cid):
    n, k = n_dp * n_pair, len(pieces)
    hops = (n - 1).bit_length() - 2
    tokens = owner.shape[1]
    table_rows, width = table.shape
    padded = -(-table_rows // 256) * 256
    sem = pltpu.SemaphoreType.DMA
    return pl.pallas_call(
        functools.partial(front_kernel, n_dp, n_pair, pieces, len(shards)),
        out_shape=[
            jax.ShapeDtypeStruct((tokens, width), jnp.bfloat16),
            jax.ShapeDtypeStruct((1, tokens), jnp.int32),
            jax.ShapeDtypeStruct((n_dp, 1, cap), jnp.int32),
        ]
        + [jax.ShapeDtypeStruct((n,) + s.shape, jnp.bfloat16) for s in shards],
        in_specs=[VM, VM, ANY] + [VM] * len(shards),
        out_specs=[VM] * 3 + [ANY] * len(shards),
        scratch_shapes=[
            pltpu.VMEM((n, shards[p[0]].shape[0], p[2] - p[1]), jnp.bfloat16) for p in pieces
        ]
        + [
            pltpu.VMEM((table_rows, width), jnp.float32),
            pltpu.VMEM((padded, width), jnp.bfloat16),
            pltpu.VMEM((n_dp, 8, cap), jnp.float32),
            pltpu.VMEM((n_dp, 8, cap), jnp.float32),
            pltpu.VMEM((n_dp, cap, width), jnp.bfloat16),
            pltpu.VMEM((n_dp, cap, width), jnp.bfloat16),
            pltpu.VMEM((tokens, width), jnp.float32),
            sem,
            sem((2, n_dp)),
            sem((2, n_dp)),
            sem((2, k, hops)),
            sem((2, k, hops + 1)),
            sem((2, k, 2 * hops + 2)),
            sem((k,)),
        ],
        compiler_params=pltpu.CompilerParams(
            collective_id=cid, has_side_effects=True, vmem_limit_bytes=VMEM_LIMIT
        ),
        name="rows_and_weights",
    )(owner, row, table, *shards)


class Scatter:
    def __init__(self, n_dp, n_pair, pieces, ins, outs, boxes, sems):
        self.n_pair, self.pieces, self.ins, self.outs = n_pair, pieces, ins, outs
        k = len(pieces)
        self.acc, self.from_core = boxes[:k], boxes[k : 2 * k]
        self.from_side, self.from_hop = boxes[2 * k : 3 * k], boxes[3 * k :]
        self.load_sem, self.core_sem, self.side_sem, self.hop_sem = sems
        self.me = my_index(n_pair)
        self.hops = (n_dp * n_pair - 1).bit_length() - 2
        self.orders = [bit_order(n_dp, n_pair, piece[3]) for piece in pieces]
        self.count = k

    def source(self, a, block):
        which, low, high, _ = self.pieces[a]
        return self.ins[which].at[block, :, pl.ds(low, high - low)]

    def near(self, bit):
        return place(self.me ^ (1 << bit), self.n_pair)

    def load(self):
        for a in range(self.count):
            for p in range(2 << self.hops):
                pltpu.make_async_copy(
                    self.source(a, self.me ^ offset(self.orders[a], p)),
                    self.acc[a].at[p],
                    self.load_sem.at[a],
                ).start()

    def loaded(self):
        for a in range(self.count):
            pltpu.make_async_copy(self.acc[a], self.acc[a], self.load_sem.at[a]).wait()

    def core(self, a, r, sided, part=None):
        lo, count = stage(r)
        lo = lo + (sided << self.hops)
        to = self.from_core[a].at[pl.ds(lo, count)]
        source = to
        if part is not None:
            to = self.from_core[a].at[lo + part]
            source = self.source(a, self.me ^ (offset(self.orders[a], lo + part) + 1))
        slot = 2 * r + sided
        return remote(
            source, to, self.core_sem.at[0, a, slot], self.core_sem.at[1, a, slot], self.near(0)
        )

    def core_out(self, r):
        for sided in (1, 0):
            for a in range(self.count):
                for part in range(stage(r)[1]):
                    self.core(a, r, sided, part).start()

    def add(self, a, lo, count, box, at):
        acc = self.acc[a]

        def body(j, carry):
            acc[lo + j] = (
                acc[lo + j].astype(jnp.float32) + box[at + j].astype(jnp.float32)
            ).astype(jnp.bfloat16)
            return carry

        lax.fori_loop(0, count, body, 0)

    def side(self, a, r):
        lo, count = stage(r)
        return remote(
            self.acc[a].at[pl.ds((1 << self.hops) + lo, count)],
            self.from_side[a].at[pl.ds(lo, count)],
            self.side_sem.at[0, a, r],
            self.side_sem.at[1, a, r],
            self.near(self.orders[a][self.hops]),
        )

    def hop(self, a, r):
        return remote(
            self.acc[a].at[pl.ds(1 << r, 1 << r)],
            self.from_hop[a].at[pl.ds(self.hop_base(r), 1 << r)],
            self.hop_sem.at[0, a, r],
            self.hop_sem.at[1, a, r],
            self.near(self.orders[a][r]),
        )

    def hop_base(self, r):
        return (1 << self.hops) - (2 << r)

    def core_in(self, r):
        lo, count = stage(r)
        for sided in (1, 0):
            for a in range(self.count):
                self.core(a, r, sided).wait_recv()
                at = lo + (sided << self.hops)
                self.add(a, at, count, self.from_core[a], at)
                if sided:
                    self.side(a, r).start()

    def side_in(self, r):
        lo, count = stage(r)
        for a in range(self.count):
            self.side(a, r).wait_recv()
            self.add(a, lo, count, self.from_side[a], lo)
            if r == self.hops:
                self.hop(a, r - 1).start()

    def hop_in(self, r):
        for a in range(self.count):
            self.hop(a, r).wait_recv()
            base = self.hop_base(r)
            if r:
                mid = 1 << (r - 1)
                self.add(a, mid, mid, self.from_hop[a], base + mid)
                self.hop(a, r - 1).start()
                self.add(a, 0, mid, self.from_hop[a], base)
            else:
                which, low, high, _ = self.pieces[a]
                self.outs[which][:, low:high] = self.acc[a][0].astype(jnp.float32) + self.from_hop[
                    a
                ][base].astype(jnp.float32)

    def finish(self):
        for a in range(self.count):
            for r in range(self.hops):
                self.hop(a, r).wait_send()
            for r in range(self.hops + 1):
                self.side(a, r).wait_send()
                self.core(a, r, 0).wait_send()
                self.core(a, r, 1).wait_send()


def back_kernel(n_dp, n_pair, pieces, n_in, chunk, *refs):
    k = len(pieces)
    grad_ref, key_ref, ask_ref = refs[:3]
    ins = refs[3 : 3 + n_in]
    out_ref, square_ref = refs[3 + n_in : 5 + n_in]
    outs = refs[5 + n_in : 5 + 2 * n_in]
    rest = refs[5 + 2 * n_in :]
    boxes, rest = rest[: 4 * k], rest[4 * k :]
    hits, rows_out, rows_in, hot, part, stage_out, got_core, out_side, got_side, other = rest[:10]
    row_sem, core_sem, side_sem, last_sem, out_sem, *sems = rest[10:]
    dp, pair = lax.axis_index("dp"), lax.axis_index("pair")
    core = lax.rem(pair, 2)
    weights = Scatter(n_dp, n_pair, pieces, ins, outs, boxes, sems)
    groups, _, cap, width = rows_out.shape
    slots = ask_ref.shape[1]
    count = stage_out.shape[1]
    half = count * chunk
    tokens = key_ref.shape[1]
    peers = [{"dp": dp ^ j, "pair": pair} for j in range(1, n_dp)]
    partner, across = {"dp": dp, "pair": pair ^ 1}, {"dp": dp, "pair": pair ^ 2}
    weights.load()
    greet(peers + [partner, across])
    weights.core_out(weights.hops)

    def row(g, j):
        return remote(
            rows_out.at[g, j],
            rows_in.at[g, pl.ds(j * cap, cap)],
            row_sem.at[0, g, j],
            row_sem.at[1, g, j],
            peers[j - 1],
        )

    far = sorted(range(1, n_dp), reverse=True)

    def rows_send(g):
        columns = pl.ds(g * width, width)
        for j in far + [0]:
            if g == 0:
                slot = lax.broadcasted_iota(jnp.int32, (cap, tokens), 0) + (dp ^ j) * cap
                hits[j] = jnp.where(slot == key_ref[...], 1.0, 0.0).astype(jnp.bfloat16)
            got = jnp.dot(hits[j], grad_ref[:, columns], preferred_element_type=jnp.float32)
            if j:
                rows_out[g, j] = got.astype(jnp.bfloat16)
                row(g, j).start()
            else:
                rows_in[g, 0:cap] = got.astype(jnp.bfloat16)

    def summed(g, base):
        ids = lax.broadcasted_iota(jnp.int32, (chunk, slots), 0) + base
        hot[...] = jnp.where(ids == ask_ref[...], 1.0, 0.0).astype(jnp.bfloat16)
        return jnp.dot(hot[...], rows_in[g], preferred_element_type=jnp.float32)

    def to_core(g, i):
        return remote(
            stage_out.at[g, i], got_core.at[g, i], core_sem.at[0, g, i], core_sem.at[1, g, i], partner
        )

    def to_side(g, i):
        return remote(
            out_side.at[g, i], got_side.at[g, i], side_sem.at[0, g, i], side_sem.at[1, g, i], across
        )

    def to_other(g, i):
        return remote(
            out_side.at[g, i], other.at[g, i], last_sem.at[0, g, i], last_sem.at[1, g, i], partner
        )

    def write_out(box, g, i, which):
        rows = pl.ds(which * half + i * chunk, chunk)
        return pltpu.make_async_copy(
            box.at[g, i], out_ref.at[rows, pl.ds(g * width, width)], out_sem.at[g, i]
        )

    def local_sums(g):
        for j in far:
            row(g, j).wait_recv()
        for i in range(count):
            stage_out[g, i] = summed(g, (1 - core) * half + i * chunk).astype(jnp.bfloat16)
            to_core(g, i).start()
        for i in range(count):
            part[...] = summed(g, core * half + i * chunk)
            to_core(g, i).wait_recv()
            out_side[g, i] = (part[...] + got_core[g, i].astype(jnp.float32)).astype(jnp.bfloat16)
            to_side(g, i).start()

    def finish_sums(g, square):
        for i in range(count):
            to_side(g, i).wait()
            wide = out_side[g, i].astype(jnp.float32) + got_side[g, i].astype(jnp.float32)
            value = wide.astype(jnp.bfloat16)
            out_side[g, i] = value
            to_other(g, i).start()
            write_out(out_side, g, i, core).start()
            wide = value.astype(jnp.float32)
            square = square + jnp.sum(wide * wide, axis=0, keepdims=True)
        return square

    def hand_over(g):
        for i in range(count):
            to_other(g, i).wait_recv()
            write_out(out_side, g, i, core).wait()
            write_out(other, g, i, 1 - core).start()

    rows_send(0)
    for r in reversed(range(weights.hops)):
        weights.core_out(r)
    for g in range(1, groups):
        rows_send(g)
    weights.loaded()
    for r in reversed(range(weights.hops + 1)):
        weights.core_in(r)
    square = jnp.zeros((1, width), jnp.float32)
    turn = weights.hops
    for g in range(groups):
        local_sums(g)
        if g == 0:
            for r in reversed(range(weights.hops + 1)):
                weights.side_in(r)
        else:
            square = finish_sums(g - 1, square)
            if turn > 1:
                turn = turn - 1
                weights.hop_in(turn)
    square = finish_sums(groups - 1, square)
    while turn > 0:
        turn = turn - 1
        weights.hop_in(turn)
    square = jnp.sum(square, axis=1, keepdims=True)
    square = jnp.where(pair < 2, square, 0.0)
    for ref in outs:
        rows_square = jnp.sum(ref[...] * ref[...], axis=0, keepdims=True)
        square = square + jnp.sum(rows_square, axis=1, keepdims=True)
    square_ref[...] = square
    for g in range(groups):
        hand_over(g)
    for g in range(groups):
        for j in far:
            row(g, j).wait_send()
        for i in range(count):
            to_core(g, i).wait_send()
            to_other(g, i).wait_send()
            write_out(other, g, i, 1 - core).wait()
    weights.finish()


def back(grad, key, asked, grads, pieces, table_rows, groups, cid):
    n_dp, n_pair = lax.axis_size("dp"), lax.axis_size("pair")
    n, k = n_dp * n_pair, len(pieces)
    hops = (n - 1).bit_length() - 2
    chunk = 512
    rows = -(-table_rows // (2 * chunk)) * 2 * chunk
    count = rows // 2 // chunk
    tokens, full = grad.shape
    width = full // groups
    slots = asked.shape[1]
    cap = slots // n_dp
    sem = pltpu.SemaphoreType.DMA
    box = pltpu.VMEM((groups, count, chunk, width), jnp.bfloat16)

    def blocks(lead):
        return [
            pltpu.VMEM((lead, grads[p[0]].shape[1], p[2] - p[1]), jnp.bfloat16) for p in pieces
        ]

    return pl.pallas_call(
        functools.partial(back_kernel, n_dp, n_pair, pieces, len(grads), chunk),
        out_shape=[
            jax.ShapeDtypeStruct((rows, full), jnp.bfloat16),
            jax.ShapeDtypeStruct((1, 1), jnp.float32),
        ]
        + [jax.ShapeDtypeStruct(g.shape[1:], jnp.float32) for g in grads],
        in_specs=[VM] * 3 + [ANY] * len(grads),
        out_specs=[ANY, VM] + [VM] * len(grads),
        scratch_shapes=blocks(n // 2)
        + blocks(n // 2)
        + blocks(n // 4)
        + blocks(n // 4 - 1)
        + [
            pltpu.VMEM((n_dp, cap, tokens), jnp.bfloat16),
            pltpu.VMEM((groups, n_dp, cap, width), jnp.bfloat16),
            pltpu.VMEM((groups, slots, width), jnp.bfloat16),
            pltpu.VMEM((chunk, slots), jnp.bfloat16),
            pltpu.VMEM((chunk, width), jnp.float32),
            box,
            box,
            box,
            box,
            box,
            sem((2, groups, n_dp)),
            sem((2, groups, count)),
            sem((2, groups, count)),
            sem((2, groups, count)),
            sem((groups, count)),
            sem((k,)),
            sem((2, k, 2 * hops + 2)),
            sem((2, k, hops + 1)),
            sem((2, k, hops)),
        ],
        compiler_params=pltpu.CompilerParams(
            collective_id=cid, has_side_effects=True, vmem_limit_bytes=VMEM_LIMIT
        ),
        name="table_and_weights",
    )(grad, key, asked, *grads)


BIAS_CORRECT = (1.0 - beta_one**STEP, 1.0 - beta_two**STEP)


def adam_parts(weight, first, second, grad, factor, rate, shrink):
    clipped = grad * factor
    first_new = beta_one * first + (1.0 - beta_one) * clipped
    second_new = beta_two * second + (1.0 - beta_two) * (clipped * clipped)
    root = jnp.sqrt(second_new * (1.0 / BIAS_CORRECT[1])) + adam_eps
    step = (rate / BIAS_CORRECT[0]) * first_new / root
    return (weight * (1.0 - rate * shrink) - step, first_new, second_new)


def packed_base(gains, width):
    return -(-gains * width // 128 // 8) * 8


def norm_kernel(n_dp, n_pair, n_gain, *refs):
    gain_refs = refs[:n_gain]
    bias_ref, square_ref, total_ref, block, by_dp, by_pair = refs[n_gain : n_gain + 6]
    rounds = Rounds(n_dp, n_pair, *refs[n_gain + 6 :])
    width = gain_refs[0].shape[1]
    base = packed_base(n_gain, width)
    block[...] = jnp.zeros_like(block)
    for c in range(width // 128):
        for g in range(n_gain):
            at = c * n_gain + g
            block[at : at + 1, :] = gain_refs[g][:, c * 128 : (c + 1) * 128]
    block[base : base + bias_ref.shape[0], : bias_ref.shape[1]] = bias_ref[...]
    block[base : base + 1, 127:128] = square_ref[...]
    rounds.entered()
    rounds.over_dp(block, by_dp)
    total = by_dp[0]
    for d in range(1, n_dp):
        total = total + by_dp[d]
    block[...] = total
    rounds.over_pair(block, by_pair)
    total = by_pair[0]
    for p in range(1, n_pair):
        total = total + by_pair[p]
    total_ref[...] = total


def small_total(gain_grads, bias_grad, square, cid):
    n_dp, n_pair = lax.axis_size("dp"), lax.axis_size("pair")
    count, width = len(gain_grads), gain_grads[0].shape[1]
    height = -(-(packed_base(count, width) + bias_grad.shape[0]) // 8) * 8
    return pl.pallas_call(
        functools.partial(norm_kernel, n_dp, n_pair, count),
        out_shape=jax.ShapeDtypeStruct((height, 128), jnp.float32),
        in_specs=[VM] * (count + 2),
        out_specs=VM,
        scratch_shapes=[
            pltpu.VMEM((height, 128), jnp.float32),
            pltpu.VMEM((n_dp, height, 128), jnp.float32),
            pltpu.VMEM((n_pair, height, 128), jnp.float32),
        ]
        + round_sems(n_dp, n_pair),
        compiler_params=pltpu.CompilerParams(collective_id=cid, has_side_effects=True),
        name="small_total",
    )(*gain_grads, bias_grad, square)


def update_kernel(mats, *refs):
    total_ref, loss_ref, low = refs[:3]
    table, small = refs[3:6], refs[6:12]
    grads = refs[12 : 12 + mats]
    states = refs[12 + mats : 12 + 4 * mats]
    rest = refs[12 + 4 * mats :]
    norm_out, loss_out, table_out, small_out = rest[0], rest[1], rest[2:5], rest[5:11]
    mat_out = rest[11:]
    gains, width = small[0].shape
    base = packed_base(gains, width)
    total = total_ref[...]
    row = lax.broadcasted_iota(jnp.int32, total.shape, 0)
    lane = lax.broadcasted_iota(jnp.int32, total.shape, 1)
    plain = jnp.where((row == base) & (lane == 127), total, total * total)
    norm = jnp.sqrt(jnp.sum(jnp.sum(plain, axis=1, keepdims=True), axis=0, keepdims=True))
    factor = jnp.minimum(1.0, clip_limit / norm)
    step = pl.program_id(0)

    @pl.when(step == 0)
    def _():
        norm_out[...] = norm
        loss_out[...] = loss_ref[...]
        for c in range(width // 128):
            columns = slice(c * 128, (c + 1) * 128)
            grad = total_ref[c * gains : (c + 1) * gains, :]
            new = adam_parts(*(ref[:, columns] for ref in small[:3]), grad, factor, 1.0, 0.0)
            for ref, value in zip(small_out[:3], new):
                ref[:, columns] = value
        heads = small[3].shape[1]
        grad = total_ref[base : base + small[3].shape[0], :heads]
        new = adam_parts(*(ref[...] for ref in small[3:]), grad, factor, 0.3, 0.0)
        for ref, value in zip(small_out[3:], new):
            ref[...] = value

    for which in range(mats):
        three = slice(3 * which, 3 * which + 3)
        new = adam_parts(*(ref[...] for ref in states[three]), grads[which][...], factor, 0.05, 0.01)
        for ref, value in zip(mat_out[three], new):
            ref[...] = value

    def body(j, carry):
        rows = pl.ds(pl.multiple_of(j * 16, 16), 16)
        new = adam_parts(*(ref[rows] for ref in table), low[rows].astype(jnp.float32), factor, 1.0, 0.01)
        for ref, value in zip(table_out, new):
            ref[rows] = value
        return carry

    lax.fori_loop(0, low.shape[0] // 16, body, 0)


def update(total, loss, table_grad, table, small, grads, states):
    rows, width = table[0].shape
    steps = 6
    tall = -(-rows // steps // 16) * 16
    flat = [array for group in states for array in group]
    like = lambda array: jax.ShapeDtypeStruct(array.shape, jnp.float32)
    whole = lambda array: pl.BlockSpec(array.shape, lambda i: (0, 0))
    table_spec = pl.BlockSpec((tall, width), lambda i: (i, 0))

    def part(array):
        if array.shape[1] % (128 * steps) == 0 and array.shape[0] < 32:
            return pl.BlockSpec((array.shape[0], array.shape[1] // steps), lambda i: (0, i))
        if array.shape[0] % (8 * steps) == 0:
            return pl.BlockSpec((array.shape[0] // steps, array.shape[1]), lambda i: (i, 0))
        return whole(array)

    return pl.pallas_call(
        functools.partial(update_kernel, len(grads)),
        grid=(steps,),
        out_shape=[like(loss), like(loss)] + [like(array) for array in (*table, *small, *flat)],
        in_specs=[whole(total), whole(loss)]
        + [table_spec] * 4
        + [whole(array) for array in small]
        + [part(array) for array in (*grads, *flat)],
        out_specs=[whole(loss)] * 2
        + [table_spec] * 3
        + [whole(array) for array in small]
        + [part(array) for array in flat],
        compiler_params=pltpu.CompilerParams(
            dimension_semantics=("arbitrary",), vmem_limit_bytes=VMEM_LIMIT
        ),
        name="update",
    )(total, loss, table_grad, *table, *small, *grads, *flat)


def local_plain(
    token_owner,
    token_row,
    lengths,
    positives,
    negatives,
    neg_counts,
    embed_table,
    embed_first,
    embed_second,
    qkv_weight,
    qkv_first,
    qkv_second,
    out_weight,
    out_first,
    out_second,
    in_weight,
    in_first,
    in_second,
    down_weight,
    down_first,
    down_second,
    norm_gains,
    gains_first,
    gains_second,
    position_bias,
    bias_first,
    bias_second,
):
    doc_count = lengths.shape[0]
    seq_len = token_row.shape[1]
    model_width = embed_table.shape[1]
    head_count = position_bias.shape[1]
    bucket_count = position_bias.shape[0]
    tok_total = doc_count * seq_len
    owners = lax.axis_size("dp")
    capacity = max(2, 2 * tok_total // owners)
    low_mats = (
        qkv_weight.astype(jnp.bfloat16),
        out_weight.astype(jnp.bfloat16),
        in_weight.astype(jnp.bfloat16),
        down_weight.astype(jnp.bfloat16),
    )
    qkv_full, out_full, in_full, down_full = (
        lax.all_gather(low_mats[0], ("dp", "pair"), axis=0, tiled=True),
        lax.all_gather(low_mats[1], ("dp", "pair"), axis=0, tiled=True),
        lax.all_gather(low_mats[2], ("dp", "pair"), axis=0, tiled=True),
        lax.all_gather(low_mats[3], ("dp", "pair"), axis=0, tiled=True),
    )
    tok_owner = token_owner.reshape(-1)
    tok_row = token_row.reshape(-1)
    owner_hits = (tok_owner[:, None] == jnp.arange(owners, dtype=jnp.int32)[None, :]).astype(
        jnp.int32
    )
    slot_rank = jnp.sum((jnp.cumsum(owner_hits, axis=0) - 1) * owner_hits, axis=1)
    requests = jnp.zeros((owners, capacity), jnp.int32).at[tok_owner, slot_rank].set(tok_row)
    asked_rows = lax.all_to_all(requests, "dp", split_axis=0, concat_axis=0, tiled=True)
    looked = jnp.take(embed_table, asked_rows.reshape(-1), axis=0).astype(jnp.bfloat16)
    answer = lax.all_to_all(
        looked.reshape(asked_rows.shape + (model_width,)),
        "dp",
        split_axis=0,
        concat_axis=0,
        tiled=True,
    )
    replies, asked_rows = (answer, asked_rows)
    embedded = replies[tok_owner, slot_rank].astype(jnp.float32)
    positions = jnp.arange(seq_len)
    live = positions[None, :] < lengths[:, None]
    pair_buckets = bucket_of(
        (positions[None, :] - positions[:, None]).reshape(-1), bucket_count, REACH
    )
    pair_hits = (jnp.arange(bucket_count)[:, None] == pair_buckets[None, :]).astype(jnp.float32)
    bias_full = jnp.dot(position_bias.T, pair_hits, precision=HIGHEST).reshape(
        head_count, seq_len, seq_len
    )
    bucket_map = pair_hits.astype(jnp.bfloat16)

    def split_doc(source, doc_index):
        doc_rows = source[doc_index * seq_len : (doc_index + 1) * seq_len]
        return tuple(
            (
                doc_rows[:, member * model_width : (member + 1) * model_width].reshape(
                    seq_len, head_count, -1
                )
                for member in range(3)
            )
        )

    normed_one, inverse_one = rms_forward(embedded, norm_gains[0])
    normed_one = normed_one.astype(jnp.bfloat16)
    qkv_rows = jnp.dot(normed_one, qkv_full, preferred_element_type=jnp.float32).astype(
        jnp.bfloat16
    )
    attended_parts = []
    logsum_parts = []
    for doc_index in range(doc_count):
        query_heads, key_heads, value_heads = split_doc(qkv_rows, doc_index)
        doc_out, logsum = attend_forward(
            query_heads, key_heads, value_heads, bias_full, live[doc_index]
        )
        attended_parts.append(doc_out.reshape(seq_len, model_width))
        logsum_parts.append(logsum)
    attended = jnp.concatenate(attended_parts, axis=0).astype(jnp.bfloat16)
    residual = embedded + jnp.dot(attended, out_full, preferred_element_type=jnp.float32)
    normed_two, inverse_two = rms_forward(residual, norm_gains[1])
    normed_two = normed_two.astype(jnp.bfloat16)
    hidden = jax.nn.relu(jnp.dot(normed_two, in_full, preferred_element_type=jnp.float32)).astype(
        jnp.bfloat16
    )
    output_rows = residual + jnp.dot(hidden, down_full, preferred_element_type=jnp.float32)
    normed_three, inverse_three = rms_forward(output_rows, norm_gains[2])
    live_rows = live.reshape(-1, 1)
    length_float = lengths.astype(jnp.float32)
    pooled_local = (
        jnp.sum(
            jnp.where(live_rows, normed_three, 0.0).reshape(doc_count, seq_len, model_width), axis=1
        )
        / length_float[:, None]
    )
    pooled_all = lax.all_gather(pooled_local, ("dp", "pair"), axis=0, tiled=True)
    loss_value, loss_pullback = jax.vjp(
        lambda pooled_in: margin_loss(pooled_in, positives, negatives, neg_counts), pooled_all
    )
    grad_pooled_all = loss_pullback(jnp.ones((), jnp.float32))[0]
    grad_pooled = lax.dynamic_slice_in_dim(
        grad_pooled_all, lax.axis_index(("dp", "pair")) * doc_count, doc_count, 0
    )
    grad_three = jnp.where(
        live_rows, jnp.repeat(grad_pooled / length_float[:, None], seq_len, axis=0), 0.0
    )
    qkv_back, out_back, in_back, down_back = (qkv_full, out_full, in_full, down_full)
    grad_output, gain_three = rms_backward(output_rows, inverse_three, norm_gains[2], grad_three)
    grad_branch = grad_output.astype(jnp.bfloat16)
    grad_down = lax.dot_general(
        hidden, grad_branch, CONTRACT_ROWS, preferred_element_type=jnp.float32
    )
    grad_hidden = lax.dot_general(
        grad_branch, down_back, CONTRACT_COLS, preferred_element_type=jnp.float32
    )
    grad_pre = jnp.where(hidden > 0, grad_hidden, 0.0).astype(jnp.bfloat16)
    grad_in = lax.dot_general(
        normed_two, grad_pre, CONTRACT_ROWS, preferred_element_type=jnp.float32
    )
    grad_normed_two = lax.dot_general(
        grad_pre, in_back, CONTRACT_COLS, preferred_element_type=jnp.float32
    )
    grad_res_part, gain_two = rms_backward(residual, inverse_two, norm_gains[1], grad_normed_two)
    grad_residual = grad_output + grad_res_part
    grad_attn_branch = grad_residual.astype(jnp.bfloat16)
    grad_out = lax.dot_general(
        attended, grad_attn_branch, CONTRACT_ROWS, preferred_element_type=jnp.float32
    )
    grad_attended = lax.dot_general(
        grad_attn_branch, out_back, CONTRACT_COLS, preferred_element_type=jnp.float32
    ).astype(jnp.bfloat16)
    grad_qkv_parts = []
    bias_grad_heads = jnp.zeros((head_count, bucket_count), jnp.float32)
    for doc_index in range(doc_count):
        query_heads, key_heads, value_heads = split_doc(qkv_rows, doc_index)
        grad_doc = grad_attended[doc_index * seq_len : (doc_index + 1) * seq_len].reshape(
            seq_len, head_count, -1
        )
        grad_query, grad_key, grad_value, grad_low = attend_backward(
            query_heads,
            key_heads,
            value_heads,
            bias_full,
            live[doc_index],
            logsum_parts[doc_index],
            grad_doc,
        )
        grad_qkv_parts.append(
            jnp.concatenate(
                [
                    grad_query.reshape(seq_len, model_width),
                    grad_key.reshape(seq_len, model_width),
                    grad_value.reshape(seq_len, model_width),
                ],
                axis=1,
            )
        )
        bias_grad_heads = bias_grad_heads + lax.dot_general(
            grad_low.reshape(head_count, -1),
            bucket_map,
            CONTRACT_COLS,
            preferred_element_type=jnp.float32,
        )
    bias_grad_local = bias_grad_heads.T
    grad_qkv_rows = jnp.concatenate(grad_qkv_parts, axis=0).astype(jnp.bfloat16)
    grad_qkv = lax.dot_general(
        normed_one, grad_qkv_rows, CONTRACT_ROWS, preferred_element_type=jnp.float32
    )
    grad_normed_one = lax.dot_general(
        grad_qkv_rows, qkv_back, CONTRACT_COLS, preferred_element_type=jnp.float32
    )
    grad_emb_part, gain_one = rms_backward(embedded, inverse_one, norm_gains[0], grad_normed_one)
    grad_embedded = grad_residual + grad_emb_part
    sendback = (
        jnp.zeros((owners, capacity, model_width), jnp.float32)
        .at[tok_owner, slot_rank]
        .set(grad_embedded)
    )
    arrived = lax.all_to_all(sendback, "dp", split_axis=0, concat_axis=0, tiled=True)
    table_grad = jax.ops.segment_sum(
        arrived.reshape(-1, model_width), asked_rows.reshape(-1), num_segments=embed_table.shape[0]
    )
    table_grad = lax.psum(table_grad, "pair")
    weight_grads = (
        lax.psum_scatter(grad_qkv, ("dp", "pair"), scatter_dimension=0, tiled=True),
        lax.psum_scatter(grad_out, ("dp", "pair"), scatter_dimension=0, tiled=True),
        lax.psum_scatter(grad_in, ("dp", "pair"), scatter_dimension=0, tiled=True),
        lax.psum_scatter(grad_down, ("dp", "pair"), scatter_dimension=0, tiled=True),
    )
    pair_first = (lax.axis_index("pair") == 0).astype(jnp.float32)
    square_part = jnp.sum(
        jnp.stack([jnp.sum(grad_piece * grad_piece) for grad_piece in weight_grads])
    ) + pair_first * jnp.sum(table_grad * table_grad)
    gain_grad, bias_grad, square_sum = lax.psum(
        (jnp.stack([gain_one, gain_two, gain_three]), bias_grad_local, square_part), ("dp", "pair")
    )
    clip_norm = jnp.sqrt(
        square_sum + jnp.sum(gain_grad * gain_grad) + jnp.sum(bias_grad * bias_grad)
    )
    factor = jnp.minimum(1.0, clip_limit / clip_norm)
    table_out = adam_step(embed_table, embed_first, embed_second, table_grad * factor, 1.0, 0.01)
    qkv_out = adam_step(qkv_weight, qkv_first, qkv_second, weight_grads[0] * factor, 0.05, 0.01)
    out_out = adam_step(out_weight, out_first, out_second, weight_grads[1] * factor, 0.05, 0.01)
    in_out = adam_step(in_weight, in_first, in_second, weight_grads[2] * factor, 0.05, 0.01)
    down_out = adam_step(down_weight, down_first, down_second, weight_grads[3] * factor, 0.05, 0.01)
    gains_out = adam_step(norm_gains, gains_first, gains_second, gain_grad * factor, 1.0, 0.0)
    bias_out = adam_step(position_bias, bias_first, bias_second, bias_grad * factor, 0.3, 0.0)
    return (
        loss_value,
        clip_norm,
        table_out[0],
        table_out[1],
        table_out[2],
        qkv_out[0],
        qkv_out[1],
        qkv_out[2],
        out_out[0],
        out_out[1],
        out_out[2],
        in_out[0],
        in_out[1],
        in_out[2],
        down_out[0],
        down_out[1],
        down_out[2],
        gains_out[0],
        gains_out[1],
        gains_out[2],
        bias_out[0],
        bias_out[1],
        bias_out[2],
    )


def local_fast(
    token_owner,
    token_row,
    lengths,
    positives,
    negatives,
    neg_counts,
    embed_table,
    embed_first,
    embed_second,
    qkv_weight,
    qkv_first,
    qkv_second,
    out_weight,
    out_first,
    out_second,
    in_weight,
    in_first,
    in_second,
    down_weight,
    down_first,
    down_second,
    norm_gains,
    gains_first,
    gains_second,
    position_bias,
    bias_first,
    bias_second,
):
    doc_count = lengths.shape[0]
    seq_len = token_row.shape[1]
    model_width = embed_table.shape[1]
    head_count = position_bias.shape[1]
    bucket_count = position_bias.shape[0]
    tok_total = doc_count * seq_len
    owners = lax.axis_size("dp")
    capacity = max(2, 2 * tok_total // owners)
    holders = lax.axis_size("pair")
    shards = (qkv_weight, out_weight, in_weight, down_weight)
    embedded_low, slot_keys, asked_rows, *full = front(
        token_owner.reshape(1, -1),
        token_row.reshape(1, -1),
        embed_table,
        shards,
        weight_pieces([shard.shape[1] for shard in shards]),
        capacity,
        owners,
        holders,
        1,
    )
    qkv_full, out_full, in_full, down_full = (
        matrix.reshape(-1, matrix.shape[2]) for matrix in full
    )
    embedded = embedded_low.astype(jnp.float32)
    positions = jnp.arange(seq_len)
    live = positions[None, :] < lengths[:, None]
    normed_one, inverse_one = rms_forward(embedded, norm_gains[0])
    normed_one = normed_one.astype(jnp.bfloat16)
    qkv_rows = jnp.dot(normed_one, qkv_full, preferred_element_type=jnp.float32).astype(
        jnp.bfloat16
    )
    attended = attention(lengths, qkv_rows, bias_rows(position_bias.T, seq_len, 1), seq_len)
    residual = embedded + jnp.dot(attended, out_full, preferred_element_type=jnp.float32)
    normed_two, inverse_two = rms_forward(residual, norm_gains[1])
    normed_two = normed_two.astype(jnp.bfloat16)
    hidden = jax.nn.relu(jnp.dot(normed_two, in_full, preferred_element_type=jnp.float32)).astype(
        jnp.bfloat16
    )
    output_rows = residual + jnp.dot(hidden, down_full, preferred_element_type=jnp.float32)
    normed_three, inverse_three = rms_forward(output_rows, norm_gains[2])
    live_rows = live.reshape(-1, 1)
    length_float = lengths.astype(jnp.float32)
    pooled_local = (
        jnp.sum(
            jnp.where(live_rows, normed_three, 0.0).reshape(doc_count, seq_len, model_width), axis=1
        )
        / length_float[:, None]
    )
    loss_cell, grad_pooled = pooled_loss(
        pooled_local, positives, negatives, neg_counts, 3
    )
    grad_three = jnp.where(
        live_rows, jnp.repeat(grad_pooled / length_float[:, None], seq_len, axis=0), 0.0
    )
    qkv_back, out_back, in_back, down_back = (qkv_full, out_full, in_full, down_full)
    grad_output, gain_three = rms_backward(output_rows, inverse_three, norm_gains[2], grad_three)
    grad_branch = grad_output.astype(jnp.bfloat16)
    grad_down = lax.dot_general(
        hidden, grad_branch, CONTRACT_ROWS, preferred_element_type=jnp.float32
    )
    grad_hidden = lax.dot_general(
        grad_branch, down_back, CONTRACT_COLS, preferred_element_type=jnp.float32
    )
    grad_pre = jnp.where(hidden > 0, grad_hidden, 0.0).astype(jnp.bfloat16)
    grad_in = lax.dot_general(
        normed_two, grad_pre, CONTRACT_ROWS, preferred_element_type=jnp.float32
    )
    grad_normed_two = lax.dot_general(
        grad_pre, in_back, CONTRACT_COLS, preferred_element_type=jnp.float32
    )
    grad_res_part, gain_two = rms_backward(residual, inverse_two, norm_gains[1], grad_normed_two)
    grad_residual = grad_output + grad_res_part
    grad_attn_branch = grad_residual.astype(jnp.bfloat16)
    grad_out = lax.dot_general(
        attended, grad_attn_branch, CONTRACT_ROWS, preferred_element_type=jnp.float32
    )
    grad_attended = lax.dot_general(
        grad_attn_branch, out_back, CONTRACT_COLS, preferred_element_type=jnp.float32
    ).astype(jnp.bfloat16)
    grad_qkv_rows, diagonals = attention_back(
        lengths, qkv_rows, grad_attended, bias_rows(position_bias.T, seq_len, -1), seq_len
    )
    bias_grad_local = bias_gradient(diagonals, seq_len, bucket_count)
    grad_qkv = lax.dot_general(
        normed_one, grad_qkv_rows, CONTRACT_ROWS, preferred_element_type=jnp.float32
    )
    grad_normed_one = lax.dot_general(
        grad_qkv_rows, qkv_back, CONTRACT_COLS, preferred_element_type=jnp.float32
    )
    grad_emb_part, gain_one = rms_backward(embedded, inverse_one, norm_gains[0], grad_normed_one)
    grad_embedded = grad_residual + grad_emb_part
    table_rows = embed_table.shape[0]
    parts = owners * holders
    table_grad, square_part, *weight_grads = back(
        grad_embedded.astype(jnp.bfloat16),
        slot_keys,
        asked_rows.reshape(1, -1),
        [
            grad.astype(jnp.bfloat16).reshape(parts, -1, grad.shape[1])
            for grad in (grad_qkv, grad_out, grad_in, grad_down)
        ],
        gradient_pieces([grad.shape[1] for grad in (grad_qkv, grad_out, grad_in, grad_down)]),
        table_rows,
        3 if model_width % 384 == 0 else 1,
        2,
    )
    total = small_total(
        [gain.reshape(1, -1) for gain in (gain_one, gain_two, gain_three)],
        bias_grad_local,
        square_part,
        4,
    )
    norm_cell, loss_cell, *updated = update(
        total,
        loss_cell,
        table_grad,
        (embed_table, embed_first, embed_second),
        (
            norm_gains,
            gains_first,
            gains_second,
            position_bias.T,
            bias_first.T,
            bias_second.T,
        ),
        weight_grads,
        (
            (qkv_weight, qkv_first, qkv_second),
            (out_weight, out_first, out_second),
            (in_weight, in_first, in_second),
            (down_weight, down_first, down_second),
        ),
    )
    return (loss_cell[0, 0], norm_cell[0, 0], *updated[:3], *updated[9:], *updated[3:6], *(new.T for new in updated[6:9]))


def local(*arrays):
    n_dp, n_pair = lax.axis_size("dp"), lax.axis_size("pair")
    lengths, qkv_weight, down_weight = arrays[2], arrays[9], arrays[18]
    fits = (
        n_pair == 4
        and n_dp & (n_dp - 1) == 0
        and qkv_weight.shape[0] % 8 == 0
        and down_weight.shape[0] % 8 == 0
        and lengths.shape[0] == 2
        and 2 * arrays[1].size // n_dp % 128 == 0
    )
    return (local_fast if fits else local_plain)(*arrays)


def solution(mesh):
    return jax.shard_map(
        local,
        mesh=mesh,
        in_specs=(
            P(("dp", "pair"), None, None),
            P(("dp", "pair"), None),
            P(("dp", "pair")),
            P(),
            P(),
            P(),
            P("dp", None),
            P("dp", None),
            P("dp", None),
            P(("dp", "pair"), None),
            P(("dp", "pair"), None),
            P(("dp", "pair"), None),
            P(("dp", "pair"), None),
            P(("dp", "pair"), None),
            P(("dp", "pair"), None),
            P(("dp", "pair"), None),
            P(("dp", "pair"), None),
            P(("dp", "pair"), None),
            P(("dp", "pair"), None),
            P(("dp", "pair"), None),
            P(("dp", "pair"), None),
            P(),
            P(),
            P(),
            P(),
            P(),
            P(),
        ),
        out_specs=(
            P(),
            P(),
            P("dp", None),
            P("dp", None),
            P("dp", None),
            P(("dp", "pair"), None),
            P(("dp", "pair"), None),
            P(("dp", "pair"), None),
            P(("dp", "pair"), None),
            P(("dp", "pair"), None),
            P(("dp", "pair"), None),
            P(("dp", "pair"), None),
            P(("dp", "pair"), None),
            P(("dp", "pair"), None),
            P(("dp", "pair"), None),
            P(("dp", "pair"), None),
            P(("dp", "pair"), None),
            P(),
            P(),
            P(),
            P(),
            P(),
            P(),
        ),
        check_vma=False,
    )
```

```python
import functools
import math

import jax
import jax.numpy as jnp
import numpy as np
from jax import lax
from jax.experimental import pallas as pl
from jax.experimental.pallas import tpu as pltpu
from jax.sharding import PartitionSpec as P

REACH = 128
STEP = 5


rms_eps = 1e-06
clip_limit = 0.05
margin = 1.0
sim_scale = 20.0
beta_one = 0.9
beta_two = 0.999
adam_eps = 1e-08
HIGHEST = lax.Precision.HIGHEST
CONTRACT_ROWS = (((0,), (0,)), ((), ()))
CONTRACT_COLS = (((1,), (1,)), ((), ()))


def bucket_of(offsets, bucket_count, reach_limit):
    half_count = bucket_count // 2
    exact_count = half_count // 2
    sign_base = jnp.where(offsets > 0, half_count, 0).astype(jnp.int32)
    distance = jnp.abs(offsets)
    far_bucket = jnp.full(offsets.shape, exact_count, jnp.int32)
    for level_index in range(1, half_count - exact_count):
        threshold = int(
            math.ceil(
                exact_count
                * (reach_limit / exact_count) ** (level_index / (half_count - exact_count))
                - 1e-09
            )
        )
        far_bucket = far_bucket + (distance >= threshold).astype(jnp.int32)
    return sign_base + jnp.where(distance < exact_count, distance, far_bucket)


def rms_forward(values, gain):
    inverse = lax.rsqrt(jnp.mean(values * values, axis=-1, keepdims=True) + rms_eps)
    return (values * inverse * gain, inverse)


def rms_backward(values, inverse, gain, upstream):
    scaled = upstream * gain
    normed = values * inverse
    grad_values = inverse * (scaled - normed * jnp.mean(scaled * normed, axis=-1, keepdims=True))
    return (grad_values, jnp.sum(upstream * normed, axis=0))


def margin_loss(pooled, positives, negatives, neg_counts):
    unit = pooled * lax.rsqrt(jnp.sum(pooled * pooled, axis=-1, keepdims=True) + 1e-06)
    similar = sim_scale * jnp.dot(unit, unit.T, precision=HIGHEST)
    chosen = jnp.take_along_axis(similar, positives[:, None], axis=1)
    against = jnp.take_along_axis(similar, negatives, axis=1)
    live_slots = jnp.arange(negatives.shape[1])[None, :] < neg_counts[:, None]
    terms = jnp.where(live_slots, jax.nn.softplus(margin - chosen + against), 0.0)
    return jnp.mean(jnp.sum(terms, axis=1) / neg_counts.astype(jnp.float32))


def doc_scores(query_heads, key_heads, bias_full, live_keys):
    scores = (
        jnp.einsum("qhd,khd->hqk", query_heads, key_heads, preferred_element_type=jnp.float32)
        * 0.125
        + bias_full
    )
    return jnp.where(live_keys[None, None, :], scores, -1000000000.0)


def attend_forward(query_heads, key_heads, value_heads, bias_full, live_keys):
    scores = doc_scores(query_heads, key_heads, bias_full, live_keys)
    highest = jnp.max(scores, axis=-1, keepdims=True)
    weights = jnp.exp(scores - highest)
    totals = jnp.sum(weights, axis=-1, keepdims=True)
    probabilities = (weights / totals).astype(jnp.bfloat16)
    attended = jnp.einsum(
        "hqk,khd->qhd", probabilities, value_heads, preferred_element_type=jnp.float32
    )
    return (attended, highest + jnp.log(totals))


def attend_backward(
    query_heads, key_heads, value_heads, bias_full, live_keys, logsum, grad_attended
):
    probabilities = jnp.exp(doc_scores(query_heads, key_heads, bias_full, live_keys) - logsum)
    grad_value = jnp.einsum(
        "hqk,qhd->khd",
        probabilities.astype(jnp.bfloat16),
        grad_attended,
        preferred_element_type=jnp.float32,
    )
    grad_prob = jnp.einsum(
        "qhd,khd->hqk", grad_attended, value_heads, preferred_element_type=jnp.float32
    )
    grad_score = probabilities * (
        grad_prob - jnp.sum(probabilities * grad_prob, axis=-1, keepdims=True)
    )
    grad_low = grad_score.astype(jnp.bfloat16)
    grad_query = (
        jnp.einsum("hqk,khd->qhd", grad_low, key_heads, preferred_element_type=jnp.float32) * 0.125
    )
    grad_key = (
        jnp.einsum("hqk,qhd->khd", grad_low, query_heads, preferred_element_type=jnp.float32)
        * 0.125
    )
    return (grad_query, grad_key, grad_value, grad_low)


def adam_step(weight, first, second, grad, rate, shrink):
    first_new = beta_one * first + (1.0 - beta_one) * grad
    second_new = beta_two * second + (1.0 - beta_two) * grad * grad
    first_hat = first_new / (1.0 - beta_one**STEP)
    second_hat = second_new / (1.0 - beta_two**STEP)
    weight_new = weight - rate * (first_hat / (jnp.sqrt(second_hat) + adam_eps) + shrink * weight)
    return (weight_new, first_new, second_new)


MESH = pl.DeviceIdType.MESH
VMEM_LIMIT = 64 * 1024 * 1024 - 65536
ANY = pl.BlockSpec(memory_space=pl.ANY)
VM = pl.BlockSpec(memory_space=pltpu.VMEM)


def place(index, n_pair):
    return {"dp": index // n_pair, "pair": lax.rem(index, n_pair)}


def remote(src, dst, send, recv, target):
    return pltpu.make_async_remote_copy(
        src, dst, send, recv, device_id=target, device_id_type=MESH
    )


def greet(targets):
    sem = pltpu.get_barrier_semaphore()
    for target in targets:
        pl.semaphore_signal(sem, inc=1, device_id=target, device_id_type=MESH)
    pl.semaphore_wait(sem, len(targets))


def my_index(n_pair):
    return lax.axis_index("dp") * n_pair + lax.axis_index("pair")


def bit_order(n_dp, n_pair, color):
    dp_bits, pair_bits = (n_dp - 1).bit_length(), (n_pair - 1).bit_length()
    high = list(reversed(range(pair_bits + 1, pair_bits + dp_bits))) + [pair_bits]
    side = list(reversed(range(1, pair_bits)))
    return high + side if color == 0 else side + high


def offset(order, position):
    return sum(((position >> step) & 1) << bit for step, bit in enumerate(order))


class Rounds:
    def __init__(self, n_dp, n_pair, dp_sem, pair_sem, own_sem):
        self.n_dp, self.n_pair = n_dp, n_pair
        self.dp_sem, self.pair_sem, self.own_sem = dp_sem, pair_sem, own_sem
        self.dp, self.pair = lax.axis_index("dp"), lax.axis_index("pair")
        sem = pltpu.get_barrier_semaphore()
        targets = [{"dp": self.dp ^ j, "pair": self.pair} for j in range(1, n_dp)]
        targets += [{"dp": self.dp, "pair": self.pair ^ j} for j in range(1, n_pair)]
        for target in targets:
            pl.semaphore_signal(sem, inc=1, device_id=target, device_id_type=MESH)
        self.entered = lambda: pl.semaphore_wait(sem, len(targets))

    def over_dp(self, block, by_dp):
        def copy(j, slot):
            target = {"dp": self.dp ^ j, "pair": self.pair}
            return remote(block, by_dp.at[slot], self.dp_sem.at[0, j], self.dp_sem.at[1, j], target)

        self.exchange(block, by_dp, self.dp, self.n_dp, copy)

    def over_pair(self, block, by_pair):
        def copy(j, slot):
            target = {"dp": self.dp, "pair": self.pair ^ j}
            return remote(
                block, by_pair.at[slot], self.pair_sem.at[0, j], self.pair_sem.at[1, j], target
            )

        self.exchange(block, by_pair, self.pair, self.n_pair, copy)

    def exchange(self, block, places, me, size, copy):
        own = pltpu.make_async_copy(block, places.at[me], self.own_sem)
        own.start()
        for j in reversed(range(1, size)):
            copy(j, me).start()
        own.wait()
        for j in range(1, size):
            copy(j, me ^ j).wait_recv()
        for j in range(1, size):
            copy(j, me).wait_send()


def round_sems(n_dp, n_pair):
    sem = pltpu.SemaphoreType.DMA
    return [sem((2, n_dp)), sem((2, n_pair)), sem]


def loss_kernel(
    n_dp, n_pair, x_ref, pos_ref, neg_ref, count_ref, loss_ref, grad_ref, by_dp, by_pair, unit, *sems
):
    rounds = Rounds(n_dp, n_pair, *sems)
    rounds.entered()
    rounds.over_dp(x_ref, by_dp)
    rounds.over_pair(by_dp, by_pair)
    docs, width = x_ref.shape
    total = n_dp * n_pair * docs
    for d in range(n_dp):
        for p in range(n_pair):
            base = (d * n_pair + p) * docs
            unit[base : base + docs] = by_pair[p, d]
    pooled = unit[...]
    inverse = lax.rsqrt(jnp.sum(pooled * pooled, axis=1, keepdims=True) + 1e-06)
    units = pooled * inverse
    similar = 20.0 * lax.dot_general(
        units, units, NT, precision=HIGHEST, preferred_element_type=jnp.float32
    )
    partner = lax.broadcasted_iota(jnp.int32, (total, total), 0)
    is_pos = partner == pos_ref[...]
    chosen = jnp.sum(jnp.where(is_pos, similar, 0.0), axis=0, keepdims=True)
    counts = count_ref[...]
    weight = 1.0 / (counts.astype(jnp.float32) * total)
    losses = jnp.zeros((1, total), jnp.float32)
    slopes = jnp.zeros((1, total), jnp.float32)
    grad_similar = jnp.zeros((total, total), jnp.float32)
    for slot in range(neg_ref.shape[0]):
        is_neg = partner == neg_ref[slot : slot + 1, :]
        against = jnp.sum(jnp.where(is_neg, similar, 0.0), axis=0, keepdims=True)
        value = margin - chosen + against
        used = slot < counts
        soft = jnp.maximum(value, 0.0) + jnp.log1p(jnp.exp(-jnp.abs(value)))
        losses = losses + jnp.where(used, soft, 0.0)
        slope = jnp.where(used, weight / (1.0 + jnp.exp(-value)), 0.0)
        grad_similar = grad_similar + jnp.where(is_neg, slope, 0.0)
        slopes = slopes + slope
    grad_similar = grad_similar - jnp.where(is_pos, slopes, 0.0)
    loss_ref[...] = jnp.sum(losses * weight, axis=1, keepdims=True)
    grad_units = sim_scale * (
        jnp.dot(grad_similar, units, precision=HIGHEST, preferred_element_type=jnp.float32)
        + lax.dot_general(
            grad_similar, units, TN, precision=HIGHEST, preferred_element_type=jnp.float32
        )
    )
    inner = jnp.sum(grad_units * units, axis=1, keepdims=True)
    unit[...] = inverse * (grad_units - units * inner)
    for d in range(n_dp):
        for p in range(n_pair):
            base = (d * n_pair + p) * docs

            @pl.when((rounds.dp == d) & (rounds.pair == p))
            def _():
                grad_ref[...] = unit[base : base + docs]


def pooled_loss(pooled, positives, negatives, counts, cid):
    n_dp, n_pair = lax.axis_size("dp"), lax.axis_size("pair")
    docs, width = pooled.shape
    return pl.pallas_call(
        functools.partial(loss_kernel, n_dp, n_pair),
        out_shape=[
            jax.ShapeDtypeStruct((1, 1), jnp.float32),
            jax.ShapeDtypeStruct(pooled.shape, jnp.float32),
        ],
        in_specs=[VM] * 4,
        out_specs=[VM] * 2,
        scratch_shapes=[
            pltpu.VMEM((n_dp, docs, width), jnp.float32),
            pltpu.VMEM((n_pair, n_dp, docs, width), jnp.float32),
            pltpu.VMEM((n_dp * n_pair * docs, width), jnp.float32),
        ]
        + round_sems(n_dp, n_pair),
        compiler_params=pltpu.CompilerParams(collective_id=cid, has_side_effects=True),
        name="pooled_loss",
    )(pooled, positives.reshape(1, -1), negatives.T, counts.reshape(1, -1))


NT = (((1,), (1,)), ((), ()))
TN = (((0,), (0,)), ((), ()))

def band(w_ref, row, h, table, seq):
    tiles = seq // 128
    for d in range(1 - tiles, tiles):
        low = seq + 128 * d - 128
        x = jnp.broadcast_to(w_ref[pl.ds(row, 1), low : low + 256], (128, 256))
        tile = pltpu.roll(x, 0, 1, stride=1, stride_axis=0)[:, 128:]
        for a in range(tiles):
            if 0 <= a + d < tiles:
                table[h, a * 128 : a * 128 + 128, (a + d) * 128 : (a + d) * 128 + 128] = tile

def forward_kernel(len_ref, q_ref, k_ref, v_ref, w_ref, o_ref, table):
    seq = q_ref.shape[0]
    doc = pl.program_id(1)
    @pl.when(doc == 0)
    def _():
        for h in range(2):
            band(w_ref, 2 * pl.program_id(0) + h, h, table, seq)
    length = len_ref[doc]
    lane = lax.broadcasted_iota(jnp.int32, (seq, 128), 1)
    column = lax.broadcasted_iota(jnp.int32, (1, seq), 1)
    q = q_ref[...] * jnp.bfloat16(0.125)
    k = k_ref[...]
    v = v_ref[...]
    got = []
    for h in range(2):
        mine = (lane < 64) == (h == 0)
        s = lax.dot_general(jnp.where(mine, q, 0), k, NT, preferred_element_type=jnp.float32)
        s = jnp.where(column < length, s + table[h], -1000000000.0)
        e = jnp.exp(s - jnp.max(s, axis=1, keepdims=True))
        p = (e * (1.0 / jnp.sum(e, axis=1, keepdims=True))).astype(jnp.bfloat16)
        got.append(jnp.dot(p, v, preferred_element_type=jnp.float32))
    o_ref[...] = jnp.where(lane < 64, got[0], got[1]).astype(o_ref.dtype)

def attention(lengths, qkv, w, seq):
    tokens = qkv.shape[0]
    pairs = w.shape[0] // 2
    docs = tokens // seq
    spec = lambda base: pl.BlockSpec((seq, 128), lambda h, d, *_: (d, base + h))
    return pl.pallas_call(
        forward_kernel,
        grid_spec=pltpu.PrefetchScalarGridSpec(
            num_scalar_prefetch=1, grid=(pairs, docs),
            in_specs=[spec(0), spec(pairs), spec(2 * pairs), pl.BlockSpec(w.shape, lambda h, d, *_: (0, 0))],
            out_specs=spec(0),
            scratch_shapes=[pltpu.VMEM((2, seq, seq), jnp.float32)]),
        out_shape=jax.ShapeDtypeStruct((tokens, pairs * 128), jnp.bfloat16),
        compiler_params=pltpu.CompilerParams(dimension_semantics=("arbitrary", "arbitrary"), vmem_limit_bytes=50 * 1024 * 1024),
        name="attention",
    )(lengths, qkv, qkv, qkv, w)

def bucket_hits(offsets, buckets):
    half = buckets // 2
    exact = half // 2
    distance = np.abs(offsets)
    far = np.full(offsets.shape, exact)
    for level in range(1, half - exact):
        limit = math.ceil(exact * (REACH / exact) ** (level / (half - exact)) - 1e-09)
        far = far + (distance >= limit)
    bucket = np.where(offsets > 0, half, 0) + np.where(distance < exact, distance, far)
    return (bucket[:, None] == np.arange(buckets)[None, :]).astype(np.float32)


def bias_rows(bias, seq, sign):
    hits = bucket_hits(sign * (np.arange(2 * seq) - seq), bias.shape[1])
    return jnp.dot(bias, hits.T, precision=HIGHEST)


def bias_gradient(sums, seq, buckets):
    heads, width = sums.shape[0] * 2, sums.shape[2] * sums.shape[3]
    j = np.arange(256)
    offsets = [np.where(j < 255, 128 * d + 127 - j, 0) for d in (-1, 0, 1)]
    offsets += [np.full((256,), 1 - seq), np.full((256,), seq - 1)]
    hits = bucket_hits(np.concatenate(offsets), buckets)
    hits = np.concatenate([hits, np.zeros((width - hits.shape[0], buckets), np.float32)])
    return jnp.dot(sums.reshape(heads, width), hits, precision=HIGHEST)


def weight_pieces(widths):
    cut = widths[3] * 2 // 3 // 128 * 128
    return [
        (0, 0, widths[0], 1),
        (2, 0, widths[2], 0),
        (1, 0, widths[1], 0),
        (3, 0, cut, 0),
        (3, cut, widths[3], 1),
    ]


def early_pieces(width):
    cut = width * 2 // 3 // 128 * 128
    return [(0, 0, cut, 0), (0, cut, width, 1)]


def late_pieces(widths):
    return [(2, 0, widths[2], 0), (0, 0, widths[0], 1), (1, 0, widths[1], 1)]


NN = (((1,), (0,)), ((), ()))


def stage(r):
    return (0, 1) if r == 0 else (1 << (r - 1), 1 << (r - 1))


class Gather:
    def __init__(self, n_dp, n_pair, pieces, outs, bufs, sems):
        self.n_pair, self.pieces, self.outs, self.bufs = n_pair, pieces, outs, bufs
        self.hop_sem, self.side_sem, self.core_sem, self.out_sem = sems
        self.me = my_index(n_pair)
        self.hops = (n_dp * n_pair - 1).bit_length() - 2
        self.orders = [bit_order(n_dp, n_pair, piece[3]) for piece in pieces]
        self.count = len(pieces)

    def send(self, a, lo, count, to, sem, which, bit):
        return remote(
            self.bufs[a].at[pl.ds(lo, count)],
            self.bufs[a].at[pl.ds(to, count)],
            sem.at[0, a, which],
            sem.at[1, a, which],
            place(self.me ^ (1 << bit), self.n_pair),
        )

    def hop(self, a, r):
        return self.send(a, 0, 1 << r, 1 << r, self.hop_sem, r, self.orders[a][r])

    def side(self, a, r):
        lo, count = stage(r)
        return self.send(a, lo, count, (1 << self.hops) + lo, self.side_sem, r, self.orders[a][self.hops])

    def core(self, a, r, sided):
        lo, count = stage(r)
        lo = lo + (sided << self.hops)
        return self.send(
            a, lo, count, (2 << self.hops) + lo, self.core_sem, 2 * r + sided, 0
        )

    def write_out(self, a, lo, count):
        which, low, high, _ = self.pieces[a]
        for p in range(lo, lo + count):
            block = self.me ^ offset(self.orders[a] + [0], p)
            pltpu.make_async_copy(
                self.bufs[a].at[p], self.outs[which].at[block, :, pl.ds(low, high - low)], self.out_sem.at[a]
            ).start()

    def held(self, r):
        lo, count = stage(r)
        for a in range(self.count):
            if r:
                self.hop(a, r - 1).wait_recv()
            if r < self.hops:
                self.hop(a, r).start()
            self.side(a, r).start()
            self.core(a, r, 0).start()
        for a in range(self.count):
            self.write_out(a, lo, count)

    def sided(self, r):
        lo, count = stage(r)
        for a in range(self.count):
            self.side(a, r).wait_recv()
            self.core(a, r, 1).start()
            self.write_out(a, (1 << self.hops) + lo, count)

    def cored(self, r):
        lo, count = stage(r)
        for sided in (0, 1):
            for a in range(self.count):
                self.core(a, r, sided).wait_recv()
                self.write_out(a, (2 << self.hops) + (sided << self.hops) + lo, count)

    def finish(self):
        for a in range(self.count):
            for r in range(self.hops):
                self.hop(a, r).wait_send()
            for r in range(self.hops + 1):
                self.side(a, r).wait_send()
                self.core(a, r, 0).wait_send()
                self.core(a, r, 1).wait_send()
            pltpu.make_async_copy(self.bufs[a], self.bufs[a], self.out_sem.at[a]).wait()


def triangle(size):
    rows = lax.broadcasted_iota(jnp.int32, (size, size), 0)
    columns = lax.broadcasted_iota(jnp.int32, (size, size), 1)
    return jnp.where(rows < columns, 1.0, 0.0).astype(jnp.bfloat16)


def digits(numbers):
    high = numbers // 64
    row = lax.broadcasted_iota(jnp.int32, (8, numbers.shape[1]), 0)
    both = jnp.where(row == 0, high, jnp.where(row == 1, numbers - 64 * high, 0))
    return both.astype(jnp.float32).astype(jnp.bfloat16)


def upright(pairs):
    row = lax.broadcasted_iota(jnp.int32, (8, 128), 0)
    value = jnp.where(row == 0, 64.0, jnp.where(row == 1, 1.0, 0.0)).astype(jnp.bfloat16)
    return lax.dot_general(pairs, value, TN, preferred_element_type=jnp.float32)


def hits_by_lane(numbers, width, base):
    lane = lax.broadcasted_iota(jnp.int32, (1, 128), 1).astype(jnp.float32) + base
    tiles = [
        jnp.where(numbers == lane + 128.0 * tile, 1.0, 0.0).astype(jnp.bfloat16)
        for tile in range(width // 128)
    ]
    return jnp.concatenate(tiles, axis=1)


def front_kernel(n_dp, n_pair, pieces, n_in, *refs):
    k = len(pieces)
    owner_ref, row_ref, table_ref = refs[:3]
    shards = refs[3 : 3 + n_in]
    emb_ref, key_ref, asked_ref = refs[3 + n_in : 6 + n_in]
    outs = refs[6 + n_in : 6 + 2 * n_in]
    rest = refs[6 + 2 * n_in :]
    bufs, rest = rest[:k], rest[k:]
    wide, table, ask_out, ask_in, rows_out, rows_in, total = rest[:7]
    table_sem, ask_sem, row_sem, *sems = rest[7:]
    dp, pair = lax.axis_index("dp"), lax.axis_index("pair")
    weights = Gather(n_dp, n_pair, pieces, outs, bufs, sems)
    tokens = owner_ref.shape[1]
    cap = ask_out.shape[2]
    table_rows = table_ref.shape[0]
    load = pltpu.make_async_copy(table_ref, wide, table_sem)
    load.start()
    peers = [{"dp": dp ^ j, "pair": pair} for j in range(1, n_dp)]
    sem = pltpu.get_barrier_semaphore()
    mates = [{"dp": dp, "pair": pair ^ j} for j in (1, 2)]
    for target in peers + mates:
        pl.semaphore_signal(sem, inc=1, device_id=target, device_id_type=MESH)
    for a, (which, low, high, _) in enumerate(pieces):
        bufs[a][0] = shards[which][:, low:high].astype(jnp.bfloat16)
    pl.semaphore_wait(sem, n_dp + 1)
    weights.held(0)

    owner = owner_ref[...]
    by_owner = lax.broadcasted_iota(jnp.int32, (n_dp, tokens), 0) == owner
    ranks = jnp.dot(
        jnp.where(by_owner, 1.0, 0.0).astype(jnp.bfloat16),
        triangle(tokens),
        preferred_element_type=jnp.float32,
    )
    rank = jnp.sum(jnp.where(by_owner, ranks, 0.0), axis=0, keepdims=True)
    key = owner * cap + rank.astype(jnp.int32)
    key_ref[...] = key
    wanted = digits(row_ref[...])

    def peer(j):
        return {"dp": dp ^ j, "pair": pair}

    def ask(j):
        return remote(ask_out.at[j], ask_in.at[j], ask_sem.at[0, j], ask_sem.at[1, j], peer(j))

    def reply(j):
        return remote(rows_out.at[j], rows_in.at[j], row_sem.at[0, j], row_sem.at[1, j], peer(j))

    def loop(first, last, body):
        def turn(t, carry):
            body(n_dp - 1 - t)
            return carry

        lax.fori_loop(first, last, turn, 0)

    def request(j):
        slot = lax.broadcasted_iota(jnp.int32, (cap, tokens), 0) + (dp ^ j) * cap
        chosen = jnp.where(slot == key, 1.0, 0.0).astype(jnp.bfloat16)
        ask_out[j] = lax.dot_general(wanted, chosen, NT, preferred_element_type=jnp.float32)

        @pl.when(j > 0)
        def _():
            ask(j).start()

    loop(0, n_dp, request)
    ask_in[0] = ask_out[0]
    weights.held(1)
    load.wait()

    def narrow(i, carry):
        part = pl.ds(pl.multiple_of(i * 16, 16), 16)
        table[part] = wide[part].astype(jnp.bfloat16)
        return carry

    lax.fori_loop(0, table_rows // 16, narrow, 0)
    if table.shape[0] > table_rows:
        table[table_rows:] = jnp.zeros((table.shape[0] - table_rows, table.shape[1]), jnp.bfloat16)

    def answer(j):
        @pl.when(j > 0)
        def _():
            ask(j).wait_recv()

        asked = ask_in[j]
        hit = hits_by_lane(upright(asked.astype(jnp.bfloat16)), table.shape[0], 0.0)
        got = jnp.dot(hit, table[...], preferred_element_type=jnp.float32)
        rows_out[j] = got.astype(jnp.bfloat16)
        asked_ref[j] = (64.0 * asked[0:1] + asked[1:2]).astype(jnp.int32)

        @pl.when(j > 0)
        def _():
            reply(j).start()

    early = n_dp // 4 + 1
    loop(0, early, answer)
    weights.held(2)
    weights.sided(0)
    loop(early, n_dp, answer)
    rows_in[0] = rows_out[0]
    weights.sided(1)
    upright_key = upright(digits(key))

    total[...] = jnp.zeros_like(total)

    def seat(j):
        @pl.when(j > 0)
        def _():
            reply(j).wait_recv()

        place_hit = hits_by_lane(upright_key, cap, ((dp ^ j) * cap).astype(jnp.float32))
        total[...] += jnp.dot(place_hit, rows_in[j], preferred_element_type=jnp.float32)

    weights.cored(0)
    for r in range(3, weights.hops + 1):
        weights.held(r)
        weights.sided(r - 1)
        weights.cored(r - 2)
    loop(0, n_dp, seat)
    emb_ref[...] = total[...].astype(jnp.bfloat16)
    weights.sided(weights.hops)
    for r in (weights.hops - 1, weights.hops):
        weights.cored(r)
    for j in range(1, n_dp):
        ask(j).wait_send()
        reply(j).wait_send()
    weights.finish()


def front(owner, row, table, shards, pieces, cap, n_dp, n_pair, cid):
    n, k = n_dp * n_pair, len(pieces)
    hops = (n - 1).bit_length() - 2
    tokens = owner.shape[1]
    table_rows, width = table.shape
    padded = -(-table_rows // 256) * 256
    sem = pltpu.SemaphoreType.DMA
    return pl.pallas_call(
        functools.partial(front_kernel, n_dp, n_pair, pieces, len(shards)),
        out_shape=[
            jax.ShapeDtypeStruct((tokens, width), jnp.bfloat16),
            jax.ShapeDtypeStruct((1, tokens), jnp.int32),
            jax.ShapeDtypeStruct((n_dp, 1, cap), jnp.int32),
        ]
        + [jax.ShapeDtypeStruct((n,) + s.shape, jnp.bfloat16) for s in shards],
        in_specs=[VM, VM, ANY] + [VM] * len(shards),
        out_specs=[VM] * 3 + [ANY] * len(shards),
        scratch_shapes=[
            pltpu.VMEM((n, shards[p[0]].shape[0], p[2] - p[1]), jnp.bfloat16) for p in pieces
        ]
        + [
            pltpu.VMEM((table_rows, width), jnp.float32),
            pltpu.VMEM((padded, width), jnp.bfloat16),
            pltpu.VMEM((n_dp, 8, cap), jnp.float32),
            pltpu.VMEM((n_dp, 8, cap), jnp.float32),
            pltpu.VMEM((n_dp, cap, width), jnp.bfloat16),
            pltpu.VMEM((n_dp, cap, width), jnp.bfloat16),
            pltpu.VMEM((tokens, width), jnp.float32),
            sem,
            sem((2, n_dp)),
            sem((2, n_dp)),
            sem((2, k, hops)),
            sem((2, k, hops + 1)),
            sem((2, k, 2 * hops + 2)),
            sem((k,)),
        ],
        compiler_params=pltpu.CompilerParams(
            collective_id=cid, has_side_effects=True, vmem_limit_bytes=VMEM_LIMIT
        ),
        name="rows_and_weights",
    )(owner, row, table, *shards)


class Scatter:
    def __init__(self, n_dp, n_pair, pieces, ins, outs, boxes, sems):
        self.n_pair, self.pieces, self.ins, self.outs = n_pair, pieces, ins, outs
        k = len(pieces)
        self.acc, self.from_core = boxes[:k], boxes[k : 2 * k]
        self.from_side, self.from_hop = boxes[2 * k : 3 * k], boxes[3 * k :]
        self.load_sem, self.core_sem, self.side_sem, self.hop_sem = sems
        self.me = my_index(n_pair)
        self.hops = (n_dp * n_pair - 1).bit_length() - 2
        self.orders = [bit_order(n_dp, n_pair, piece[3]) for piece in pieces]
        self.count = k

    def source(self, a, block):
        which, low, high, _ = self.pieces[a]
        return self.ins[which].at[block, :, pl.ds(low, high - low)]

    def near(self, bit):
        return place(self.me ^ (1 << bit), self.n_pair)

    def load(self):
        for a in range(self.count):
            for p in range(2 << self.hops):
                pltpu.make_async_copy(
                    self.source(a, self.me ^ offset(self.orders[a], p)),
                    self.acc[a].at[p],
                    self.load_sem.at[a],
                ).start()

    def loaded(self):
        for a in range(self.count):
            pltpu.make_async_copy(self.acc[a], self.acc[a], self.load_sem.at[a]).wait()

    def core(self, a, r, sided, part=None):
        lo, count = stage(r)
        lo = lo + (sided << self.hops)
        to = self.from_core[a].at[pl.ds(lo, count)]
        source = to
        if part is not None:
            to = self.from_core[a].at[lo + part]
            source = self.source(a, self.me ^ (offset(self.orders[a], lo + part) + 1))
        slot = 2 * r + sided
        return remote(
            source, to, self.core_sem.at[0, a, slot], self.core_sem.at[1, a, slot], self.near(0)
        )

    def core_out(self, r):
        for sided in (1, 0):
            for a in range(self.count):
                for part in range(stage(r)[1]):
                    self.core(a, r, sided, part).start()

    def add(self, a, lo, count, box, at):
        acc = self.acc[a]

        def body(j, carry):
            acc[lo + j] = (
                acc[lo + j].astype(jnp.float32) + box[at + j].astype(jnp.float32)
            ).astype(jnp.bfloat16)
            return carry

        lax.fori_loop(0, count, body, 0)

    def side(self, a, r):
        lo, count = stage(r)
        return remote(
            self.acc[a].at[pl.ds((1 << self.hops) + lo, count)],
            self.from_side[a].at[pl.ds(lo, count)],
            self.side_sem.at[0, a, r],
            self.side_sem.at[1, a, r],
            self.near(self.orders[a][self.hops]),
        )

    def hop(self, a, r):
        return remote(
            self.acc[a].at[pl.ds(1 << r, 1 << r)],
            self.from_hop[a].at[pl.ds(self.hop_base(r), 1 << r)],
            self.hop_sem.at[0, a, r],
            self.hop_sem.at[1, a, r],
            self.near(self.orders[a][r]),
        )

    def hop_base(self, r):
        return (1 << self.hops) - (2 << r)

    def core_in(self, r):
        lo, count = stage(r)
        for sided in (1, 0):
            for a in range(self.count):
                self.core(a, r, sided).wait_recv()
                at = lo + (sided << self.hops)
                self.add(a, at, count, self.from_core[a], at)
                if sided:
                    self.side(a, r).start()

    def side_in(self, r):
        lo, count = stage(r)
        for a in range(self.count):
            self.side(a, r).wait_recv()
            self.add(a, lo, count, self.from_side[a], lo)
            if r == self.hops:
                self.hop(a, r - 1).start()

    def hop_in(self, r):
        for a in range(self.count):
            self.hop(a, r).wait_recv()
            base = self.hop_base(r)
            if r:
                mid = 1 << (r - 1)
                self.add(a, mid, mid, self.from_hop[a], base + mid)
                self.hop(a, r - 1).start()
                self.add(a, 0, mid, self.from_hop[a], base)
            else:
                which, low, high, _ = self.pieces[a]
                self.outs[which][:, low:high] = self.acc[a][0].astype(jnp.float32) + self.from_hop[
                    a
                ][base].astype(jnp.float32)

    def finish(self):
        for a in range(self.count):
            for r in range(self.hops):
                self.hop(a, r).wait_send()
            for r in range(self.hops + 1):
                self.side(a, r).wait_send()
                self.core(a, r, 0).wait_send()
                self.core(a, r, 1).wait_send()


def backward_kernel(n_dp, n_pair, pieces, n_in, *refs):
    k_count = len(pieces)
    len_ref, q_ref, k_ref, v_ref, g_ref, w_ref = refs[:6]
    ins = refs[6 : 6 + n_in]
    o_ref, z_ref, square_ref = refs[6 + n_in : 9 + n_in]
    outs = refs[9 + n_in : 9 + 2 * n_in]
    table, total, box, sem = refs[9 + 2 * n_in : 13 + 2 * n_in]
    rest = refs[13 + 2 * n_in :]
    weights = Scatter(n_dp, n_pair, pieces, ins, outs, rest[: 4 * k_count], rest[4 * k_count :])
    at = pl.program_id(0) * pl.num_programs(1) + pl.program_id(1)
    hops = weights.hops

    @pl.when(at == 0)
    def _():
        weights.load()
        greet([weights.near(bit) for bit in range(hops + 2)])
        for r in reversed(range(hops + 1)):
            weights.core_out(r)

    @pl.when(at == 2)
    def _():
        weights.loaded()
        weights.core_in(hops)

    @pl.when(at == 3)
    def _():
        for r in reversed(range(hops)):
            weights.core_in(r)

    @pl.when(at == 6)
    def _():
        weights.side_in(hops)

    @pl.when(at == 7)
    def _():
        for r in reversed(range(hops)):
            weights.side_in(r)

    seq = q_ref.shape[0]
    tiles = seq // 128
    doc = pl.program_id(1)
    @pl.when(doc == 0)
    def _():
        for h in range(2):
            band(w_ref, 2 * pl.program_id(0) + h, h, table, seq)
        total[...] = jnp.zeros_like(total)
    length = len_ref[doc]
    lane = lax.broadcasted_iota(jnp.int32, (seq, 128), 1)
    row = lax.broadcasted_iota(jnp.int32, (seq, 1), 0)
    q = q_ref[...] * jnp.bfloat16(0.125)
    k = k_ref[...]
    v = v_ref[...]
    g = g_ref[...]
    parts = []
    for h in range(2):
        mine = (lane < 64) == (h == 0)
        s = lax.dot_general(k, jnp.where(mine, q, 0), NT, preferred_element_type=jnp.float32)
        s = jnp.where(row < length, s + table[h], -1000000000.0)
        e = jnp.exp(s - jnp.max(s, axis=0, keepdims=True))
        p = e * (1.0 / jnp.sum(e, axis=0, keepdims=True))
        dv = jnp.dot(p.astype(jnp.bfloat16), g, preferred_element_type=jnp.float32)
        dp = lax.dot_general(v, jnp.where(mine, g, 0), NT, preferred_element_type=jnp.float32)
        ds = (p * (dp - jnp.sum(p * dp, axis=0, keepdims=True))).astype(jnp.bfloat16)
        total[h] += ds.astype(jnp.float32)
        dk = jnp.dot(ds, q, preferred_element_type=jnp.float32)
        dq = lax.dot_general(ds, k, TN, preferred_element_type=jnp.float32) * 0.125
        parts.append((dq, dk, dv))
    pair, pairs, docs = pl.program_id(0), pl.num_programs(0), pl.num_programs(1)
    step = pair * docs + doc
    slot = lax.rem(step, 2)

    def out(i):
        rows = pl.ds(pl.multiple_of(doc * seq, seq), seq)
        columns = pl.ds(pl.multiple_of((i * pairs + pair) * 128, 128), 128)
        return pltpu.make_async_copy(box.at[slot, i], o_ref.at[rows, columns], sem.at[slot, i])

    for i in range(3):
        @pl.when(step >= 2)
        def _():
            out(i).wait()
        box[slot, i] = jnp.where(lane < 64, parts[0][i], parts[1][i]).astype(o_ref.dtype)
        out(i).start()

    for r in range(1, hops):
        @pl.when(step == pairs * docs - 1 - r)
        def _():
            weights.hop_in(r)

    @pl.when(step == pairs * docs - 1)
    def _():
        weights.hop_in(0)
        weights.finish()
        square_ref[...] = jnp.zeros_like(square_ref)
        for ref in outs:
            square = jnp.sum(ref[...] * ref[...], axis=0, keepdims=True)
            square_ref[...] += jnp.sum(square, axis=1, keepdims=True)
        for i in range(3):
            out(i).wait()
            pltpu.make_async_copy(box.at[1 - slot, i], box.at[1 - slot, i], sem.at[1 - slot, i]).wait()
    @pl.when(doc == pl.num_programs(1) - 1)
    def _():
        r = lax.broadcasted_iota(jnp.int32, (128, 128), 0)
        c = lax.broadcasted_iota(jnp.int32, (128, 128), 1)
        flip = jnp.where(r + c == 127, 1.0, 0.0)
        z_ref[...] = jnp.zeros_like(z_ref)
        for h in range(2):
            def block(d):
                return sum(total[h, a * 128 : a * 128 + 128, (a - d) * 128 : (a - d) * 128 + 128] for a in range(tiles) if 0 <= a - d < tiles)
            for d in (-1, 0, 1):
                x = jnp.dot(flip, block(d), precision=HIGHEST, preferred_element_type=jnp.float32)
                x = jnp.concatenate([x, jnp.zeros_like(x)], axis=1)
                x = pltpu.roll(x, 0, 1, stride=1, stride_axis=0)
                z_ref[0, h, d + 1 : d + 2, :] = jnp.sum(x, axis=0, keepdims=True)
            z_ref[0, h, 3:4, 0:128] = jnp.sum(sum(block(-d) for d in range(2, tiles)), axis=0, keepdims=True)
            z_ref[0, h, 4:5, 0:128] = jnp.sum(sum(block(d) for d in range(2, tiles)), axis=0, keepdims=True)

def attention_back(lengths, qkv, g, w, seq, grads, pieces, cid):
    n_dp, n_pair = lax.axis_size("dp"), lax.axis_size("pair")
    tokens = qkv.shape[0]
    pairs = w.shape[0] // 2
    docs = tokens // seq
    spec = lambda base: pl.BlockSpec((seq, 128), lambda h, d, *_: (d, base + h))
    still = lambda shape: pl.BlockSpec(shape, lambda h, d, *_: (0, 0))
    boxes, sems = scatter_scratch(n_dp * n_pair, grads, pieces)
    return pl.pallas_call(
        functools.partial(backward_kernel, n_dp, n_pair, pieces, len(grads)),
        grid_spec=pltpu.PrefetchScalarGridSpec(
            num_scalar_prefetch=1,
            grid=(pairs, docs),
            in_specs=[spec(0), spec(pairs), spec(2 * pairs), spec(0), still(w.shape)]
            + [ANY] * len(grads),
            out_specs=[
                ANY,
                pl.BlockSpec((1, 2, 8, 256), lambda h, d, *_: (h, 0, 0, 0)),
                still((1, 1)),
            ]
            + [still(grad.shape[1:]) for grad in grads],
            scratch_shapes=[
                pltpu.VMEM((2, seq, seq), jnp.float32),
                pltpu.VMEM((2, seq, seq), jnp.float32),
                pltpu.VMEM((2, 3, seq, 128), jnp.bfloat16),
                pltpu.SemaphoreType.DMA((2, 3)),
            ]
            + boxes
            + sems,
        ),
        out_shape=[
            jax.ShapeDtypeStruct((tokens, 3 * pairs * 128), jnp.bfloat16),
            jax.ShapeDtypeStruct((pairs, 2, 8, 256), jnp.float32),
            jax.ShapeDtypeStruct((1, 1), jnp.float32),
        ]
        + [jax.ShapeDtypeStruct(grad.shape[1:], jnp.float32) for grad in grads],
        compiler_params=pltpu.CompilerParams(
            dimension_semantics=("arbitrary", "arbitrary"),
            collective_id=cid,
            has_side_effects=True,
            vmem_limit_bytes=VMEM_LIMIT,
        ),
        name="attention_back",
    )(lengths, qkv, qkv, qkv, g, w, *grads)


def back_kernel(n_dp, n_pair, pieces, n_in, chunk, *refs):
    k = len(pieces)
    grad_ref, key_ref, ask_ref, squares_ref = refs[:4]
    ins = refs[4 : 4 + n_in]
    out_ref, square_ref = refs[4 + n_in : 6 + n_in]
    outs = refs[6 + n_in : 6 + 2 * n_in]
    rest = refs[6 + 2 * n_in :]
    boxes, rest = rest[: 4 * k], rest[4 * k :]
    rows_out, rows_in, hot, part, stage_out, got_core, out_side, got_side, other = rest[:9]
    row_sem, core_sem, side_sem, last_sem, out_sem, *sems = rest[9:]
    dp, pair = lax.axis_index("dp"), lax.axis_index("pair")
    core = lax.rem(pair, 2)
    weights = Scatter(n_dp, n_pair, pieces, ins, outs, boxes, sems)
    groups, _, cap, width = rows_out.shape
    slots = ask_ref.shape[1]
    count = stage_out.shape[1]
    half = count * chunk
    tokens = key_ref.shape[1]
    peers = [{"dp": dp ^ j, "pair": pair} for j in range(1, n_dp)]
    partner, across = {"dp": dp, "pair": pair ^ 1}, {"dp": dp, "pair": pair ^ 2}
    weights.load()
    sem = pltpu.get_barrier_semaphore()
    for target in peers + [partner, across]:
        pl.semaphore_signal(sem, inc=1, device_id=target, device_id_type=MESH)

    def row(g, j):
        return remote(
            rows_out.at[g, j],
            rows_in.at[g, pl.ds(pl.multiple_of(j * cap, cap), cap)],
            row_sem.at[0, g, j],
            row_sem.at[1, g, j],
            {"dp": dp ^ j, "pair": pair},
        )

    def loop(size, body):
        def turn(i, carry):
            body(i)
            return carry

        lax.fori_loop(0, size, turn, 0)

    far = sorted(range(1, n_dp), reverse=True)

    pl.semaphore_wait(sem, n_dp + 1)

    def rows_of(t):
        j = n_dp - 1 - t
        slot = lax.broadcasted_iota(jnp.int32, (cap, tokens), 0) + (dp ^ j) * cap
        hits = jnp.where(slot == key_ref[...], 1.0, 0.0).astype(jnp.bfloat16)
        got = jnp.dot(hits, grad_ref[...], preferred_element_type=jnp.float32)
        got = got.astype(jnp.bfloat16)
        for g in range(groups):
            rows_out[g, j] = got[:, g * width : (g + 1) * width]

        @pl.when(j > 0)
        def _():
            row(0, j).start()

    loop(n_dp, rows_of)
    for g in range(1, groups):
        for j in far:
            row(g, j).start()
    for g in range(groups):
        rows_in[g, 0:cap] = rows_out[g, 0]
    for r in reversed(range(weights.hops + 1)):
        weights.core_out(r)

    def tell(c):
        ids = lax.broadcasted_iota(jnp.int32, (chunk, slots), 0) + c * chunk
        hot[c] = jnp.where(ids == ask_ref[...], 1.0, 0.0).astype(jnp.bfloat16)

    loop(2 * count, tell)

    def summed(g, c):
        return jnp.dot(hot[c], rows_in[g], preferred_element_type=jnp.float32)

    def to_core(g, i):
        return remote(
            stage_out.at[g, i], got_core.at[g, i], core_sem.at[0, g, i], core_sem.at[1, g, i], partner
        )

    def to_side(g, i):
        return remote(
            out_side.at[g, i], got_side.at[g, i], side_sem.at[0, g, i], side_sem.at[1, g, i], across
        )

    def to_other(g, i):
        return remote(
            out_side.at[g, i], other.at[g, i], last_sem.at[0, g, i], last_sem.at[1, g, i], partner
        )

    def write_out(box, g, i, which):
        rows = pl.ds(pl.multiple_of(which * half + i * chunk, chunk), chunk)
        return pltpu.make_async_copy(
            box.at[g, i], out_ref.at[rows, pl.ds(g * width, width)], out_sem.at[g, i]
        )

    def local_sums(g):
        for j in far:
            row(g, j).wait_recv()

        def combine(i):
            to_core(g, i).wait_recv()
            out_side[g, i] = (part[i] + got_core[g, i].astype(jnp.float32)).astype(jnp.bfloat16)
            to_side(g, i).start()

        def one(i):
            stage_out[g, i] = summed(g, (1 - core) * count + i).astype(jnp.bfloat16)
            to_core(g, i).start()
            part[i] = summed(g, core * count + i)

            @pl.when(i > 0)
            def _():
                combine(i - 1)

        loop(count, one)
        combine(count - 1)

    square_ref[...] = squares_ref[...]

    def finish_sums(g):
        def one(i):
            to_side(g, i).wait()
            wide = out_side[g, i].astype(jnp.float32) + got_side[g, i].astype(jnp.float32)
            value = wide.astype(jnp.bfloat16)
            out_side[g, i] = value
            to_other(g, i).start()
            write_out(out_side, g, i, core).start()
            wide = value.astype(jnp.float32)
            square = jnp.sum(wide * wide, axis=0, keepdims=True)
            square = jnp.sum(square, axis=1, keepdims=True)
            square_ref[...] += jnp.where(pair < 2, square, 0.0)

        loop(count, one)

    def hand_over(g):
        def one(i):
            to_other(g, i).wait_recv()
            write_out(out_side, g, i, core).wait()
            write_out(other, g, i, 1 - core).start()

        loop(count, one)

    weights.loaded()
    for r in reversed(range(weights.hops + 1)):
        weights.core_in(r)
    for g in range(groups):
        local_sums(g)
        if g:
            finish_sums(g - 1)
        if g == groups // 2:
            for r in reversed(range(weights.hops + 1)):
                weights.side_in(r)
    for r in reversed(range(1, weights.hops)):
        weights.hop_in(r)
    finish_sums(groups - 1)
    weights.hop_in(0)
    for ref in outs:
        square = jnp.sum(ref[...] * ref[...], axis=0, keepdims=True)
        square_ref[...] += jnp.sum(square, axis=1, keepdims=True)
    for g in range(groups):
        hand_over(g)
    for g in range(groups):
        for j in far:
            row(g, j).wait_send()

        def one(i):
            to_core(g, i).wait_send()
            to_other(g, i).wait_send()
            write_out(other, g, i, 1 - core).wait()

        loop(count, one)
    weights.finish()


def scatter_scratch(n, grads, pieces):
    k, hops, sem = len(pieces), (n - 1).bit_length() - 2, pltpu.SemaphoreType.DMA
    boxes = [
        pltpu.VMEM((lead, grads[p[0]].shape[1], p[2] - p[1]), jnp.bfloat16)
        for lead in (n // 2, n // 2, n // 4, n // 4 - 1)
        for p in pieces
    ]
    return boxes, [
        sem((k,)),
        sem((2, k, 2 * hops + 2)),
        sem((2, k, hops + 1)),
        sem((2, k, hops)),
    ]


def back(grad, key, asked, squares, grads, pieces, table_rows, groups, cid):
    n_dp, n_pair = lax.axis_size("dp"), lax.axis_size("pair")
    boxes, sems = scatter_scratch(n_dp * n_pair, grads, pieces)
    chunk = 512
    rows = -(-table_rows // (2 * chunk)) * 2 * chunk
    count = rows // 2 // chunk
    tokens, full = grad.shape
    width = full // groups
    slots = asked.shape[1]
    cap = slots // n_dp
    sem = pltpu.SemaphoreType.DMA
    box = pltpu.VMEM((groups, count, chunk, width), jnp.bfloat16)

    return pl.pallas_call(
        functools.partial(back_kernel, n_dp, n_pair, pieces, len(grads), chunk),
        out_shape=[
            jax.ShapeDtypeStruct((rows, full), jnp.bfloat16),
            jax.ShapeDtypeStruct((1, 1), jnp.float32),
        ]
        + [jax.ShapeDtypeStruct(g.shape[1:], jnp.float32) for g in grads],
        in_specs=[VM] * 4 + [ANY] * len(grads),
        out_specs=[ANY, VM] + [VM] * len(grads),
        scratch_shapes=boxes
        + [
            pltpu.VMEM((groups, n_dp, cap, width), jnp.bfloat16),
            pltpu.VMEM((groups, slots, width), jnp.bfloat16),
            pltpu.VMEM((2 * count, chunk, slots), jnp.bfloat16),
            pltpu.VMEM((count, chunk, width), jnp.float32),
            box,
            box,
            box,
            box,
            box,
            sem((2, groups, n_dp)),
            sem((2, groups, count)),
            sem((2, groups, count)),
            sem((2, groups, count)),
            sem((groups, count)),
        ]
        + sems,
        compiler_params=pltpu.CompilerParams(
            collective_id=cid, has_side_effects=True, vmem_limit_bytes=VMEM_LIMIT
        ),
        name="table_and_weights",
    )(grad, key, asked, squares, *grads)


BIAS_CORRECT = (1.0 - beta_one**STEP, 1.0 - beta_two**STEP)


def adam_parts(weight, first, second, grad, factor, rate, shrink):
    clipped = grad * factor
    first_new = beta_one * first + (1.0 - beta_one) * clipped
    second_new = beta_two * second + (1.0 - beta_two) * (clipped * clipped)
    root = jnp.sqrt(second_new * (1.0 / BIAS_CORRECT[1])) + adam_eps
    step = (rate / BIAS_CORRECT[0]) * first_new / root
    return (weight * (1.0 - rate * shrink) - step, first_new, second_new)


def packed_base(gains, width):
    return -(-gains * width // 128 // 8) * 8


def norm_kernel(n_dp, n_pair, n_gain, *refs):
    gain_refs = refs[:n_gain]
    bias_ref, square_ref, total_ref, block, by_dp, by_pair = refs[n_gain : n_gain + 6]
    rounds = Rounds(n_dp, n_pair, *refs[n_gain + 6 :])
    width = gain_refs[0].shape[1]
    base = packed_base(n_gain, width)
    block[...] = jnp.zeros_like(block)
    for c in range(width // 128):
        for g in range(n_gain):
            at = c * n_gain + g
            block[at : at + 1, :] = gain_refs[g][:, c * 128 : (c + 1) * 128]
    block[base : base + bias_ref.shape[0], : bias_ref.shape[1]] = bias_ref[...]
    block[base : base + 1, 127:128] = square_ref[...]
    rounds.entered()
    rounds.over_dp(block, by_dp)
    total = by_dp[0]
    for d in range(1, n_dp):
        total = total + by_dp[d]
    block[...] = total
    rounds.over_pair(block, by_pair)
    total = by_pair[0]
    for p in range(1, n_pair):
        total = total + by_pair[p]
    total_ref[...] = total


def small_total(gain_grads, bias_grad, square, cid):
    n_dp, n_pair = lax.axis_size("dp"), lax.axis_size("pair")
    count, width = len(gain_grads), gain_grads[0].shape[1]
    height = -(-(packed_base(count, width) + bias_grad.shape[0]) // 8) * 8
    return pl.pallas_call(
        functools.partial(norm_kernel, n_dp, n_pair, count),
        out_shape=jax.ShapeDtypeStruct((height, 128), jnp.float32),
        in_specs=[VM] * (count + 2),
        out_specs=VM,
        scratch_shapes=[
            pltpu.VMEM((height, 128), jnp.float32),
            pltpu.VMEM((n_dp, height, 128), jnp.float32),
            pltpu.VMEM((n_pair, height, 128), jnp.float32),
        ]
        + round_sems(n_dp, n_pair),
        compiler_params=pltpu.CompilerParams(collective_id=cid, has_side_effects=True),
        name="small_total",
    )(*gain_grads, bias_grad, square)


def update_kernel(mats, *refs):
    total_ref, loss_ref, low = refs[:3]
    table, small = refs[3:6], refs[6:12]
    grads = refs[12 : 12 + mats]
    states = refs[12 + mats : 12 + 4 * mats]
    rest = refs[12 + 4 * mats :]
    norm_out, loss_out, table_out, small_out = rest[0], rest[1], rest[2:5], rest[5:11]
    mat_out = rest[11:]
    gains, width = small[0].shape
    base = packed_base(gains, width)
    total = total_ref[...]
    row = lax.broadcasted_iota(jnp.int32, total.shape, 0)
    lane = lax.broadcasted_iota(jnp.int32, total.shape, 1)
    plain = jnp.where((row == base) & (lane == 127), total, total * total)
    norm = jnp.sqrt(jnp.sum(jnp.sum(plain, axis=1, keepdims=True), axis=0, keepdims=True))
    factor = jnp.minimum(1.0, clip_limit / norm)
    step = pl.program_id(0)

    @pl.when(step == 0)
    def _():
        norm_out[...] = norm
        loss_out[...] = loss_ref[...]
        for c in range(width // 128):
            columns = slice(c * 128, (c + 1) * 128)
            grad = total_ref[c * gains : (c + 1) * gains, :]
            new = adam_parts(*(ref[:, columns] for ref in small[:3]), grad, factor, 1.0, 0.0)
            for ref, value in zip(small_out[:3], new):
                ref[:, columns] = value
        heads = small[3].shape[1]
        grad = total_ref[base : base + small[3].shape[0], :heads]
        new = adam_parts(*(ref[...] for ref in small[3:]), grad, factor, 0.3, 0.0)
        for ref, value in zip(small_out[3:], new):
            ref[...] = value

    for which in range(mats):
        three = slice(3 * which, 3 * which + 3)
        new = adam_parts(*(ref[...] for ref in states[three]), grads[which][...], factor, 0.05, 0.01)
        for ref, value in zip(mat_out[three], new):
            ref[...] = value

    def body(j, carry):
        rows = pl.ds(pl.multiple_of(j * 16, 16), 16)
        new = adam_parts(*(ref[rows] for ref in table), low[rows].astype(jnp.float32), factor, 1.0, 0.01)
        for ref, value in zip(table_out, new):
            ref[rows] = value
        return carry

    lax.fori_loop(0, low.shape[0] // 16, body, 0)


def update(total, loss, table_grad, table, small, grads, states):
    rows, width = table[0].shape
    steps = 6
    tall = -(-rows // steps // 16) * 16
    flat = [array for group in states for array in group]
    like = lambda array: jax.ShapeDtypeStruct(array.shape, jnp.float32)
    whole = lambda array: pl.BlockSpec(array.shape, lambda i: (0, 0))
    table_spec = pl.BlockSpec((tall, width), lambda i: (i, 0))

    def part(array):
        if array.shape[1] % (128 * steps) == 0 and array.shape[0] < 32:
            return pl.BlockSpec((array.shape[0], array.shape[1] // steps), lambda i: (0, i))
        if array.shape[0] % (8 * steps) == 0:
            return pl.BlockSpec((array.shape[0] // steps, array.shape[1]), lambda i: (i, 0))
        return whole(array)

    return pl.pallas_call(
        functools.partial(update_kernel, len(grads)),
        grid=(steps,),
        out_shape=[like(loss), like(loss)] + [like(array) for array in (*table, *small, *flat)],
        in_specs=[whole(total), whole(loss)]
        + [table_spec] * 4
        + [whole(array) for array in small]
        + [part(array) for array in (*grads, *flat)],
        out_specs=[whole(loss)] * 2
        + [table_spec] * 3
        + [whole(array) for array in small]
        + [part(array) for array in flat],
        compiler_params=pltpu.CompilerParams(
            dimension_semantics=("arbitrary",), vmem_limit_bytes=VMEM_LIMIT
        ),
        name="update",
    )(total, loss, table_grad, *table, *small, *grads, *flat)


def local_plain(
    token_owner,
    token_row,
    lengths,
    positives,
    negatives,
    neg_counts,
    embed_table,
    embed_first,
    embed_second,
    qkv_weight,
    qkv_first,
    qkv_second,
    out_weight,
    out_first,
    out_second,
    in_weight,
    in_first,
    in_second,
    down_weight,
    down_first,
    down_second,
    norm_gains,
    gains_first,
    gains_second,
    position_bias,
    bias_first,
    bias_second,
):
    doc_count = lengths.shape[0]
    seq_len = token_row.shape[1]
    model_width = embed_table.shape[1]
    head_count = position_bias.shape[1]
    bucket_count = position_bias.shape[0]
    tok_total = doc_count * seq_len
    owners = lax.axis_size("dp")
    capacity = max(2, 2 * tok_total // owners)
    low_mats = (
        qkv_weight.astype(jnp.bfloat16),
        out_weight.astype(jnp.bfloat16),
        in_weight.astype(jnp.bfloat16),
        down_weight.astype(jnp.bfloat16),
    )
    qkv_full, out_full, in_full, down_full = (
        lax.all_gather(low_mats[0], ("dp", "pair"), axis=0, tiled=True),
        lax.all_gather(low_mats[1], ("dp", "pair"), axis=0, tiled=True),
        lax.all_gather(low_mats[2], ("dp", "pair"), axis=0, tiled=True),
        lax.all_gather(low_mats[3], ("dp", "pair"), axis=0, tiled=True),
    )
    tok_owner = token_owner.reshape(-1)
    tok_row = token_row.reshape(-1)
    owner_hits = (tok_owner[:, None] == jnp.arange(owners, dtype=jnp.int32)[None, :]).astype(
        jnp.int32
    )
    slot_rank = jnp.sum((jnp.cumsum(owner_hits, axis=0) - 1) * owner_hits, axis=1)
    requests = jnp.zeros((owners, capacity), jnp.int32).at[tok_owner, slot_rank].set(tok_row)
    asked_rows = lax.all_to_all(requests, "dp", split_axis=0, concat_axis=0, tiled=True)
    looked = jnp.take(embed_table, asked_rows.reshape(-1), axis=0).astype(jnp.bfloat16)
    answer = lax.all_to_all(
        looked.reshape(asked_rows.shape + (model_width,)),
        "dp",
        split_axis=0,
        concat_axis=0,
        tiled=True,
    )
    replies, asked_rows = (answer, asked_rows)
    embedded = replies[tok_owner, slot_rank].astype(jnp.float32)
    positions = jnp.arange(seq_len)
    live = positions[None, :] < lengths[:, None]
    pair_buckets = bucket_of(
        (positions[None, :] - positions[:, None]).reshape(-1), bucket_count, REACH
    )
    pair_hits = (jnp.arange(bucket_count)[:, None] == pair_buckets[None, :]).astype(jnp.float32)
    bias_full = jnp.dot(position_bias.T, pair_hits, precision=HIGHEST).reshape(
        head_count, seq_len, seq_len
    )
    bucket_map = pair_hits.astype(jnp.bfloat16)

    def split_doc(source, doc_index):
        doc_rows = source[doc_index * seq_len : (doc_index + 1) * seq_len]
        return tuple(
            (
                doc_rows[:, member * model_width : (member + 1) * model_width].reshape(
                    seq_len, head_count, -1
                )
                for member in range(3)
            )
        )

    normed_one, inverse_one = rms_forward(embedded, norm_gains[0])
    normed_one = normed_one.astype(jnp.bfloat16)
    qkv_rows = jnp.dot(normed_one, qkv_full, preferred_element_type=jnp.float32).astype(
        jnp.bfloat16
    )
    attended_parts = []
    logsum_parts = []
    for doc_index in range(doc_count):
        query_heads, key_heads, value_heads = split_doc(qkv_rows, doc_index)
        doc_out, logsum = attend_forward(
            query_heads, key_heads, value_heads, bias_full, live[doc_index]
        )
        attended_parts.append(doc_out.reshape(seq_len, model_width))
        logsum_parts.append(logsum)
    attended = jnp.concatenate(attended_parts, axis=0).astype(jnp.bfloat16)
    residual = embedded + jnp.dot(attended, out_full, preferred_element_type=jnp.float32)
    normed_two, inverse_two = rms_forward(residual, norm_gains[1])
    normed_two = normed_two.astype(jnp.bfloat16)
    hidden = jax.nn.relu(jnp.dot(normed_two, in_full, preferred_element_type=jnp.float32)).astype(
        jnp.bfloat16
    )
    output_rows = residual + jnp.dot(hidden, down_full, preferred_element_type=jnp.float32)
    normed_three, inverse_three = rms_forward(output_rows, norm_gains[2])
    live_rows = live.reshape(-1, 1)
    length_float = lengths.astype(jnp.float32)
    pooled_local = (
        jnp.sum(
            jnp.where(live_rows, normed_three, 0.0).reshape(doc_count, seq_len, model_width), axis=1
        )
        / length_float[:, None]
    )
    pooled_all = lax.all_gather(pooled_local, ("dp", "pair"), axis=0, tiled=True)
    loss_value, loss_pullback = jax.vjp(
        lambda pooled_in: margin_loss(pooled_in, positives, negatives, neg_counts), pooled_all
    )
    grad_pooled_all = loss_pullback(jnp.ones((), jnp.float32))[0]
    grad_pooled = lax.dynamic_slice_in_dim(
        grad_pooled_all, lax.axis_index(("dp", "pair")) * doc_count, doc_count, 0
    )
    grad_three = jnp.where(
        live_rows, jnp.repeat(grad_pooled / length_float[:, None], seq_len, axis=0), 0.0
    )
    qkv_back, out_back, in_back, down_back = (qkv_full, out_full, in_full, down_full)
    grad_output, gain_three = rms_backward(output_rows, inverse_three, norm_gains[2], grad_three)
    grad_branch = grad_output.astype(jnp.bfloat16)
    grad_down = lax.dot_general(
        hidden, grad_branch, CONTRACT_ROWS, preferred_element_type=jnp.float32
    )
    grad_hidden = lax.dot_general(
        grad_branch, down_back, CONTRACT_COLS, preferred_element_type=jnp.float32
    )
    grad_pre = jnp.where(hidden > 0, grad_hidden, 0.0).astype(jnp.bfloat16)
    grad_in = lax.dot_general(
        normed_two, grad_pre, CONTRACT_ROWS, preferred_element_type=jnp.float32
    )
    grad_normed_two = lax.dot_general(
        grad_pre, in_back, CONTRACT_COLS, preferred_element_type=jnp.float32
    )
    grad_res_part, gain_two = rms_backward(residual, inverse_two, norm_gains[1], grad_normed_two)
    grad_residual = grad_output + grad_res_part
    grad_attn_branch = grad_residual.astype(jnp.bfloat16)
    grad_out = lax.dot_general(
        attended, grad_attn_branch, CONTRACT_ROWS, preferred_element_type=jnp.float32
    )
    grad_attended = lax.dot_general(
        grad_attn_branch, out_back, CONTRACT_COLS, preferred_element_type=jnp.float32
    ).astype(jnp.bfloat16)
    grad_qkv_parts = []
    bias_grad_heads = jnp.zeros((head_count, bucket_count), jnp.float32)
    for doc_index in range(doc_count):
        query_heads, key_heads, value_heads = split_doc(qkv_rows, doc_index)
        grad_doc = grad_attended[doc_index * seq_len : (doc_index + 1) * seq_len].reshape(
            seq_len, head_count, -1
        )
        grad_query, grad_key, grad_value, grad_low = attend_backward(
            query_heads,
            key_heads,
            value_heads,
            bias_full,
            live[doc_index],
            logsum_parts[doc_index],
            grad_doc,
        )
        grad_qkv_parts.append(
            jnp.concatenate(
                [
                    grad_query.reshape(seq_len, model_width),
                    grad_key.reshape(seq_len, model_width),
                    grad_value.reshape(seq_len, model_width),
                ],
                axis=1,
            )
        )
        bias_grad_heads = bias_grad_heads + lax.dot_general(
            grad_low.reshape(head_count, -1),
            bucket_map,
            CONTRACT_COLS,
            preferred_element_type=jnp.float32,
        )
    bias_grad_local = bias_grad_heads.T
    grad_qkv_rows = jnp.concatenate(grad_qkv_parts, axis=0).astype(jnp.bfloat16)
    grad_qkv = lax.dot_general(
        normed_one, grad_qkv_rows, CONTRACT_ROWS, preferred_element_type=jnp.float32
    )
    grad_normed_one = lax.dot_general(
        grad_qkv_rows, qkv_back, CONTRACT_COLS, preferred_element_type=jnp.float32
    )
    grad_emb_part, gain_one = rms_backward(embedded, inverse_one, norm_gains[0], grad_normed_one)
    grad_embedded = grad_residual + grad_emb_part
    sendback = (
        jnp.zeros((owners, capacity, model_width), jnp.float32)
        .at[tok_owner, slot_rank]
        .set(grad_embedded)
    )
    arrived = lax.all_to_all(sendback, "dp", split_axis=0, concat_axis=0, tiled=True)
    table_grad = jax.ops.segment_sum(
        arrived.reshape(-1, model_width), asked_rows.reshape(-1), num_segments=embed_table.shape[0]
    )
    table_grad = lax.psum(table_grad, "pair")
    weight_grads = (
        lax.psum_scatter(grad_qkv, ("dp", "pair"), scatter_dimension=0, tiled=True),
        lax.psum_scatter(grad_out, ("dp", "pair"), scatter_dimension=0, tiled=True),
        lax.psum_scatter(grad_in, ("dp", "pair"), scatter_dimension=0, tiled=True),
        lax.psum_scatter(grad_down, ("dp", "pair"), scatter_dimension=0, tiled=True),
    )
    pair_first = (lax.axis_index("pair") == 0).astype(jnp.float32)
    square_part = jnp.sum(
        jnp.stack([jnp.sum(grad_piece * grad_piece) for grad_piece in weight_grads])
    ) + pair_first * jnp.sum(table_grad * table_grad)
    gain_grad, bias_grad, square_sum = lax.psum(
        (jnp.stack([gain_one, gain_two, gain_three]), bias_grad_local, square_part), ("dp", "pair")
    )
    clip_norm = jnp.sqrt(
        square_sum + jnp.sum(gain_grad * gain_grad) + jnp.sum(bias_grad * bias_grad)
    )
    factor = jnp.minimum(1.0, clip_limit / clip_norm)
    table_out = adam_step(embed_table, embed_first, embed_second, table_grad * factor, 1.0, 0.01)
    qkv_out = adam_step(qkv_weight, qkv_first, qkv_second, weight_grads[0] * factor, 0.05, 0.01)
    out_out = adam_step(out_weight, out_first, out_second, weight_grads[1] * factor, 0.05, 0.01)
    in_out = adam_step(in_weight, in_first, in_second, weight_grads[2] * factor, 0.05, 0.01)
    down_out = adam_step(down_weight, down_first, down_second, weight_grads[3] * factor, 0.05, 0.01)
    gains_out = adam_step(norm_gains, gains_first, gains_second, gain_grad * factor, 1.0, 0.0)
    bias_out = adam_step(position_bias, bias_first, bias_second, bias_grad * factor, 0.3, 0.0)
    return (
        loss_value,
        clip_norm,
        table_out[0],
        table_out[1],
        table_out[2],
        qkv_out[0],
        qkv_out[1],
        qkv_out[2],
        out_out[0],
        out_out[1],
        out_out[2],
        in_out[0],
        in_out[1],
        in_out[2],
        down_out[0],
        down_out[1],
        down_out[2],
        gains_out[0],
        gains_out[1],
        gains_out[2],
        bias_out[0],
        bias_out[1],
        bias_out[2],
    )


def local_fast(
    token_owner,
    token_row,
    lengths,
    positives,
    negatives,
    neg_counts,
    embed_table,
    embed_first,
    embed_second,
    qkv_weight,
    qkv_first,
    qkv_second,
    out_weight,
    out_first,
    out_second,
    in_weight,
    in_first,
    in_second,
    down_weight,
    down_first,
    down_second,
    norm_gains,
    gains_first,
    gains_second,
    position_bias,
    bias_first,
    bias_second,
):
    doc_count = lengths.shape[0]
    seq_len = token_row.shape[1]
    model_width = embed_table.shape[1]
    head_count = position_bias.shape[1]
    bucket_count = position_bias.shape[0]
    tok_total = doc_count * seq_len
    owners = lax.axis_size("dp")
    capacity = max(2, 2 * tok_total // owners)
    holders = lax.axis_size("pair")
    shards = (qkv_weight, out_weight, in_weight, down_weight)
    embedded_low, slot_keys, asked_rows, *full = front(
        token_owner.reshape(1, -1),
        token_row.reshape(1, -1),
        embed_table,
        shards,
        weight_pieces([shard.shape[1] for shard in shards]),
        capacity,
        owners,
        holders,
        1,
    )
    qkv_full, out_full, in_full, down_full = (
        matrix.reshape(-1, matrix.shape[2]) for matrix in full
    )
    embedded = embedded_low.astype(jnp.float32)
    positions = jnp.arange(seq_len)
    live = positions[None, :] < lengths[:, None]
    normed_one, inverse_one = rms_forward(embedded, norm_gains[0])
    normed_one = normed_one.astype(jnp.bfloat16)
    qkv_rows = jnp.dot(normed_one, qkv_full, preferred_element_type=jnp.float32).astype(
        jnp.bfloat16
    )
    attended = attention(lengths, qkv_rows, bias_rows(position_bias.T, seq_len, 1), seq_len)
    residual = embedded + jnp.dot(attended, out_full, preferred_element_type=jnp.float32)
    normed_two, inverse_two = rms_forward(residual, norm_gains[1])
    normed_two = normed_two.astype(jnp.bfloat16)
    hidden = jax.nn.relu(jnp.dot(normed_two, in_full, preferred_element_type=jnp.float32)).astype(
        jnp.bfloat16
    )
    output_rows = residual + jnp.dot(hidden, down_full, preferred_element_type=jnp.float32)
    normed_three, inverse_three = rms_forward(output_rows, norm_gains[2])
    live_rows = live.reshape(-1, 1)
    length_float = lengths.astype(jnp.float32)
    pooled_local = (
        jnp.sum(
            jnp.where(live_rows, normed_three, 0.0).reshape(doc_count, seq_len, model_width), axis=1
        )
        / length_float[:, None]
    )
    loss_cell, grad_pooled = pooled_loss(
        pooled_local, positives, negatives, neg_counts, 3
    )
    grad_three = jnp.where(
        live_rows, jnp.repeat(grad_pooled / length_float[:, None], seq_len, axis=0), 0.0
    )
    qkv_back, out_back, in_back, down_back = (qkv_full, out_full, in_full, down_full)
    grad_output, gain_three = rms_backward(output_rows, inverse_three, norm_gains[2], grad_three)
    grad_branch = grad_output.astype(jnp.bfloat16)
    grad_down = lax.dot_general(
        hidden, grad_branch, CONTRACT_ROWS, preferred_element_type=jnp.float32
    )
    grad_hidden = lax.dot_general(
        grad_branch, down_back, CONTRACT_COLS, preferred_element_type=jnp.float32
    )
    grad_pre = jnp.where(hidden > 0, grad_hidden, 0.0).astype(jnp.bfloat16)
    grad_in = lax.dot_general(
        normed_two, grad_pre, CONTRACT_ROWS, preferred_element_type=jnp.float32
    )
    grad_normed_two = lax.dot_general(
        grad_pre, in_back, CONTRACT_COLS, preferred_element_type=jnp.float32
    )
    grad_res_part, gain_two = rms_backward(residual, inverse_two, norm_gains[1], grad_normed_two)
    grad_residual = grad_output + grad_res_part
    grad_attn_branch = grad_residual.astype(jnp.bfloat16)
    grad_out = lax.dot_general(
        attended, grad_attn_branch, CONTRACT_ROWS, preferred_element_type=jnp.float32
    )
    grad_attended = lax.dot_general(
        grad_attn_branch, out_back, CONTRACT_COLS, preferred_element_type=jnp.float32
    ).astype(jnp.bfloat16)
    parts = owners * holders

    def blocks(*grads):
        return [grad.astype(jnp.bfloat16).reshape(parts, -1, grad.shape[1]) for grad in grads]

    grad_qkv_rows, diagonals, squares, down_grad = attention_back(
        lengths,
        qkv_rows,
        grad_attended,
        bias_rows(position_bias.T, seq_len, -1),
        seq_len,
        blocks(grad_down),
        early_pieces(model_width),
        5,
    )
    bias_grad_local = bias_gradient(diagonals, seq_len, bucket_count)
    grad_qkv = lax.dot_general(
        normed_one, grad_qkv_rows, CONTRACT_ROWS, preferred_element_type=jnp.float32
    )
    grad_normed_one = lax.dot_general(
        grad_qkv_rows, qkv_back, CONTRACT_COLS, preferred_element_type=jnp.float32
    )
    grad_emb_part, gain_one = rms_backward(embedded, inverse_one, norm_gains[0], grad_normed_one)
    grad_embedded = grad_residual + grad_emb_part
    table_grad, square_part, qkv_grad, out_grad, in_grad = back(
        grad_embedded.astype(jnp.bfloat16),
        slot_keys,
        asked_rows.reshape(1, -1),
        squares,
        blocks(grad_qkv, grad_out, grad_in),
        late_pieces([grad.shape[1] for grad in (grad_qkv, grad_out, grad_in)]),
        embed_table.shape[0],
        model_width // 128,
        2,
    )
    weight_grads = (qkv_grad, out_grad, in_grad, down_grad)
    total = small_total(
        [gain.reshape(1, -1) for gain in (gain_one, gain_two, gain_three)],
        bias_grad_local,
        square_part,
        4,
    )
    norm_cell, loss_cell, *updated = update(
        total,
        loss_cell,
        table_grad,
        (embed_table, embed_first, embed_second),
        (
            norm_gains,
            gains_first,
            gains_second,
            position_bias.T,
            bias_first.T,
            bias_second.T,
        ),
        weight_grads,
        (
            (qkv_weight, qkv_first, qkv_second),
            (out_weight, out_first, out_second),
            (in_weight, in_first, in_second),
            (down_weight, down_first, down_second),
        ),
    )
    return (loss_cell[0, 0], norm_cell[0, 0], *updated[:3], *updated[9:], *updated[3:6], *(new.T for new in updated[6:9]))


def local(*arrays):
    n_dp, n_pair = lax.axis_size("dp"), lax.axis_size("pair")
    lengths, qkv_weight, down_weight = arrays[2], arrays[9], arrays[18]
    fits = (
        n_pair == 4
        and n_dp & (n_dp - 1) == 0
        and qkv_weight.shape[0] % 8 == 0
        and down_weight.shape[0] % 8 == 0
        and lengths.shape[0] == 2
        and 2 * arrays[1].size // n_dp % 128 == 0
    )
    return (local_fast if fits else local_plain)(*arrays)


def solution(mesh):
    return jax.shard_map(
        local,
        mesh=mesh,
        in_specs=(
            P(("dp", "pair"), None, None),
            P(("dp", "pair"), None),
            P(("dp", "pair")),
            P(),
            P(),
            P(),
            P("dp", None),
            P("dp", None),
            P("dp", None),
            P(("dp", "pair"), None),
            P(("dp", "pair"), None),
            P(("dp", "pair"), None),
            P(("dp", "pair"), None),
            P(("dp", "pair"), None),
            P(("dp", "pair"), None),
            P(("dp", "pair"), None),
            P(("dp", "pair"), None),
            P(("dp", "pair"), None),
            P(("dp", "pair"), None),
            P(("dp", "pair"), None),
            P(("dp", "pair"), None),
            P(),
            P(),
            P(),
            P(),
            P(),
            P(),
        ),
        out_specs=(
            P(),
            P(),
            P("dp", None),
            P("dp", None),
            P("dp", None),
            P(("dp", "pair"), None),
            P(("dp", "pair"), None),
            P(("dp", "pair"), None),
            P(("dp", "pair"), None),
            P(("dp", "pair"), None),
            P(("dp", "pair"), None),
            P(("dp", "pair"), None),
            P(("dp", "pair"), None),
            P(("dp", "pair"), None),
            P(("dp", "pair"), None),
            P(("dp", "pair"), None),
            P(("dp", "pair"), None),
            P(),
            P(),
            P(),
            P(),
            P(),
            P(),
        ),
        check_vma=False,
    )
```

```python
import functools
import math

import jax
import jax.numpy as jnp
import numpy as np
from jax import lax
from jax.experimental import pallas as pl
from jax.experimental.pallas import tpu as pltpu
from jax.sharding import PartitionSpec as P

REACH = 128
STEP = 5


rms_eps = 1e-06
clip_limit = 0.05
margin = 1.0
sim_scale = 20.0
beta_one = 0.9
beta_two = 0.999
adam_eps = 1e-08
HIGHEST = lax.Precision.HIGHEST
CONTRACT_ROWS = (((0,), (0,)), ((), ()))
CONTRACT_COLS = (((1,), (1,)), ((), ()))


def bucket_of(offsets, bucket_count, reach_limit):
    half_count = bucket_count // 2
    exact_count = half_count // 2
    sign_base = jnp.where(offsets > 0, half_count, 0).astype(jnp.int32)
    distance = jnp.abs(offsets)
    far_bucket = jnp.full(offsets.shape, exact_count, jnp.int32)
    for level_index in range(1, half_count - exact_count):
        threshold = int(
            math.ceil(
                exact_count
                * (reach_limit / exact_count) ** (level_index / (half_count - exact_count))
                - 1e-09
            )
        )
        far_bucket = far_bucket + (distance >= threshold).astype(jnp.int32)
    return sign_base + jnp.where(distance < exact_count, distance, far_bucket)


def rms_forward(values, gain):
    inverse = lax.rsqrt(jnp.mean(values * values, axis=-1, keepdims=True) + rms_eps)
    return (values * inverse * gain, inverse)


def rms_backward(values, inverse, gain, upstream):
    scaled = upstream * gain
    normed = values * inverse
    grad_values = inverse * (scaled - normed * jnp.mean(scaled * normed, axis=-1, keepdims=True))
    return (grad_values, jnp.sum(upstream * normed, axis=0))


def margin_loss(pooled, positives, negatives, neg_counts):
    unit = pooled * lax.rsqrt(jnp.sum(pooled * pooled, axis=-1, keepdims=True) + 1e-06)
    similar = sim_scale * jnp.dot(unit, unit.T, precision=HIGHEST)
    chosen = jnp.take_along_axis(similar, positives[:, None], axis=1)
    against = jnp.take_along_axis(similar, negatives, axis=1)
    live_slots = jnp.arange(negatives.shape[1])[None, :] < neg_counts[:, None]
    terms = jnp.where(live_slots, jax.nn.softplus(margin - chosen + against), 0.0)
    return jnp.mean(jnp.sum(terms, axis=1) / neg_counts.astype(jnp.float32))


def doc_scores(query_heads, key_heads, bias_full, live_keys):
    scores = (
        jnp.einsum("qhd,khd->hqk", query_heads, key_heads, preferred_element_type=jnp.float32)
        * 0.125
        + bias_full
    )
    return jnp.where(live_keys[None, None, :], scores, -1000000000.0)


def attend_forward(query_heads, key_heads, value_heads, bias_full, live_keys):
    scores = doc_scores(query_heads, key_heads, bias_full, live_keys)
    highest = jnp.max(scores, axis=-1, keepdims=True)
    weights = jnp.exp(scores - highest)
    totals = jnp.sum(weights, axis=-1, keepdims=True)
    probabilities = (weights / totals).astype(jnp.bfloat16)
    attended = jnp.einsum(
        "hqk,khd->qhd", probabilities, value_heads, preferred_element_type=jnp.float32
    )
    return (attended, highest + jnp.log(totals))


def attend_backward(
    query_heads, key_heads, value_heads, bias_full, live_keys, logsum, grad_attended
):
    probabilities = jnp.exp(doc_scores(query_heads, key_heads, bias_full, live_keys) - logsum)
    grad_value = jnp.einsum(
        "hqk,qhd->khd",
        probabilities.astype(jnp.bfloat16),
        grad_attended,
        preferred_element_type=jnp.float32,
    )
    grad_prob = jnp.einsum(
        "qhd,khd->hqk", grad_attended, value_heads, preferred_element_type=jnp.float32
    )
    grad_score = probabilities * (
        grad_prob - jnp.sum(probabilities * grad_prob, axis=-1, keepdims=True)
    )
    grad_low = grad_score.astype(jnp.bfloat16)
    grad_query = (
        jnp.einsum("hqk,khd->qhd", grad_low, key_heads, preferred_element_type=jnp.float32) * 0.125
    )
    grad_key = (
        jnp.einsum("hqk,qhd->khd", grad_low, query_heads, preferred_element_type=jnp.float32)
        * 0.125
    )
    return (grad_query, grad_key, grad_value, grad_low)


def adam_step(weight, first, second, grad, rate, shrink):
    first_new = beta_one * first + (1.0 - beta_one) * grad
    second_new = beta_two * second + (1.0 - beta_two) * grad * grad
    first_hat = first_new / (1.0 - beta_one**STEP)
    second_hat = second_new / (1.0 - beta_two**STEP)
    weight_new = weight - rate * (first_hat / (jnp.sqrt(second_hat) + adam_eps) + shrink * weight)
    return (weight_new, first_new, second_new)


MESH = pl.DeviceIdType.MESH
VMEM_LIMIT = 64 * 1024 * 1024 - 65536
ANY = pl.BlockSpec(memory_space=pl.ANY)
VM = pl.BlockSpec(memory_space=pltpu.VMEM)


def place(index, n_pair):
    return {"dp": index // n_pair, "pair": lax.rem(index, n_pair)}


def remote(src, dst, send, recv, target):
    return pltpu.make_async_remote_copy(
        src, dst, send, recv, device_id=target, device_id_type=MESH
    )


def greet(targets):
    sem = pltpu.get_barrier_semaphore()
    for target in targets:
        pl.semaphore_signal(sem, inc=1, device_id=target, device_id_type=MESH)
    pl.semaphore_wait(sem, len(targets))


def my_index(n_pair):
    return lax.axis_index("dp") * n_pair + lax.axis_index("pair")


def bit_order(n_dp, n_pair, color):
    dp_bits, pair_bits = (n_dp - 1).bit_length(), (n_pair - 1).bit_length()
    high = list(reversed(range(pair_bits + 1, pair_bits + dp_bits))) + [pair_bits]
    side = list(reversed(range(1, pair_bits)))
    return high + side if color == 0 else side + high


def offset(order, position):
    return sum(((position >> step) & 1) << bit for step, bit in enumerate(order))


class Rounds:
    def __init__(self, n_dp, n_pair, dp_sem, pair_sem, own_sem):
        self.n_dp, self.n_pair = n_dp, n_pair
        self.dp_sem, self.pair_sem, self.own_sem = dp_sem, pair_sem, own_sem
        self.dp, self.pair = lax.axis_index("dp"), lax.axis_index("pair")
        sem = pltpu.get_barrier_semaphore()
        targets = [{"dp": self.dp ^ j, "pair": self.pair} for j in range(1, n_dp)]
        targets += [{"dp": self.dp, "pair": self.pair ^ j} for j in range(1, n_pair)]
        for target in targets:
            pl.semaphore_signal(sem, inc=1, device_id=target, device_id_type=MESH)
        self.entered = lambda: pl.semaphore_wait(sem, len(targets))

    def over_dp(self, block, by_dp):
        def copy(j, slot):
            target = {"dp": self.dp ^ j, "pair": self.pair}
            return remote(block, by_dp.at[slot], self.dp_sem.at[0, j], self.dp_sem.at[1, j], target)

        self.exchange(block, by_dp, self.dp, self.n_dp, copy)

    def over_pair(self, block, by_pair):
        def copy(j, slot):
            target = {"dp": self.dp, "pair": self.pair ^ j}
            return remote(
                block, by_pair.at[slot], self.pair_sem.at[0, j], self.pair_sem.at[1, j], target
            )

        self.exchange(block, by_pair, self.pair, self.n_pair, copy)

    def exchange(self, block, places, me, size, copy):
        own = pltpu.make_async_copy(block, places.at[me], self.own_sem)
        own.start()
        for j in reversed(range(1, size)):
            copy(j, me).start()
        own.wait()
        for j in range(1, size):
            copy(j, me ^ j).wait_recv()
        for j in range(1, size):
            copy(j, me).wait_send()


def round_sems(n_dp, n_pair):
    sem = pltpu.SemaphoreType.DMA
    return [sem((2, n_dp)), sem((2, n_pair)), sem]


def loss_kernel(
    n_dp, n_pair, x_ref, pos_ref, neg_ref, count_ref, loss_ref, grad_ref, by_dp, by_pair, unit, *sems
):
    rounds = Rounds(n_dp, n_pair, *sems)
    rounds.entered()
    rounds.over_dp(x_ref, by_dp)
    rounds.over_pair(by_dp, by_pair)
    docs, width = x_ref.shape
    total = n_dp * n_pair * docs
    for d in range(n_dp):
        for p in range(n_pair):
            base = (d * n_pair + p) * docs
            unit[base : base + docs] = by_pair[p, d]
    pooled = unit[...]
    inverse = lax.rsqrt(jnp.sum(pooled * pooled, axis=1, keepdims=True) + 1e-06)
    units = pooled * inverse
    similar = 20.0 * lax.dot_general(
        units, units, NT, precision=HIGHEST, preferred_element_type=jnp.float32
    )
    partner = lax.broadcasted_iota(jnp.int32, (total, total), 0)
    is_pos = partner == pos_ref[...]
    chosen = jnp.sum(jnp.where(is_pos, similar, 0.0), axis=0, keepdims=True)
    counts = count_ref[...]
    weight = 1.0 / (counts.astype(jnp.float32) * total)
    losses = jnp.zeros((1, total), jnp.float32)
    slopes = jnp.zeros((1, total), jnp.float32)
    grad_similar = jnp.zeros((total, total), jnp.float32)
    for slot in range(neg_ref.shape[0]):
        is_neg = partner == neg_ref[slot : slot + 1, :]
        against = jnp.sum(jnp.where(is_neg, similar, 0.0), axis=0, keepdims=True)
        value = margin - chosen + against
        used = slot < counts
        soft = jnp.maximum(value, 0.0) + jnp.log1p(jnp.exp(-jnp.abs(value)))
        losses = losses + jnp.where(used, soft, 0.0)
        slope = jnp.where(used, weight / (1.0 + jnp.exp(-value)), 0.0)
        grad_similar = grad_similar + jnp.where(is_neg, slope, 0.0)
        slopes = slopes + slope
    grad_similar = grad_similar - jnp.where(is_pos, slopes, 0.0)
    loss_ref[...] = jnp.sum(losses * weight, axis=1, keepdims=True)
    grad_units = sim_scale * (
        jnp.dot(grad_similar, units, precision=HIGHEST, preferred_element_type=jnp.float32)
        + lax.dot_general(
            grad_similar, units, TN, precision=HIGHEST, preferred_element_type=jnp.float32
        )
    )
    inner = jnp.sum(grad_units * units, axis=1, keepdims=True)
    unit[...] = inverse * (grad_units - units * inner)
    for d in range(n_dp):
        for p in range(n_pair):
            base = (d * n_pair + p) * docs

            @pl.when((rounds.dp == d) & (rounds.pair == p))
            def _():
                grad_ref[...] = unit[base : base + docs]


def pooled_loss(pooled, positives, negatives, counts, cid):
    n_dp, n_pair = lax.axis_size("dp"), lax.axis_size("pair")
    docs, width = pooled.shape
    return pl.pallas_call(
        functools.partial(loss_kernel, n_dp, n_pair),
        out_shape=[
            jax.ShapeDtypeStruct((1, 1), jnp.float32),
            jax.ShapeDtypeStruct(pooled.shape, jnp.float32),
        ],
        in_specs=[VM] * 4,
        out_specs=[VM] * 2,
        scratch_shapes=[
            pltpu.VMEM((n_dp, docs, width), jnp.float32),
            pltpu.VMEM((n_pair, n_dp, docs, width), jnp.float32),
            pltpu.VMEM((n_dp * n_pair * docs, width), jnp.float32),
        ]
        + round_sems(n_dp, n_pair),
        compiler_params=pltpu.CompilerParams(collective_id=cid, has_side_effects=True),
        name="pooled_loss",
    )(pooled, positives.reshape(1, -1), negatives.T, counts.reshape(1, -1))


NT = (((1,), (1,)), ((), ()))
TN = (((0,), (0,)), ((), ()))

def band(w_ref, row, base, h, table, seq):
    tiles = seq // 128
    for d in range(1 - tiles, tiles):
        low = base + seq + 128 * d - 128
        x = jnp.broadcast_to(w_ref[pl.ds(row, 1), low : low + 256], (128, 256))
        tile = pltpu.roll(x, 0, 1, stride=1, stride_axis=0)[:, 128:]
        for a in range(tiles):
            if 0 <= a + d < tiles:
                table[h, a * 128 : a * 128 + 128, (a + d) * 128 : (a + d) * 128 + 128] = tile

def forward_kernel(len_ref, q_ref, k_ref, v_ref, w_ref, o_ref, table):
    seq = q_ref.shape[0]
    doc = pl.program_id(1)
    @pl.when(doc == 0)
    def _():
        for h in range(2):
            band(w_ref, 2 * pl.program_id(0) + h, 0, h, table, seq)
    length = len_ref[doc]
    lane = lax.broadcasted_iota(jnp.int32, (seq, 128), 1)
    column = lax.broadcasted_iota(jnp.int32, (1, seq), 1)
    q = q_ref[...] * jnp.bfloat16(0.125)
    k = k_ref[...]
    v = v_ref[...]
    got = []
    for h in range(2):
        mine = (lane < 64) == (h == 0)
        s = lax.dot_general(jnp.where(mine, q, 0), k, NT, preferred_element_type=jnp.float32)
        s = jnp.where(column < length, s + table[h], -1000000000.0)
        e = jnp.exp(s - jnp.max(s, axis=1, keepdims=True))
        p = (e * (1.0 / jnp.sum(e, axis=1, keepdims=True))).astype(jnp.bfloat16)
        got.append(jnp.dot(p, v, preferred_element_type=jnp.float32))
    o_ref[...] = jnp.where(lane < 64, got[0], got[1]).astype(o_ref.dtype)

def attention(lengths, qkv, w, seq):
    tokens = qkv.shape[0]
    pairs = w.shape[0] // 2
    docs = tokens // seq
    spec = lambda base: pl.BlockSpec((seq, 128), lambda h, d, *_: (d, base + h))
    return pl.pallas_call(
        forward_kernel,
        grid_spec=pltpu.PrefetchScalarGridSpec(
            num_scalar_prefetch=1, grid=(pairs, docs),
            in_specs=[spec(0), spec(pairs), spec(2 * pairs), pl.BlockSpec(w.shape, lambda h, d, *_: (0, 0))],
            out_specs=spec(0),
            scratch_shapes=[pltpu.VMEM((2, seq, seq), jnp.float32)]),
        out_shape=jax.ShapeDtypeStruct((tokens, pairs * 128), jnp.bfloat16),
        compiler_params=pltpu.CompilerParams(dimension_semantics=("arbitrary", "arbitrary"), vmem_limit_bytes=50 * 1024 * 1024),
        name="attention",
    )(lengths, qkv, qkv, qkv, w)

def bucket_hits(offsets, buckets):
    half = buckets // 2
    exact = half // 2
    distance = np.abs(offsets)
    far = np.full(offsets.shape, exact)
    for level in range(1, half - exact):
        limit = math.ceil(exact * (REACH / exact) ** (level / (half - exact)) - 1e-09)
        far = far + (distance >= limit)
    bucket = np.where(offsets > 0, half, 0) + np.where(distance < exact, distance, far)
    return (bucket[:, None] == np.arange(buckets)[None, :]).astype(np.float32)


def bias_rows(bias, seq):
    offsets = np.arange(2 * seq) - seq
    hits = bucket_hits(np.concatenate([offsets, -offsets]), bias.shape[1])
    return jnp.dot(bias, hits.T, precision=HIGHEST)


def bias_gradient(sums, seq, buckets):
    heads, width = sums.shape[0] * 2, sums.shape[2] * sums.shape[3]
    j = np.arange(256)
    offsets = [np.where(j < 255, 128 * d + 127 - j, 0) for d in (-1, 0, 1)]
    offsets += [np.full((256,), 1 - seq), np.full((256,), seq - 1)]
    hits = bucket_hits(np.concatenate(offsets), buckets)
    hits = np.concatenate([hits, np.zeros((width - hits.shape[0], buckets), np.float32)])
    return jnp.dot(sums.reshape(heads, width), hits, precision=HIGHEST)


def weight_pieces(widths):
    cut = widths[3] * 2 // 3 // 128 * 128
    return [
        (0, 0, widths[0], 1),
        (2, 0, widths[2], 0),
        (1, 0, widths[1], 0),
        (3, 0, cut, 0),
        (3, cut, widths[3], 1),
    ]


def early_pieces(width):
    cut = width // 2 // 128 * 128
    return [(0, 0, cut, 0), (0, cut, width, 1)]


def late_pieces(widths):
    return [(2, 0, widths[2], 0), (0, 0, widths[0], 1), (1, 0, widths[1], 1)]


NN = (((1,), (0,)), ((), ()))


def stage(r):
    return (0, 1) if r == 0 else (1 << (r - 1), 1 << (r - 1))


class Gather:
    def __init__(self, n_dp, n_pair, pieces, outs, bufs, sems):
        self.n_pair, self.pieces, self.outs, self.bufs = n_pair, pieces, outs, bufs
        self.hop_sem, self.side_sem, self.core_sem, self.out_sem = sems
        self.me = my_index(n_pair)
        self.hops = (n_dp * n_pair - 1).bit_length() - 2
        self.orders = [bit_order(n_dp, n_pair, piece[3]) for piece in pieces]
        self.count = len(pieces)

    def send(self, a, lo, count, to, sem, which, bit):
        return remote(
            self.bufs[a].at[pl.ds(lo, count)],
            self.bufs[a].at[pl.ds(to, count)],
            sem.at[0, a, which],
            sem.at[1, a, which],
            place(self.me ^ (1 << bit), self.n_pair),
        )

    def hop(self, a, r):
        return self.send(a, 0, 1 << r, 1 << r, self.hop_sem, r, self.orders[a][r])

    def side(self, a, r):
        lo, count = stage(r)
        return self.send(a, lo, count, (1 << self.hops) + lo, self.side_sem, r, self.orders[a][self.hops])

    def core(self, a, r, sided):
        lo, count = stage(r)
        lo = lo + (sided << self.hops)
        return self.send(
            a, lo, count, (2 << self.hops) + lo, self.core_sem, 2 * r + sided, 0
        )

    def write_out(self, a, lo, count):
        which, low, high, _ = self.pieces[a]
        for p in range(lo, lo + count):
            block = self.me ^ offset(self.orders[a] + [0], p)
            pltpu.make_async_copy(
                self.bufs[a].at[p], self.outs[which].at[block, :, pl.ds(low, high - low)], self.out_sem.at[a]
            ).start()

    def held(self, r):
        lo, count = stage(r)
        for a in range(self.count):
            if r:
                self.hop(a, r - 1).wait_recv()
            if r < self.hops:
                self.hop(a, r).start()
            self.side(a, r).start()
            self.core(a, r, 0).start()
        for a in range(self.count):
            self.write_out(a, lo, count)

    def sided(self, r):
        lo, count = stage(r)
        for a in range(self.count):
            self.side(a, r).wait_recv()
            self.core(a, r, 1).start()
            self.write_out(a, (1 << self.hops) + lo, count)

    def cored(self, r):
        lo, count = stage(r)
        for sided in (0, 1):
            for a in range(self.count):
                self.core(a, r, sided).wait_recv()
                self.write_out(a, (2 << self.hops) + (sided << self.hops) + lo, count)

    def finish(self):
        for a in range(self.count):
            for r in range(self.hops):
                self.hop(a, r).wait_send()
            for r in range(self.hops + 1):
                self.side(a, r).wait_send()
                self.core(a, r, 0).wait_send()
                self.core(a, r, 1).wait_send()
            pltpu.make_async_copy(self.bufs[a], self.bufs[a], self.out_sem.at[a]).wait()


def triangle(size):
    rows = lax.broadcasted_iota(jnp.int32, (size, size), 0)
    columns = lax.broadcasted_iota(jnp.int32, (size, size), 1)
    return jnp.where(rows < columns, 1.0, 0.0).astype(jnp.bfloat16)


def digits(numbers):
    high = numbers // 64
    row = lax.broadcasted_iota(jnp.int32, (8, numbers.shape[1]), 0)
    both = jnp.where(row == 0, high, jnp.where(row == 1, numbers - 64 * high, 0))
    return both.astype(jnp.float32).astype(jnp.bfloat16)


def upright(pairs):
    row = lax.broadcasted_iota(jnp.int32, (8, 128), 0)
    value = jnp.where(row == 0, 64.0, jnp.where(row == 1, 1.0, 0.0)).astype(jnp.bfloat16)
    return lax.dot_general(pairs, value, TN, preferred_element_type=jnp.float32)


def hits_by_lane(numbers, width, base):
    lane = lax.broadcasted_iota(jnp.int32, (1, 128), 1).astype(jnp.float32) + base
    tiles = [
        jnp.where(numbers == lane + 128.0 * tile, 1.0, 0.0).astype(jnp.bfloat16)
        for tile in range(width // 128)
    ]
    return jnp.concatenate(tiles, axis=1)


def front_kernel(n_dp, n_pair, pieces, n_in, *refs):
    k = len(pieces)
    owner_ref, row_ref, table_ref = refs[:3]
    shards = refs[3 : 3 + n_in]
    emb_ref, key_ref, asked_ref = refs[3 + n_in : 6 + n_in]
    outs = refs[6 + n_in : 6 + 2 * n_in]
    rest = refs[6 + 2 * n_in :]
    bufs, rest = rest[:k], rest[k:]
    wide, table, ask_out, ask_in, rows_out, rows_in, total = rest[:7]
    table_sem, ask_sem, row_sem, *sems = rest[7:]
    dp, pair = lax.axis_index("dp"), lax.axis_index("pair")
    weights = Gather(n_dp, n_pair, pieces, outs, bufs, sems)
    docs, seq = owner_ref.shape
    tokens = docs * seq
    cap = ask_out.shape[2]

    def in_line(ref):
        return jnp.concatenate([ref[d : d + 1, :] for d in range(docs)], axis=1)

    table_rows = table_ref.shape[0]
    load = pltpu.make_async_copy(table_ref, wide, table_sem)
    load.start()
    peers = [{"dp": dp ^ j, "pair": pair} for j in range(1, n_dp)]
    sem = pltpu.get_barrier_semaphore()
    mates = [{"dp": dp, "pair": pair ^ j} for j in (1, 2)]
    for target in peers + mates:
        pl.semaphore_signal(sem, inc=1, device_id=target, device_id_type=MESH)
    for a, (which, low, high, _) in enumerate(pieces):
        bufs[a][0] = shards[which][:, low:high].astype(jnp.bfloat16)
    pl.semaphore_wait(sem, n_dp + 1)
    weights.held(0)

    owner = in_line(owner_ref)
    by_owner = lax.broadcasted_iota(jnp.int32, (n_dp, tokens), 0) == owner
    ranks = jnp.dot(
        jnp.where(by_owner, 1.0, 0.0).astype(jnp.bfloat16),
        triangle(tokens),
        preferred_element_type=jnp.float32,
    )
    rank = jnp.sum(jnp.where(by_owner, ranks, 0.0), axis=0, keepdims=True)
    key = owner * cap + rank.astype(jnp.int32)
    key_ref[...] = key
    wanted = digits(in_line(row_ref))

    def peer(j):
        return {"dp": dp ^ j, "pair": pair}

    def ask(j):
        return remote(ask_out.at[j], ask_in.at[j], ask_sem.at[0, j], ask_sem.at[1, j], peer(j))

    def reply(j):
        return remote(rows_out.at[j], rows_in.at[j], row_sem.at[0, j], row_sem.at[1, j], peer(j))

    def loop(first, last, body):
        def turn(t, carry):
            body(n_dp - 1 - t)
            return carry

        lax.fori_loop(first, last, turn, 0)

    def request(j):
        slot = lax.broadcasted_iota(jnp.int32, (cap, tokens), 0) + (dp ^ j) * cap
        chosen = jnp.where(slot == key, 1.0, 0.0).astype(jnp.bfloat16)
        ask_out[j] = lax.dot_general(wanted, chosen, NT, preferred_element_type=jnp.float32)

        @pl.when(j > 0)
        def _():
            ask(j).start()

    loop(0, n_dp, request)
    ask_in[0] = ask_out[0]
    weights.held(1)
    load.wait()

    def narrow(i, carry):
        part = pl.ds(pl.multiple_of(i * 16, 16), 16)
        table[part] = wide[part].astype(jnp.bfloat16)
        return carry

    lax.fori_loop(0, table_rows // 16, narrow, 0)
    if table.shape[0] > table_rows:
        table[table_rows:] = jnp.zeros((table.shape[0] - table_rows, table.shape[1]), jnp.bfloat16)

    def answer(j):
        @pl.when(j > 0)
        def _():
            ask(j).wait_recv()

        asked = ask_in[j]
        hit = hits_by_lane(upright(asked.astype(jnp.bfloat16)), table.shape[0], 0.0)
        got = jnp.dot(hit, table[...], preferred_element_type=jnp.float32)
        rows_out[j] = got.astype(jnp.bfloat16)
        asked_ref[j] = (64.0 * asked[0:1] + asked[1:2]).astype(jnp.int32)

        @pl.when(j > 0)
        def _():
            reply(j).start()

    early = n_dp // 4 + 1
    loop(0, early, answer)
    weights.held(2)
    weights.sided(0)
    loop(early, n_dp, answer)
    rows_in[0] = rows_out[0]
    weights.sided(1)
    upright_key = upright(digits(key))

    total[...] = jnp.zeros_like(total)

    def seat(j):
        @pl.when(j > 0)
        def _():
            reply(j).wait_recv()

        place_hit = hits_by_lane(upright_key, cap, ((dp ^ j) * cap).astype(jnp.float32))
        total[...] += jnp.dot(place_hit, rows_in[j], preferred_element_type=jnp.float32)

    weights.cored(0)
    for r in range(3, weights.hops + 1):
        weights.held(r)
        weights.sided(r - 1)
        weights.cored(r - 2)
    loop(0, n_dp, seat)
    emb_ref[...] = total[...].astype(jnp.bfloat16)
    weights.sided(weights.hops)
    for r in (weights.hops - 1, weights.hops):
        weights.cored(r)
    for j in range(1, n_dp):
        ask(j).wait_send()
        reply(j).wait_send()
    weights.finish()


def front(owner, row, table, shards, pieces, cap, n_dp, n_pair, cid):
    n, k = n_dp * n_pair, len(pieces)
    hops = (n - 1).bit_length() - 2
    tokens = owner.size
    table_rows, width = table.shape
    padded = -(-table_rows // 256) * 256
    sem = pltpu.SemaphoreType.DMA
    return pl.pallas_call(
        functools.partial(front_kernel, n_dp, n_pair, pieces, len(shards)),
        out_shape=[
            jax.ShapeDtypeStruct((tokens, width), jnp.bfloat16),
            jax.ShapeDtypeStruct((1, tokens), jnp.int32),
            jax.ShapeDtypeStruct((n_dp, 1, cap), jnp.int32),
        ]
        + [jax.ShapeDtypeStruct((n,) + s.shape, jnp.bfloat16) for s in shards],
        in_specs=[VM, VM, ANY] + [VM] * len(shards),
        out_specs=[VM] * 3 + [ANY] * len(shards),
        scratch_shapes=[
            pltpu.VMEM((n, shards[p[0]].shape[0], p[2] - p[1]), jnp.bfloat16) for p in pieces
        ]
        + [
            pltpu.VMEM((table_rows, width), jnp.float32),
            pltpu.VMEM((padded, width), jnp.bfloat16),
            pltpu.VMEM((n_dp, 8, cap), jnp.float32),
            pltpu.VMEM((n_dp, 8, cap), jnp.float32),
            pltpu.VMEM((n_dp, cap, width), jnp.bfloat16),
            pltpu.VMEM((n_dp, cap, width), jnp.bfloat16),
            pltpu.VMEM((tokens, width), jnp.float32),
            sem,
            sem((2, n_dp)),
            sem((2, n_dp)),
            sem((2, k, hops)),
            sem((2, k, hops + 1)),
            sem((2, k, 2 * hops + 2)),
            sem((k,)),
        ],
        compiler_params=pltpu.CompilerParams(
            collective_id=cid, has_side_effects=True, vmem_limit_bytes=VMEM_LIMIT
        ),
        name="rows_and_weights",
    )(owner, row, table, *shards)


class Scatter:
    def __init__(self, n_dp, n_pair, pieces, ins, outs, boxes, sems):
        self.n_pair, self.pieces, self.ins, self.outs = n_pair, pieces, ins, outs
        k = len(pieces)
        self.acc, self.from_core = boxes[:k], boxes[k : 2 * k]
        self.from_side, self.from_hop = boxes[2 * k : 3 * k], boxes[3 * k :]
        self.load_sem, self.core_sem, self.side_sem, self.hop_sem = sems
        self.me = my_index(n_pair)
        self.hops = (n_dp * n_pair - 1).bit_length() - 2
        self.orders = [bit_order(n_dp, n_pair, piece[3]) for piece in pieces]
        self.count = k

    def source(self, a, block):
        which, low, high, _ = self.pieces[a]
        return self.ins[which].at[block, :, pl.ds(low, high - low)]

    def near(self, bit):
        return place(self.me ^ (1 << bit), self.n_pair)

    def load(self):
        for a in range(self.count):
            for p in range(2 << self.hops):
                pltpu.make_async_copy(
                    self.source(a, self.me ^ offset(self.orders[a], p)),
                    self.acc[a].at[p],
                    self.load_sem.at[a],
                ).start()

    def loaded(self):
        for a in range(self.count):
            pltpu.make_async_copy(self.acc[a], self.acc[a], self.load_sem.at[a]).wait()

    def core(self, a, r, sided, part=None):
        lo, count = stage(r)
        lo = lo + (sided << self.hops)
        to = self.from_core[a].at[pl.ds(lo, count)]
        source = to
        if part is not None:
            to = self.from_core[a].at[lo + part]
            source = self.source(a, self.me ^ (offset(self.orders[a], lo + part) + 1))
        slot = 2 * r + sided
        return remote(
            source, to, self.core_sem.at[0, a, slot], self.core_sem.at[1, a, slot], self.near(0)
        )

    def core_out(self, r):
        for sided in (1, 0):
            for a in range(self.count):
                for part in range(stage(r)[1]):
                    self.core(a, r, sided, part).start()

    def add(self, a, lo, count, box, at):
        acc = self.acc[a]

        def body(j, carry):
            acc[lo + j] = (
                acc[lo + j].astype(jnp.float32) + box[at + j].astype(jnp.float32)
            ).astype(jnp.bfloat16)
            return carry

        lax.fori_loop(0, count, body, 0)

    def side(self, a, r):
        lo, count = stage(r)
        return remote(
            self.acc[a].at[pl.ds((1 << self.hops) + lo, count)],
            self.from_side[a].at[pl.ds(lo, count)],
            self.side_sem.at[0, a, r],
            self.side_sem.at[1, a, r],
            self.near(self.orders[a][self.hops]),
        )

    def hop(self, a, r):
        return remote(
            self.acc[a].at[pl.ds(1 << r, 1 << r)],
            self.from_hop[a].at[pl.ds(self.hop_base(r), 1 << r)],
            self.hop_sem.at[0, a, r],
            self.hop_sem.at[1, a, r],
            self.near(self.orders[a][r]),
        )

    def hop_base(self, r):
        return (1 << self.hops) - (2 << r)

    def core_in(self, r):
        lo, count = stage(r)
        for sided in (1, 0):
            for a in range(self.count):
                self.core(a, r, sided).wait_recv()
                at = lo + (sided << self.hops)
                self.add(a, at, count, self.from_core[a], at)
                if sided:
                    self.side(a, r).start()

    def side_in(self, r):
        lo, count = stage(r)
        for a in range(self.count):
            self.side(a, r).wait_recv()
            self.add(a, lo, count, self.from_side[a], lo)
            if r == self.hops:
                self.hop(a, r - 1).start()

    def hop_in(self, r):
        for a in range(self.count):
            self.hop(a, r).wait_recv()
            base = self.hop_base(r)
            if r:
                mid = 1 << (r - 1)
                self.add(a, mid, mid, self.from_hop[a], base + mid)
                self.hop(a, r - 1).start()
                self.add(a, 0, mid, self.from_hop[a], base)
            else:
                which, low, high, _ = self.pieces[a]
                self.outs[which][:, low:high] = self.acc[a][0].astype(jnp.float32) + self.from_hop[
                    a
                ][base].astype(jnp.float32)

    def finish(self):
        for a in range(self.count):
            for r in range(self.hops):
                self.hop(a, r).wait_send()
            for r in range(self.hops + 1):
                self.side(a, r).wait_send()
                self.core(a, r, 0).wait_send()
                self.core(a, r, 1).wait_send()


def backward_kernel(n_dp, n_pair, pieces, n_in, *refs):
    k_count = len(pieces)
    len_ref, q_ref, k_ref, v_ref, g_ref, w_ref = refs[:6]
    ins = refs[6 : 6 + n_in]
    o_ref, z_ref, square_ref = refs[6 + n_in : 9 + n_in]
    outs = refs[9 + n_in : 9 + 2 * n_in]
    table, total, box, sem = refs[9 + 2 * n_in : 13 + 2 * n_in]
    rest = refs[13 + 2 * n_in :]
    weights = Scatter(n_dp, n_pair, pieces, ins, outs, rest[: 4 * k_count], rest[4 * k_count :])
    at = pl.program_id(0) * pl.num_programs(1) + pl.program_id(1)
    hops = weights.hops

    @pl.when(at == 0)
    def _():
        weights.load()
        greet([weights.near(bit) for bit in range(hops + 2)])
        for r in reversed(range(hops + 1)):
            weights.core_out(r)

    @pl.when(at == 1)
    def _():
        weights.loaded()
        weights.core_in(hops)

    @pl.when(at == 2)
    def _():
        for r in reversed(range(hops)):
            weights.core_in(r)

    @pl.when(at == 5)
    def _():
        weights.side_in(hops)

    @pl.when(at == 6)
    def _():
        for r in reversed(range(hops)):
            weights.side_in(r)

    seq = q_ref.shape[0]
    tiles = seq // 128
    doc = pl.program_id(1)
    @pl.when(doc == 0)
    def _():
        for h in range(2):
            band(w_ref, 2 * pl.program_id(0) + h, 2 * seq, h, table, seq)
        total[...] = jnp.zeros_like(total)
    length = len_ref[doc]
    lane = lax.broadcasted_iota(jnp.int32, (seq, 128), 1)
    row = lax.broadcasted_iota(jnp.int32, (seq, 1), 0)
    q = q_ref[...] * jnp.bfloat16(0.125)
    k = k_ref[...]
    v = v_ref[...]
    g = g_ref[...]
    parts = []
    for h in range(2):
        mine = (lane < 64) == (h == 0)
        s = lax.dot_general(k, jnp.where(mine, q, 0), NT, preferred_element_type=jnp.float32)
        s = jnp.where(row < length, s + table[h], -1000000000.0)
        e = jnp.exp(s - jnp.max(s, axis=0, keepdims=True))
        p = e * (1.0 / jnp.sum(e, axis=0, keepdims=True))
        dv = jnp.dot(p.astype(jnp.bfloat16), g, preferred_element_type=jnp.float32)
        dp = lax.dot_general(v, jnp.where(mine, g, 0), NT, preferred_element_type=jnp.float32)
        ds = (p * (dp - jnp.sum(p * dp, axis=0, keepdims=True))).astype(jnp.bfloat16)
        total[h] += ds.astype(jnp.float32)
        dk = jnp.dot(ds, q, preferred_element_type=jnp.float32)
        dq = lax.dot_general(ds, k, TN, preferred_element_type=jnp.float32) * 0.125
        parts.append((dq, dk, dv))
    pair, pairs, docs = pl.program_id(0), pl.num_programs(0), pl.num_programs(1)
    step = pair * docs + doc
    slot = lax.rem(step, 2)

    def out(i):
        rows = pl.ds(pl.multiple_of(doc * seq, seq), seq)
        columns = pl.ds(pl.multiple_of((i * pairs + pair) * 128, 128), 128)
        return pltpu.make_async_copy(box.at[slot, i], o_ref.at[rows, columns], sem.at[slot, i])

    for i in range(3):
        @pl.when(step >= 2)
        def _():
            out(i).wait()
        box[slot, i] = jnp.where(lane < 64, parts[0][i], parts[1][i]).astype(o_ref.dtype)
        out(i).start()

    for r in range(1, hops):
        @pl.when(step == pairs * docs - 2 * r)
        def _():
            weights.hop_in(r)

    @pl.when(step == pairs * docs - 1)
    def _():
        weights.hop_in(0)
        weights.finish()
        square_ref[...] = jnp.zeros_like(square_ref)
        for ref in outs:
            square = jnp.sum(ref[...] * ref[...], axis=0, keepdims=True)
            square_ref[...] += jnp.sum(square, axis=1, keepdims=True)
        for i in range(3):
            out(i).wait()
            pltpu.make_async_copy(box.at[1 - slot, i], box.at[1 - slot, i], sem.at[1 - slot, i]).wait()
    @pl.when(doc == pl.num_programs(1) - 1)
    def _():
        r = lax.broadcasted_iota(jnp.int32, (128, 128), 0)
        c = lax.broadcasted_iota(jnp.int32, (128, 128), 1)
        flip = jnp.where(r + c == 127, 1.0, 0.0)
        z_ref[...] = jnp.zeros_like(z_ref)
        for h in range(2):
            def block(d):
                return sum(total[h, a * 128 : a * 128 + 128, (a - d) * 128 : (a - d) * 128 + 128] for a in range(tiles) if 0 <= a - d < tiles)
            for d in (-1, 0, 1):
                x = jnp.dot(flip, block(d), precision=HIGHEST, preferred_element_type=jnp.float32)
                x = jnp.concatenate([x, jnp.zeros_like(x)], axis=1)
                x = pltpu.roll(x, 0, 1, stride=1, stride_axis=0)
                z_ref[0, h, d + 1 : d + 2, :] = jnp.sum(x, axis=0, keepdims=True)
            z_ref[0, h, 3:4, 0:128] = jnp.sum(sum(block(-d) for d in range(2, tiles)), axis=0, keepdims=True)
            z_ref[0, h, 4:5, 0:128] = jnp.sum(sum(block(d) for d in range(2, tiles)), axis=0, keepdims=True)

def attention_back(lengths, qkv, g, w, seq, grads, pieces, cid):
    n_dp, n_pair = lax.axis_size("dp"), lax.axis_size("pair")
    tokens = qkv.shape[0]
    pairs = w.shape[0] // 2
    docs = tokens // seq
    spec = lambda base: pl.BlockSpec((seq, 128), lambda h, d, *_: (d, base + h))
    still = lambda shape: pl.BlockSpec(shape, lambda h, d, *_: (0, 0))
    boxes, sems = scatter_scratch(n_dp * n_pair, grads, pieces)
    return pl.pallas_call(
        functools.partial(backward_kernel, n_dp, n_pair, pieces, len(grads)),
        grid_spec=pltpu.PrefetchScalarGridSpec(
            num_scalar_prefetch=1,
            grid=(pairs, docs),
            in_specs=[spec(0), spec(pairs), spec(2 * pairs), spec(0), still(w.shape)]
            + [ANY] * len(grads),
            out_specs=[
                ANY,
                pl.BlockSpec((1, 2, 8, 256), lambda h, d, *_: (h, 0, 0, 0)),
                still((1, 1)),
            ]
            + [still(grad.shape[1:]) for grad in grads],
            scratch_shapes=[
                pltpu.VMEM((2, seq, seq), jnp.float32),
                pltpu.VMEM((2, seq, seq), jnp.float32),
                pltpu.VMEM((2, 3, seq, 128), jnp.bfloat16),
                pltpu.SemaphoreType.DMA((2, 3)),
            ]
            + boxes
            + sems,
        ),
        out_shape=[
            jax.ShapeDtypeStruct((tokens, 3 * pairs * 128), jnp.bfloat16),
            jax.ShapeDtypeStruct((pairs, 2, 8, 256), jnp.float32),
            jax.ShapeDtypeStruct((1, 1), jnp.float32),
        ]
        + [jax.ShapeDtypeStruct(grad.shape[1:], jnp.float32) for grad in grads],
        compiler_params=pltpu.CompilerParams(
            dimension_semantics=("arbitrary", "arbitrary"),
            collective_id=cid,
            has_side_effects=True,
            vmem_limit_bytes=VMEM_LIMIT,
        ),
        name="attention_back",
    )(lengths, qkv, qkv, qkv, g, w, *grads)


def packed_base(gains, width):
    return -(-gains * width // 128 // 8) * 8


def back_kernel(n_dp, n_pair, pieces, n_gain, n_in, chunk, *refs):
    k = len(pieces)
    grad_ref, key_ref, ask_ref, squares_ref, bias_ref = refs[:5]
    gain_refs = refs[5 : 5 + n_gain]
    ins, rest = refs[5 + n_gain : 5 + n_gain + n_in], refs[5 + n_gain + n_in :]
    out_ref, total_ref = rest[:2]
    outs = rest[2 : 2 + n_in]
    rest = rest[2 + n_in :]
    boxes, rest = rest[: 4 * k], rest[4 * k :]
    rows_out, rows_in, hot, part, stage_out, got_core, out_side, got_side, other = rest[:9]
    square_ref, small, by_dp, from_pair = rest[9:13]
    row_sem, core_sem, side_sem, last_sem, out_sem, dp_sem, pair_sem, *sems = rest[13:]
    dp, pair = lax.axis_index("dp"), lax.axis_index("pair")
    core = lax.rem(pair, 2)
    weights = Scatter(n_dp, n_pair, pieces, ins, outs, boxes, sems)
    groups, _, cap, width = rows_out.shape
    slots = ask_ref.shape[1]
    count = stage_out.shape[1]
    half = count * chunk
    tokens = key_ref.shape[1]
    peers = [{"dp": dp ^ j, "pair": pair} for j in range(1, n_dp)]
    partner, across = {"dp": dp, "pair": pair ^ 1}, {"dp": dp, "pair": pair ^ 2}
    weights.load()
    sem = pltpu.get_barrier_semaphore()
    for target in peers + [partner, across]:
        pl.semaphore_signal(sem, inc=1, device_id=target, device_id_type=MESH)

    def row(g, j):
        return remote(
            rows_out.at[g, j],
            rows_in.at[g, pl.ds(pl.multiple_of(j * cap, cap), cap)],
            row_sem.at[0, g, j],
            row_sem.at[1, g, j],
            {"dp": dp ^ j, "pair": pair},
        )

    def loop(size, body):
        def turn(i, carry):
            body(i)
            return carry

        lax.fori_loop(0, size, turn, 0)

    far = sorted(range(1, n_dp), reverse=True)

    pl.semaphore_wait(sem, n_dp + 1)

    def rows_of(t):
        j = n_dp - 1 - t
        slot = lax.broadcasted_iota(jnp.int32, (cap, tokens), 0) + (dp ^ j) * cap
        hits = jnp.where(slot == key_ref[...], 1.0, 0.0).astype(jnp.bfloat16)
        got = jnp.dot(hits, grad_ref[...], preferred_element_type=jnp.float32)
        got = got.astype(jnp.bfloat16)
        for g in range(groups):
            rows_out[g, j] = got[:, g * width : (g + 1) * width]

        @pl.when(j > 0)
        def _():
            row(0, j).start()

    loop(n_dp, rows_of)
    for g in range(1, groups):
        for j in far:
            row(g, j).start()
    for g in range(groups):
        rows_in[g, 0:cap] = rows_out[g, 0]
    for r in reversed(range(weights.hops + 1)):
        weights.core_out(r)

    def tell(c):
        ids = lax.broadcasted_iota(jnp.int32, (chunk, slots), 0) + c * chunk
        hot[c] = jnp.where(ids == ask_ref[...], 1.0, 0.0).astype(jnp.bfloat16)

    loop(2 * count, tell)

    def summed(g, c):
        return jnp.dot(hot[c], rows_in[g], preferred_element_type=jnp.float32)

    def to_core(g, i):
        return remote(
            stage_out.at[g, i], got_core.at[g, i], core_sem.at[0, g, i], core_sem.at[1, g, i], partner
        )

    def to_side(g, i):
        return remote(
            out_side.at[g, i], got_side.at[g, i], side_sem.at[0, g, i], side_sem.at[1, g, i], across
        )

    def to_other(g, i):
        return remote(
            out_side.at[g, i], other.at[g, i], last_sem.at[0, g, i], last_sem.at[1, g, i], partner
        )

    def write_out(box, g, i, which):
        rows = pl.ds(pl.multiple_of(which * half + i * chunk, chunk), chunk)
        return pltpu.make_async_copy(
            box.at[g, i], out_ref.at[rows, pl.ds(g * width, width)], out_sem.at[g, i]
        )

    def local_sums(g):
        for j in far:
            row(g, j).wait_recv()

        def combine(i):
            to_core(g, i).wait_recv()
            out_side[g, i] = (part[i] + got_core[g, i].astype(jnp.float32)).astype(jnp.bfloat16)
            to_side(g, i).start()

        def one(i):
            stage_out[g, i] = summed(g, (1 - core) * count + i).astype(jnp.bfloat16)
            to_core(g, i).start()
            part[i] = summed(g, core * count + i)

            @pl.when(i > 0)
            def _():
                combine(i - 1)

        loop(count, one)
        combine(count - 1)

    square_ref[...] = squares_ref[...]

    def finish_sums(g):
        def one(i):
            to_side(g, i).wait()
            wide = out_side[g, i].astype(jnp.float32) + got_side[g, i].astype(jnp.float32)
            value = wide.astype(jnp.bfloat16)
            out_side[g, i] = value
            to_other(g, i).start()
            write_out(out_side, g, i, core).start()
            wide = value.astype(jnp.float32)
            square = jnp.sum(wide * wide, axis=0, keepdims=True)
            square = jnp.sum(square, axis=1, keepdims=True)
            square_ref[...] += jnp.where(pair < 2, square, 0.0)

        loop(count, one)

    def hand_over(g):
        def one(i):
            to_other(g, i).wait_recv()
            write_out(out_side, g, i, core).wait()
            write_out(other, g, i, 1 - core).start()

        loop(count, one)

    weights.loaded()
    for r in reversed(range(weights.hops + 1)):
        weights.core_in(r)
    for g in range(groups):
        local_sums(g)
        if g:
            finish_sums(g - 1)
        if g == groups // 2:
            for r in reversed(range(weights.hops + 1)):
                weights.side_in(r)
    for r in reversed(range(1, weights.hops)):
        weights.hop_in(r)
    finish_sums(groups - 1)
    weights.hop_in(0)
    for ref in outs:
        square = jnp.sum(ref[...] * ref[...], axis=0, keepdims=True)
        square_ref[...] += jnp.sum(square, axis=1, keepdims=True)
    gains_width = gain_refs[0].shape[1]
    base = packed_base(n_gain, gains_width)
    small[...] = jnp.zeros_like(small)
    for c in range(gains_width // 128):
        for which in range(n_gain):
            at = c * n_gain + which
            small[0, at : at + 1, :] = gain_refs[which][:, c * 128 : (c + 1) * 128]
    small[0, base : base + bias_ref.shape[0], : bias_ref.shape[1]] = bias_ref[...]
    small[0, base : base + 1, 127:128] = square_ref[...]

    def to_dp(j, slot):
        return remote(
            small.at[0],
            by_dp.at[slot],
            dp_sem.at[0, j],
            dp_sem.at[1, j],
            {"dp": dp ^ j, "pair": pair},
        )

    def to_pair(turn, target):
        return remote(
            small.at[1 + turn],
            from_pair.at[turn],
            pair_sem.at[0, turn],
            pair_sem.at[1, turn],
            target,
        )

    for j in far:
        to_dp(j, dp).start()
    by_dp[dp] = small[0]
    for g in range(groups):
        hand_over(g)
    for j in far:
        to_dp(j, dp ^ j).wait_recv()
    total = by_dp[0]
    for d in range(1, n_dp):
        total = total + by_dp[d]
    for turn, target in enumerate((partner, across)):
        small[1 + turn] = total
        to_pair(turn, target).start()
        to_pair(turn, target).wait_recv()
        total = total + from_pair[turn]
    total_ref[...] = total
    for j in far:
        to_dp(j, dp).wait_send()
    for turn, target in enumerate((partner, across)):
        to_pair(turn, target).wait_send()
    for g in range(groups):
        for j in far:
            row(g, j).wait_send()

        def one(i):
            to_core(g, i).wait_send()
            to_other(g, i).wait_send()
            write_out(other, g, i, 1 - core).wait()

        loop(count, one)
    weights.finish()


def scatter_scratch(n, grads, pieces):
    k, hops, sem = len(pieces), (n - 1).bit_length() - 2, pltpu.SemaphoreType.DMA
    boxes = [
        pltpu.VMEM((lead, grads[p[0]].shape[1], p[2] - p[1]), jnp.bfloat16)
        for lead in (n // 2, n // 2, n // 4, n // 4 - 1)
        for p in pieces
    ]
    return boxes, [
        sem((k,)),
        sem((2, k, 2 * hops + 2)),
        sem((2, k, hops + 1)),
        sem((2, k, hops)),
    ]


def back(grad, key, asked, squares, bias, gains, grads, pieces, table_rows, groups, cid):
    n_dp, n_pair = lax.axis_size("dp"), lax.axis_size("pair")
    boxes, sems = scatter_scratch(n_dp * n_pair, grads, pieces)
    chunk = 512
    rows = -(-table_rows // (2 * chunk)) * 2 * chunk
    count = rows // 2 // chunk
    tokens, full = grad.shape
    width = full // groups
    slots = asked.shape[1]
    height = -(-(packed_base(len(gains), full) + bias.shape[0]) // 8) * 8
    cap = slots // n_dp
    sem = pltpu.SemaphoreType.DMA
    box = pltpu.VMEM((groups, count, chunk, width), jnp.bfloat16)

    return pl.pallas_call(
        functools.partial(back_kernel, n_dp, n_pair, pieces, len(gains), len(grads), chunk),
        out_shape=[
            jax.ShapeDtypeStruct((rows, full), jnp.bfloat16),
            jax.ShapeDtypeStruct((height, 128), jnp.float32),
        ]
        + [jax.ShapeDtypeStruct(g.shape[1:], jnp.float32) for g in grads],
        in_specs=[VM] * (5 + len(gains)) + [ANY] * len(grads),
        out_specs=[ANY, VM] + [VM] * len(grads),
        scratch_shapes=boxes
        + [
            pltpu.VMEM((groups, n_dp, cap, width), jnp.bfloat16),
            pltpu.VMEM((groups, slots, width), jnp.bfloat16),
            pltpu.VMEM((2 * count, chunk, slots), jnp.bfloat16),
            pltpu.VMEM((count, chunk, width), jnp.float32),
            box,
            box,
            box,
            box,
            box,
            pltpu.VMEM((1, 1), jnp.float32),
            pltpu.VMEM((3, height, 128), jnp.float32),
            pltpu.VMEM((n_dp, height, 128), jnp.float32),
            pltpu.VMEM((2, height, 128), jnp.float32),
            sem((2, groups, n_dp)),
            sem((2, groups, count)),
            sem((2, groups, count)),
            sem((2, groups, count)),
            sem((groups, count)),
            sem((2, n_dp)),
            sem((2, 2)),
        ]
        + sems,
        compiler_params=pltpu.CompilerParams(
            collective_id=cid, has_side_effects=True, vmem_limit_bytes=VMEM_LIMIT
        ),
        name="table_and_weights",
    )(grad, key, asked, squares, bias, *gains, *grads)


BIAS_CORRECT = (1.0 - beta_one**STEP, 1.0 - beta_two**STEP)


def adam_parts(weight, first, second, grad, factor, rate, shrink):
    clipped = grad * factor
    first_new = beta_one * first + (1.0 - beta_one) * clipped
    second_new = beta_two * second + (1.0 - beta_two) * (clipped * clipped)
    root = jnp.sqrt(second_new * (1.0 / BIAS_CORRECT[1])) + adam_eps
    step = (rate / BIAS_CORRECT[0]) * first_new / root
    return (weight * (1.0 - rate * shrink) - step, first_new, second_new)


def update_kernel(mats, *refs):
    total_ref, loss_ref, low = refs[:3]
    table, small = refs[3:6], refs[6:12]
    grads = refs[12 : 12 + mats]
    states = refs[12 + mats : 12 + 4 * mats]
    rest = refs[12 + 4 * mats :]
    norm_out, loss_out, table_out, small_out = rest[0], rest[1], rest[2:5], rest[5:11]
    mat_out = rest[11:]
    gains, width = small[0].shape
    base = packed_base(gains, width)
    total = total_ref[...]
    row = lax.broadcasted_iota(jnp.int32, total.shape, 0)
    lane = lax.broadcasted_iota(jnp.int32, total.shape, 1)
    plain = jnp.where((row == base) & (lane == 127), total, total * total)
    norm = jnp.sqrt(jnp.sum(jnp.sum(plain, axis=1, keepdims=True), axis=0, keepdims=True))
    factor = jnp.minimum(1.0, clip_limit / norm)
    step = pl.program_id(0)

    @pl.when(step == 0)
    def _():
        norm_out[...] = norm
        loss_out[...] = loss_ref[...]
        for c in range(width // 128):
            columns = slice(c * 128, (c + 1) * 128)
            grad = total_ref[c * gains : (c + 1) * gains, :]
            new = adam_parts(*(ref[:, columns] for ref in small[:3]), grad, factor, 1.0, 0.0)
            for ref, value in zip(small_out[:3], new):
                ref[:, columns] = value
        heads = small[3].shape[1]
        grad = total_ref[base : base + small[3].shape[0], :heads]
        new = adam_parts(*(ref[...] for ref in small[3:]), grad, factor, 0.3, 0.0)
        for ref, value in zip(small_out[3:], new):
            ref[...] = value

    for which in range(mats):
        three = slice(3 * which, 3 * which + 3)
        new = adam_parts(*(ref[...] for ref in states[three]), grads[which][...], factor, 0.05, 0.01)
        for ref, value in zip(mat_out[three], new):
            ref[...] = value

    def body(j, carry):
        rows = pl.ds(pl.multiple_of(j * 16, 16), 16)
        new = adam_parts(*(ref[rows] for ref in table), low[rows].astype(jnp.float32), factor, 1.0, 0.01)
        for ref, value in zip(table_out, new):
            ref[rows] = value
        return carry

    lax.fori_loop(0, low.shape[0] // 16, body, 0)


def update(total, loss, table_grad, table, small, grads, states):
    rows, width = table[0].shape
    steps = 6
    tall = -(-rows // steps // 16) * 16
    flat = [array for group in states for array in group]
    like = lambda array: jax.ShapeDtypeStruct(array.shape, jnp.float32)
    whole = lambda array: pl.BlockSpec(array.shape, lambda i: (0, 0))
    table_spec = pl.BlockSpec((tall, width), lambda i: (i, 0))

    def part(array):
        if array.shape[1] % (128 * steps) == 0 and array.shape[0] < 32:
            return pl.BlockSpec((array.shape[0], array.shape[1] // steps), lambda i: (0, i))
        if array.shape[0] % (8 * steps) == 0:
            return pl.BlockSpec((array.shape[0] // steps, array.shape[1]), lambda i: (i, 0))
        return whole(array)

    return pl.pallas_call(
        functools.partial(update_kernel, len(grads)),
        grid=(steps,),
        out_shape=[like(loss), like(loss)] + [like(array) for array in (*table, *small, *flat)],
        in_specs=[whole(total), whole(loss)]
        + [table_spec] * 4
        + [whole(array) for array in small]
        + [part(array) for array in (*grads, *flat)],
        out_specs=[whole(loss)] * 2
        + [table_spec] * 3
        + [whole(array) for array in small]
        + [part(array) for array in flat],
        compiler_params=pltpu.CompilerParams(
            dimension_semantics=("arbitrary",), vmem_limit_bytes=VMEM_LIMIT
        ),
        name="update",
    )(total, loss, table_grad, *table, *small, *grads, *flat)


def local_plain(
    token_owner,
    token_row,
    lengths,
    positives,
    negatives,
    neg_counts,
    embed_table,
    embed_first,
    embed_second,
    qkv_weight,
    qkv_first,
    qkv_second,
    out_weight,
    out_first,
    out_second,
    in_weight,
    in_first,
    in_second,
    down_weight,
    down_first,
    down_second,
    norm_gains,
    gains_first,
    gains_second,
    position_bias,
    bias_first,
    bias_second,
):
    doc_count = lengths.shape[0]
    seq_len = token_row.shape[1]
    model_width = embed_table.shape[1]
    head_count = position_bias.shape[1]
    bucket_count = position_bias.shape[0]
    tok_total = doc_count * seq_len
    owners = lax.axis_size("dp")
    capacity = max(2, 2 * tok_total // owners)
    low_mats = (
        qkv_weight.astype(jnp.bfloat16),
        out_weight.astype(jnp.bfloat16),
        in_weight.astype(jnp.bfloat16),
        down_weight.astype(jnp.bfloat16),
    )
    qkv_full, out_full, in_full, down_full = (
        lax.all_gather(low_mats[0], ("dp", "pair"), axis=0, tiled=True),
        lax.all_gather(low_mats[1], ("dp", "pair"), axis=0, tiled=True),
        lax.all_gather(low_mats[2], ("dp", "pair"), axis=0, tiled=True),
        lax.all_gather(low_mats[3], ("dp", "pair"), axis=0, tiled=True),
    )
    tok_owner = token_owner.reshape(-1)
    tok_row = token_row.reshape(-1)
    owner_hits = (tok_owner[:, None] == jnp.arange(owners, dtype=jnp.int32)[None, :]).astype(
        jnp.int32
    )
    slot_rank = jnp.sum((jnp.cumsum(owner_hits, axis=0) - 1) * owner_hits, axis=1)
    requests = jnp.zeros((owners, capacity), jnp.int32).at[tok_owner, slot_rank].set(tok_row)
    asked_rows = lax.all_to_all(requests, "dp", split_axis=0, concat_axis=0, tiled=True)
    looked = jnp.take(embed_table, asked_rows.reshape(-1), axis=0).astype(jnp.bfloat16)
    answer = lax.all_to_all(
        looked.reshape(asked_rows.shape + (model_width,)),
        "dp",
        split_axis=0,
        concat_axis=0,
        tiled=True,
    )
    replies, asked_rows = (answer, asked_rows)
    embedded = replies[tok_owner, slot_rank].astype(jnp.float32)
    positions = jnp.arange(seq_len)
    live = positions[None, :] < lengths[:, None]
    pair_buckets = bucket_of(
        (positions[None, :] - positions[:, None]).reshape(-1), bucket_count, REACH
    )
    pair_hits = (jnp.arange(bucket_count)[:, None] == pair_buckets[None, :]).astype(jnp.float32)
    bias_full = jnp.dot(position_bias.T, pair_hits, precision=HIGHEST).reshape(
        head_count, seq_len, seq_len
    )
    bucket_map = pair_hits.astype(jnp.bfloat16)

    def split_doc(source, doc_index):
        doc_rows = source[doc_index * seq_len : (doc_index + 1) * seq_len]
        return tuple(
            (
                doc_rows[:, member * model_width : (member + 1) * model_width].reshape(
                    seq_len, head_count, -1
                )
                for member in range(3)
            )
        )

    normed_one, inverse_one = rms_forward(embedded, norm_gains[0])
    normed_one = normed_one.astype(jnp.bfloat16)
    qkv_rows = jnp.dot(normed_one, qkv_full, preferred_element_type=jnp.float32).astype(
        jnp.bfloat16
    )
    attended_parts = []
    logsum_parts = []
    for doc_index in range(doc_count):
        query_heads, key_heads, value_heads = split_doc(qkv_rows, doc_index)
        doc_out, logsum = attend_forward(
            query_heads, key_heads, value_heads, bias_full, live[doc_index]
        )
        attended_parts.append(doc_out.reshape(seq_len, model_width))
        logsum_parts.append(logsum)
    attended = jnp.concatenate(attended_parts, axis=0).astype(jnp.bfloat16)
    residual = embedded + jnp.dot(attended, out_full, preferred_element_type=jnp.float32)
    normed_two, inverse_two = rms_forward(residual, norm_gains[1])
    normed_two = normed_two.astype(jnp.bfloat16)
    hidden = jax.nn.relu(jnp.dot(normed_two, in_full, preferred_element_type=jnp.float32)).astype(
        jnp.bfloat16
    )
    output_rows = residual + jnp.dot(hidden, down_full, preferred_element_type=jnp.float32)
    normed_three, inverse_three = rms_forward(output_rows, norm_gains[2])
    live_rows = live.reshape(-1, 1)
    length_float = lengths.astype(jnp.float32)
    pooled_local = (
        jnp.sum(
            jnp.where(live_rows, normed_three, 0.0).reshape(doc_count, seq_len, model_width), axis=1
        )
        / length_float[:, None]
    )
    pooled_all = lax.all_gather(pooled_local, ("dp", "pair"), axis=0, tiled=True)
    loss_value, loss_pullback = jax.vjp(
        lambda pooled_in: margin_loss(pooled_in, positives, negatives, neg_counts), pooled_all
    )
    grad_pooled_all = loss_pullback(jnp.ones((), jnp.float32))[0]
    grad_pooled = lax.dynamic_slice_in_dim(
        grad_pooled_all, lax.axis_index(("dp", "pair")) * doc_count, doc_count, 0
    )
    grad_three = jnp.where(
        live_rows, jnp.repeat(grad_pooled / length_float[:, None], seq_len, axis=0), 0.0
    )
    qkv_back, out_back, in_back, down_back = (qkv_full, out_full, in_full, down_full)
    grad_output, gain_three = rms_backward(output_rows, inverse_three, norm_gains[2], grad_three)
    grad_branch = grad_output.astype(jnp.bfloat16)
    grad_down = lax.dot_general(
        hidden, grad_branch, CONTRACT_ROWS, preferred_element_type=jnp.float32
    )
    grad_hidden = lax.dot_general(
        grad_branch, down_back, CONTRACT_COLS, preferred_element_type=jnp.float32
    )
    grad_pre = jnp.where(hidden > 0, grad_hidden, 0.0).astype(jnp.bfloat16)
    grad_in = lax.dot_general(
        normed_two, grad_pre, CONTRACT_ROWS, preferred_element_type=jnp.float32
    )
    grad_normed_two = lax.dot_general(
        grad_pre, in_back, CONTRACT_COLS, preferred_element_type=jnp.float32
    )
    grad_res_part, gain_two = rms_backward(residual, inverse_two, norm_gains[1], grad_normed_two)
    grad_residual = grad_output + grad_res_part
    grad_attn_branch = grad_residual.astype(jnp.bfloat16)
    grad_out = lax.dot_general(
        attended, grad_attn_branch, CONTRACT_ROWS, preferred_element_type=jnp.float32
    )
    grad_attended = lax.dot_general(
        grad_attn_branch, out_back, CONTRACT_COLS, preferred_element_type=jnp.float32
    ).astype(jnp.bfloat16)
    grad_qkv_parts = []
    bias_grad_heads = jnp.zeros((head_count, bucket_count), jnp.float32)
    for doc_index in range(doc_count):
        query_heads, key_heads, value_heads = split_doc(qkv_rows, doc_index)
        grad_doc = grad_attended[doc_index * seq_len : (doc_index + 1) * seq_len].reshape(
            seq_len, head_count, -1
        )
        grad_query, grad_key, grad_value, grad_low = attend_backward(
            query_heads,
            key_heads,
            value_heads,
            bias_full,
            live[doc_index],
            logsum_parts[doc_index],
            grad_doc,
        )
        grad_qkv_parts.append(
            jnp.concatenate(
                [
                    grad_query.reshape(seq_len, model_width),
                    grad_key.reshape(seq_len, model_width),
                    grad_value.reshape(seq_len, model_width),
                ],
                axis=1,
            )
        )
        bias_grad_heads = bias_grad_heads + lax.dot_general(
            grad_low.reshape(head_count, -1),
            bucket_map,
            CONTRACT_COLS,
            preferred_element_type=jnp.float32,
        )
    bias_grad_local = bias_grad_heads.T
    grad_qkv_rows = jnp.concatenate(grad_qkv_parts, axis=0).astype(jnp.bfloat16)
    grad_qkv = lax.dot_general(
        normed_one, grad_qkv_rows, CONTRACT_ROWS, preferred_element_type=jnp.float32
    )
    grad_normed_one = lax.dot_general(
        grad_qkv_rows, qkv_back, CONTRACT_COLS, preferred_element_type=jnp.float32
    )
    grad_emb_part, gain_one = rms_backward(embedded, inverse_one, norm_gains[0], grad_normed_one)
    grad_embedded = grad_residual + grad_emb_part
    sendback = (
        jnp.zeros((owners, capacity, model_width), jnp.float32)
        .at[tok_owner, slot_rank]
        .set(grad_embedded)
    )
    arrived = lax.all_to_all(sendback, "dp", split_axis=0, concat_axis=0, tiled=True)
    table_grad = jax.ops.segment_sum(
        arrived.reshape(-1, model_width), asked_rows.reshape(-1), num_segments=embed_table.shape[0]
    )
    table_grad = lax.psum(table_grad, "pair")
    weight_grads = (
        lax.psum_scatter(grad_qkv, ("dp", "pair"), scatter_dimension=0, tiled=True),
        lax.psum_scatter(grad_out, ("dp", "pair"), scatter_dimension=0, tiled=True),
        lax.psum_scatter(grad_in, ("dp", "pair"), scatter_dimension=0, tiled=True),
        lax.psum_scatter(grad_down, ("dp", "pair"), scatter_dimension=0, tiled=True),
    )
    pair_first = (lax.axis_index("pair") == 0).astype(jnp.float32)
    square_part = jnp.sum(
        jnp.stack([jnp.sum(grad_piece * grad_piece) for grad_piece in weight_grads])
    ) + pair_first * jnp.sum(table_grad * table_grad)
    gain_grad, bias_grad, square_sum = lax.psum(
        (jnp.stack([gain_one, gain_two, gain_three]), bias_grad_local, square_part), ("dp", "pair")
    )
    clip_norm = jnp.sqrt(
        square_sum + jnp.sum(gain_grad * gain_grad) + jnp.sum(bias_grad * bias_grad)
    )
    factor = jnp.minimum(1.0, clip_limit / clip_norm)
    table_out = adam_step(embed_table, embed_first, embed_second, table_grad * factor, 1.0, 0.01)
    qkv_out = adam_step(qkv_weight, qkv_first, qkv_second, weight_grads[0] * factor, 0.05, 0.01)
    out_out = adam_step(out_weight, out_first, out_second, weight_grads[1] * factor, 0.05, 0.01)
    in_out = adam_step(in_weight, in_first, in_second, weight_grads[2] * factor, 0.05, 0.01)
    down_out = adam_step(down_weight, down_first, down_second, weight_grads[3] * factor, 0.05, 0.01)
    gains_out = adam_step(norm_gains, gains_first, gains_second, gain_grad * factor, 1.0, 0.0)
    bias_out = adam_step(position_bias, bias_first, bias_second, bias_grad * factor, 0.3, 0.0)
    return (
        loss_value,
        clip_norm,
        table_out[0],
        table_out[1],
        table_out[2],
        qkv_out[0],
        qkv_out[1],
        qkv_out[2],
        out_out[0],
        out_out[1],
        out_out[2],
        in_out[0],
        in_out[1],
        in_out[2],
        down_out[0],
        down_out[1],
        down_out[2],
        gains_out[0],
        gains_out[1],
        gains_out[2],
        bias_out[0],
        bias_out[1],
        bias_out[2],
    )


def local_fast(
    token_owner,
    token_row,
    lengths,
    positives,
    negatives,
    neg_counts,
    embed_table,
    embed_first,
    embed_second,
    qkv_weight,
    qkv_first,
    qkv_second,
    out_weight,
    out_first,
    out_second,
    in_weight,
    in_first,
    in_second,
    down_weight,
    down_first,
    down_second,
    norm_gains,
    gains_first,
    gains_second,
    position_bias,
    bias_first,
    bias_second,
):
    doc_count = lengths.shape[0]
    seq_len = token_row.shape[1]
    model_width = embed_table.shape[1]
    head_count = position_bias.shape[1]
    bucket_count = position_bias.shape[0]
    tok_total = doc_count * seq_len
    owners = lax.axis_size("dp")
    capacity = max(2, 2 * tok_total // owners)
    holders = lax.axis_size("pair")
    shards = (qkv_weight, out_weight, in_weight, down_weight)
    embedded_low, slot_keys, asked_rows, *full = front(
        token_owner.reshape(token_row.shape),
        token_row,
        embed_table,
        shards,
        weight_pieces([shard.shape[1] for shard in shards]),
        capacity,
        owners,
        holders,
        1,
    )
    qkv_full, out_full, in_full, down_full = (
        matrix.reshape(-1, matrix.shape[2]) for matrix in full
    )
    embedded = embedded_low.astype(jnp.float32)
    positions = jnp.arange(seq_len)
    live = positions[None, :] < lengths[:, None]
    offset_bias = bias_rows(position_bias.T, seq_len)
    normed_one, inverse_one = rms_forward(embedded, norm_gains[0])
    normed_one = normed_one.astype(jnp.bfloat16)
    qkv_rows = jnp.dot(normed_one, qkv_full, preferred_element_type=jnp.float32).astype(
        jnp.bfloat16
    )
    attended = attention(lengths, qkv_rows, offset_bias, seq_len)
    residual = embedded + jnp.dot(attended, out_full, preferred_element_type=jnp.float32)
    normed_two, inverse_two = rms_forward(residual, norm_gains[1])
    normed_two = normed_two.astype(jnp.bfloat16)
    hidden = jax.nn.relu(jnp.dot(normed_two, in_full, preferred_element_type=jnp.float32)).astype(
        jnp.bfloat16
    )
    output_rows = residual + jnp.dot(hidden, down_full, preferred_element_type=jnp.float32)
    normed_three, inverse_three = rms_forward(output_rows, norm_gains[2])
    live_rows = live.reshape(-1, 1)
    length_float = lengths.astype(jnp.float32)
    pooled_local = (
        jnp.sum(
            jnp.where(live_rows, normed_three, 0.0).reshape(doc_count, seq_len, model_width), axis=1
        )
        / length_float[:, None]
    )
    loss_cell, grad_pooled = pooled_loss(
        pooled_local, positives, negatives, neg_counts, 3
    )
    grad_three = jnp.where(
        live_rows, jnp.repeat(grad_pooled / length_float[:, None], seq_len, axis=0), 0.0
    )
    qkv_back, out_back, in_back, down_back = (qkv_full, out_full, in_full, down_full)
    grad_output, gain_three = rms_backward(output_rows, inverse_three, norm_gains[2], grad_three)
    grad_branch = grad_output.astype(jnp.bfloat16)
    grad_down = lax.dot_general(
        hidden, grad_branch, CONTRACT_ROWS, preferred_element_type=jnp.float32
    )
    grad_hidden = lax.dot_general(
        grad_branch, down_back, CONTRACT_COLS, preferred_element_type=jnp.float32
    )
    grad_pre = jnp.where(hidden > 0, grad_hidden, 0.0).astype(jnp.bfloat16)
    grad_in = lax.dot_general(
        normed_two, grad_pre, CONTRACT_ROWS, preferred_element_type=jnp.float32
    )
    grad_normed_two = lax.dot_general(
        grad_pre, in_back, CONTRACT_COLS, preferred_element_type=jnp.float32
    )
    grad_res_part, gain_two = rms_backward(residual, inverse_two, norm_gains[1], grad_normed_two)
    grad_residual = grad_output + grad_res_part
    grad_attn_branch = grad_residual.astype(jnp.bfloat16)
    grad_out = lax.dot_general(
        attended, grad_attn_branch, CONTRACT_ROWS, preferred_element_type=jnp.float32
    )
    grad_attended = lax.dot_general(
        grad_attn_branch, out_back, CONTRACT_COLS, preferred_element_type=jnp.float32
    ).astype(jnp.bfloat16)
    parts = owners * holders

    def blocks(*grads):
        return [grad.astype(jnp.bfloat16).reshape(parts, -1, grad.shape[1]) for grad in grads]

    grad_qkv_rows, diagonals, squares, down_grad = attention_back(
        lengths,
        qkv_rows,
        grad_attended,
        offset_bias,
        seq_len,
        blocks(grad_down),
        early_pieces(model_width),
        5,
    )
    bias_grad_local = bias_gradient(diagonals, seq_len, bucket_count)
    grad_qkv = lax.dot_general(
        normed_one, grad_qkv_rows, CONTRACT_ROWS, preferred_element_type=jnp.float32
    )
    grad_normed_one = lax.dot_general(
        grad_qkv_rows, qkv_back, CONTRACT_COLS, preferred_element_type=jnp.float32
    )
    grad_emb_part, gain_one = rms_backward(embedded, inverse_one, norm_gains[0], grad_normed_one)
    grad_embedded = grad_residual + grad_emb_part
    table_grad, total, qkv_grad, out_grad, in_grad = back(
        grad_embedded.astype(jnp.bfloat16),
        slot_keys,
        asked_rows.reshape(1, -1),
        squares,
        bias_grad_local,
        [gain.reshape(1, -1) for gain in (gain_one, gain_two, gain_three)],
        blocks(grad_qkv, grad_out, grad_in),
        late_pieces([grad.shape[1] for grad in (grad_qkv, grad_out, grad_in)]),
        embed_table.shape[0],
        model_width // 128,
        2,
    )
    weight_grads = (qkv_grad, out_grad, in_grad, down_grad)
    norm_cell, loss_cell, *updated = update(
        total,
        loss_cell,
        table_grad,
        (embed_table, embed_first, embed_second),
        (
            norm_gains,
            gains_first,
            gains_second,
            position_bias.T,
            bias_first.T,
            bias_second.T,
        ),
        weight_grads,
        (
            (qkv_weight, qkv_first, qkv_second),
            (out_weight, out_first, out_second),
            (in_weight, in_first, in_second),
            (down_weight, down_first, down_second),
        ),
    )
    return (loss_cell[0, 0], norm_cell[0, 0], *updated[:3], *updated[9:], *updated[3:6], *(new.T for new in updated[6:9]))


def local(*arrays):
    n_dp, n_pair = lax.axis_size("dp"), lax.axis_size("pair")
    lengths, qkv_weight, down_weight = arrays[2], arrays[9], arrays[18]
    fits = (
        n_pair == 4
        and n_dp & (n_dp - 1) == 0
        and qkv_weight.shape[0] % 8 == 0
        and down_weight.shape[0] % 8 == 0
        and lengths.shape[0] == 2
        and 2 * arrays[1].size // n_dp % 128 == 0
    )
    return (local_fast if fits else local_plain)(*arrays)


def solution(mesh):
    return jax.shard_map(
        local,
        mesh=mesh,
        in_specs=(
            P(("dp", "pair"), None, None),
            P(("dp", "pair"), None),
            P(("dp", "pair")),
            P(),
            P(),
            P(),
            P("dp", None),
            P("dp", None),
            P("dp", None),
            P(("dp", "pair"), None),
            P(("dp", "pair"), None),
            P(("dp", "pair"), None),
            P(("dp", "pair"), None),
            P(("dp", "pair"), None),
            P(("dp", "pair"), None),
            P(("dp", "pair"), None),
            P(("dp", "pair"), None),
            P(("dp", "pair"), None),
            P(("dp", "pair"), None),
            P(("dp", "pair"), None),
            P(("dp", "pair"), None),
            P(),
            P(),
            P(),
            P(),
            P(),
            P(),
        ),
        out_specs=(
            P(),
            P(),
            P("dp", None),
            P("dp", None),
            P("dp", None),
            P(("dp", "pair"), None),
            P(("dp", "pair"), None),
            P(("dp", "pair"), None),
            P(("dp", "pair"), None),
            P(("dp", "pair"), None),
            P(("dp", "pair"), None),
            P(("dp", "pair"), None),
            P(("dp", "pair"), None),
            P(("dp", "pair"), None),
            P(("dp", "pair"), None),
            P(("dp", "pair"), None),
            P(("dp", "pair"), None),
            P(),
            P(),
            P(),
            P(),
            P(),
            P(),
        ),
        check_vma=False,
    )
```

```python
import functools
import math

import jax
import jax.numpy as jnp
import numpy as np
from jax import lax
from jax.experimental import pallas as pl
from jax.experimental.pallas import tpu as pltpu
from jax.sharding import PartitionSpec as P

REACH = 128
STEP = 5


rms_eps = 1e-06
clip_limit = 0.05
margin = 1.0
sim_scale = 20.0
beta_one = 0.9
beta_two = 0.999
adam_eps = 1e-08
HIGHEST = lax.Precision.HIGHEST
CONTRACT_ROWS = (((0,), (0,)), ((), ()))
CONTRACT_COLS = (((1,), (1,)), ((), ()))


def bucket_of(offsets, bucket_count, reach_limit):
    half_count = bucket_count // 2
    exact_count = half_count // 2
    sign_base = jnp.where(offsets > 0, half_count, 0).astype(jnp.int32)
    distance = jnp.abs(offsets)
    far_bucket = jnp.full(offsets.shape, exact_count, jnp.int32)
    for level_index in range(1, half_count - exact_count):
        threshold = int(
            math.ceil(
                exact_count
                * (reach_limit / exact_count) ** (level_index / (half_count - exact_count))
                - 1e-09
            )
        )
        far_bucket = far_bucket + (distance >= threshold).astype(jnp.int32)
    return sign_base + jnp.where(distance < exact_count, distance, far_bucket)


def rms_forward(values, gain):
    inverse = lax.rsqrt(jnp.mean(values * values, axis=-1, keepdims=True) + rms_eps)
    return (values * inverse * gain, inverse)


def rms_backward(values, inverse, gain, upstream):
    scaled = upstream * gain
    normed = values * inverse
    grad_values = inverse * (scaled - normed * jnp.mean(scaled * normed, axis=-1, keepdims=True))
    return (grad_values, jnp.sum(upstream * normed, axis=0))


def margin_loss(pooled, positives, negatives, neg_counts):
    unit = pooled * lax.rsqrt(jnp.sum(pooled * pooled, axis=-1, keepdims=True) + 1e-06)
    similar = sim_scale * jnp.dot(unit, unit.T, precision=HIGHEST)
    chosen = jnp.take_along_axis(similar, positives[:, None], axis=1)
    against = jnp.take_along_axis(similar, negatives, axis=1)
    live_slots = jnp.arange(negatives.shape[1])[None, :] < neg_counts[:, None]
    terms = jnp.where(live_slots, jax.nn.softplus(margin - chosen + against), 0.0)
    return jnp.mean(jnp.sum(terms, axis=1) / neg_counts.astype(jnp.float32))


def doc_scores(query_heads, key_heads, bias_full, live_keys):
    scores = (
        jnp.einsum("qhd,khd->hqk", query_heads, key_heads, preferred_element_type=jnp.float32)
        * 0.125
        + bias_full
    )
    return jnp.where(live_keys[None, None, :], scores, -1000000000.0)


def attend_forward(query_heads, key_heads, value_heads, bias_full, live_keys):
    scores = doc_scores(query_heads, key_heads, bias_full, live_keys)
    highest = jnp.max(scores, axis=-1, keepdims=True)
    weights = jnp.exp(scores - highest)
    totals = jnp.sum(weights, axis=-1, keepdims=True)
    probabilities = (weights / totals).astype(jnp.bfloat16)
    attended = jnp.einsum(
        "hqk,khd->qhd", probabilities, value_heads, preferred_element_type=jnp.float32
    )
    return (attended, highest + jnp.log(totals))


def attend_backward(
    query_heads, key_heads, value_heads, bias_full, live_keys, logsum, grad_attended
):
    probabilities = jnp.exp(doc_scores(query_heads, key_heads, bias_full, live_keys) - logsum)
    grad_value = jnp.einsum(
        "hqk,qhd->khd",
        probabilities.astype(jnp.bfloat16),
        grad_attended,
        preferred_element_type=jnp.float32,
    )
    grad_prob = jnp.einsum(
        "qhd,khd->hqk", grad_attended, value_heads, preferred_element_type=jnp.float32
    )
    grad_score = probabilities * (
        grad_prob - jnp.sum(probabilities * grad_prob, axis=-1, keepdims=True)
    )
    grad_low = grad_score.astype(jnp.bfloat16)
    grad_query = (
        jnp.einsum("hqk,khd->qhd", grad_low, key_heads, preferred_element_type=jnp.float32) * 0.125
    )
    grad_key = (
        jnp.einsum("hqk,qhd->khd", grad_low, query_heads, preferred_element_type=jnp.float32)
        * 0.125
    )
    return (grad_query, grad_key, grad_value, grad_low)


def adam_step(weight, first, second, grad, rate, shrink):
    first_new = beta_one * first + (1.0 - beta_one) * grad
    second_new = beta_two * second + (1.0 - beta_two) * grad * grad
    first_hat = first_new / (1.0 - beta_one**STEP)
    second_hat = second_new / (1.0 - beta_two**STEP)
    weight_new = weight - rate * (first_hat / (jnp.sqrt(second_hat) + adam_eps) + shrink * weight)
    return (weight_new, first_new, second_new)


MESH = pl.DeviceIdType.MESH
VMEM_LIMIT = 64 * 1024 * 1024 - 65536
ANY = pl.BlockSpec(memory_space=pl.ANY)
VM = pl.BlockSpec(memory_space=pltpu.VMEM)


def place(index, n_pair):
    return {"dp": index // n_pair, "pair": lax.rem(index, n_pair)}


def remote(src, dst, send, recv, target):
    return pltpu.make_async_remote_copy(
        src, dst, send, recv, device_id=target, device_id_type=MESH
    )


def greet(targets):
    sem = pltpu.get_barrier_semaphore()
    for target in targets:
        pl.semaphore_signal(sem, inc=1, device_id=target, device_id_type=MESH)
    pl.semaphore_wait(sem, len(targets))


def my_index(n_pair):
    return lax.axis_index("dp") * n_pair + lax.axis_index("pair")


def bit_order(n_dp, n_pair, color):
    dp_bits, pair_bits = (n_dp - 1).bit_length(), (n_pair - 1).bit_length()
    high = list(reversed(range(pair_bits + 1, pair_bits + dp_bits))) + [pair_bits]
    side = list(reversed(range(1, pair_bits)))
    return high + side if color == 0 else side + high


def offset(order, position):
    return sum(((position >> step) & 1) << bit for step, bit in enumerate(order))


class Rounds:
    def __init__(self, n_dp, n_pair, dp_sem, pair_sem, own_sem):
        self.n_dp, self.n_pair = n_dp, n_pair
        self.dp_sem, self.pair_sem, self.own_sem = dp_sem, pair_sem, own_sem
        self.dp, self.pair = lax.axis_index("dp"), lax.axis_index("pair")
        sem = pltpu.get_barrier_semaphore()
        targets = [{"dp": self.dp ^ j, "pair": self.pair} for j in range(1, n_dp)]
        targets += [{"dp": self.dp, "pair": self.pair ^ j} for j in range(1, n_pair)]
        for target in targets:
            pl.semaphore_signal(sem, inc=1, device_id=target, device_id_type=MESH)
        self.entered = lambda: pl.semaphore_wait(sem, len(targets))

    def over_dp(self, block, by_dp):
        def copy(j, slot):
            target = {"dp": self.dp ^ j, "pair": self.pair}
            return remote(block, by_dp.at[slot], self.dp_sem.at[0, j], self.dp_sem.at[1, j], target)

        self.exchange(block, by_dp, self.dp, self.n_dp, copy)

    def over_pair(self, block, by_pair):
        def copy(j, slot):
            target = {"dp": self.dp, "pair": self.pair ^ j}
            return remote(
                block, by_pair.at[slot], self.pair_sem.at[0, j], self.pair_sem.at[1, j], target
            )

        self.exchange(block, by_pair, self.pair, self.n_pair, copy)

    def exchange(self, block, places, me, size, copy):
        own = pltpu.make_async_copy(block, places.at[me], self.own_sem)
        own.start()
        for j in reversed(range(1, size)):
            copy(j, me).start()
        own.wait()
        for j in range(1, size):
            copy(j, me ^ j).wait_recv()
        for j in range(1, size):
            copy(j, me).wait_send()


def round_sems(n_dp, n_pair):
    sem = pltpu.SemaphoreType.DMA
    return [sem((2, n_dp)), sem((2, n_pair)), sem]


def loss_kernel(
    n_dp,
    n_pair,
    len_ref,
    x_ref,
    pos_ref,
    neg_ref,
    count_ref,
    loss_ref,
    grad_ref,
    own,
    by_dp,
    by_pair,
    unit,
    *sems,
):
    rounds = Rounds(n_dp, n_pair, *sems)
    docs, width = x_ref.shape
    lengths = [len_ref[d].astype(jnp.float32) for d in range(docs)]
    for d in range(docs):
        own[d : d + 1] = x_ref[d : d + 1] / lengths[d]
    rounds.entered()
    rounds.over_dp(own, by_dp)
    rounds.over_pair(by_dp, by_pair)
    total = n_dp * n_pair * docs
    for d in range(n_dp):
        for p in range(n_pair):
            base = (d * n_pair + p) * docs
            unit[base : base + docs] = by_pair[p, d]
    pooled = unit[...]
    inverse = lax.rsqrt(jnp.sum(pooled * pooled, axis=1, keepdims=True) + 1e-06)
    units = pooled * inverse
    similar = 20.0 * lax.dot_general(
        units, units, NT, precision=HIGHEST, preferred_element_type=jnp.float32
    )
    partner = lax.broadcasted_iota(jnp.int32, (total, total), 0)
    is_pos = partner == pos_ref[...]
    chosen = jnp.sum(jnp.where(is_pos, similar, 0.0), axis=0, keepdims=True)
    counts = count_ref[...]
    weight = 1.0 / (counts.astype(jnp.float32) * total)
    losses = jnp.zeros((1, total), jnp.float32)
    slopes = jnp.zeros((1, total), jnp.float32)
    grad_similar = jnp.zeros((total, total), jnp.float32)
    for slot in range(neg_ref.shape[0]):
        is_neg = partner == neg_ref[slot : slot + 1, :]
        against = jnp.sum(jnp.where(is_neg, similar, 0.0), axis=0, keepdims=True)
        value = margin - chosen + against
        used = slot < counts
        soft = jnp.maximum(value, 0.0) + jnp.log1p(jnp.exp(-jnp.abs(value)))
        losses = losses + jnp.where(used, soft, 0.0)
        slope = jnp.where(used, weight / (1.0 + jnp.exp(-value)), 0.0)
        grad_similar = grad_similar + jnp.where(is_neg, slope, 0.0)
        slopes = slopes + slope
    grad_similar = grad_similar - jnp.where(is_pos, slopes, 0.0)
    loss_ref[...] = jnp.sum(losses * weight, axis=1, keepdims=True)
    grad_units = sim_scale * (
        jnp.dot(grad_similar, units, precision=HIGHEST, preferred_element_type=jnp.float32)
        + lax.dot_general(
            grad_similar, units, TN, precision=HIGHEST, preferred_element_type=jnp.float32
        )
    )
    inner = jnp.sum(grad_units * units, axis=1, keepdims=True)
    unit[...] = inverse * (grad_units - units * inner)
    for d in range(n_dp):
        for p in range(n_pair):
            base = (d * n_pair + p) * docs

            @pl.when((rounds.dp == d) & (rounds.pair == p))
            def _():
                for doc in range(docs):
                    grad_ref[doc : doc + 1] = unit[base + doc : base + doc + 1] / lengths[doc]


def pooled_loss(sums, lengths, positives, negatives, counts, cid):
    n_dp, n_pair = lax.axis_size("dp"), lax.axis_size("pair")
    docs, width = sums.shape
    return pl.pallas_call(
        functools.partial(loss_kernel, n_dp, n_pair),
        out_shape=[
            jax.ShapeDtypeStruct((1, 1), jnp.float32),
            jax.ShapeDtypeStruct(sums.shape, jnp.float32),
        ],
        in_specs=[pl.BlockSpec(memory_space=pltpu.SMEM)] + [VM] * 4,
        out_specs=[VM] * 2,
        scratch_shapes=[
            pltpu.VMEM((docs, width), jnp.float32),
            pltpu.VMEM((n_dp, docs, width), jnp.float32),
            pltpu.VMEM((n_pair, n_dp, docs, width), jnp.float32),
            pltpu.VMEM((n_dp * n_pair * docs, width), jnp.float32),
        ]
        + round_sems(n_dp, n_pair),
        compiler_params=pltpu.CompilerParams(collective_id=cid, has_side_effects=True),
        name="pooled_loss",
    )(lengths, sums, positives.reshape(1, -1), negatives.T, counts.reshape(1, -1))


NT = (((1,), (1,)), ((), ()))
TN = (((0,), (0,)), ((), ()))

def band(w_ref, row, base, h, table, seq):
    tiles = seq // 128
    for d in range(1 - tiles, tiles):
        low = base + seq + 128 * d - 128
        line = w_ref[pl.ds(row, 1), low : low + 256]
        if 128 * (abs(d) - 1) < REACH:
            x = jnp.broadcast_to(line, (128, 256))
            tile = pltpu.roll(x, 0, 1, stride=1, stride_axis=0)[:, 128:]
        else:
            tile = jnp.broadcast_to(line, (128, 256))[:, 128:]
        for a in range(tiles):
            if 0 <= a + d < tiles:
                table[h, a * 128 : a * 128 + 128, (a + d) * 128 : (a + d) * 128 + 128] = tile

def forward_kernel(len_ref, q_ref, k_ref, v_ref, w_ref, o_ref, table):
    seq = q_ref.shape[0]
    doc = pl.program_id(1)
    @pl.when(doc == 0)
    def _():
        for h in range(2):
            band(w_ref, 2 * pl.program_id(0) + h, 0, h, table, seq)
    length = len_ref[doc]
    lane = lax.broadcasted_iota(jnp.int32, (seq, 128), 1)
    column = lax.broadcasted_iota(jnp.int32, (1, seq), 1)
    q = q_ref[...] * jnp.bfloat16(0.125)
    k = k_ref[...]
    v = v_ref[...]
    got = []
    for h in range(2):
        mine = (lane < 64) == (h == 0)
        s = lax.dot_general(jnp.where(mine, q, 0), k, NT, preferred_element_type=jnp.float32)
        s = jnp.where(column < length, s + table[h], -1000000000.0)
        e = jnp.exp(s - jnp.max(s, axis=1, keepdims=True))
        p = (e * (1.0 / jnp.sum(e, axis=1, keepdims=True))).astype(jnp.bfloat16)
        got.append(jnp.dot(p, v, preferred_element_type=jnp.float32))
    o_ref[...] = jnp.where(lane < 64, got[0], got[1]).astype(o_ref.dtype)

def attention(lengths, qkv, w, seq):
    tokens = qkv.shape[0]
    pairs = w.shape[0] // 2
    docs = tokens // seq
    spec = lambda base: pl.BlockSpec((seq, 128), lambda h, d, *_: (d, base + h))
    return pl.pallas_call(
        forward_kernel,
        grid_spec=pltpu.PrefetchScalarGridSpec(
            num_scalar_prefetch=1, grid=(pairs, docs),
            in_specs=[spec(0), spec(pairs), spec(2 * pairs), pl.BlockSpec(w.shape, lambda h, d, *_: (0, 0))],
            out_specs=spec(0),
            scratch_shapes=[pltpu.VMEM((2, seq, seq), jnp.float32)]),
        out_shape=jax.ShapeDtypeStruct((tokens, pairs * 128), jnp.bfloat16),
        compiler_params=pltpu.CompilerParams(dimension_semantics=("arbitrary", "arbitrary"), vmem_limit_bytes=50 * 1024 * 1024),
        name="attention",
    )(lengths, qkv, qkv, qkv, w)

def bucket_hits(offsets, buckets):
    half = buckets // 2
    exact = half // 2
    distance = np.abs(offsets)
    far = np.full(offsets.shape, exact)
    for level in range(1, half - exact):
        limit = math.ceil(exact * (REACH / exact) ** (level / (half - exact)) - 1e-09)
        far = far + (distance >= limit)
    bucket = np.where(offsets > 0, half, 0) + np.where(distance < exact, distance, far)
    return (bucket[:, None] == np.arange(buckets)[None, :]).astype(np.float32)


def bias_rows(bias, seq):
    offsets = np.arange(2 * seq) - seq
    hits = bucket_hits(np.concatenate([offsets, -offsets]), bias.shape[1])
    return jnp.dot(bias, hits.T, precision=HIGHEST)


def bias_gradient(sums, seq, buckets):
    heads, width = sums.shape[0] * 2, sums.shape[2] * sums.shape[3]
    j = np.arange(256)
    offsets = [np.where(j < 255, 128 * d + 127 - j, 0) for d in (-1, 0, 1)]
    offsets += [np.full((256,), 1 - seq), np.full((256,), seq - 1)]
    hits = bucket_hits(np.concatenate(offsets), buckets)
    hits = np.concatenate([hits, np.zeros((width - hits.shape[0], buckets), np.float32)])
    return jnp.dot(sums.reshape(heads, width), hits, precision=HIGHEST)


def weight_pieces(widths):
    cut = widths[3] * 2 // 3 // 128 * 128
    return [
        (0, 0, widths[0], 1),
        (2, 0, widths[2], 0),
        (1, 0, widths[1], 0),
        (3, 0, cut, 0),
        (3, cut, widths[3], 1),
    ]


def early_pieces(width):
    cut = width // 2 // 128 * 128
    return [(0, 0, cut, 0), (0, cut, width, 1)]


def late_pieces(widths):
    return [(2, 0, widths[2], 0), (0, 0, widths[0], 1), (1, 0, widths[1], 1)]


NN = (((1,), (0,)), ((), ()))


def stage(r):
    return (0, 1) if r == 0 else (1 << (r - 1), 1 << (r - 1))


class Gather:
    def __init__(self, n_dp, n_pair, pieces, outs, bufs, sems):
        self.n_pair, self.pieces, self.outs, self.bufs = n_pair, pieces, outs, bufs
        self.hop_sem, self.side_sem, self.core_sem, self.out_sem = sems
        self.me = my_index(n_pair)
        self.hops = (n_dp * n_pair - 1).bit_length() - 2
        self.orders = [bit_order(n_dp, n_pair, piece[3]) for piece in pieces]
        self.count = len(pieces)

    def send(self, a, lo, count, to, sem, which, bit):
        return remote(
            self.bufs[a].at[pl.ds(lo, count)],
            self.bufs[a].at[pl.ds(to, count)],
            sem.at[0, a, which],
            sem.at[1, a, which],
            place(self.me ^ (1 << bit), self.n_pair),
        )

    def hop(self, a, r):
        return self.send(a, 0, 1 << r, 1 << r, self.hop_sem, r, self.orders[a][r])

    def side(self, a, r):
        lo, count = stage(r)
        return self.send(a, lo, count, (1 << self.hops) + lo, self.side_sem, r, self.orders[a][self.hops])

    def core(self, a, r, sided):
        lo, count = stage(r)
        lo = lo + (sided << self.hops)
        return self.send(
            a, lo, count, (2 << self.hops) + lo, self.core_sem, 2 * r + sided, 0
        )

    def write_out(self, a, lo, count):
        which, low, high, _ = self.pieces[a]
        for p in range(lo, lo + count):
            block = self.me ^ offset(self.orders[a] + [0], p)
            pltpu.make_async_copy(
                self.bufs[a].at[p], self.outs[which].at[block, :, pl.ds(low, high - low)], self.out_sem.at[a]
            ).start()

    def held(self, r):
        lo, count = stage(r)
        for a in range(self.count):
            if r:
                self.hop(a, r - 1).wait_recv()
            if r < self.hops:
                self.hop(a, r).start()
            self.side(a, r).start()
            self.core(a, r, 0).start()
        for a in range(self.count):
            self.write_out(a, lo, count)

    def sided(self, r):
        lo, count = stage(r)
        for a in range(self.count):
            self.side(a, r).wait_recv()
            self.core(a, r, 1).start()
            self.write_out(a, (1 << self.hops) + lo, count)

    def cored(self, r):
        lo, count = stage(r)
        for sided in (0, 1):
            for a in range(self.count):
                self.core(a, r, sided).wait_recv()
                self.write_out(a, (2 << self.hops) + (sided << self.hops) + lo, count)

    def finish(self):
        for a in range(self.count):
            for r in range(self.hops):
                self.hop(a, r).wait_send()
            for r in range(self.hops + 1):
                self.side(a, r).wait_send()
                self.core(a, r, 0).wait_send()
                self.core(a, r, 1).wait_send()
            pltpu.make_async_copy(self.bufs[a], self.bufs[a], self.out_sem.at[a]).wait()


def triangle(size):
    rows = lax.broadcasted_iota(jnp.int32, (size, size), 0)
    columns = lax.broadcasted_iota(jnp.int32, (size, size), 1)
    return jnp.where(rows < columns, 1.0, 0.0).astype(jnp.bfloat16)


def digits(numbers):
    high = numbers // 64
    row = lax.broadcasted_iota(jnp.int32, (8, numbers.shape[1]), 0)
    both = jnp.where(row == 0, high, jnp.where(row == 1, numbers - 64 * high, 0))
    return both.astype(jnp.float32).astype(jnp.bfloat16)


def upright(pairs):
    row = lax.broadcasted_iota(jnp.int32, (8, 128), 0)
    value = jnp.where(row == 0, 64.0, jnp.where(row == 1, 1.0, 0.0)).astype(jnp.bfloat16)
    return lax.dot_general(pairs, value, TN, preferred_element_type=jnp.float32)


def hits_by_lane(numbers, width, base):
    lane = lax.broadcasted_iota(jnp.int32, (1, 128), 1).astype(jnp.float32) + base
    tiles = [
        jnp.where(numbers == lane + 128.0 * tile, 1.0, 0.0).astype(jnp.bfloat16)
        for tile in range(width // 128)
    ]
    return jnp.concatenate(tiles, axis=1)


def front_kernel(n_dp, n_pair, pieces, n_in, *refs):
    k = len(pieces)
    owner_ref, row_ref, table_ref = refs[:3]
    shards = refs[3 : 3 + n_in]
    emb_ref, key_ref, asked_ref = refs[3 + n_in : 6 + n_in]
    outs = refs[6 + n_in : 6 + 2 * n_in]
    rest = refs[6 + 2 * n_in :]
    bufs, rest = rest[:k], rest[k:]
    wide, table, ask_out, ask_in, rows_out, rows_in, total = rest[:7]
    table_sem, ask_sem, row_sem, *sems = rest[7:]
    dp, pair = lax.axis_index("dp"), lax.axis_index("pair")
    weights = Gather(n_dp, n_pair, pieces, outs, bufs, sems)
    docs, seq = owner_ref.shape
    tokens = docs * seq
    cap = ask_out.shape[2]

    def in_line(ref):
        return jnp.concatenate([ref[d : d + 1, :] for d in range(docs)], axis=1)

    table_rows = table_ref.shape[0]
    load = pltpu.make_async_copy(table_ref, wide, table_sem)
    load.start()
    peers = [{"dp": dp ^ j, "pair": pair} for j in range(1, n_dp)]
    sem = pltpu.get_barrier_semaphore()
    mates = [{"dp": dp, "pair": pair ^ j} for j in (1, 2)]
    for target in peers + mates:
        pl.semaphore_signal(sem, inc=1, device_id=target, device_id_type=MESH)
    for a, (which, low, high, _) in enumerate(pieces):
        bufs[a][0] = shards[which][:, low:high].astype(jnp.bfloat16)
    pl.semaphore_wait(sem, n_dp + 1)
    weights.held(0)

    owner = in_line(owner_ref)
    by_owner = lax.broadcasted_iota(jnp.int32, (n_dp, tokens), 0) == owner
    ranks = jnp.dot(
        jnp.where(by_owner, 1.0, 0.0).astype(jnp.bfloat16),
        triangle(tokens),
        preferred_element_type=jnp.float32,
    )
    rank = jnp.sum(jnp.where(by_owner, ranks, 0.0), axis=0, keepdims=True)
    key = owner * cap + rank.astype(jnp.int32)
    key_ref[...] = key
    wanted = digits(in_line(row_ref))

    def peer(j):
        return {"dp": dp ^ j, "pair": pair}

    def ask(j):
        return remote(ask_out.at[j], ask_in.at[j], ask_sem.at[0, j], ask_sem.at[1, j], peer(j))

    def reply(j):
        return remote(rows_out.at[j], rows_in.at[j], row_sem.at[0, j], row_sem.at[1, j], peer(j))

    def loop(first, last, body):
        def turn(t, carry):
            body(n_dp - 1 - t)
            return carry

        lax.fori_loop(first, last, turn, 0)

    def request(j):
        slot = lax.broadcasted_iota(jnp.int32, (cap, tokens), 0) + (dp ^ j) * cap
        chosen = jnp.where(slot == key, 1.0, 0.0).astype(jnp.bfloat16)
        ask_out[j] = lax.dot_general(wanted, chosen, NT, preferred_element_type=jnp.float32)

        @pl.when(j > 0)
        def _():
            ask(j).start()

    loop(0, n_dp, request)
    ask_in[0] = ask_out[0]
    weights.held(1)
    load.wait()

    def narrow(i, carry):
        part = pl.ds(pl.multiple_of(i * 16, 16), 16)
        table[part] = wide[part].astype(jnp.bfloat16)
        return carry

    lax.fori_loop(0, table_rows // 16, narrow, 0)
    if table.shape[0] > table_rows:
        table[table_rows:] = jnp.zeros((table.shape[0] - table_rows, table.shape[1]), jnp.bfloat16)

    def answer(j):
        @pl.when(j > 0)
        def _():
            ask(j).wait_recv()

        asked = ask_in[j]
        hit = hits_by_lane(upright(asked.astype(jnp.bfloat16)), table.shape[0], 0.0)
        got = jnp.dot(hit, table[...], preferred_element_type=jnp.float32)
        rows_out[j] = got.astype(jnp.bfloat16)
        asked_ref[j] = (64.0 * asked[0:1] + asked[1:2]).astype(jnp.int32)

        @pl.when(j > 0)
        def _():
            reply(j).start()

    early = n_dp // 4 + 1
    loop(0, early, answer)
    weights.held(2)
    weights.sided(0)
    loop(early, n_dp, answer)
    rows_in[0] = rows_out[0]
    weights.sided(1)
    upright_key = upright(digits(key))

    total[...] = jnp.zeros_like(total)

    def seat(j):
        @pl.when(j > 0)
        def _():
            reply(j).wait_recv()

        place_hit = hits_by_lane(upright_key, cap, ((dp ^ j) * cap).astype(jnp.float32))
        total[...] += jnp.dot(place_hit, rows_in[j], preferred_element_type=jnp.float32)

    weights.cored(0)
    for r in range(3, weights.hops + 1):
        weights.held(r)
        weights.sided(r - 1)
        weights.cored(r - 2)
    loop(0, n_dp, seat)
    emb_ref[...] = total[...].astype(jnp.bfloat16)
    weights.sided(weights.hops)
    for r in (weights.hops - 1, weights.hops):
        weights.cored(r)
    for j in range(1, n_dp):
        ask(j).wait_send()
        reply(j).wait_send()
    weights.finish()


def front(owner, row, table, shards, pieces, cap, n_dp, n_pair, cid):
    n, k = n_dp * n_pair, len(pieces)
    hops = (n - 1).bit_length() - 2
    tokens = owner.size
    table_rows, width = table.shape
    padded = -(-table_rows // 256) * 256
    sem = pltpu.SemaphoreType.DMA
    return pl.pallas_call(
        functools.partial(front_kernel, n_dp, n_pair, pieces, len(shards)),
        out_shape=[
            jax.ShapeDtypeStruct((tokens, width), jnp.bfloat16),
            jax.ShapeDtypeStruct((1, tokens), jnp.int32),
            jax.ShapeDtypeStruct((n_dp, 1, cap), jnp.int32),
        ]
        + [jax.ShapeDtypeStruct((n,) + s.shape, jnp.bfloat16) for s in shards],
        in_specs=[VM, VM, ANY] + [VM] * len(shards),
        out_specs=[VM] * 3 + [ANY] * len(shards),
        scratch_shapes=[
            pltpu.VMEM((n, shards[p[0]].shape[0], p[2] - p[1]), jnp.bfloat16) for p in pieces
        ]
        + [
            pltpu.VMEM((table_rows, width), jnp.float32),
            pltpu.VMEM((padded, width), jnp.bfloat16),
            pltpu.VMEM((n_dp, 8, cap), jnp.float32),
            pltpu.VMEM((n_dp, 8, cap), jnp.float32),
            pltpu.VMEM((n_dp, cap, width), jnp.bfloat16),
            pltpu.VMEM((n_dp, cap, width), jnp.bfloat16),
            pltpu.VMEM((tokens, width), jnp.float32),
            sem,
            sem((2, n_dp)),
            sem((2, n_dp)),
            sem((2, k, hops)),
            sem((2, k, hops + 1)),
            sem((2, k, 2 * hops + 2)),
            sem((k,)),
        ],
        compiler_params=pltpu.CompilerParams(
            collective_id=cid, has_side_effects=True, vmem_limit_bytes=VMEM_LIMIT
        ),
        name="rows_and_weights",
    )(owner, row, table, *shards)


class Scatter:
    def __init__(self, n_dp, n_pair, pieces, ins, outs, boxes, sems):
        self.n_pair, self.pieces, self.ins, self.outs = n_pair, pieces, ins, outs
        k = len(pieces)
        self.acc, self.from_core = boxes[:k], boxes[k : 2 * k]
        self.from_side, self.from_hop = boxes[2 * k : 3 * k], boxes[3 * k :]
        self.load_sem, self.core_sem, self.side_sem, self.hop_sem = sems
        self.me = my_index(n_pair)
        self.hops = (n_dp * n_pair - 1).bit_length() - 2
        self.orders = [bit_order(n_dp, n_pair, piece[3]) for piece in pieces]
        self.count = k

    def source(self, a, block):
        which, low, high, _ = self.pieces[a]
        return self.ins[which].at[block, :, pl.ds(low, high - low)]

    def near(self, bit):
        return place(self.me ^ (1 << bit), self.n_pair)

    def load(self):
        for a in range(self.count):
            for p in range(2 << self.hops):
                pltpu.make_async_copy(
                    self.source(a, self.me ^ offset(self.orders[a], p)),
                    self.acc[a].at[p],
                    self.load_sem.at[a],
                ).start()

    def loaded(self):
        for a in range(self.count):
            pltpu.make_async_copy(self.acc[a], self.acc[a], self.load_sem.at[a]).wait()

    def core(self, a, r, sided, part=None):
        lo, count = stage(r)
        lo = lo + (sided << self.hops)
        to = self.from_core[a].at[pl.ds(lo, count)]
        source = to
        if part is not None:
            to = self.from_core[a].at[lo + part]
            source = self.source(a, self.me ^ (offset(self.orders[a], lo + part) + 1))
        slot = 2 * r + sided
        return remote(
            source, to, self.core_sem.at[0, a, slot], self.core_sem.at[1, a, slot], self.near(0)
        )

    def core_out(self, r):
        for sided in (1, 0):
            for a in range(self.count):
                for part in range(stage(r)[1]):
                    self.core(a, r, sided, part).start()

    def add(self, a, lo, count, box, at):
        acc = self.acc[a]

        def body(j, carry):
            acc[lo + j] = (
                acc[lo + j].astype(jnp.float32) + box[at + j].astype(jnp.float32)
            ).astype(jnp.bfloat16)
            return carry

        lax.fori_loop(0, count, body, 0)

    def side(self, a, r):
        lo, count = stage(r)
        return remote(
            self.acc[a].at[pl.ds((1 << self.hops) + lo, count)],
            self.from_side[a].at[pl.ds(lo, count)],
            self.side_sem.at[0, a, r],
            self.side_sem.at[1, a, r],
            self.near(self.orders[a][self.hops]),
        )

    def hop(self, a, r):
        return remote(
            self.acc[a].at[pl.ds(1 << r, 1 << r)],
            self.from_hop[a].at[pl.ds(self.hop_base(r), 1 << r)],
            self.hop_sem.at[0, a, r],
            self.hop_sem.at[1, a, r],
            self.near(self.orders[a][r]),
        )

    def hop_base(self, r):
        return (1 << self.hops) - (2 << r)

    def core_in(self, r):
        lo, count = stage(r)
        for sided in (1, 0):
            for a in range(self.count):
                self.core(a, r, sided).wait_recv()
                at = lo + (sided << self.hops)
                self.add(a, at, count, self.from_core[a], at)
                if sided:
                    self.side(a, r).start()

    def side_in(self, r):
        lo, count = stage(r)
        for a in range(self.count):
            self.side(a, r).wait_recv()
            self.add(a, lo, count, self.from_side[a], lo)
            if r == self.hops:
                self.hop(a, r - 1).start()

    def hop_in(self, r):
        for a in range(self.count):
            self.hop(a, r).wait_recv()
            base = self.hop_base(r)
            if r:
                mid = 1 << (r - 1)
                self.add(a, mid, mid, self.from_hop[a], base + mid)
                self.hop(a, r - 1).start()
                self.add(a, 0, mid, self.from_hop[a], base)
            else:
                which, low, high, _ = self.pieces[a]
                self.outs[which][:, low:high] = self.acc[a][0].astype(jnp.float32) + self.from_hop[
                    a
                ][base].astype(jnp.float32)

    def finish(self):
        for a in range(self.count):
            for r in range(self.hops):
                self.hop(a, r).wait_send()
            for r in range(self.hops + 1):
                self.side(a, r).wait_send()
                self.core(a, r, 0).wait_send()
                self.core(a, r, 1).wait_send()


def backward_kernel(n_dp, n_pair, pieces, n_in, *refs):
    k_count = len(pieces)
    len_ref, q_ref, k_ref, v_ref, g_ref, w_ref = refs[:6]
    ins = refs[6 : 6 + n_in]
    o_ref, z_ref, square_ref = refs[6 + n_in : 9 + n_in]
    outs = refs[9 + n_in : 9 + 2 * n_in]
    table, total, box, sem = refs[9 + 2 * n_in : 13 + 2 * n_in]
    rest = refs[13 + 2 * n_in :]
    weights = Scatter(n_dp, n_pair, pieces, ins, outs, rest[: 4 * k_count], rest[4 * k_count :])
    at = pl.program_id(0) * pl.num_programs(1) + pl.program_id(1)
    hops = weights.hops

    @pl.when(at == 0)
    def _():
        weights.load()
        greet([weights.near(bit) for bit in range(hops + 2)])
        for r in reversed(range(hops + 1)):
            weights.core_out(r)

    @pl.when(at == 1)
    def _():
        weights.loaded()
        weights.core_in(hops)

    @pl.when(at == 2)
    def _():
        for r in reversed(range(hops)):
            weights.core_in(r)

    @pl.when(at == 5)
    def _():
        weights.side_in(hops)

    @pl.when(at == 6)
    def _():
        for r in reversed(range(hops)):
            weights.side_in(r)

    seq = q_ref.shape[0]
    tiles = seq // 128
    doc = pl.program_id(1)
    @pl.when(doc == 0)
    def _():
        for h in range(2):
            band(w_ref, 2 * pl.program_id(0) + h, 2 * seq, h, table, seq)
        total[...] = jnp.zeros_like(total)
    length = len_ref[doc]
    lane = lax.broadcasted_iota(jnp.int32, (seq, 128), 1)
    row = lax.broadcasted_iota(jnp.int32, (seq, 1), 0)
    q = q_ref[...] * jnp.bfloat16(0.125)
    k = k_ref[...]
    v = v_ref[...]
    g = g_ref[...]
    parts = []
    for h in range(2):
        mine = (lane < 64) == (h == 0)
        s = lax.dot_general(k, jnp.where(mine, q, 0), NT, preferred_element_type=jnp.float32)
        s = jnp.where(row < length, s + table[h], -1000000000.0)
        e = jnp.exp(s - jnp.max(s, axis=0, keepdims=True))
        p = e * (1.0 / jnp.sum(e, axis=0, keepdims=True))
        dv = jnp.dot(p.astype(jnp.bfloat16), g, preferred_element_type=jnp.float32)
        dp = lax.dot_general(v, jnp.where(mine, g, 0), NT, preferred_element_type=jnp.float32)
        ds = (p * (dp - jnp.sum(p * dp, axis=0, keepdims=True))).astype(jnp.bfloat16)
        total[h] += ds.astype(jnp.float32)
        dk = jnp.dot(ds, q, preferred_element_type=jnp.float32)
        dq = lax.dot_general(ds, k, TN, preferred_element_type=jnp.float32) * 0.125
        parts.append((dq, dk, dv))
    pair, pairs, docs = pl.program_id(0), pl.num_programs(0), pl.num_programs(1)
    step = pair * docs + doc
    slot = lax.rem(step, 2)

    def out(i):
        rows = pl.ds(pl.multiple_of(doc * seq, seq), seq)
        columns = pl.ds(pl.multiple_of((i * pairs + pair) * 128, 128), 128)
        return pltpu.make_async_copy(box.at[slot, i], o_ref.at[rows, columns], sem.at[slot, i])

    for i in range(3):
        @pl.when(step >= 2)
        def _():
            out(i).wait()
        box[slot, i] = jnp.where(lane < 64, parts[0][i], parts[1][i]).astype(o_ref.dtype)
        out(i).start()

    for r in range(1, hops):
        @pl.when(step == pairs * docs - 2 * r)
        def _():
            weights.hop_in(r)

    @pl.when(step == pairs * docs - 1)
    def _():
        weights.hop_in(0)
        weights.finish()
        square_ref[...] = jnp.zeros_like(square_ref)
        for ref in outs:
            square = jnp.sum(ref[...] * ref[...], axis=0, keepdims=True)
            square_ref[...] += jnp.sum(square, axis=1, keepdims=True)
        for i in range(3):
            out(i).wait()
            pltpu.make_async_copy(box.at[1 - slot, i], box.at[1 - slot, i], sem.at[1 - slot, i]).wait()
    @pl.when(doc == pl.num_programs(1) - 1)
    def _():
        r = lax.broadcasted_iota(jnp.int32, (128, 128), 0)
        c = lax.broadcasted_iota(jnp.int32, (128, 128), 1)
        flip = jnp.where(r + c == 127, 1.0, 0.0)
        z_ref[...] = jnp.zeros_like(z_ref)
        for h in range(2):
            def block(d):
                return sum(total[h, a * 128 : a * 128 + 128, (a - d) * 128 : (a - d) * 128 + 128] for a in range(tiles) if 0 <= a - d < tiles)
            for d in (-1, 0, 1):
                x = jnp.dot(flip, block(d), precision=HIGHEST, preferred_element_type=jnp.float32)
                x = jnp.concatenate([x, jnp.zeros_like(x)], axis=1)
                x = pltpu.roll(x, 0, 1, stride=1, stride_axis=0)
                z_ref[0, h, d + 1 : d + 2, :] = jnp.sum(x, axis=0, keepdims=True)
            z_ref[0, h, 3:4, 0:128] = jnp.sum(sum(block(-d) for d in range(2, tiles)), axis=0, keepdims=True)
            z_ref[0, h, 4:5, 0:128] = jnp.sum(sum(block(d) for d in range(2, tiles)), axis=0, keepdims=True)

def attention_back(lengths, qkv, g, w, seq, grads, pieces, cid):
    n_dp, n_pair = lax.axis_size("dp"), lax.axis_size("pair")
    tokens = qkv.shape[0]
    pairs = w.shape[0] // 2
    docs = tokens // seq
    spec = lambda base: pl.BlockSpec((seq, 128), lambda h, d, *_: (d, base + h))
    still = lambda shape: pl.BlockSpec(shape, lambda h, d, *_: (0, 0))
    boxes, sems = scatter_scratch(n_dp * n_pair, grads, pieces)
    return pl.pallas_call(
        functools.partial(backward_kernel, n_dp, n_pair, pieces, len(grads)),
        grid_spec=pltpu.PrefetchScalarGridSpec(
            num_scalar_prefetch=1,
            grid=(pairs, docs),
            in_specs=[spec(0), spec(pairs), spec(2 * pairs), spec(0), still(w.shape)]
            + [ANY] * len(grads),
            out_specs=[
                ANY,
                pl.BlockSpec((1, 2, 8, 256), lambda h, d, *_: (h, 0, 0, 0)),
                still((1, 1)),
            ]
            + [still(grad.shape[1:]) for grad in grads],
            scratch_shapes=[
                pltpu.VMEM((2, seq, seq), jnp.float32),
                pltpu.VMEM((2, seq, seq), jnp.float32),
                pltpu.VMEM((2, 3, seq, 128), jnp.bfloat16),
                pltpu.SemaphoreType.DMA((2, 3)),
            ]
            + boxes
            + sems,
        ),
        out_shape=[
            jax.ShapeDtypeStruct((tokens, 3 * pairs * 128), jnp.bfloat16),
            jax.ShapeDtypeStruct((pairs, 2, 8, 256), jnp.float32),
            jax.ShapeDtypeStruct((1, 1), jnp.float32),
        ]
        + [jax.ShapeDtypeStruct(grad.shape[1:], jnp.float32) for grad in grads],
        compiler_params=pltpu.CompilerParams(
            dimension_semantics=("arbitrary", "arbitrary"),
            collective_id=cid,
            has_side_effects=True,
            vmem_limit_bytes=VMEM_LIMIT,
        ),
        name="attention_back",
    )(lengths, qkv, qkv, qkv, g, w, *grads)


def packed_base(gains, width):
    return -(-gains * width // 128 // 8) * 8


def back_kernel(n_dp, n_pair, pieces, n_gain, n_in, chunk, *refs):
    k = len(pieces)
    grad_ref, key_ref, ask_ref, squares_ref, bias_ref = refs[:5]
    gain_refs = refs[5 : 5 + n_gain]
    ins, rest = refs[5 + n_gain : 5 + n_gain + n_in], refs[5 + n_gain + n_in :]
    out_ref, total_ref = rest[:2]
    outs = rest[2 : 2 + n_in]
    rest = rest[2 + n_in :]
    boxes, rest = rest[: 4 * k], rest[4 * k :]
    rows_out, rows_in, hot, part, stage_out, got_core, out_side, got_side, other = rest[:9]
    square_ref, small, by_dp, from_pair = rest[9:13]
    row_sem, core_sem, side_sem, last_sem, out_sem, dp_sem, pair_sem, *sems = rest[13:]
    dp, pair = lax.axis_index("dp"), lax.axis_index("pair")
    core = lax.rem(pair, 2)
    weights = Scatter(n_dp, n_pair, pieces, ins, outs, boxes, sems)
    groups, _, cap, width = rows_out.shape
    slots = ask_ref.shape[1]
    count = stage_out.shape[1]
    half = count * chunk
    tokens = key_ref.shape[1]
    peers = [{"dp": dp ^ j, "pair": pair} for j in range(1, n_dp)]
    partner, across = {"dp": dp, "pair": pair ^ 1}, {"dp": dp, "pair": pair ^ 2}
    weights.load()
    sem = pltpu.get_barrier_semaphore()
    for target in peers + [partner, across]:
        pl.semaphore_signal(sem, inc=1, device_id=target, device_id_type=MESH)

    def row(g, j):
        return remote(
            rows_out.at[g, j],
            rows_in.at[g, pl.ds(pl.multiple_of(j * cap, cap), cap)],
            row_sem.at[0, g, j],
            row_sem.at[1, g, j],
            {"dp": dp ^ j, "pair": pair},
        )

    def loop(size, body):
        def turn(i, carry):
            body(i)
            return carry

        lax.fori_loop(0, size, turn, 0)

    far = sorted(range(1, n_dp), reverse=True)

    pl.semaphore_wait(sem, n_dp + 1)

    def rows_of(t):
        j = n_dp - 1 - t
        slot = lax.broadcasted_iota(jnp.int32, (cap, tokens), 0) + (dp ^ j) * cap
        hits = jnp.where(slot == key_ref[...], 1.0, 0.0).astype(jnp.bfloat16)
        got = jnp.dot(hits, grad_ref[...], preferred_element_type=jnp.float32)
        got = got.astype(jnp.bfloat16)
        for g in range(groups):
            rows_out[g, j] = got[:, g * width : (g + 1) * width]

        @pl.when(j > 0)
        def _():
            row(0, j).start()

    loop(n_dp, rows_of)
    for g in range(1, groups):
        for j in far:
            row(g, j).start()
    for g in range(groups):
        rows_in[g, 0:cap] = rows_out[g, 0]
    for r in reversed(range(weights.hops + 1)):
        weights.core_out(r)

    def tell(c):
        ids = lax.broadcasted_iota(jnp.int32, (chunk, slots), 0) + c * chunk
        hot[c] = jnp.where(ids == ask_ref[...], 1.0, 0.0).astype(jnp.bfloat16)

    loop(2 * count, tell)

    def summed(g, c):
        return jnp.dot(hot[c], rows_in[g], preferred_element_type=jnp.float32)

    def to_core(g, i):
        return remote(
            stage_out.at[g, i], got_core.at[g, i], core_sem.at[0, g, i], core_sem.at[1, g, i], partner
        )

    def to_side(g, i):
        return remote(
            out_side.at[g, i], got_side.at[g, i], side_sem.at[0, g, i], side_sem.at[1, g, i], across
        )

    def to_other(g, i):
        return remote(
            out_side.at[g, i], other.at[g, i], last_sem.at[0, g, i], last_sem.at[1, g, i], partner
        )

    def write_out(box, g, i, which):
        rows = pl.ds(pl.multiple_of(which * half + i * chunk, chunk), chunk)
        return pltpu.make_async_copy(
            box.at[g, i], out_ref.at[rows, pl.ds(g * width, width)], out_sem.at[g, i]
        )

    def local_sums(g):
        for j in far:
            row(g, j).wait_recv()

        def combine(i):
            to_core(g, i).wait_recv()
            out_side[g, i] = (part[i] + got_core[g, i].astype(jnp.float32)).astype(jnp.bfloat16)
            to_side(g, i).start()

        def one(i):
            stage_out[g, i] = summed(g, (1 - core) * count + i).astype(jnp.bfloat16)
            to_core(g, i).start()
            part[i] = summed(g, core * count + i)

            @pl.when(i > 0)
            def _():
                combine(i - 1)

        loop(count, one)
        combine(count - 1)

    square_ref[...] = squares_ref[...]

    def finish_sums(g):
        def one(i):
            to_side(g, i).wait()
            wide = out_side[g, i].astype(jnp.float32) + got_side[g, i].astype(jnp.float32)
            value = wide.astype(jnp.bfloat16)
            out_side[g, i] = value
            to_other(g, i).start()
            write_out(out_side, g, i, core).start()
            wide = value.astype(jnp.float32)
            square = jnp.sum(wide * wide, axis=0, keepdims=True)
            square = jnp.sum(square, axis=1, keepdims=True)
            square_ref[...] += jnp.where(pair < 2, square, 0.0)

        loop(count, one)

    def hand_over(g):
        def one(i):
            to_other(g, i).wait_recv()
            write_out(out_side, g, i, core).wait()
            write_out(other, g, i, 1 - core).start()

        loop(count, one)

    weights.loaded()
    for r in reversed(range(weights.hops + 1)):
        weights.core_in(r)
    for g in range(groups):
        local_sums(g)
        if g:
            finish_sums(g - 1)
        if g == groups // 2:
            for r in reversed(range(weights.hops + 1)):
                weights.side_in(r)
    for r in reversed(range(1, weights.hops)):
        weights.hop_in(r)
    finish_sums(groups - 1)
    weights.hop_in(0)
    for ref in outs:
        square = jnp.sum(ref[...] * ref[...], axis=0, keepdims=True)
        square_ref[...] += jnp.sum(square, axis=1, keepdims=True)
    gains_width = gain_refs[0].shape[1]
    base = packed_base(n_gain, gains_width)
    small[...] = jnp.zeros_like(small)
    for c in range(gains_width // 128):
        for which in range(n_gain):
            at = c * n_gain + which
            small[0, at : at + 1, :] = gain_refs[which][:, c * 128 : (c + 1) * 128]
    small[0, base : base + bias_ref.shape[0], : bias_ref.shape[1]] = bias_ref[...]
    small[0, base : base + 1, 127:128] = square_ref[...]

    def to_dp(j, slot):
        return remote(
            small.at[0],
            by_dp.at[slot],
            dp_sem.at[0, j],
            dp_sem.at[1, j],
            {"dp": dp ^ j, "pair": pair},
        )

    def to_pair(turn, target):
        return remote(
            small.at[1 + turn],
            from_pair.at[turn],
            pair_sem.at[0, turn],
            pair_sem.at[1, turn],
            target,
        )

    for j in far:
        to_dp(j, dp).start()
    by_dp[dp] = small[0]
    for g in range(groups):
        hand_over(g)
    for j in far:
        to_dp(j, dp ^ j).wait_recv()
    total = by_dp[0]
    for d in range(1, n_dp):
        total = total + by_dp[d]
    for turn, target in enumerate((partner, across)):
        small[1 + turn] = total
        to_pair(turn, target).start()
        to_pair(turn, target).wait_recv()
        total = total + from_pair[turn]
    total_ref[...] = total
    for j in far:
        to_dp(j, dp).wait_send()
    for turn, target in enumerate((partner, across)):
        to_pair(turn, target).wait_send()
    for g in range(groups):
        for j in far:
            row(g, j).wait_send()

        def one(i):
            to_core(g, i).wait_send()
            to_other(g, i).wait_send()
            write_out(other, g, i, 1 - core).wait()

        loop(count, one)
    weights.finish()


def scatter_scratch(n, grads, pieces):
    k, hops, sem = len(pieces), (n - 1).bit_length() - 2, pltpu.SemaphoreType.DMA
    boxes = [
        pltpu.VMEM((lead, grads[p[0]].shape[1], p[2] - p[1]), jnp.bfloat16)
        for lead in (n // 2, n // 2, n // 4, n // 4 - 1)
        for p in pieces
    ]
    return boxes, [
        sem((k,)),
        sem((2, k, 2 * hops + 2)),
        sem((2, k, hops + 1)),
        sem((2, k, hops)),
    ]


def back(grad, key, asked, squares, bias, gains, grads, pieces, table_rows, groups, cid):
    n_dp, n_pair = lax.axis_size("dp"), lax.axis_size("pair")
    boxes, sems = scatter_scratch(n_dp * n_pair, grads, pieces)
    chunk = 512
    rows = -(-table_rows // (2 * chunk)) * 2 * chunk
    count = rows // 2 // chunk
    tokens, full = grad.shape
    width = full // groups
    slots = asked.shape[1]
    height = -(-(packed_base(len(gains), full) + bias.shape[0]) // 8) * 8
    cap = slots // n_dp
    sem = pltpu.SemaphoreType.DMA
    box = pltpu.VMEM((groups, count, chunk, width), jnp.bfloat16)

    return pl.pallas_call(
        functools.partial(back_kernel, n_dp, n_pair, pieces, len(gains), len(grads), chunk),
        out_shape=[
            jax.ShapeDtypeStruct((rows, full), jnp.bfloat16),
            jax.ShapeDtypeStruct((height, 128), jnp.float32),
        ]
        + [jax.ShapeDtypeStruct(g.shape[1:], jnp.float32) for g in grads],
        in_specs=[VM] * (5 + len(gains)) + [ANY] * len(grads),
        out_specs=[ANY, VM] + [VM] * len(grads),
        scratch_shapes=boxes
        + [
            pltpu.VMEM((groups, n_dp, cap, width), jnp.bfloat16),
            pltpu.VMEM((groups, slots, width), jnp.bfloat16),
            pltpu.VMEM((2 * count, chunk, slots), jnp.bfloat16),
            pltpu.VMEM((count, chunk, width), jnp.float32),
            box,
            box,
            box,
            box,
            box,
            pltpu.VMEM((1, 1), jnp.float32),
            pltpu.VMEM((3, height, 128), jnp.float32),
            pltpu.VMEM((n_dp, height, 128), jnp.float32),
            pltpu.VMEM((2, height, 128), jnp.float32),
            sem((2, groups, n_dp)),
            sem((2, groups, count)),
            sem((2, groups, count)),
            sem((2, groups, count)),
            sem((groups, count)),
            sem((2, n_dp)),
            sem((2, 2)),
        ]
        + sems,
        compiler_params=pltpu.CompilerParams(
            collective_id=cid, has_side_effects=True, vmem_limit_bytes=VMEM_LIMIT
        ),
        name="table_and_weights",
    )(grad, key, asked, squares, bias, *gains, *grads)


BIAS_CORRECT = (1.0 - beta_one**STEP, 1.0 - beta_two**STEP)


def adam_parts(weight, first, second, grad, factor, rate, shrink):
    clipped = grad * factor
    first_new = beta_one * first + (1.0 - beta_one) * clipped
    second_new = beta_two * second + (1.0 - beta_two) * (clipped * clipped)
    root = jnp.sqrt(second_new * (1.0 / BIAS_CORRECT[1])) + adam_eps
    step = (rate / BIAS_CORRECT[0]) * first_new / root
    return (weight * (1.0 - rate * shrink) - step, first_new, second_new)


def update_kernel(mats, *refs):
    total_ref, loss_ref, low = refs[:3]
    table, small = refs[3:6], refs[6:12]
    grads = refs[12 : 12 + mats]
    states = refs[12 + mats : 12 + 4 * mats]
    rest = refs[12 + 4 * mats :]
    norm_out, loss_out, table_out, small_out = rest[0], rest[1], rest[2:5], rest[5:11]
    mat_out = rest[11:]
    gains, width = small[0].shape
    base = packed_base(gains, width)
    total = total_ref[...]
    row = lax.broadcasted_iota(jnp.int32, total.shape, 0)
    lane = lax.broadcasted_iota(jnp.int32, total.shape, 1)
    plain = jnp.where((row == base) & (lane == 127), total, total * total)
    norm = jnp.sqrt(jnp.sum(jnp.sum(plain, axis=1, keepdims=True), axis=0, keepdims=True))
    factor = jnp.minimum(1.0, clip_limit / norm)
    step = pl.program_id(0)

    @pl.when(step == 0)
    def _():
        norm_out[...] = norm
        loss_out[...] = loss_ref[...]
        for c in range(width // 128):
            columns = slice(c * 128, (c + 1) * 128)
            grad = total_ref[c * gains : (c + 1) * gains, :]
            new = adam_parts(*(ref[:, columns] for ref in small[:3]), grad, factor, 1.0, 0.0)
            for ref, value in zip(small_out[:3], new):
                ref[:, columns] = value
        heads = small[3].shape[1]
        grad = total_ref[base : base + small[3].shape[0], :heads]
        new = adam_parts(*(ref[...] for ref in small[3:]), grad, factor, 0.3, 0.0)
        for ref, value in zip(small_out[3:], new):
            ref[...] = value

    for which in range(mats):
        three = slice(3 * which, 3 * which + 3)
        new = adam_parts(*(ref[...] for ref in states[three]), grads[which][...], factor, 0.05, 0.01)
        for ref, value in zip(mat_out[three], new):
            ref[...] = value

    def body(j, carry):
        rows = pl.ds(pl.multiple_of(j * 16, 16), 16)
        new = adam_parts(*(ref[rows] for ref in table), low[rows].astype(jnp.float32), factor, 1.0, 0.01)
        for ref, value in zip(table_out, new):
            ref[rows] = value
        return carry

    lax.fori_loop(0, low.shape[0] // 16, body, 0)


def update(total, loss, table_grad, table, small, grads, states):
    rows, width = table[0].shape
    steps = 6
    tall = -(-rows // steps // 16) * 16
    flat = [array for group in states for array in group]
    like = lambda array: jax.ShapeDtypeStruct(array.shape, jnp.float32)
    whole = lambda array: pl.BlockSpec(array.shape, lambda i: (0, 0))
    table_spec = pl.BlockSpec((tall, width), lambda i: (i, 0))

    def part(array):
        if array.shape[1] % (128 * steps) == 0 and array.shape[0] < 32:
            return pl.BlockSpec((array.shape[0], array.shape[1] // steps), lambda i: (0, i))
        if array.shape[0] % (8 * steps) == 0:
            return pl.BlockSpec((array.shape[0] // steps, array.shape[1]), lambda i: (i, 0))
        return whole(array)

    return pl.pallas_call(
        functools.partial(update_kernel, len(grads)),
        grid=(steps,),
        out_shape=[like(loss), like(loss)] + [like(array) for array in (*table, *small, *flat)],
        in_specs=[whole(total), whole(loss)]
        + [table_spec] * 4
        + [whole(array) for array in small]
        + [part(array) for array in (*grads, *flat)],
        out_specs=[whole(loss)] * 2
        + [table_spec] * 3
        + [whole(array) for array in small]
        + [part(array) for array in flat],
        compiler_params=pltpu.CompilerParams(
            dimension_semantics=("arbitrary",), vmem_limit_bytes=VMEM_LIMIT
        ),
        name="update",
    )(total, loss, table_grad, *table, *small, *grads, *flat)


def local_plain(
    token_owner,
    token_row,
    lengths,
    positives,
    negatives,
    neg_counts,
    embed_table,
    embed_first,
    embed_second,
    qkv_weight,
    qkv_first,
    qkv_second,
    out_weight,
    out_first,
    out_second,
    in_weight,
    in_first,
    in_second,
    down_weight,
    down_first,
    down_second,
    norm_gains,
    gains_first,
    gains_second,
    position_bias,
    bias_first,
    bias_second,
):
    doc_count = lengths.shape[0]
    seq_len = token_row.shape[1]
    model_width = embed_table.shape[1]
    head_count = position_bias.shape[1]
    bucket_count = position_bias.shape[0]
    tok_total = doc_count * seq_len
    owners = lax.axis_size("dp")
    capacity = max(2, 2 * tok_total // owners)
    low_mats = (
        qkv_weight.astype(jnp.bfloat16),
        out_weight.astype(jnp.bfloat16),
        in_weight.astype(jnp.bfloat16),
        down_weight.astype(jnp.bfloat16),
    )
    qkv_full, out_full, in_full, down_full = (
        lax.all_gather(low_mats[0], ("dp", "pair"), axis=0, tiled=True),
        lax.all_gather(low_mats[1], ("dp", "pair"), axis=0, tiled=True),
        lax.all_gather(low_mats[2], ("dp", "pair"), axis=0, tiled=True),
        lax.all_gather(low_mats[3], ("dp", "pair"), axis=0, tiled=True),
    )
    tok_owner = token_owner.reshape(-1)
    tok_row = token_row.reshape(-1)
    owner_hits = (tok_owner[:, None] == jnp.arange(owners, dtype=jnp.int32)[None, :]).astype(
        jnp.int32
    )
    slot_rank = jnp.sum((jnp.cumsum(owner_hits, axis=0) - 1) * owner_hits, axis=1)
    requests = jnp.zeros((owners, capacity), jnp.int32).at[tok_owner, slot_rank].set(tok_row)
    asked_rows = lax.all_to_all(requests, "dp", split_axis=0, concat_axis=0, tiled=True)
    looked = jnp.take(embed_table, asked_rows.reshape(-1), axis=0).astype(jnp.bfloat16)
    answer = lax.all_to_all(
        looked.reshape(asked_rows.shape + (model_width,)),
        "dp",
        split_axis=0,
        concat_axis=0,
        tiled=True,
    )
    replies, asked_rows = (answer, asked_rows)
    embedded = replies[tok_owner, slot_rank].astype(jnp.float32)
    positions = jnp.arange(seq_len)
    live = positions[None, :] < lengths[:, None]
    pair_buckets = bucket_of(
        (positions[None, :] - positions[:, None]).reshape(-1), bucket_count, REACH
    )
    pair_hits = (jnp.arange(bucket_count)[:, None] == pair_buckets[None, :]).astype(jnp.float32)
    bias_full = jnp.dot(position_bias.T, pair_hits, precision=HIGHEST).reshape(
        head_count, seq_len, seq_len
    )
    bucket_map = pair_hits.astype(jnp.bfloat16)

    def split_doc(source, doc_index):
        doc_rows = source[doc_index * seq_len : (doc_index + 1) * seq_len]
        return tuple(
            (
                doc_rows[:, member * model_width : (member + 1) * model_width].reshape(
                    seq_len, head_count, -1
                )
                for member in range(3)
            )
        )

    normed_one, inverse_one = rms_forward(embedded, norm_gains[0])
    normed_one = normed_one.astype(jnp.bfloat16)
    qkv_rows = jnp.dot(normed_one, qkv_full, preferred_element_type=jnp.float32).astype(
        jnp.bfloat16
    )
    attended_parts = []
    logsum_parts = []
    for doc_index in range(doc_count):
        query_heads, key_heads, value_heads = split_doc(qkv_rows, doc_index)
        doc_out, logsum = attend_forward(
            query_heads, key_heads, value_heads, bias_full, live[doc_index]
        )
        attended_parts.append(doc_out.reshape(seq_len, model_width))
        logsum_parts.append(logsum)
    attended = jnp.concatenate(attended_parts, axis=0).astype(jnp.bfloat16)
    residual = embedded + jnp.dot(attended, out_full, preferred_element_type=jnp.float32)
    normed_two, inverse_two = rms_forward(residual, norm_gains[1])
    normed_two = normed_two.astype(jnp.bfloat16)
    hidden = jax.nn.relu(jnp.dot(normed_two, in_full, preferred_element_type=jnp.float32)).astype(
        jnp.bfloat16
    )
    output_rows = residual + jnp.dot(hidden, down_full, preferred_element_type=jnp.float32)
    normed_three, inverse_three = rms_forward(output_rows, norm_gains[2])
    live_rows = live.reshape(-1, 1)
    length_float = lengths.astype(jnp.float32)
    pooled_local = (
        jnp.sum(
            jnp.where(live_rows, normed_three, 0.0).reshape(doc_count, seq_len, model_width), axis=1
        )
        / length_float[:, None]
    )
    pooled_all = lax.all_gather(pooled_local, ("dp", "pair"), axis=0, tiled=True)
    loss_value, loss_pullback = jax.vjp(
        lambda pooled_in: margin_loss(pooled_in, positives, negatives, neg_counts), pooled_all
    )
    grad_pooled_all = loss_pullback(jnp.ones((), jnp.float32))[0]
    grad_pooled = lax.dynamic_slice_in_dim(
        grad_pooled_all, lax.axis_index(("dp", "pair")) * doc_count, doc_count, 0
    )
    grad_three = jnp.where(
        live_rows, jnp.repeat(grad_pooled / length_float[:, None], seq_len, axis=0), 0.0
    )
    qkv_back, out_back, in_back, down_back = (qkv_full, out_full, in_full, down_full)
    grad_output, gain_three = rms_backward(output_rows, inverse_three, norm_gains[2], grad_three)
    grad_branch = grad_output.astype(jnp.bfloat16)
    grad_down = lax.dot_general(
        hidden, grad_branch, CONTRACT_ROWS, preferred_element_type=jnp.float32
    )
    grad_hidden = lax.dot_general(
        grad_branch, down_back, CONTRACT_COLS, preferred_element_type=jnp.float32
    )
    grad_pre = jnp.where(hidden > 0, grad_hidden, 0.0).astype(jnp.bfloat16)
    grad_in = lax.dot_general(
        normed_two, grad_pre, CONTRACT_ROWS, preferred_element_type=jnp.float32
    )
    grad_normed_two = lax.dot_general(
        grad_pre, in_back, CONTRACT_COLS, preferred_element_type=jnp.float32
    )
    grad_res_part, gain_two = rms_backward(residual, inverse_two, norm_gains[1], grad_normed_two)
    grad_residual = grad_output + grad_res_part
    grad_attn_branch = grad_residual.astype(jnp.bfloat16)
    grad_out = lax.dot_general(
        attended, grad_attn_branch, CONTRACT_ROWS, preferred_element_type=jnp.float32
    )
    grad_attended = lax.dot_general(
        grad_attn_branch, out_back, CONTRACT_COLS, preferred_element_type=jnp.float32
    ).astype(jnp.bfloat16)
    grad_qkv_parts = []
    bias_grad_heads = jnp.zeros((head_count, bucket_count), jnp.float32)
    for doc_index in range(doc_count):
        query_heads, key_heads, value_heads = split_doc(qkv_rows, doc_index)
        grad_doc = grad_attended[doc_index * seq_len : (doc_index + 1) * seq_len].reshape(
            seq_len, head_count, -1
        )
        grad_query, grad_key, grad_value, grad_low = attend_backward(
            query_heads,
            key_heads,
            value_heads,
            bias_full,
            live[doc_index],
            logsum_parts[doc_index],
            grad_doc,
        )
        grad_qkv_parts.append(
            jnp.concatenate(
                [
                    grad_query.reshape(seq_len, model_width),
                    grad_key.reshape(seq_len, model_width),
                    grad_value.reshape(seq_len, model_width),
                ],
                axis=1,
            )
        )
        bias_grad_heads = bias_grad_heads + lax.dot_general(
            grad_low.reshape(head_count, -1),
            bucket_map,
            CONTRACT_COLS,
            preferred_element_type=jnp.float32,
        )
    bias_grad_local = bias_grad_heads.T
    grad_qkv_rows = jnp.concatenate(grad_qkv_parts, axis=0).astype(jnp.bfloat16)
    grad_qkv = lax.dot_general(
        normed_one, grad_qkv_rows, CONTRACT_ROWS, preferred_element_type=jnp.float32
    )
    grad_normed_one = lax.dot_general(
        grad_qkv_rows, qkv_back, CONTRACT_COLS, preferred_element_type=jnp.float32
    )
    grad_emb_part, gain_one = rms_backward(embedded, inverse_one, norm_gains[0], grad_normed_one)
    grad_embedded = grad_residual + grad_emb_part
    sendback = (
        jnp.zeros((owners, capacity, model_width), jnp.float32)
        .at[tok_owner, slot_rank]
        .set(grad_embedded)
    )
    arrived = lax.all_to_all(sendback, "dp", split_axis=0, concat_axis=0, tiled=True)
    table_grad = jax.ops.segment_sum(
        arrived.reshape(-1, model_width), asked_rows.reshape(-1), num_segments=embed_table.shape[0]
    )
    table_grad = lax.psum(table_grad, "pair")
    weight_grads = (
        lax.psum_scatter(grad_qkv, ("dp", "pair"), scatter_dimension=0, tiled=True),
        lax.psum_scatter(grad_out, ("dp", "pair"), scatter_dimension=0, tiled=True),
        lax.psum_scatter(grad_in, ("dp", "pair"), scatter_dimension=0, tiled=True),
        lax.psum_scatter(grad_down, ("dp", "pair"), scatter_dimension=0, tiled=True),
    )
    pair_first = (lax.axis_index("pair") == 0).astype(jnp.float32)
    square_part = jnp.sum(
        jnp.stack([jnp.sum(grad_piece * grad_piece) for grad_piece in weight_grads])
    ) + pair_first * jnp.sum(table_grad * table_grad)
    gain_grad, bias_grad, square_sum = lax.psum(
        (jnp.stack([gain_one, gain_two, gain_three]), bias_grad_local, square_part), ("dp", "pair")
    )
    clip_norm = jnp.sqrt(
        square_sum + jnp.sum(gain_grad * gain_grad) + jnp.sum(bias_grad * bias_grad)
    )
    factor = jnp.minimum(1.0, clip_limit / clip_norm)
    table_out = adam_step(embed_table, embed_first, embed_second, table_grad * factor, 1.0, 0.01)
    qkv_out = adam_step(qkv_weight, qkv_first, qkv_second, weight_grads[0] * factor, 0.05, 0.01)
    out_out = adam_step(out_weight, out_first, out_second, weight_grads[1] * factor, 0.05, 0.01)
    in_out = adam_step(in_weight, in_first, in_second, weight_grads[2] * factor, 0.05, 0.01)
    down_out = adam_step(down_weight, down_first, down_second, weight_grads[3] * factor, 0.05, 0.01)
    gains_out = adam_step(norm_gains, gains_first, gains_second, gain_grad * factor, 1.0, 0.0)
    bias_out = adam_step(position_bias, bias_first, bias_second, bias_grad * factor, 0.3, 0.0)
    return (
        loss_value,
        clip_norm,
        table_out[0],
        table_out[1],
        table_out[2],
        qkv_out[0],
        qkv_out[1],
        qkv_out[2],
        out_out[0],
        out_out[1],
        out_out[2],
        in_out[0],
        in_out[1],
        in_out[2],
        down_out[0],
        down_out[1],
        down_out[2],
        gains_out[0],
        gains_out[1],
        gains_out[2],
        bias_out[0],
        bias_out[1],
        bias_out[2],
    )


def local_fast(
    token_owner,
    token_row,
    lengths,
    positives,
    negatives,
    neg_counts,
    embed_table,
    embed_first,
    embed_second,
    qkv_weight,
    qkv_first,
    qkv_second,
    out_weight,
    out_first,
    out_second,
    in_weight,
    in_first,
    in_second,
    down_weight,
    down_first,
    down_second,
    norm_gains,
    gains_first,
    gains_second,
    position_bias,
    bias_first,
    bias_second,
):
    doc_count = lengths.shape[0]
    seq_len = token_row.shape[1]
    model_width = embed_table.shape[1]
    head_count = position_bias.shape[1]
    bucket_count = position_bias.shape[0]
    tok_total = doc_count * seq_len
    owners = lax.axis_size("dp")
    capacity = max(2, 2 * tok_total // owners)
    holders = lax.axis_size("pair")
    shards = (qkv_weight, out_weight, in_weight, down_weight)
    embedded_low, slot_keys, asked_rows, *full = front(
        token_owner.reshape(token_row.shape),
        token_row,
        embed_table,
        shards,
        weight_pieces([shard.shape[1] for shard in shards]),
        capacity,
        owners,
        holders,
        1,
    )
    qkv_full, out_full, in_full, down_full = (
        matrix.reshape(-1, matrix.shape[2]) for matrix in full
    )
    embedded = embedded_low.astype(jnp.float32)
    positions = jnp.arange(seq_len)
    live = positions[None, :] < lengths[:, None]
    offset_bias = bias_rows(position_bias.T, seq_len)
    normed_one, inverse_one = rms_forward(embedded, norm_gains[0])
    normed_one = normed_one.astype(jnp.bfloat16)
    qkv_rows = jnp.dot(normed_one, qkv_full, preferred_element_type=jnp.float32).astype(
        jnp.bfloat16
    )
    attended = attention(lengths, qkv_rows, offset_bias, seq_len)
    residual = embedded + jnp.dot(attended, out_full, preferred_element_type=jnp.float32)
    normed_two, inverse_two = rms_forward(residual, norm_gains[1])
    normed_two = normed_two.astype(jnp.bfloat16)
    hidden = jax.nn.relu(jnp.dot(normed_two, in_full, preferred_element_type=jnp.float32)).astype(
        jnp.bfloat16
    )
    output_rows = residual + jnp.dot(hidden, down_full, preferred_element_type=jnp.float32)
    normed_three, inverse_three = rms_forward(output_rows, norm_gains[2])
    live_rows = live.reshape(-1, 1)
    live_sums = jnp.sum(
        jnp.where(live_rows, normed_three, 0.0).reshape(doc_count, seq_len, model_width), axis=1
    )
    loss_cell, grad_sums = pooled_loss(
        live_sums, lengths, positives, negatives, neg_counts, 3
    )
    grad_three = jnp.where(
        live_rows, jnp.repeat(grad_sums, seq_len, axis=0), 0.0
    )
    qkv_back, out_back, in_back, down_back = (qkv_full, out_full, in_full, down_full)
    grad_output, gain_three = rms_backward(output_rows, inverse_three, norm_gains[2], grad_three)
    grad_branch = grad_output.astype(jnp.bfloat16)
    grad_down = lax.dot_general(
        hidden, grad_branch, CONTRACT_ROWS, preferred_element_type=jnp.float32
    )
    grad_hidden = lax.dot_general(
        grad_branch, down_back, CONTRACT_COLS, preferred_element_type=jnp.float32
    )
    grad_pre = jnp.where(hidden > 0, grad_hidden, 0.0).astype(jnp.bfloat16)
    grad_in = lax.dot_general(
        normed_two, grad_pre, CONTRACT_ROWS, preferred_element_type=jnp.float32
    )
    grad_normed_two = lax.dot_general(
        grad_pre, in_back, CONTRACT_COLS, preferred_element_type=jnp.float32
    )
    grad_res_part, gain_two = rms_backward(residual, inverse_two, norm_gains[1], grad_normed_two)
    grad_residual = grad_output + grad_res_part
    grad_attn_branch = grad_residual.astype(jnp.bfloat16)
    grad_out = lax.dot_general(
        attended, grad_attn_branch, CONTRACT_ROWS, preferred_element_type=jnp.float32
    )
    grad_attended = lax.dot_general(
        grad_attn_branch, out_back, CONTRACT_COLS, preferred_element_type=jnp.float32
    ).astype(jnp.bfloat16)
    parts = owners * holders

    def blocks(*grads):
        return [grad.astype(jnp.bfloat16).reshape(parts, -1, grad.shape[1]) for grad in grads]

    grad_qkv_rows, diagonals, squares, down_grad = attention_back(
        lengths,
        qkv_rows,
        grad_attended,
        offset_bias,
        seq_len,
        blocks(grad_down),
        early_pieces(model_width),
        5,
    )
    bias_grad_local = bias_gradient(diagonals, seq_len, bucket_count)
    grad_qkv = lax.dot_general(
        normed_one, grad_qkv_rows, CONTRACT_ROWS, preferred_element_type=jnp.float32
    )
    grad_normed_one = lax.dot_general(
        grad_qkv_rows, qkv_back, CONTRACT_COLS, preferred_element_type=jnp.float32
    )
    grad_emb_part, gain_one = rms_backward(embedded, inverse_one, norm_gains[0], grad_normed_one)
    grad_embedded = grad_residual + grad_emb_part
    table_grad, total, qkv_grad, out_grad, in_grad = back(
        grad_embedded.astype(jnp.bfloat16),
        slot_keys,
        asked_rows.reshape(1, -1),
        squares,
        bias_grad_local,
        [gain.reshape(1, -1) for gain in (gain_one, gain_two, gain_three)],
        blocks(grad_qkv, grad_out, grad_in),
        late_pieces([grad.shape[1] for grad in (grad_qkv, grad_out, grad_in)]),
        embed_table.shape[0],
        model_width // 128,
        2,
    )
    weight_grads = (qkv_grad, out_grad, in_grad, down_grad)
    norm_cell, loss_cell, *updated = update(
        total,
        loss_cell,
        table_grad,
        (embed_table, embed_first, embed_second),
        (
            norm_gains,
            gains_first,
            gains_second,
            position_bias.T,
            bias_first.T,
            bias_second.T,
        ),
        weight_grads,
        (
            (qkv_weight, qkv_first, qkv_second),
            (out_weight, out_first, out_second),
            (in_weight, in_first, in_second),
            (down_weight, down_first, down_second),
        ),
    )
    return (loss_cell[0, 0], norm_cell[0, 0], *updated[:3], *updated[9:], *updated[3:6], *(new.T for new in updated[6:9]))


def local(*arrays):
    n_dp, n_pair = lax.axis_size("dp"), lax.axis_size("pair")
    lengths, qkv_weight, down_weight = arrays[2], arrays[9], arrays[18]
    fits = (
        n_pair == 4
        and n_dp & (n_dp - 1) == 0
        and qkv_weight.shape[0] % 8 == 0
        and down_weight.shape[0] % 8 == 0
        and lengths.shape[0] == 2
        and 2 * arrays[1].size // n_dp % 128 == 0
    )
    return (local_fast if fits else local_plain)(*arrays)


def solution(mesh):
    return jax.shard_map(
        local,
        mesh=mesh,
        in_specs=(
            P(("dp", "pair"), None, None),
            P(("dp", "pair"), None),
            P(("dp", "pair")),
            P(),
            P(),
            P(),
            P("dp", None),
            P("dp", None),
            P("dp", None),
            P(("dp", "pair"), None),
            P(("dp", "pair"), None),
            P(("dp", "pair"), None),
            P(("dp", "pair"), None),
            P(("dp", "pair"), None),
            P(("dp", "pair"), None),
            P(("dp", "pair"), None),
            P(("dp", "pair"), None),
            P(("dp", "pair"), None),
            P(("dp", "pair"), None),
            P(("dp", "pair"), None),
            P(("dp", "pair"), None),
            P(),
            P(),
            P(),
            P(),
            P(),
            P(),
        ),
        out_specs=(
            P(),
            P(),
            P("dp", None),
            P("dp", None),
            P("dp", None),
            P(("dp", "pair"), None),
            P(("dp", "pair"), None),
            P(("dp", "pair"), None),
            P(("dp", "pair"), None),
            P(("dp", "pair"), None),
            P(("dp", "pair"), None),
            P(("dp", "pair"), None),
            P(("dp", "pair"), None),
            P(("dp", "pair"), None),
            P(("dp", "pair"), None),
            P(("dp", "pair"), None),
            P(("dp", "pair"), None),
            P(),
            P(),
            P(),
            P(),
            P(),
            P(),
        ),
        check_vma=False,
    )
```

```python
import functools
import math

import jax
import jax.numpy as jnp
import numpy as np
from jax import lax
from jax.experimental import pallas as pl
from jax.experimental.pallas import tpu as pltpu
from jax.sharding import PartitionSpec as P

REACH = 128
STEP = 5


rms_eps = 1e-06
clip_limit = 0.05
margin = 1.0
sim_scale = 20.0
beta_one = 0.9
beta_two = 0.999
adam_eps = 1e-08
HIGHEST = lax.Precision.HIGHEST
CONTRACT_ROWS = (((0,), (0,)), ((), ()))
CONTRACT_COLS = (((1,), (1,)), ((), ()))


def bucket_of(offsets, bucket_count, reach_limit):
    half_count = bucket_count // 2
    exact_count = half_count // 2
    sign_base = jnp.where(offsets > 0, half_count, 0).astype(jnp.int32)
    distance = jnp.abs(offsets)
    far_bucket = jnp.full(offsets.shape, exact_count, jnp.int32)
    for level_index in range(1, half_count - exact_count):
        threshold = int(
            math.ceil(
                exact_count
                * (reach_limit / exact_count) ** (level_index / (half_count - exact_count))
                - 1e-09
            )
        )
        far_bucket = far_bucket + (distance >= threshold).astype(jnp.int32)
    return sign_base + jnp.where(distance < exact_count, distance, far_bucket)


def rms_forward(values, gain):
    inverse = lax.rsqrt(jnp.mean(values * values, axis=-1, keepdims=True) + rms_eps)
    return (values * inverse * gain, inverse)


def rms_backward(values, inverse, gain, upstream):
    scaled = upstream * gain
    normed = values * inverse
    grad_values = inverse * (scaled - normed * jnp.mean(scaled * normed, axis=-1, keepdims=True))
    return (grad_values, jnp.sum(upstream * normed, axis=0))


def margin_loss(pooled, positives, negatives, neg_counts):
    unit = pooled * lax.rsqrt(jnp.sum(pooled * pooled, axis=-1, keepdims=True) + 1e-06)
    similar = sim_scale * jnp.dot(unit, unit.T, precision=HIGHEST)
    chosen = jnp.take_along_axis(similar, positives[:, None], axis=1)
    against = jnp.take_along_axis(similar, negatives, axis=1)
    live_slots = jnp.arange(negatives.shape[1])[None, :] < neg_counts[:, None]
    terms = jnp.where(live_slots, jax.nn.softplus(margin - chosen + against), 0.0)
    return jnp.mean(jnp.sum(terms, axis=1) / neg_counts.astype(jnp.float32))


def doc_scores(query_heads, key_heads, bias_full, live_keys):
    scores = (
        jnp.einsum("qhd,khd->hqk", query_heads, key_heads, preferred_element_type=jnp.float32)
        * 0.125
        + bias_full
    )
    return jnp.where(live_keys[None, None, :], scores, -1000000000.0)


def attend_forward(query_heads, key_heads, value_heads, bias_full, live_keys):
    scores = doc_scores(query_heads, key_heads, bias_full, live_keys)
    highest = jnp.max(scores, axis=-1, keepdims=True)
    weights = jnp.exp(scores - highest)
    totals = jnp.sum(weights, axis=-1, keepdims=True)
    probabilities = (weights / totals).astype(jnp.bfloat16)
    attended = jnp.einsum(
        "hqk,khd->qhd", probabilities, value_heads, preferred_element_type=jnp.float32
    )
    return (attended, highest + jnp.log(totals))


def attend_backward(
    query_heads, key_heads, value_heads, bias_full, live_keys, logsum, grad_attended
):
    probabilities = jnp.exp(doc_scores(query_heads, key_heads, bias_full, live_keys) - logsum)
    grad_value = jnp.einsum(
        "hqk,qhd->khd",
        probabilities.astype(jnp.bfloat16),
        grad_attended,
        preferred_element_type=jnp.float32,
    )
    grad_prob = jnp.einsum(
        "qhd,khd->hqk", grad_attended, value_heads, preferred_element_type=jnp.float32
    )
    grad_score = probabilities * (
        grad_prob - jnp.sum(probabilities * grad_prob, axis=-1, keepdims=True)
    )
    grad_low = grad_score.astype(jnp.bfloat16)
    grad_query = (
        jnp.einsum("hqk,khd->qhd", grad_low, key_heads, preferred_element_type=jnp.float32) * 0.125
    )
    grad_key = (
        jnp.einsum("hqk,qhd->khd", grad_low, query_heads, preferred_element_type=jnp.float32)
        * 0.125
    )
    return (grad_query, grad_key, grad_value, grad_low)


def adam_step(weight, first, second, grad, rate, shrink):
    first_new = beta_one * first + (1.0 - beta_one) * grad
    second_new = beta_two * second + (1.0 - beta_two) * grad * grad
    first_hat = first_new / (1.0 - beta_one**STEP)
    second_hat = second_new / (1.0 - beta_two**STEP)
    weight_new = weight - rate * (first_hat / (jnp.sqrt(second_hat) + adam_eps) + shrink * weight)
    return (weight_new, first_new, second_new)


MESH = pl.DeviceIdType.MESH
VMEM_LIMIT = 64 * 1024 * 1024 - 65536
ANY = pl.BlockSpec(memory_space=pl.ANY)
VM = pl.BlockSpec(memory_space=pltpu.VMEM)


def place(index, n_pair):
    return {"dp": index // n_pair, "pair": lax.rem(index, n_pair)}


def remote(src, dst, send, recv, target):
    return pltpu.make_async_remote_copy(
        src, dst, send, recv, device_id=target, device_id_type=MESH
    )


def greet(targets):
    sem = pltpu.get_barrier_semaphore()
    for target in targets:
        pl.semaphore_signal(sem, inc=1, device_id=target, device_id_type=MESH)
    pl.semaphore_wait(sem, len(targets))


def my_index(n_pair):
    return lax.axis_index("dp") * n_pair + lax.axis_index("pair")


def bit_order(n_dp, n_pair, color):
    dp_bits, pair_bits = (n_dp - 1).bit_length(), (n_pair - 1).bit_length()
    high = list(reversed(range(pair_bits + 1, pair_bits + dp_bits))) + [pair_bits]
    side = list(reversed(range(1, pair_bits)))
    return high + side if color == 0 else side + high


def offset(order, position):
    return sum(((position >> step) & 1) << bit for step, bit in enumerate(order))


class Rounds:
    def __init__(self, n_dp, n_pair, dp_sem, pair_sem, own_sem):
        self.n_dp, self.n_pair = n_dp, n_pair
        self.dp_sem, self.pair_sem, self.own_sem = dp_sem, pair_sem, own_sem
        self.dp, self.pair = lax.axis_index("dp"), lax.axis_index("pair")
        sem = pltpu.get_barrier_semaphore()
        targets = [{"dp": self.dp ^ j, "pair": self.pair} for j in range(1, n_dp)]
        targets += [{"dp": self.dp, "pair": self.pair ^ j} for j in range(1, n_pair)]
        for target in targets:
            pl.semaphore_signal(sem, inc=1, device_id=target, device_id_type=MESH)
        self.entered = lambda: pl.semaphore_wait(sem, len(targets))

    def over_dp(self, block, by_dp):
        def copy(j, slot):
            target = {"dp": self.dp ^ j, "pair": self.pair}
            return remote(block, by_dp.at[slot], self.dp_sem.at[0, j], self.dp_sem.at[1, j], target)

        self.exchange(block, by_dp, self.dp, self.n_dp, copy)

    def over_pair(self, block, by_pair):
        def copy(j, slot):
            target = {"dp": self.dp, "pair": self.pair ^ j}
            return remote(
                block, by_pair.at[slot], self.pair_sem.at[0, j], self.pair_sem.at[1, j], target
            )

        self.exchange(block, by_pair, self.pair, self.n_pair, copy)

    def exchange(self, block, places, me, size, copy):
        own = pltpu.make_async_copy(block, places.at[me], self.own_sem)
        own.start()
        for j in reversed(range(1, size)):
            copy(j, me).start()
        own.wait()
        for j in range(1, size):
            copy(j, me ^ j).wait_recv()
        for j in range(1, size):
            copy(j, me).wait_send()


def round_sems(n_dp, n_pair):
    sem = pltpu.SemaphoreType.DMA
    return [sem((2, n_dp)), sem((2, n_pair)), sem]


def loss_kernel(
    n_dp,
    n_pair,
    len_ref,
    x_ref,
    pos_ref,
    neg_ref,
    count_ref,
    loss_ref,
    grad_ref,
    own,
    by_dp,
    by_pair,
    unit,
    *sems,
):
    rounds = Rounds(n_dp, n_pair, *sems)
    docs, width = x_ref.shape
    lengths = [len_ref[d].astype(jnp.float32) for d in range(docs)]
    for d in range(docs):
        own[d : d + 1] = x_ref[d : d + 1] / lengths[d]
    rounds.entered()
    rounds.over_dp(own, by_dp)
    rounds.over_pair(by_dp, by_pair)
    total = n_dp * n_pair * docs
    for d in range(n_dp):
        for p in range(n_pair):
            base = (d * n_pair + p) * docs
            unit[base : base + docs] = by_pair[p, d]
    pooled = unit[...]
    inverse = lax.rsqrt(jnp.sum(pooled * pooled, axis=1, keepdims=True) + 1e-06)
    units = pooled * inverse
    similar = 20.0 * lax.dot_general(
        units, units, NT, precision=HIGHEST, preferred_element_type=jnp.float32
    )
    partner = lax.broadcasted_iota(jnp.int32, (total, total), 0)
    is_pos = partner == pos_ref[...]
    chosen = jnp.sum(jnp.where(is_pos, similar, 0.0), axis=0, keepdims=True)
    counts = count_ref[...]
    weight = 1.0 / (counts.astype(jnp.float32) * total)
    losses = jnp.zeros((1, total), jnp.float32)
    slopes = jnp.zeros((1, total), jnp.float32)
    grad_similar = jnp.zeros((total, total), jnp.float32)
    for slot in range(neg_ref.shape[0]):
        is_neg = partner == neg_ref[slot : slot + 1, :]
        against = jnp.sum(jnp.where(is_neg, similar, 0.0), axis=0, keepdims=True)
        value = margin - chosen + against
        used = slot < counts
        soft = jnp.maximum(value, 0.0) + jnp.log1p(jnp.exp(-jnp.abs(value)))
        losses = losses + jnp.where(used, soft, 0.0)
        slope = jnp.where(used, weight / (1.0 + jnp.exp(-value)), 0.0)
        grad_similar = grad_similar + jnp.where(is_neg, slope, 0.0)
        slopes = slopes + slope
    grad_similar = grad_similar - jnp.where(is_pos, slopes, 0.0)
    loss_ref[...] = jnp.sum(losses * weight, axis=1, keepdims=True)
    grad_units = sim_scale * (
        jnp.dot(grad_similar, units, precision=HIGHEST, preferred_element_type=jnp.float32)
        + lax.dot_general(
            grad_similar, units, TN, precision=HIGHEST, preferred_element_type=jnp.float32
        )
    )
    inner = jnp.sum(grad_units * units, axis=1, keepdims=True)
    unit[...] = inverse * (grad_units - units * inner)
    for d in range(n_dp):
        for p in range(n_pair):
            base = (d * n_pair + p) * docs

            @pl.when((rounds.dp == d) & (rounds.pair == p))
            def _():
                for doc in range(docs):
                    grad_ref[doc : doc + 1] = unit[base + doc : base + doc + 1] / lengths[doc]


def pooled_loss(sums, lengths, positives, negatives, counts, cid):
    n_dp, n_pair = lax.axis_size("dp"), lax.axis_size("pair")
    docs, width = sums.shape
    return pl.pallas_call(
        functools.partial(loss_kernel, n_dp, n_pair),
        out_shape=[
            jax.ShapeDtypeStruct((1, 1), jnp.float32),
            jax.ShapeDtypeStruct(sums.shape, jnp.float32),
        ],
        in_specs=[pl.BlockSpec(memory_space=pltpu.SMEM)] + [VM] * 4,
        out_specs=[VM] * 2,
        scratch_shapes=[
            pltpu.VMEM((docs, width), jnp.float32),
            pltpu.VMEM((n_dp, docs, width), jnp.float32),
            pltpu.VMEM((n_pair, n_dp, docs, width), jnp.float32),
            pltpu.VMEM((n_dp * n_pair * docs, width), jnp.float32),
        ]
        + round_sems(n_dp, n_pair),
        compiler_params=pltpu.CompilerParams(collective_id=cid, has_side_effects=True),
        name="pooled_loss",
    )(lengths, sums, positives.reshape(1, -1), negatives.T, counts.reshape(1, -1))


NT = (((1,), (1,)), ((), ()))
TN = (((0,), (0,)), ((), ()))

def band(w_ref, row, base, h, table, seq):
    tiles = seq // 128
    for d in range(1 - tiles, tiles):
        low = base + seq + 128 * d - 128
        line = w_ref[pl.ds(row, 1), low : low + 256]
        if 128 * (abs(d) - 1) < REACH:
            x = jnp.broadcast_to(line, (128, 256))
            tile = pltpu.roll(x, 0, 1, stride=1, stride_axis=0)[:, 128:]
        else:
            tile = jnp.broadcast_to(line, (128, 256))[:, 128:]
        for a in range(tiles):
            if 0 <= a + d < tiles:
                table[h, a * 128 : a * 128 + 128, (a + d) * 128 : (a + d) * 128 + 128] = tile

def forward_kernel(len_ref, q_ref, k_ref, v_ref, w_ref, o_ref, table):
    seq = q_ref.shape[0]
    doc = pl.program_id(1)
    @pl.when(doc == 0)
    def _():
        for h in range(2):
            band(w_ref, 2 * pl.program_id(0) + h, 0, h, table, seq)
    length = len_ref[doc]
    lane = lax.broadcasted_iota(jnp.int32, (seq, 128), 1)
    column = lax.broadcasted_iota(jnp.int32, (1, seq), 1)
    q = q_ref[...] * jnp.bfloat16(0.125)
    k = k_ref[...]
    v = v_ref[...]
    got = []
    for h in range(2):
        mine = (lane < 64) == (h == 0)
        s = lax.dot_general(jnp.where(mine, q, 0), k, NT, preferred_element_type=jnp.float32)
        s = jnp.where(column < length, s + table[h], -1000000000.0)
        e = jnp.exp(s - jnp.max(s, axis=1, keepdims=True))
        p = (e * (1.0 / jnp.sum(e, axis=1, keepdims=True))).astype(jnp.bfloat16)
        got.append(jnp.dot(p, v, preferred_element_type=jnp.float32))
    o_ref[...] = jnp.where(lane < 64, got[0], got[1]).astype(o_ref.dtype)

def attention(lengths, qkv, w, seq):
    tokens = qkv.shape[0]
    pairs = w.shape[0] // 2
    docs = tokens // seq
    spec = lambda base: pl.BlockSpec((seq, 128), lambda h, d, *_: (d, base + h))
    return pl.pallas_call(
        forward_kernel,
        grid_spec=pltpu.PrefetchScalarGridSpec(
            num_scalar_prefetch=1, grid=(pairs, docs),
            in_specs=[spec(0), spec(pairs), spec(2 * pairs), pl.BlockSpec(w.shape, lambda h, d, *_: (0, 0))],
            out_specs=spec(0),
            scratch_shapes=[pltpu.VMEM((2, seq, seq), jnp.float32)]),
        out_shape=jax.ShapeDtypeStruct((tokens, pairs * 128), jnp.bfloat16),
        compiler_params=pltpu.CompilerParams(dimension_semantics=("arbitrary", "arbitrary"), vmem_limit_bytes=50 * 1024 * 1024),
        name="attention",
    )(lengths, qkv, qkv, qkv, w)

def bucket_hits(offsets, buckets):
    half = buckets // 2
    exact = half // 2
    distance = np.abs(offsets)
    far = np.full(offsets.shape, exact)
    for level in range(1, half - exact):
        limit = math.ceil(exact * (REACH / exact) ** (level / (half - exact)) - 1e-09)
        far = far + (distance >= limit)
    bucket = np.where(offsets > 0, half, 0) + np.where(distance < exact, distance, far)
    return (bucket[:, None] == np.arange(buckets)[None, :]).astype(np.float32)


def bias_rows(bias, seq):
    offsets = np.arange(2 * seq) - seq
    hits = bucket_hits(np.concatenate([offsets, -offsets]), bias.shape[1])
    return jnp.dot(bias, hits.T, precision=HIGHEST)


def bias_gradient(sums, seq, buckets):
    heads, width = sums.shape[0] * 2, sums.shape[2] * sums.shape[3]
    j = np.arange(256)
    offsets = [np.where(j < 255, 128 * d + 127 - j, 0) for d in (-1, 0, 1)]
    offsets += [np.full((256,), 1 - seq), np.full((256,), seq - 1)]
    hits = bucket_hits(np.concatenate(offsets), buckets)
    hits = np.concatenate([hits, np.zeros((width - hits.shape[0], buckets), np.float32)])
    return jnp.dot(sums.reshape(heads, width), hits, precision=HIGHEST)


def weight_pieces(widths):
    first = widths[0] * 2 // 3 // 128 * 128
    cut = widths[3] * 2 // 3 // 128 * 128
    return [
        (0, 0, first, 0),
        (0, first, widths[0], 1),
        (2, 0, widths[2], 0),
        (1, 0, widths[1], 0),
        (3, 0, cut, 0),
        (3, cut, widths[3], 1),
    ]


def early_pieces(width):
    cut = width // 2 // 128 * 128
    return [(0, 0, cut, 0), (0, cut, width, 1)]


def late_pieces(widths):
    return [(2, 0, widths[2], 0), (0, 0, widths[0], 1), (1, 0, widths[1], 1)]


NN = (((1,), (0,)), ((), ()))


def stage(r):
    return (0, 1) if r == 0 else (1 << (r - 1), 1 << (r - 1))


class Gather:
    def __init__(self, n_dp, n_pair, pieces, outs, bufs, sems):
        self.n_pair, self.pieces, self.outs, self.bufs = n_pair, pieces, outs, bufs
        self.hop_sem, self.side_sem, self.core_sem, self.out_sem = sems
        self.me = my_index(n_pair)
        self.hops = (n_dp * n_pair - 1).bit_length() - 2
        self.orders = [bit_order(n_dp, n_pair, piece[3]) for piece in pieces]
        self.count = len(pieces)

    def send(self, a, lo, count, to, sem, which, bit):
        return remote(
            self.bufs[a].at[pl.ds(lo, count)],
            self.bufs[a].at[pl.ds(to, count)],
            sem.at[0, a, which],
            sem.at[1, a, which],
            place(self.me ^ (1 << bit), self.n_pair),
        )

    def hop(self, a, r):
        return self.send(a, 0, 1 << r, 1 << r, self.hop_sem, r, self.orders[a][r])

    def side(self, a, r):
        lo, count = stage(r)
        return self.send(a, lo, count, (1 << self.hops) + lo, self.side_sem, r, self.orders[a][self.hops])

    def core(self, a, r, sided):
        lo, count = stage(r)
        lo = lo + (sided << self.hops)
        return self.send(
            a, lo, count, (2 << self.hops) + lo, self.core_sem, 2 * r + sided, 0
        )

    def write_out(self, a, lo, count):
        which, low, high, _ = self.pieces[a]
        for p in range(lo, lo + count):
            block = self.me ^ offset(self.orders[a] + [0], p)
            pltpu.make_async_copy(
                self.bufs[a].at[p], self.outs[which].at[block, :, pl.ds(low, high - low)], self.out_sem.at[a]
            ).start()

    def held(self, r):
        lo, count = stage(r)
        for a in range(self.count):
            if r:
                self.hop(a, r - 1).wait_recv()
            if r < self.hops:
                self.hop(a, r).start()
            self.side(a, r).start()
            self.core(a, r, 0).start()
        for a in range(self.count):
            self.write_out(a, lo, count)

    def sided(self, r):
        lo, count = stage(r)
        for a in range(self.count):
            self.side(a, r).wait_recv()
            self.core(a, r, 1).start()
            self.write_out(a, (1 << self.hops) + lo, count)

    def cored(self, r):
        lo, count = stage(r)
        for sided in (0, 1):
            for a in range(self.count):
                self.core(a, r, sided).wait_recv()
                self.write_out(a, (2 << self.hops) + (sided << self.hops) + lo, count)

    def finish(self):
        for a in range(self.count):
            for r in range(self.hops):
                self.hop(a, r).wait_send()
            for r in range(self.hops + 1):
                self.side(a, r).wait_send()
                self.core(a, r, 0).wait_send()
                self.core(a, r, 1).wait_send()
            pltpu.make_async_copy(self.bufs[a], self.bufs[a], self.out_sem.at[a]).wait()


def triangle(size):
    rows = lax.broadcasted_iota(jnp.int32, (size, size), 0)
    columns = lax.broadcasted_iota(jnp.int32, (size, size), 1)
    return jnp.where(rows < columns, 1.0, 0.0).astype(jnp.bfloat16)


def digits(numbers):
    high = numbers // 64
    row = lax.broadcasted_iota(jnp.int32, (8, numbers.shape[1]), 0)
    both = jnp.where(row == 0, high, jnp.where(row == 1, numbers - 64 * high, 0))
    return both.astype(jnp.float32).astype(jnp.bfloat16)


def upright(pairs):
    row = lax.broadcasted_iota(jnp.int32, (8, 128), 0)
    value = jnp.where(row == 0, 64.0, jnp.where(row == 1, 1.0, 0.0)).astype(jnp.bfloat16)
    return lax.dot_general(pairs, value, TN, preferred_element_type=jnp.float32)


def hits_by_lane(numbers, width, base):
    lane = lax.broadcasted_iota(jnp.int32, (1, 128), 1).astype(jnp.float32) + base
    tiles = [
        jnp.where(numbers == lane + 128.0 * tile, 1.0, 0.0).astype(jnp.bfloat16)
        for tile in range(width // 128)
    ]
    return jnp.concatenate(tiles, axis=1)


def front_kernel(n_dp, n_pair, pieces, n_in, *refs):
    k = len(pieces)
    owner_ref, row_ref, table_ref = refs[:3]
    shards = refs[3 : 3 + n_in]
    emb_ref, key_ref, asked_ref = refs[3 + n_in : 6 + n_in]
    outs = refs[6 + n_in : 6 + 2 * n_in]
    rest = refs[6 + 2 * n_in :]
    bufs, rest = rest[:k], rest[k:]
    wide, table, ask_out, ask_in, rows_out, rows_in, total = rest[:7]
    table_sem, ask_sem, row_sem, *sems = rest[7:]
    dp, pair = lax.axis_index("dp"), lax.axis_index("pair")
    weights = Gather(n_dp, n_pair, pieces, outs, bufs, sems)
    docs, seq = owner_ref.shape
    tokens = docs * seq
    cap = ask_out.shape[2]

    def in_line(ref):
        return jnp.concatenate([ref[d : d + 1, :] for d in range(docs)], axis=1)

    table_rows = table_ref.shape[0]
    load = pltpu.make_async_copy(table_ref, wide, table_sem)
    load.start()
    peers = [{"dp": dp ^ j, "pair": pair} for j in range(1, n_dp)]
    sem = pltpu.get_barrier_semaphore()
    mates = [{"dp": dp, "pair": pair ^ j} for j in (1, 2)]
    for target in peers + mates:
        pl.semaphore_signal(sem, inc=1, device_id=target, device_id_type=MESH)
    for a, (which, low, high, _) in enumerate(pieces):
        bufs[a][0] = shards[which][:, low:high].astype(jnp.bfloat16)
    pl.semaphore_wait(sem, n_dp + 1)
    weights.held(0)

    owner = in_line(owner_ref)
    by_owner = lax.broadcasted_iota(jnp.int32, (n_dp, tokens), 0) == owner
    ranks = jnp.dot(
        jnp.where(by_owner, 1.0, 0.0).astype(jnp.bfloat16),
        triangle(tokens),
        preferred_element_type=jnp.float32,
    )
    rank = jnp.sum(jnp.where(by_owner, ranks, 0.0), axis=0, keepdims=True)
    key = owner * cap + rank.astype(jnp.int32)
    key_ref[...] = key
    wanted = digits(in_line(row_ref))

    def peer(j):
        return {"dp": dp ^ j, "pair": pair}

    def ask(j):
        return remote(ask_out.at[j], ask_in.at[j], ask_sem.at[0, j], ask_sem.at[1, j], peer(j))

    def reply(j):
        return remote(rows_out.at[j], rows_in.at[j], row_sem.at[0, j], row_sem.at[1, j], peer(j))

    def loop(first, last, body):
        def turn(t, carry):
            body(n_dp - 1 - t)
            return carry

        lax.fori_loop(first, last, turn, 0)

    def request(j):
        slot = lax.broadcasted_iota(jnp.int32, (cap, tokens), 0) + (dp ^ j) * cap
        chosen = jnp.where(slot == key, 1.0, 0.0).astype(jnp.bfloat16)
        ask_out[j] = lax.dot_general(wanted, chosen, NT, preferred_element_type=jnp.float32)

        @pl.when(j > 0)
        def _():
            ask(j).start()

    loop(0, n_dp, request)
    ask_in[0] = ask_out[0]
    weights.held(1)
    load.wait()

    def narrow(i, carry):
        part = pl.ds(pl.multiple_of(i * 16, 16), 16)
        table[part] = wide[part].astype(jnp.bfloat16)
        return carry

    lax.fori_loop(0, table_rows // 16, narrow, 0)
    if table.shape[0] > table_rows:
        table[table_rows:] = jnp.zeros((table.shape[0] - table_rows, table.shape[1]), jnp.bfloat16)

    def answer(j):
        @pl.when(j > 0)
        def _():
            ask(j).wait_recv()

        asked = ask_in[j]
        hit = hits_by_lane(upright(asked.astype(jnp.bfloat16)), table.shape[0], 0.0)
        got = jnp.dot(hit, table[...], preferred_element_type=jnp.float32)
        rows_out[j] = got.astype(jnp.bfloat16)
        asked_ref[j] = (64.0 * asked[0:1] + asked[1:2]).astype(jnp.int32)

        @pl.when(j > 0)
        def _():
            reply(j).start()

    early = n_dp // 4 + 1
    loop(0, early, answer)
    weights.held(2)
    weights.sided(0)
    loop(early, n_dp, answer)
    rows_in[0] = rows_out[0]
    weights.sided(1)
    upright_key = upright(digits(key))

    total[...] = jnp.zeros_like(total)

    def seat(j):
        @pl.when(j > 0)
        def _():
            reply(j).wait_recv()

        place_hit = hits_by_lane(upright_key, cap, ((dp ^ j) * cap).astype(jnp.float32))
        total[...] += jnp.dot(place_hit, rows_in[j], preferred_element_type=jnp.float32)

    weights.cored(0)
    for r in range(3, weights.hops + 1):
        weights.held(r)
        weights.sided(r - 1)
        weights.cored(r - 2)
    loop(0, n_dp, seat)
    emb_ref[...] = total[...].astype(jnp.bfloat16)
    weights.sided(weights.hops)
    for r in (weights.hops - 1, weights.hops):
        weights.cored(r)
    for j in range(1, n_dp):
        ask(j).wait_send()
        reply(j).wait_send()
    weights.finish()


def front(owner, row, table, shards, pieces, cap, n_dp, n_pair, cid):
    n, k = n_dp * n_pair, len(pieces)
    hops = (n - 1).bit_length() - 2
    tokens = owner.size
    table_rows, width = table.shape
    padded = -(-table_rows // 256) * 256
    sem = pltpu.SemaphoreType.DMA
    return pl.pallas_call(
        functools.partial(front_kernel, n_dp, n_pair, pieces, len(shards)),
        out_shape=[
            jax.ShapeDtypeStruct((tokens, width), jnp.bfloat16),
            jax.ShapeDtypeStruct((1, tokens), jnp.int32),
            jax.ShapeDtypeStruct((n_dp, 1, cap), jnp.int32),
        ]
        + [jax.ShapeDtypeStruct((n,) + s.shape, jnp.bfloat16) for s in shards],
        in_specs=[VM, VM, ANY] + [VM] * len(shards),
        out_specs=[VM] * 3 + [ANY] * len(shards),
        scratch_shapes=[
            pltpu.VMEM((n, shards[p[0]].shape[0], p[2] - p[1]), jnp.bfloat16) for p in pieces
        ]
        + [
            pltpu.VMEM((table_rows, width), jnp.float32),
            pltpu.VMEM((padded, width), jnp.bfloat16),
            pltpu.VMEM((n_dp, 8, cap), jnp.float32),
            pltpu.VMEM((n_dp, 8, cap), jnp.float32),
            pltpu.VMEM((n_dp, cap, width), jnp.bfloat16),
            pltpu.VMEM((n_dp, cap, width), jnp.bfloat16),
            pltpu.VMEM((tokens, width), jnp.float32),
            sem,
            sem((2, n_dp)),
            sem((2, n_dp)),
            sem((2, k, hops)),
            sem((2, k, hops + 1)),
            sem((2, k, 2 * hops + 2)),
            sem((k,)),
        ],
        compiler_params=pltpu.CompilerParams(
            collective_id=cid, has_side_effects=True, vmem_limit_bytes=VMEM_LIMIT
        ),
        name="rows_and_weights",
    )(owner, row, table, *shards)


class Scatter:
    def __init__(self, n_dp, n_pair, pieces, ins, outs, boxes, sems):
        self.n_pair, self.pieces, self.ins, self.outs = n_pair, pieces, ins, outs
        k = len(pieces)
        self.acc, self.from_core = boxes[:k], boxes[k : 2 * k]
        self.from_side, self.from_hop = boxes[2 * k : 3 * k], boxes[3 * k :]
        self.load_sem, self.core_sem, self.side_sem, self.hop_sem = sems
        self.me = my_index(n_pair)
        self.hops = (n_dp * n_pair - 1).bit_length() - 2
        self.orders = [bit_order(n_dp, n_pair, piece[3]) for piece in pieces]
        self.count = k

    def source(self, a, block):
        which, low, high, _ = self.pieces[a]
        return self.ins[which].at[block, :, pl.ds(low, high - low)]

    def near(self, bit):
        return place(self.me ^ (1 << bit), self.n_pair)

    def load(self):
        for a in range(self.count):
            for p in range(2 << self.hops):
                pltpu.make_async_copy(
                    self.source(a, self.me ^ offset(self.orders[a], p)),
                    self.acc[a].at[p],
                    self.load_sem.at[a],
                ).start()

    def loaded(self):
        for a in range(self.count):
            pltpu.make_async_copy(self.acc[a], self.acc[a], self.load_sem.at[a]).wait()

    def core(self, a, r, sided, part=None):
        lo, count = stage(r)
        lo = lo + (sided << self.hops)
        to = self.from_core[a].at[pl.ds(lo, count)]
        source = to
        if part is not None:
            to = self.from_core[a].at[lo + part]
            source = self.source(a, self.me ^ (offset(self.orders[a], lo + part) + 1))
        slot = 2 * r + sided
        return remote(
            source, to, self.core_sem.at[0, a, slot], self.core_sem.at[1, a, slot], self.near(0)
        )

    def core_out(self, r):
        for sided in (1, 0):
            for a in range(self.count):
                for part in range(stage(r)[1]):
                    self.core(a, r, sided, part).start()

    def add(self, a, lo, count, box, at):
        acc = self.acc[a]

        def body(j, carry):
            acc[lo + j] = (
                acc[lo + j].astype(jnp.float32) + box[at + j].astype(jnp.float32)
            ).astype(jnp.bfloat16)
            return carry

        lax.fori_loop(0, count, body, 0)

    def side(self, a, r):
        lo, count = stage(r)
        return remote(
            self.acc[a].at[pl.ds((1 << self.hops) + lo, count)],
            self.from_side[a].at[pl.ds(lo, count)],
            self.side_sem.at[0, a, r],
            self.side_sem.at[1, a, r],
            self.near(self.orders[a][self.hops]),
        )

    def hop(self, a, r):
        return remote(
            self.acc[a].at[pl.ds(1 << r, 1 << r)],
            self.from_hop[a].at[pl.ds(self.hop_base(r), 1 << r)],
            self.hop_sem.at[0, a, r],
            self.hop_sem.at[1, a, r],
            self.near(self.orders[a][r]),
        )

    def hop_base(self, r):
        return (1 << self.hops) - (2 << r)

    def core_in(self, r):
        lo, count = stage(r)
        for sided in (1, 0):
            for a in range(self.count):
                self.core(a, r, sided).wait_recv()
                at = lo + (sided << self.hops)
                self.add(a, at, count, self.from_core[a], at)
                if sided:
                    self.side(a, r).start()

    def side_in(self, r):
        lo, count = stage(r)
        for a in range(self.count):
            self.side(a, r).wait_recv()
            self.add(a, lo, count, self.from_side[a], lo)
            if r == self.hops:
                self.hop(a, r - 1).start()

    def hop_in(self, r):
        for a in range(self.count):
            self.hop(a, r).wait_recv()
            base = self.hop_base(r)
            if r:
                mid = 1 << (r - 1)
                self.add(a, mid, mid, self.from_hop[a], base + mid)
                self.hop(a, r - 1).start()
                self.add(a, 0, mid, self.from_hop[a], base)
            else:
                which, low, high, _ = self.pieces[a]
                self.outs[which][:, low:high] = self.acc[a][0].astype(jnp.float32) + self.from_hop[
                    a
                ][base].astype(jnp.float32)

    def finish(self):
        for a in range(self.count):
            for r in range(self.hops):
                self.hop(a, r).wait_send()
            for r in range(self.hops + 1):
                self.side(a, r).wait_send()
                self.core(a, r, 0).wait_send()
                self.core(a, r, 1).wait_send()


def backward_kernel(n_dp, n_pair, pieces, n_in, *refs):
    k_count = len(pieces)
    len_ref, q_ref, k_ref, v_ref, g_ref, w_ref = refs[:6]
    ins = refs[6 : 6 + n_in]
    o_ref, z_ref, square_ref = refs[6 + n_in : 9 + n_in]
    outs = refs[9 + n_in : 9 + 2 * n_in]
    table, total, box, sem = refs[9 + 2 * n_in : 13 + 2 * n_in]
    rest = refs[13 + 2 * n_in :]
    weights = Scatter(n_dp, n_pair, pieces, ins, outs, rest[: 4 * k_count], rest[4 * k_count :])
    at = pl.program_id(0) * pl.num_programs(1) + pl.program_id(1)
    hops = weights.hops

    @pl.when(at == 0)
    def _():
        weights.load()
        greet([weights.near(bit) for bit in range(hops + 2)])
        for r in reversed(range(hops + 1)):
            weights.core_out(r)

    @pl.when(at == 1)
    def _():
        weights.loaded()
        weights.core_in(hops)

    @pl.when(at == 2)
    def _():
        for r in reversed(range(hops)):
            weights.core_in(r)

    @pl.when(at == 5)
    def _():
        weights.side_in(hops)

    @pl.when(at == 6)
    def _():
        for r in reversed(range(hops)):
            weights.side_in(r)

    seq = q_ref.shape[0]
    tiles = seq // 128
    doc = pl.program_id(1)
    @pl.when(doc == 0)
    def _():
        for h in range(2):
            band(w_ref, 2 * pl.program_id(0) + h, 2 * seq, h, table, seq)
        total[...] = jnp.zeros_like(total)
    length = len_ref[doc]
    lane = lax.broadcasted_iota(jnp.int32, (seq, 128), 1)
    row = lax.broadcasted_iota(jnp.int32, (seq, 1), 0)
    q = q_ref[...] * jnp.bfloat16(0.125)
    k = k_ref[...]
    v = v_ref[...]
    g = g_ref[...]
    parts = []
    for h in range(2):
        mine = (lane < 64) == (h == 0)
        s = lax.dot_general(k, jnp.where(mine, q, 0), NT, preferred_element_type=jnp.float32)
        s = jnp.where(row < length, s + table[h], -1000000000.0)
        e = jnp.exp(s - jnp.max(s, axis=0, keepdims=True))
        p = e * (1.0 / jnp.sum(e, axis=0, keepdims=True))
        dv = jnp.dot(p.astype(jnp.bfloat16), g, preferred_element_type=jnp.float32)
        dp = lax.dot_general(v, jnp.where(mine, g, 0), NT, preferred_element_type=jnp.float32)
        ds = (p * (dp - jnp.sum(p * dp, axis=0, keepdims=True))).astype(jnp.bfloat16)
        total[h] += ds.astype(jnp.float32)
        dk = jnp.dot(ds, q, preferred_element_type=jnp.float32)
        dq = lax.dot_general(ds, k, TN, preferred_element_type=jnp.float32) * 0.125
        parts.append((dq, dk, dv))
    pair, pairs, docs = pl.program_id(0), pl.num_programs(0), pl.num_programs(1)
    step = pair * docs + doc
    slot = lax.rem(step, 2)

    def out(i):
        rows = pl.ds(pl.multiple_of(doc * seq, seq), seq)
        columns = pl.ds(pl.multiple_of((i * pairs + pair) * 128, 128), 128)
        return pltpu.make_async_copy(box.at[slot, i], o_ref.at[rows, columns], sem.at[slot, i])

    for i in range(3):
        @pl.when(step >= 2)
        def _():
            out(i).wait()
        box[slot, i] = jnp.where(lane < 64, parts[0][i], parts[1][i]).astype(o_ref.dtype)
        out(i).start()

    for r in range(1, hops):
        @pl.when(step == pairs * docs - 2 * r)
        def _():
            weights.hop_in(r)

    @pl.when(step == pairs * docs - 1)
    def _():
        weights.hop_in(0)
        weights.finish()
        square_ref[...] = jnp.zeros_like(square_ref)
        for ref in outs:
            square = jnp.sum(ref[...] * ref[...], axis=0, keepdims=True)
            square_ref[...] += jnp.sum(square, axis=1, keepdims=True)
        for i in range(3):
            out(i).wait()
            pltpu.make_async_copy(box.at[1 - slot, i], box.at[1 - slot, i], sem.at[1 - slot, i]).wait()
    @pl.when(doc == pl.num_programs(1) - 1)
    def _():
        r = lax.broadcasted_iota(jnp.int32, (128, 128), 0)
        c = lax.broadcasted_iota(jnp.int32, (128, 128), 1)
        flip = jnp.where(r + c == 127, 1.0, 0.0)
        z_ref[...] = jnp.zeros_like(z_ref)
        for h in range(2):
            def block(d):
                return sum(total[h, a * 128 : a * 128 + 128, (a - d) * 128 : (a - d) * 128 + 128] for a in range(tiles) if 0 <= a - d < tiles)
            for d in (-1, 0, 1):
                x = jnp.dot(flip, block(d), precision=HIGHEST, preferred_element_type=jnp.float32)
                x = jnp.concatenate([x, jnp.zeros_like(x)], axis=1)
                x = pltpu.roll(x, 0, 1, stride=1, stride_axis=0)
                z_ref[0, h, d + 1 : d + 2, :] = jnp.sum(x, axis=0, keepdims=True)
            z_ref[0, h, 3:4, 0:128] = jnp.sum(sum(block(-d) for d in range(2, tiles)), axis=0, keepdims=True)
            z_ref[0, h, 4:5, 0:128] = jnp.sum(sum(block(d) for d in range(2, tiles)), axis=0, keepdims=True)

def attention_back(lengths, qkv, g, w, seq, grads, pieces, cid):
    n_dp, n_pair = lax.axis_size("dp"), lax.axis_size("pair")
    tokens = qkv.shape[0]
    pairs = w.shape[0] // 2
    docs = tokens // seq
    spec = lambda base: pl.BlockSpec((seq, 128), lambda h, d, *_: (d, base + h))
    still = lambda shape: pl.BlockSpec(shape, lambda h, d, *_: (0, 0))
    boxes, sems = scatter_scratch(n_dp * n_pair, grads, pieces)
    return pl.pallas_call(
        functools.partial(backward_kernel, n_dp, n_pair, pieces, len(grads)),
        grid_spec=pltpu.PrefetchScalarGridSpec(
            num_scalar_prefetch=1,
            grid=(pairs, docs),
            in_specs=[spec(0), spec(pairs), spec(2 * pairs), spec(0), still(w.shape)]
            + [ANY] * len(grads),
            out_specs=[
                ANY,
                pl.BlockSpec((1, 2, 8, 256), lambda h, d, *_: (h, 0, 0, 0)),
                still((1, 1)),
            ]
            + [still(grad.shape[1:]) for grad in grads],
            scratch_shapes=[
                pltpu.VMEM((2, seq, seq), jnp.float32),
                pltpu.VMEM((2, seq, seq), jnp.float32),
                pltpu.VMEM((2, 3, seq, 128), jnp.bfloat16),
                pltpu.SemaphoreType.DMA((2, 3)),
            ]
            + boxes
            + sems,
        ),
        out_shape=[
            jax.ShapeDtypeStruct((tokens, 3 * pairs * 128), jnp.bfloat16),
            jax.ShapeDtypeStruct((pairs, 2, 8, 256), jnp.float32),
            jax.ShapeDtypeStruct((1, 1), jnp.float32),
        ]
        + [jax.ShapeDtypeStruct(grad.shape[1:], jnp.float32) for grad in grads],
        compiler_params=pltpu.CompilerParams(
            dimension_semantics=("arbitrary", "arbitrary"),
            collective_id=cid,
            has_side_effects=True,
            vmem_limit_bytes=VMEM_LIMIT,
        ),
        name="attention_back",
    )(lengths, qkv, qkv, qkv, g, w, *grads)


def packed_base(gains, width):
    return -(-gains * width // 128 // 8) * 8


def back_kernel(n_dp, n_pair, pieces, n_gain, n_in, chunk, *refs):
    k = len(pieces)
    grad_ref, key_ref, ask_ref, squares_ref, bias_ref = refs[:5]
    gain_refs = refs[5 : 5 + n_gain]
    ins, rest = refs[5 + n_gain : 5 + n_gain + n_in], refs[5 + n_gain + n_in :]
    out_ref, total_ref = rest[:2]
    outs = rest[2 : 2 + n_in]
    rest = rest[2 + n_in :]
    boxes, rest = rest[: 4 * k], rest[4 * k :]
    rows_out, rows_in, hot, part, stage_out, got_core, out_side, got_side, other = rest[:9]
    square_ref, small, by_dp, from_pair = rest[9:13]
    row_sem, core_sem, side_sem, last_sem, out_sem, dp_sem, pair_sem, *sems = rest[13:]
    dp, pair = lax.axis_index("dp"), lax.axis_index("pair")
    core = lax.rem(pair, 2)
    weights = Scatter(n_dp, n_pair, pieces, ins, outs, boxes, sems)
    groups, _, cap, width = rows_out.shape
    slots = ask_ref.shape[1]
    count = stage_out.shape[1]
    half = count * chunk
    tokens = key_ref.shape[1]
    peers = [{"dp": dp ^ j, "pair": pair} for j in range(1, n_dp)]
    partner, across = {"dp": dp, "pair": pair ^ 1}, {"dp": dp, "pair": pair ^ 2}
    weights.load()
    sem = pltpu.get_barrier_semaphore()
    for target in peers + [partner, across]:
        pl.semaphore_signal(sem, inc=1, device_id=target, device_id_type=MESH)

    def row(g, j):
        return remote(
            rows_out.at[g, j],
            rows_in.at[g, pl.ds(pl.multiple_of(j * cap, cap), cap)],
            row_sem.at[0, g, j],
            row_sem.at[1, g, j],
            {"dp": dp ^ j, "pair": pair},
        )

    def loop(size, body):
        def turn(i, carry):
            body(i)
            return carry

        lax.fori_loop(0, size, turn, 0)

    far = sorted(range(1, n_dp), reverse=True)

    pl.semaphore_wait(sem, n_dp + 1)

    def rows_of(t):
        j = n_dp - 1 - t
        slot = lax.broadcasted_iota(jnp.int32, (cap, tokens), 0) + (dp ^ j) * cap
        hits = jnp.where(slot == key_ref[...], 1.0, 0.0).astype(jnp.bfloat16)
        got = jnp.dot(hits, grad_ref[...], preferred_element_type=jnp.float32)
        got = got.astype(jnp.bfloat16)
        for g in range(groups):
            rows_out[g, j] = got[:, g * width : (g + 1) * width]

        @pl.when(j > 0)
        def _():
            row(0, j).start()

    loop(n_dp, rows_of)
    for g in range(1, groups):
        for j in far:
            row(g, j).start()
    for g in range(groups):
        rows_in[g, 0:cap] = rows_out[g, 0]
    for r in reversed(range(weights.hops + 1)):
        weights.core_out(r)

    def tell(c):
        ids = lax.broadcasted_iota(jnp.int32, (chunk, slots), 0) + c * chunk
        hot[c] = jnp.where(ids == ask_ref[...], 1.0, 0.0).astype(jnp.bfloat16)

    loop(2 * count, tell)

    def summed(g, c):
        return jnp.dot(hot[c], rows_in[g], preferred_element_type=jnp.float32)

    def to_core(g, i):
        return remote(
            stage_out.at[g, i], got_core.at[g, i], core_sem.at[0, g, i], core_sem.at[1, g, i], partner
        )

    def to_side(g, i):
        return remote(
            out_side.at[g, i], got_side.at[g, i], side_sem.at[0, g, i], side_sem.at[1, g, i], across
        )

    def to_other(g, i):
        return remote(
            out_side.at[g, i], other.at[g, i], last_sem.at[0, g, i], last_sem.at[1, g, i], partner
        )

    def write_out(box, g, i, which):
        rows = pl.ds(pl.multiple_of(which * half + i * chunk, chunk), chunk)
        return pltpu.make_async_copy(
            box.at[g, i], out_ref.at[rows, pl.ds(g * width, width)], out_sem.at[g, i]
        )

    def local_sums(g):
        for j in far:
            row(g, j).wait_recv()

        def combine(i):
            to_core(g, i).wait_recv()
            out_side[g, i] = (part[i] + got_core[g, i].astype(jnp.float32)).astype(jnp.bfloat16)
            to_side(g, i).start()

        def one(i):
            stage_out[g, i] = summed(g, (1 - core) * count + i).astype(jnp.bfloat16)
            to_core(g, i).start()
            part[i] = summed(g, core * count + i)

            @pl.when(i > 0)
            def _():
                combine(i - 1)

        loop(count, one)
        combine(count - 1)

    square_ref[...] = squares_ref[...]

    def finish_sums(g):
        def one(i):
            to_side(g, i).wait()
            wide = out_side[g, i].astype(jnp.float32) + got_side[g, i].astype(jnp.float32)
            value = wide.astype(jnp.bfloat16)
            out_side[g, i] = value
            to_other(g, i).start()
            write_out(out_side, g, i, core).start()
            wide = value.astype(jnp.float32)
            square = jnp.sum(wide * wide, axis=0, keepdims=True)
            square = jnp.sum(square, axis=1, keepdims=True)
            square_ref[...] += jnp.where(pair < 2, square, 0.0)

        loop(count, one)

    def hand_over(g):
        def one(i):
            to_other(g, i).wait_recv()
            write_out(out_side, g, i, core).wait()
            write_out(other, g, i, 1 - core).start()

        loop(count, one)

    weights.loaded()
    for r in reversed(range(weights.hops + 1)):
        weights.core_in(r)
    for g in range(groups):
        local_sums(g)
        if g:
            finish_sums(g - 1)
        if g == groups // 2:
            for r in reversed(range(weights.hops + 1)):
                weights.side_in(r)
    for r in reversed(range(1, weights.hops)):
        weights.hop_in(r)
    finish_sums(groups - 1)
    weights.hop_in(0)
    for ref in outs:
        square = jnp.sum(ref[...] * ref[...], axis=0, keepdims=True)
        square_ref[...] += jnp.sum(square, axis=1, keepdims=True)
    gains_width = gain_refs[0].shape[1]
    base = packed_base(n_gain, gains_width)
    small[...] = jnp.zeros_like(small)
    for c in range(gains_width // 128):
        for which in range(n_gain):
            at = c * n_gain + which
            small[0, at : at + 1, :] = gain_refs[which][:, c * 128 : (c + 1) * 128]
    small[0, base : base + bias_ref.shape[0], : bias_ref.shape[1]] = bias_ref[...]
    small[0, base : base + 1, 127:128] = square_ref[...]

    def to_dp(j, slot):
        return remote(
            small.at[0],
            by_dp.at[slot],
            dp_sem.at[0, j],
            dp_sem.at[1, j],
            {"dp": dp ^ j, "pair": pair},
        )

    def to_pair(turn, target):
        return remote(
            small.at[1 + turn],
            from_pair.at[turn],
            pair_sem.at[0, turn],
            pair_sem.at[1, turn],
            target,
        )

    for j in far:
        to_dp(j, dp).start()
    by_dp[dp] = small[0]
    for g in range(groups):
        hand_over(g)
    for j in far:
        to_dp(j, dp ^ j).wait_recv()
    total = by_dp[0]
    for d in range(1, n_dp):
        total = total + by_dp[d]
    for turn, target in enumerate((partner, across)):
        small[1 + turn] = total
        to_pair(turn, target).start()
        to_pair(turn, target).wait_recv()
        total = total + from_pair[turn]
    total_ref[...] = total
    for j in far:
        to_dp(j, dp).wait_send()
    for turn, target in enumerate((partner, across)):
        to_pair(turn, target).wait_send()
    for g in range(groups):
        for j in far:
            row(g, j).wait_send()

        def one(i):
            to_core(g, i).wait_send()
            to_other(g, i).wait_send()
            write_out(other, g, i, 1 - core).wait()

        loop(count, one)
    weights.finish()


def scatter_scratch(n, grads, pieces):
    k, hops, sem = len(pieces), (n - 1).bit_length() - 2, pltpu.SemaphoreType.DMA
    boxes = [
        pltpu.VMEM((lead, grads[p[0]].shape[1], p[2] - p[1]), jnp.bfloat16)
        for lead in (n // 2, n // 2, n // 4, n // 4 - 1)
        for p in pieces
    ]
    return boxes, [
        sem((k,)),
        sem((2, k, 2 * hops + 2)),
        sem((2, k, hops + 1)),
        sem((2, k, hops)),
    ]


def back(grad, key, asked, squares, bias, gains, grads, pieces, table_rows, groups, cid):
    n_dp, n_pair = lax.axis_size("dp"), lax.axis_size("pair")
    boxes, sems = scatter_scratch(n_dp * n_pair, grads, pieces)
    chunk = 512
    rows = -(-table_rows // (2 * chunk)) * 2 * chunk
    count = rows // 2 // chunk
    tokens, full = grad.shape
    width = full // groups
    slots = asked.shape[1]
    height = -(-(packed_base(len(gains), full) + bias.shape[0]) // 8) * 8
    cap = slots // n_dp
    sem = pltpu.SemaphoreType.DMA
    box = pltpu.VMEM((groups, count, chunk, width), jnp.bfloat16)

    return pl.pallas_call(
        functools.partial(back_kernel, n_dp, n_pair, pieces, len(gains), len(grads), chunk),
        out_shape=[
            jax.ShapeDtypeStruct((rows, full), jnp.bfloat16),
            jax.ShapeDtypeStruct((height, 128), jnp.float32),
        ]
        + [jax.ShapeDtypeStruct(g.shape[1:], jnp.float32) for g in grads],
        in_specs=[VM] * (5 + len(gains)) + [ANY] * len(grads),
        out_specs=[ANY, VM] + [VM] * len(grads),
        scratch_shapes=boxes
        + [
            pltpu.VMEM((groups, n_dp, cap, width), jnp.bfloat16),
            pltpu.VMEM((groups, slots, width), jnp.bfloat16),
            pltpu.VMEM((2 * count, chunk, slots), jnp.bfloat16),
            pltpu.VMEM((count, chunk, width), jnp.float32),
            box,
            box,
            box,
            box,
            box,
            pltpu.VMEM((1, 1), jnp.float32),
            pltpu.VMEM((3, height, 128), jnp.float32),
            pltpu.VMEM((n_dp, height, 128), jnp.float32),
            pltpu.VMEM((2, height, 128), jnp.float32),
            sem((2, groups, n_dp)),
            sem((2, groups, count)),
            sem((2, groups, count)),
            sem((2, groups, count)),
            sem((groups, count)),
            sem((2, n_dp)),
            sem((2, 2)),
        ]
        + sems,
        compiler_params=pltpu.CompilerParams(
            collective_id=cid, has_side_effects=True, vmem_limit_bytes=VMEM_LIMIT
        ),
        name="table_and_weights",
    )(grad, key, asked, squares, bias, *gains, *grads)


BIAS_CORRECT = (1.0 - beta_one**STEP, 1.0 - beta_two**STEP)


def adam_parts(weight, first, second, grad, factor, rate, shrink):
    clipped = grad * factor
    first_new = beta_one * first + (1.0 - beta_one) * clipped
    second_new = beta_two * second + (1.0 - beta_two) * (clipped * clipped)
    root = jnp.sqrt(second_new * (1.0 / BIAS_CORRECT[1])) + adam_eps
    step = (rate / BIAS_CORRECT[0]) * first_new / root
    return (weight * (1.0 - rate * shrink) - step, first_new, second_new)


def update_kernel(mats, *refs):
    total_ref, loss_ref, low = refs[:3]
    table, small = refs[3:6], refs[6:12]
    grads = refs[12 : 12 + mats]
    states = refs[12 + mats : 12 + 4 * mats]
    rest = refs[12 + 4 * mats :]
    norm_out, loss_out, table_out, small_out = rest[0], rest[1], rest[2:5], rest[5:11]
    mat_out = rest[11:]
    gains, width = small[0].shape
    base = packed_base(gains, width)
    total = total_ref[...]
    row = lax.broadcasted_iota(jnp.int32, total.shape, 0)
    lane = lax.broadcasted_iota(jnp.int32, total.shape, 1)
    plain = jnp.where((row == base) & (lane == 127), total, total * total)
    norm = jnp.sqrt(jnp.sum(jnp.sum(plain, axis=1, keepdims=True), axis=0, keepdims=True))
    factor = jnp.minimum(1.0, clip_limit / norm)
    step = pl.program_id(0)

    @pl.when(step == 0)
    def _():
        norm_out[...] = norm
        loss_out[...] = loss_ref[...]
        for c in range(width // 128):
            columns = slice(c * 128, (c + 1) * 128)
            grad = total_ref[c * gains : (c + 1) * gains, :]
            new = adam_parts(*(ref[:, columns] for ref in small[:3]), grad, factor, 1.0, 0.0)
            for ref, value in zip(small_out[:3], new):
                ref[:, columns] = value
        heads = small[3].shape[1]
        grad = total_ref[base : base + small[3].shape[0], :heads]
        new = adam_parts(*(ref[...] for ref in small[3:]), grad, factor, 0.3, 0.0)
        for ref, value in zip(small_out[3:], new):
            ref[...] = value

    for which in range(mats):
        three = slice(3 * which, 3 * which + 3)
        new = adam_parts(*(ref[...] for ref in states[three]), grads[which][...], factor, 0.05, 0.01)
        for ref, value in zip(mat_out[three], new):
            ref[...] = value

    def body(j, carry):
        rows = pl.ds(pl.multiple_of(j * 16, 16), 16)
        new = adam_parts(*(ref[rows] for ref in table), low[rows].astype(jnp.float32), factor, 1.0, 0.01)
        for ref, value in zip(table_out, new):
            ref[rows] = value
        return carry

    lax.fori_loop(0, low.shape[0] // 16, body, 0)


def update(total, loss, table_grad, table, small, grads, states):
    rows, width = table[0].shape
    steps = 6
    tall = -(-rows // steps // 16) * 16
    flat = [array for group in states for array in group]
    like = lambda array: jax.ShapeDtypeStruct(array.shape, jnp.float32)
    whole = lambda array: pl.BlockSpec(array.shape, lambda i: (0, 0))
    table_spec = pl.BlockSpec((tall, width), lambda i: (i, 0))

    def part(array):
        if array.shape[1] % (128 * steps) == 0 and array.shape[0] < 32:
            return pl.BlockSpec((array.shape[0], array.shape[1] // steps), lambda i: (0, i))
        if array.shape[0] % (8 * steps) == 0:
            return pl.BlockSpec((array.shape[0] // steps, array.shape[1]), lambda i: (i, 0))
        return whole(array)

    return pl.pallas_call(
        functools.partial(update_kernel, len(grads)),
        grid=(steps,),
        out_shape=[like(loss), like(loss)] + [like(array) for array in (*table, *small, *flat)],
        in_specs=[whole(total), whole(loss)]
        + [table_spec] * 4
        + [whole(array) for array in small]
        + [part(array) for array in (*grads, *flat)],
        out_specs=[whole(loss)] * 2
        + [table_spec] * 3
        + [whole(array) for array in small]
        + [part(array) for array in flat],
        compiler_params=pltpu.CompilerParams(
            dimension_semantics=("arbitrary",), vmem_limit_bytes=VMEM_LIMIT
        ),
        name="update",
    )(total, loss, table_grad, *table, *small, *grads, *flat)


def local_plain(
    token_owner,
    token_row,
    lengths,
    positives,
    negatives,
    neg_counts,
    embed_table,
    embed_first,
    embed_second,
    qkv_weight,
    qkv_first,
    qkv_second,
    out_weight,
    out_first,
    out_second,
    in_weight,
    in_first,
    in_second,
    down_weight,
    down_first,
    down_second,
    norm_gains,
    gains_first,
    gains_second,
    position_bias,
    bias_first,
    bias_second,
):
    doc_count = lengths.shape[0]
    seq_len = token_row.shape[1]
    model_width = embed_table.shape[1]
    head_count = position_bias.shape[1]
    bucket_count = position_bias.shape[0]
    tok_total = doc_count * seq_len
    owners = lax.axis_size("dp")
    capacity = max(2, 2 * tok_total // owners)
    low_mats = (
        qkv_weight.astype(jnp.bfloat16),
        out_weight.astype(jnp.bfloat16),
        in_weight.astype(jnp.bfloat16),
        down_weight.astype(jnp.bfloat16),
    )
    qkv_full, out_full, in_full, down_full = (
        lax.all_gather(low_mats[0], ("dp", "pair"), axis=0, tiled=True),
        lax.all_gather(low_mats[1], ("dp", "pair"), axis=0, tiled=True),
        lax.all_gather(low_mats[2], ("dp", "pair"), axis=0, tiled=True),
        lax.all_gather(low_mats[3], ("dp", "pair"), axis=0, tiled=True),
    )
    tok_owner = token_owner.reshape(-1)
    tok_row = token_row.reshape(-1)
    owner_hits = (tok_owner[:, None] == jnp.arange(owners, dtype=jnp.int32)[None, :]).astype(
        jnp.int32
    )
    slot_rank = jnp.sum((jnp.cumsum(owner_hits, axis=0) - 1) * owner_hits, axis=1)
    requests = jnp.zeros((owners, capacity), jnp.int32).at[tok_owner, slot_rank].set(tok_row)
    asked_rows = lax.all_to_all(requests, "dp", split_axis=0, concat_axis=0, tiled=True)
    looked = jnp.take(embed_table, asked_rows.reshape(-1), axis=0).astype(jnp.bfloat16)
    answer = lax.all_to_all(
        looked.reshape(asked_rows.shape + (model_width,)),
        "dp",
        split_axis=0,
        concat_axis=0,
        tiled=True,
    )
    replies, asked_rows = (answer, asked_rows)
    embedded = replies[tok_owner, slot_rank].astype(jnp.float32)
    positions = jnp.arange(seq_len)
    live = positions[None, :] < lengths[:, None]
    pair_buckets = bucket_of(
        (positions[None, :] - positions[:, None]).reshape(-1), bucket_count, REACH
    )
    pair_hits = (jnp.arange(bucket_count)[:, None] == pair_buckets[None, :]).astype(jnp.float32)
    bias_full = jnp.dot(position_bias.T, pair_hits, precision=HIGHEST).reshape(
        head_count, seq_len, seq_len
    )
    bucket_map = pair_hits.astype(jnp.bfloat16)

    def split_doc(source, doc_index):
        doc_rows = source[doc_index * seq_len : (doc_index + 1) * seq_len]
        return tuple(
            (
                doc_rows[:, member * model_width : (member + 1) * model_width].reshape(
                    seq_len, head_count, -1
                )
                for member in range(3)
            )
        )

    normed_one, inverse_one = rms_forward(embedded, norm_gains[0])
    normed_one = normed_one.astype(jnp.bfloat16)
    qkv_rows = jnp.dot(normed_one, qkv_full, preferred_element_type=jnp.float32).astype(
        jnp.bfloat16
    )
    attended_parts = []
    logsum_parts = []
    for doc_index in range(doc_count):
        query_heads, key_heads, value_heads = split_doc(qkv_rows, doc_index)
        doc_out, logsum = attend_forward(
            query_heads, key_heads, value_heads, bias_full, live[doc_index]
        )
        attended_parts.append(doc_out.reshape(seq_len, model_width))
        logsum_parts.append(logsum)
    attended = jnp.concatenate(attended_parts, axis=0).astype(jnp.bfloat16)
    residual = embedded + jnp.dot(attended, out_full, preferred_element_type=jnp.float32)
    normed_two, inverse_two = rms_forward(residual, norm_gains[1])
    normed_two = normed_two.astype(jnp.bfloat16)
    hidden = jax.nn.relu(jnp.dot(normed_two, in_full, preferred_element_type=jnp.float32)).astype(
        jnp.bfloat16
    )
    output_rows = residual + jnp.dot(hidden, down_full, preferred_element_type=jnp.float32)
    normed_three, inverse_three = rms_forward(output_rows, norm_gains[2])
    live_rows = live.reshape(-1, 1)
    length_float = lengths.astype(jnp.float32)
    pooled_local = (
        jnp.sum(
            jnp.where(live_rows, normed_three, 0.0).reshape(doc_count, seq_len, model_width), axis=1
        )
        / length_float[:, None]
    )
    pooled_all = lax.all_gather(pooled_local, ("dp", "pair"), axis=0, tiled=True)
    loss_value, loss_pullback = jax.vjp(
        lambda pooled_in: margin_loss(pooled_in, positives, negatives, neg_counts), pooled_all
    )
    grad_pooled_all = loss_pullback(jnp.ones((), jnp.float32))[0]
    grad_pooled = lax.dynamic_slice_in_dim(
        grad_pooled_all, lax.axis_index(("dp", "pair")) * doc_count, doc_count, 0
    )
    grad_three = jnp.where(
        live_rows, jnp.repeat(grad_pooled / length_float[:, None], seq_len, axis=0), 0.0
    )
    qkv_back, out_back, in_back, down_back = (qkv_full, out_full, in_full, down_full)
    grad_output, gain_three = rms_backward(output_rows, inverse_three, norm_gains[2], grad_three)
    grad_branch = grad_output.astype(jnp.bfloat16)
    grad_down = lax.dot_general(
        hidden, grad_branch, CONTRACT_ROWS, preferred_element_type=jnp.float32
    )
    grad_hidden = lax.dot_general(
        grad_branch, down_back, CONTRACT_COLS, preferred_element_type=jnp.float32
    )
    grad_pre = jnp.where(hidden > 0, grad_hidden, 0.0).astype(jnp.bfloat16)
    grad_in = lax.dot_general(
        normed_two, grad_pre, CONTRACT_ROWS, preferred_element_type=jnp.float32
    )
    grad_normed_two = lax.dot_general(
        grad_pre, in_back, CONTRACT_COLS, preferred_element_type=jnp.float32
    )
    grad_res_part, gain_two = rms_backward(residual, inverse_two, norm_gains[1], grad_normed_two)
    grad_residual = grad_output + grad_res_part
    grad_attn_branch = grad_residual.astype(jnp.bfloat16)
    grad_out = lax.dot_general(
        attended, grad_attn_branch, CONTRACT_ROWS, preferred_element_type=jnp.float32
    )
    grad_attended = lax.dot_general(
        grad_attn_branch, out_back, CONTRACT_COLS, preferred_element_type=jnp.float32
    ).astype(jnp.bfloat16)
    grad_qkv_parts = []
    bias_grad_heads = jnp.zeros((head_count, bucket_count), jnp.float32)
    for doc_index in range(doc_count):
        query_heads, key_heads, value_heads = split_doc(qkv_rows, doc_index)
        grad_doc = grad_attended[doc_index * seq_len : (doc_index + 1) * seq_len].reshape(
            seq_len, head_count, -1
        )
        grad_query, grad_key, grad_value, grad_low = attend_backward(
            query_heads,
            key_heads,
            value_heads,
            bias_full,
            live[doc_index],
            logsum_parts[doc_index],
            grad_doc,
        )
        grad_qkv_parts.append(
            jnp.concatenate(
                [
                    grad_query.reshape(seq_len, model_width),
                    grad_key.reshape(seq_len, model_width),
                    grad_value.reshape(seq_len, model_width),
                ],
                axis=1,
            )
        )
        bias_grad_heads = bias_grad_heads + lax.dot_general(
            grad_low.reshape(head_count, -1),
            bucket_map,
            CONTRACT_COLS,
            preferred_element_type=jnp.float32,
        )
    bias_grad_local = bias_grad_heads.T
    grad_qkv_rows = jnp.concatenate(grad_qkv_parts, axis=0).astype(jnp.bfloat16)
    grad_qkv = lax.dot_general(
        normed_one, grad_qkv_rows, CONTRACT_ROWS, preferred_element_type=jnp.float32
    )
    grad_normed_one = lax.dot_general(
        grad_qkv_rows, qkv_back, CONTRACT_COLS, preferred_element_type=jnp.float32
    )
    grad_emb_part, gain_one = rms_backward(embedded, inverse_one, norm_gains[0], grad_normed_one)
    grad_embedded = grad_residual + grad_emb_part
    sendback = (
        jnp.zeros((owners, capacity, model_width), jnp.float32)
        .at[tok_owner, slot_rank]
        .set(grad_embedded)
    )
    arrived = lax.all_to_all(sendback, "dp", split_axis=0, concat_axis=0, tiled=True)
    table_grad = jax.ops.segment_sum(
        arrived.reshape(-1, model_width), asked_rows.reshape(-1), num_segments=embed_table.shape[0]
    )
    table_grad = lax.psum(table_grad, "pair")
    weight_grads = (
        lax.psum_scatter(grad_qkv, ("dp", "pair"), scatter_dimension=0, tiled=True),
        lax.psum_scatter(grad_out, ("dp", "pair"), scatter_dimension=0, tiled=True),
        lax.psum_scatter(grad_in, ("dp", "pair"), scatter_dimension=0, tiled=True),
        lax.psum_scatter(grad_down, ("dp", "pair"), scatter_dimension=0, tiled=True),
    )
    pair_first = (lax.axis_index("pair") == 0).astype(jnp.float32)
    square_part = jnp.sum(
        jnp.stack([jnp.sum(grad_piece * grad_piece) for grad_piece in weight_grads])
    ) + pair_first * jnp.sum(table_grad * table_grad)
    gain_grad, bias_grad, square_sum = lax.psum(
        (jnp.stack([gain_one, gain_two, gain_three]), bias_grad_local, square_part), ("dp", "pair")
    )
    clip_norm = jnp.sqrt(
        square_sum + jnp.sum(gain_grad * gain_grad) + jnp.sum(bias_grad * bias_grad)
    )
    factor = jnp.minimum(1.0, clip_limit / clip_norm)
    table_out = adam_step(embed_table, embed_first, embed_second, table_grad * factor, 1.0, 0.01)
    qkv_out = adam_step(qkv_weight, qkv_first, qkv_second, weight_grads[0] * factor, 0.05, 0.01)
    out_out = adam_step(out_weight, out_first, out_second, weight_grads[1] * factor, 0.05, 0.01)
    in_out = adam_step(in_weight, in_first, in_second, weight_grads[2] * factor, 0.05, 0.01)
    down_out = adam_step(down_weight, down_first, down_second, weight_grads[3] * factor, 0.05, 0.01)
    gains_out = adam_step(norm_gains, gains_first, gains_second, gain_grad * factor, 1.0, 0.0)
    bias_out = adam_step(position_bias, bias_first, bias_second, bias_grad * factor, 0.3, 0.0)
    return (
        loss_value,
        clip_norm,
        table_out[0],
        table_out[1],
        table_out[2],
        qkv_out[0],
        qkv_out[1],
        qkv_out[2],
        out_out[0],
        out_out[1],
        out_out[2],
        in_out[0],
        in_out[1],
        in_out[2],
        down_out[0],
        down_out[1],
        down_out[2],
        gains_out[0],
        gains_out[1],
        gains_out[2],
        bias_out[0],
        bias_out[1],
        bias_out[2],
    )


def local_fast(
    token_owner,
    token_row,
    lengths,
    positives,
    negatives,
    neg_counts,
    embed_table,
    embed_first,
    embed_second,
    qkv_weight,
    qkv_first,
    qkv_second,
    out_weight,
    out_first,
    out_second,
    in_weight,
    in_first,
    in_second,
    down_weight,
    down_first,
    down_second,
    norm_gains,
    gains_first,
    gains_second,
    position_bias,
    bias_first,
    bias_second,
):
    doc_count = lengths.shape[0]
    seq_len = token_row.shape[1]
    model_width = embed_table.shape[1]
    head_count = position_bias.shape[1]
    bucket_count = position_bias.shape[0]
    tok_total = doc_count * seq_len
    owners = lax.axis_size("dp")
    capacity = max(2, 2 * tok_total // owners)
    holders = lax.axis_size("pair")
    shards = (qkv_weight, out_weight, in_weight, down_weight)
    embedded_low, slot_keys, asked_rows, *full = front(
        token_owner.reshape(token_row.shape),
        token_row,
        embed_table,
        shards,
        weight_pieces([shard.shape[1] for shard in shards]),
        capacity,
        owners,
        holders,
        1,
    )
    qkv_full, out_full, in_full, down_full = (
        matrix.reshape(-1, matrix.shape[2]) for matrix in full
    )
    embedded = embedded_low.astype(jnp.float32)
    positions = jnp.arange(seq_len)
    live = positions[None, :] < lengths[:, None]
    offset_bias = bias_rows(position_bias.T, seq_len)
    normed_one, inverse_one = rms_forward(embedded, norm_gains[0])
    normed_one = normed_one.astype(jnp.bfloat16)
    qkv_rows = jnp.dot(normed_one, qkv_full, preferred_element_type=jnp.float32).astype(
        jnp.bfloat16
    )
    attended = attention(lengths, qkv_rows, offset_bias, seq_len)
    residual = embedded + jnp.dot(attended, out_full, preferred_element_type=jnp.float32)
    normed_two, inverse_two = rms_forward(residual, norm_gains[1])
    normed_two = normed_two.astype(jnp.bfloat16)
    hidden = jax.nn.relu(jnp.dot(normed_two, in_full, preferred_element_type=jnp.float32)).astype(
        jnp.bfloat16
    )
    output_rows = residual + jnp.dot(hidden, down_full, preferred_element_type=jnp.float32)
    normed_three, inverse_three = rms_forward(output_rows, norm_gains[2])
    live_rows = live.reshape(-1, 1)
    live_sums = jnp.sum(
        jnp.where(live_rows, normed_three, 0.0).reshape(doc_count, seq_len, model_width), axis=1
    )
    loss_cell, grad_sums = pooled_loss(
        live_sums, lengths, positives, negatives, neg_counts, 3
    )
    grad_three = jnp.where(
        live_rows, jnp.repeat(grad_sums, seq_len, axis=0), 0.0
    )
    qkv_back, out_back, in_back, down_back = (qkv_full, out_full, in_full, down_full)
    grad_output, gain_three = rms_backward(output_rows, inverse_three, norm_gains[2], grad_three)
    grad_branch = grad_output.astype(jnp.bfloat16)
    grad_down = lax.dot_general(
        hidden, grad_branch, CONTRACT_ROWS, preferred_element_type=jnp.float32
    )
    grad_hidden = lax.dot_general(
        grad_branch, down_back, CONTRACT_COLS, preferred_element_type=jnp.float32
    )
    grad_pre = jnp.where(hidden > 0, grad_hidden, 0.0).astype(jnp.bfloat16)
    grad_in = lax.dot_general(
        normed_two, grad_pre, CONTRACT_ROWS, preferred_element_type=jnp.float32
    )
    grad_normed_two = lax.dot_general(
        grad_pre, in_back, CONTRACT_COLS, preferred_element_type=jnp.float32
    )
    grad_res_part, gain_two = rms_backward(residual, inverse_two, norm_gains[1], grad_normed_two)
    grad_residual = grad_output + grad_res_part
    grad_attn_branch = grad_residual.astype(jnp.bfloat16)
    grad_out = lax.dot_general(
        attended, grad_attn_branch, CONTRACT_ROWS, preferred_element_type=jnp.float32
    )
    grad_attended = lax.dot_general(
        grad_attn_branch, out_back, CONTRACT_COLS, preferred_element_type=jnp.float32
    ).astype(jnp.bfloat16)
    parts = owners * holders

    def blocks(*grads):
        return [grad.astype(jnp.bfloat16).reshape(parts, -1, grad.shape[1]) for grad in grads]

    grad_qkv_rows, diagonals, squares, down_grad = attention_back(
        lengths,
        qkv_rows,
        grad_attended,
        offset_bias,
        seq_len,
        blocks(grad_down),
        early_pieces(model_width),
        5,
    )
    bias_grad_local = bias_gradient(diagonals, seq_len, bucket_count)
    grad_qkv = lax.dot_general(
        normed_one, grad_qkv_rows, CONTRACT_ROWS, preferred_element_type=jnp.float32
    )
    grad_normed_one = lax.dot_general(
        grad_qkv_rows, qkv_back, CONTRACT_COLS, preferred_element_type=jnp.float32
    )
    grad_emb_part, gain_one = rms_backward(embedded, inverse_one, norm_gains[0], grad_normed_one)
    grad_embedded = grad_residual + grad_emb_part
    table_grad, total, qkv_grad, out_grad, in_grad = back(
        grad_embedded.astype(jnp.bfloat16),
        slot_keys,
        asked_rows.reshape(1, -1),
        squares,
        bias_grad_local,
        [gain.reshape(1, -1) for gain in (gain_one, gain_two, gain_three)],
        blocks(grad_qkv, grad_out, grad_in),
        late_pieces([grad.shape[1] for grad in (grad_qkv, grad_out, grad_in)]),
        embed_table.shape[0],
        model_width // 128,
        2,
    )
    weight_grads = (qkv_grad, out_grad, in_grad, down_grad)
    norm_cell, loss_cell, *updated = update(
        total,
        loss_cell,
        table_grad,
        (embed_table, embed_first, embed_second),
        (
            norm_gains,
            gains_first,
            gains_second,
            position_bias.T,
            bias_first.T,
            bias_second.T,
        ),
        weight_grads,
        (
            (qkv_weight, qkv_first, qkv_second),
            (out_weight, out_first, out_second),
            (in_weight, in_first, in_second),
            (down_weight, down_first, down_second),
        ),
    )
    return (loss_cell[0, 0], norm_cell[0, 0], *updated[:3], *updated[9:], *updated[3:6], *(new.T for new in updated[6:9]))


def local(*arrays):
    n_dp, n_pair = lax.axis_size("dp"), lax.axis_size("pair")
    lengths, qkv_weight, down_weight = arrays[2], arrays[9], arrays[18]
    fits = (
        n_pair == 4
        and n_dp & (n_dp - 1) == 0
        and qkv_weight.shape[0] % 8 == 0
        and down_weight.shape[0] % 8 == 0
        and lengths.shape[0] == 2
        and 2 * arrays[1].size // n_dp % 128 == 0
    )
    return (local_fast if fits else local_plain)(*arrays)


def solution(mesh):
    return jax.shard_map(
        local,
        mesh=mesh,
        in_specs=(
            P(("dp", "pair"), None, None),
            P(("dp", "pair"), None),
            P(("dp", "pair")),
            P(),
            P(),
            P(),
            P("dp", None),
            P("dp", None),
            P("dp", None),
            P(("dp", "pair"), None),
            P(("dp", "pair"), None),
            P(("dp", "pair"), None),
            P(("dp", "pair"), None),
            P(("dp", "pair"), None),
            P(("dp", "pair"), None),
            P(("dp", "pair"), None),
            P(("dp", "pair"), None),
            P(("dp", "pair"), None),
            P(("dp", "pair"), None),
            P(("dp", "pair"), None),
            P(("dp", "pair"), None),
            P(),
            P(),
            P(),
            P(),
            P(),
            P(),
        ),
        out_specs=(
            P(),
            P(),
            P("dp", None),
            P("dp", None),
            P("dp", None),
            P(("dp", "pair"), None),
            P(("dp", "pair"), None),
            P(("dp", "pair"), None),
            P(("dp", "pair"), None),
            P(("dp", "pair"), None),
            P(("dp", "pair"), None),
            P(("dp", "pair"), None),
            P(("dp", "pair"), None),
            P(("dp", "pair"), None),
            P(("dp", "pair"), None),
            P(("dp", "pair"), None),
            P(("dp", "pair"), None),
            P(),
            P(),
            P(),
            P(),
            P(),
            P(),
        ),
        check_vma=False,
    )
```
